32 devices in a mesh: wide: 8 (over z, y), narrow: 4 (over x, core).
Axes of the slice: x: 2, y: 2, z: 4, core: 2. Of those that a mesh axis runs over, the one named last changes fastest.
Arguments:
- tokens: bfloat16 [8, 1024, 2048], P('wide', 'narrow'), may hold values from -6 to 6
- w_in: bfloat16 [3, 2048, 2048], P(None, None, ('wide', 'narrow')), may hold values from -0.125 to 0.125
- w_out: bfloat16 [2048, 2048], P(('wide', 'narrow')), may hold values from -0.125 to 0.125
- gain_one: bfloat16 [2048], P(('wide', 'narrow')), may hold values from 0.5 to 1.5
- short_kernel: bfloat16 [3, 3, 2048], P(None, None, ('wide', 'narrow')), may hold values from -3 to 3
- decay_rate: bfloat16 [2048, 16], P(('wide', 'narrow')), may hold values from 0.00024414062 to 0.099609375
- pole_angle: bfloat16 [2048, 16], P(('wide', 'narrow')), may hold values from -3.140625 to 3.140625
- residue: bfloat16 [2048, 32], P(('wide', 'narrow')), may hold values from -0.1796875 to 0.1796875
- gain_two: bfloat16 [2048], P(('wide', 'narrow')), may hold values from 0.5 to 1.5
- w_gate: bfloat16 [2048, 5632], P(None, ('wide', 'narrow')), may hold values from -0.125 to 0.125
- w_up: bfloat16 [2048, 5632], P(None, ('wide', 'narrow')), may hold values from -0.125 to 0.125
- w_down: bfloat16 [2048, 5632], P(None, ('wide', 'narrow')), may hold values from -0.078125 to 0.078125
- doc_blocks: int32 [8, 3], P('wide'), may hold values from 1 to 4, 8 in all within a row
- doc_pad: int32 [8, 3], P('wide'), may hold values from 0 to 127
- cotangent: bfloat16 [8, 1024, 2048], P('wide', 'narrow'), may hold values from -6 to 6
Outputs:
- block_output: bfloat16 [8, 1024, 2048], P('wide', 'narrow')
- input_grad: bfloat16 [8, 1024, 2048], P('wide', 'narrow')
- grad_w_in: float32 [3, 2048, 2048], P(None, None, ('wide', 'narrow'))
- grad_w_out: float32 [2048, 2048], P(('wide', 'narrow'))
- grad_gain_one: float32 [2048], P(('wide', 'narrow'))
- grad_short_kernel: float32 [3, 3, 2048], P(None, None, ('wide', 'narrow'))
- grad_decay_rate: float32 [2048, 16], P(('wide', 'narrow'))
- grad_pole_angle: float32 [2048, 16], P(('wide', 'narrow'))
- grad_residue: float32 [2048, 32], P(('wide', 'narrow'))
- grad_gain_two: float32 [2048], P(('wide', 'narrow'))
- grad_w_gate: float32 [2048, 5632], P(None, ('wide', 'narrow'))
- grad_w_up: float32 [2048, 5632], P(None, ('wide', 'narrow'))
- grad_w_down: float32 [2048, 5632], P(None, ('wide', 'narrow'))
The draws below stay inside these ranges and needn't reach their ends.
Inputs may be any that keep to these rules, and one draw needn't show every extreme that they name: `doc_blocks`: each row's 3 counts sum to 8, and the largest is exactly 4.
All inputs are finite; a program needn't handle non-finite values.
Results may differ from the reference program's by a relative error of at most 0.02.
Values may be sent and summed in bfloat16 or wider, within the bound.
No kernel may reach another device: no remote copies, remote signals or barrier semaphores. Data moves between devices by JAX's collectives and lax.ppermute only.
A program may use at most 216 MiB of HBM per device.

```python
import math
import jax
import jax.numpy as jnp
import numpy as np
from jax import lax

D = 2048
FF = 5632
ORDER = 16
BLOCK = 128
DOCS = 3
ROW = 1024
NBLK = 8
ROWS = 8


def touch_ends(values, own_key, least, largest):
    longest = values.shape.index(max(values.shape))
    spots = []
    for shift in (0, 1):
        where = [jax.random.randint(jax.random.fold_in(own_key, axis), (), 0, length) for axis, length in enumerate(values.shape)]
        where[longest] = (where[longest] + shift) % values.shape[longest]
        spots.append(tuple(where))
    return values.at[spots[0]].set(least).at[spots[1]].set(largest)


def raised(drawn, own_key, source, target, shards_of, factor):
    owner, partner = [(jnp.arange(drawn.shape[position]) // (drawn.shape[position] // shards_of)).reshape([-1 if axis == position else 1 for axis in range(drawn.ndim)]) for position in (source, target)]
    chosen = jax.random.permutation(own_key, shards_of)[partner]
    strong = (owner == chosen) | (owner == (partner + shards_of // 2) % shards_of)
    return jnp.where(strong, factor * drawn, drawn)


def block_scale(stream_key, extent, shards, least, top_value):
    def one(position, blocks):
        steps = jax.random.uniform(jax.random.fold_in(jax.random.fold_in(stream_key, 6), position), (blocks,), jnp.float32, least / len(shards), top_value / len(shards))
        return jnp.repeat(jnp.exp(steps), extent[position] // blocks).reshape((-1,) + (1,) * (len(extent) - position - 1))

    factor_of = one(*shards[0])
    for cut in shards[1:]:
        factor_of = factor_of * one(*cut)
    return factor_of


def split_up(count, total, limit, lean):
    portions = [(1 << 20) // math.isqrt(standing ** lean) + 1 for standing in range(2, count + 1)]
    rest, holding = total - limit - (count - 1), [1] * (count - 1)
    while rest > 0:
        movable = [i for i in range(count - 1) if holding[i] < limit]
        mass, left = sum([portions[i] for i in movable]), rest
        for i in movable:
            more = min(limit - holding[i], max(1, left * portions[i] // mass), rest)
            holding[i] = holding[i] + more
            rest = rest - more
    return np.array([limit] + holding)


def ragged(key, count, total, most, skew):
    if count == 2:
        one = jax.random.randint(key, (), max(1, total - most), min(most, total - 1) + 1)
        return jnp.stack([one, total - one])
    lengths = jnp.asarray(split_up(count, total, most, skew), jnp.int32)
    couples = (count - 1) // 2
    giver, sink = lengths[1:1 + 2 * couples:2], lengths[2:2 + 2 * couples:2]
    margin = jnp.minimum(giver - 1, most - sink)
    shifted = jax.random.randint(jax.random.fold_in(key, 1), (couples,), 0, 1 << 20) % (margin + 1)
    lengths = lengths.at[1:1 + 2 * couples:2].set(giver - shifted).at[2:2 + 2 * couples:2].set(sink + shifted)
    return lengths[jax.random.permutation(jax.random.fold_in(key, 2), count)]


def normal_values(stream_key, dims, scale, bound, split=(), held_as=jnp.bfloat16):
    loudness = block_scale(stream_key, dims, split, -0.22, 0.18) if split else 1.0
    result = jax.random.normal(stream_key, dims, jnp.float32) * scale * loudness
    return jnp.minimum(jnp.maximum(result, -bound), bound).astype(held_as)


def heavy_noise(key, shape, width, limit, cuts, heavy, kind=jnp.bfloat16):
    values = width * jax.random.normal(key, shape, jnp.float32)
    if cuts:
        values = values * block_scale(key, shape, cuts, -0.22, 0.18)
    return jnp.clip(raised(values, jax.random.fold_in(key, 3), *heavy), -limit, limit).astype(kind)


def setup_inputs(seed: int = 0) -> dict:
    seeds = jax.random.split(jax.random.key(seed), 16)
    return {
        "tokens": heavy_noise(seeds[0], (ROWS, ROW, D), 1.0, 6.0, ((0, 8), (1, 4)), (0, 2, 8, 2.0)),
        "w_in": normal_values(seeds[1], (3, D, D), D ** -0.5, 0.125, ((2, 32),)),
        "w_out": normal_values(seeds[2], (D, D), D ** -0.5, 0.125, ((0, 32),)),
        "gain_one": jnp.clip(1.0 + 0.1 * jax.random.normal(seeds[3], (D,), jnp.float32), 0.5, 1.5).astype(jnp.bfloat16),
        "short_kernel": normal_values(seeds[4], (3, 3, D), 0.6, 3.0, ((2, 32),)),
        "decay_rate": jnp.clip(jnp.exp(math.log(0.099609375) - 6.011267 * jax.random.uniform(seeds[5], (D, ORDER), jnp.float32) ** block_scale(seeds[5], (D, ORDER), ((0, 32),), -0.2, 0.2)), 0.00024414062, 0.099609375).astype(jnp.bfloat16),
        "pole_angle": jnp.clip(jax.random.uniform(seeds[6], (D, ORDER), jnp.float32, -3.140625, 3.140625), -3.140625, 3.140625).astype(jnp.bfloat16),
        "residue": normal_values(seeds[7], (D, 2 * ORDER), 0.03, 0.1796875, ((0, 32),)),
        "gain_two": jnp.clip(1.0 + 0.1 * jax.random.normal(seeds[8], (D,), jnp.float32), 0.5, 1.5).astype(jnp.bfloat16),
        "w_gate": normal_values(seeds[9], (D, FF), D ** -0.5, 0.125, ((1, 32),)),
        "w_up": normal_values(seeds[10], (D, FF), D ** -0.5, 0.125, ((1, 32),)),
        "w_down": normal_values(seeds[11], (D, FF), FF ** -0.5, 0.078125, ((1, 32),)),
        "doc_blocks": jax.vmap(lambda own: ragged(own, DOCS, NBLK, NBLK // 2, 2))(jax.random.split(seeds[12], ROWS)).reshape((ROWS, DOCS)).astype(jnp.int32),
        "doc_pad": touch_ends(jax.random.randint(seeds[13], (ROWS, DOCS), 0, BLOCK), jax.random.fold_in(seeds[13], 1), 0, BLOCK - 1).astype(jnp.int32),
        "cotangent": heavy_noise(seeds[14], (ROWS, ROW, D), 1.0, 6.0, ((0, 8), (1, 4)), (0, 2, 8, 2.0)),
    }


epsilon = 1e-06
highest = lax.Precision.HIGHEST

@jax.custom_vjp
def low(v):
    return lax.optimization_barrier(v.astype(jnp.bfloat16)).astype(jnp.float32)

@jax.custom_vjp
def low_back(v):
    return v

def low_keep(v):
    return (low(v), None)

def low_pass(kept, grad):
    return (grad,)

def back_keep(v):
    return (v, None)

def back_low(kept, grad):
    return (low(grad),)
low.defvjp(low_keep, low_pass)
low_back.defvjp(back_keep, back_low)

def layout(doc_blocks, doc_pad):
    block_ends = (jnp.cumsum(doc_blocks) * BLOCK).astype(jnp.int32)
    starts = (block_ends - doc_blocks * BLOCK).astype(jnp.int32)
    places = jnp.arange(ROW, dtype=jnp.int32)
    inside = ((places[None, :] >= starts[:, None]) & (places[None, :] < block_ends[:, None])).astype(jnp.float32)
    living = (places[None, :] >= starts[:, None]) & (places[None, :] < (block_ends - doc_pad)[:, None])
    live_mask = lax.optimization_barrier(jnp.sum(living.astype(jnp.float32), axis=0))
    opening = lax.optimization_barrier(jnp.sum((places[None, :] == starts[:, None]).astype(jnp.float32), axis=0))
    return (inside, live_mask, opening)

def rms_norm(values, gain):
    return values * lax.rsqrt(lax.optimization_barrier(jnp.mean(values * values, axis=-1, keepdims=True)) + epsilon) * gain

def earlier(values):
    return jnp.concatenate([jnp.zeros_like(values[:1]), values[:-1]], axis=0)

def short_mix(masked, kernel_taps, opening):
    keep_one = (1.0 - opening)[:, None]
    keep_two = keep_one * earlier(keep_one)
    once = earlier(masked)
    return kernel_taps[0] * masked + kernel_taps[1] * keep_one * once + kernel_taps[2] * keep_two * earlier(once)

def modal_filter(decay_rate, pole_angle, residue, steps):
    pole_count = decay_rate.shape[1]
    lag_steps = jnp.arange(steps, dtype=jnp.float32)
    fading = jnp.exp(-decay_rate[:, :, None] * lag_steps)
    turning = pole_angle[:, :, None] * lag_steps
    waves = residue[:, :pole_count, None] * jnp.cos(turning) + residue[:, pole_count:, None] * jnp.sin(turning)
    return lax.optimization_barrier(jnp.sum(fading * waves, axis=1))

def long_conv(signal, filter_taps, inside):
    slots = signal.shape[0]
    fft_size = 2 * slots
    spectrum = jnp.fft.rfft(filter_taps.T, n=fft_size, axis=0)
    pieces = signal[None] * inside[:, :, None]
    mixed = jnp.fft.irfft(jnp.fft.rfft(pieces, n=fft_size, axis=1) * spectrum[None], n=fft_size, axis=1)[:, :slots]
    return lax.optimization_barrier(jnp.sum(mixed * inside[:, :, None], axis=0))

def forward_row(tokens, w_in, w_out, gain_one, short_kernel, decay_rate, pole_angle, residue, gain_two, w_gate, w_up, w_down, inside, live_mask, opening):
    model_width = tokens.shape[1]
    normed = low(rms_norm(tokens, gain_one))
    projected = jnp.concatenate([jnp.dot(normed, w_in[stream], precision=highest) for stream in range(3)], axis=1)
    mixed = low_back(projected) * live_mask[:, None]
    short = short_mix(mixed, short_kernel.reshape(3, 3 * model_width), opening)
    query_part = short[:, :model_width]
    key_part = short[:, model_width:2 * model_width]
    value_part = short[:, 2 * model_width:]
    long_out = long_conv(key_part * value_part, modal_filter(decay_rate, pole_angle, residue, tokens.shape[0]), inside)
    gated = low(query_part * long_out)
    middle = tokens + low_back(jnp.dot(gated, w_out, precision=highest))
    normed_two = low(rms_norm(middle, gain_two))
    gate_pre = low_back(jnp.dot(normed_two, w_gate, precision=highest))
    up_pre = low_back(jnp.dot(normed_two, w_up, precision=highest))
    hidden = low(jax.nn.silu(gate_pre) * up_pre)
    return middle + low_back(jnp.dot(hidden, w_down.T, precision=highest))

def reference(tokens, w_in, w_out, gain_one, short_kernel, decay_rate, pole_angle, residue, gain_two, w_gate, w_up, w_down, doc_blocks, doc_pad, cotangent):
    weights = tuple((weight.astype(jnp.float32) for weight in (w_in, w_out, gain_one, short_kernel, decay_rate, pole_angle, residue, gain_two, w_gate, w_up, w_down)))
    row_count = tokens.shape[0]
    group_rows = math.gcd(row_count, max(1, 4096 // ROW))
    group_count = row_count // group_rows

    def regroup(source):
        return source.reshape((group_count, group_rows) + source.shape[1:])

    def one_group(carry, pieces):
        block_tokens, blocks, pad_counts, block_cot = pieces
        inside, live_mask, opening = jax.vmap(layout)(blocks, pad_counts)

        def run_block(token_input, *params):
            mapped = jax.vmap(forward_row, in_axes=(0,) + (None,) * 11 + (0, 0, 0))
            return mapped(token_input, *params, inside, live_mask, opening)
        outputs, pull = jax.vjp(run_block, block_tokens.astype(jnp.float32), *weights)
        gradients = pull(block_cot.astype(jnp.float32))
        summed = tuple((held + fresh for held, fresh in zip(carry, gradients[1:])))
        return (summed, (outputs.astype(jnp.bfloat16), gradients[0].astype(jnp.bfloat16)))
    zero_grads = tuple((jnp.zeros(weight.shape, jnp.float32) for weight in weights))
    totals, (outputs, input_grads) = lax.scan(one_group, zero_grads, (regroup(tokens), regroup(doc_blocks), regroup(doc_pad), regroup(cotangent)))
    return (outputs.reshape(tokens.shape), input_grads.reshape(tokens.shape), totals[0], totals[1], totals[2], totals[3], totals[4], totals[5], totals[6], totals[7], totals[8], totals[9], totals[10])
```

```python
from functools import partial

import jax
import jax.numpy as jnp
import numpy as np
from jax import lax
from jax.experimental import pallas as pl
from jax.experimental.pallas import tpu as pltpu
from jax.sharding import PartitionSpec as P

BLOCK = 128
LONGEST = 4
SPAN = LONGEST * BLOCK
FREQ = SPAN

epsilon = 1e-06
bf16 = jnp.bfloat16
f32 = jnp.float32


def transform():
    k = np.arange(FREQ)[:, None] * 2 + 1
    t = np.arange(SPAN)[None, :]
    turn = (k * t % (4 * SPAN)) * (2 * np.pi / (4 * SPAN))
    return np.concatenate([np.cos(turn), -np.sin(turn)], axis=0).astype(np.float32)


def nn(a, b):
    return lax.dot_general(a, b, (((1,), (0,)), ((), ())), preferred_element_type=f32)


def nt(a, b):
    return lax.dot_general(a, b, (((1,), (1,)), ((), ())), preferred_element_type=f32)


def tn(a, b):
    return lax.dot_general(a, b, (((0,), (0,)), ((), ())), preferred_element_type=f32)


def swap(values, axis, shift):
    size = lax.axis_size(axis)
    return lax.ppermute(values, axis, [(i, i ^ shift) for i in range(size)])


def gather_wide(piece, axis=0):
    size = lax.axis_size("wide")
    parts = [piece] + [swap(piece, "wide", k) for k in range(2, size, 2)]
    near = jnp.concatenate(parts, axis=axis)
    return near, swap(near, "wide", 1)


def scatter_wide(near, far, axis=0):
    size = lax.axis_size("wide")
    got = swap(far, "wide", 1)
    total = near.astype(f32) + got.astype(f32)
    chunks = jnp.split(total, size // 2, axis=axis)
    out = chunks[0]
    for k in range(1, size // 2):
        out = out + swap(chunks[k].astype(bf16), "wide", 2 * k).astype(f32)
    return out


def gather_rows(own):
    size = lax.axis_size("narrow")
    even = jnp.concatenate([own] + [swap(own, "narrow", k) for k in range(2, size, 2)], axis=0)
    return jnp.concatenate([even, swap(even, "narrow", 1)], axis=0)


def scatter_rows(even, odd):
    size = lax.axis_size("narrow")
    got = swap(odd, "narrow", 1)
    total = even.astype(f32) + got.astype(f32)
    rows = total.shape[0] // (size // 2)
    out = total[:rows]
    for k in range(1, size // 2):
        chunk = total[k * rows : (k + 1) * rows].astype(bf16)
        out = out + swap(chunk, "narrow", 2 * k).astype(f32)
    return out


def inverse_rms(values):
    return lax.rsqrt(jnp.mean(values * values, axis=-1, keepdims=True) + epsilon)


def norm_back(values, rate, gain, grad):
    a = grad * gain
    inner = jnp.mean(a * values, axis=-1, keepdims=True)
    return rate * a - values * (rate * rate * rate) * inner


def filter_kernel(base_re, base_im, step_re, step_im, out):
    poles = base_re.shape[0]
    width = out.shape[1]
    for g in range(width // 128 if width % 128 == 0 else 1):
        lanes = pl.ds(g * 128, min(128, width))
        start = tuple(base_re[j, :, lanes] for j in range(poles)) + tuple(
            base_im[j, :, lanes] for j in range(poles)
        )

        def step(b, state):
            total = state[0]
            for j in range(1, poles):
                total = total + state[j]
            out[pl.ds(pl.multiple_of(b * 8, 8), 8), lanes] = total
            new_re, new_im = [], []
            for j in range(poles):
                sr = step_re[j, :, lanes]
                si = step_im[j, :, lanes]
                new_re.append(state[j] * sr - state[poles + j] * si)
                new_im.append(state[j] * si + state[poles + j] * sr)
            return tuple(new_re) + tuple(new_im)

        lax.fori_loop(0, SPAN // 8, step, start)


def filter_taps(base_re, base_im, step_re, step_im):
    width = base_re.shape[2]
    return pl.pallas_call(
        filter_kernel,
        out_shape=jax.ShapeDtypeStruct((SPAN, width), f32),
        cost_estimate=pl.CostEstimate(
            flops=16 * 7 * SPAN * width, bytes_accessed=4 * SPAN * width, transcendentals=0
        ),
        name="taps",
    )(base_re, base_im, step_re, step_im)


def moment_kernel(grad, step_re, step_im, sum_re, sum_im, mom_re, mom_im):
    poles = step_re.shape[0]
    width = grad.shape[1]
    per = 8
    for g in range(width // 128 if width % 128 == 0 else 1):
        lanes = pl.ds(g * 128, min(128, width))
        for j0 in range(0, poles, per):
            zero = jnp.zeros((8, min(128, width)), f32)

            def step(i, state):
                b = SPAN // 8 - 1 - i
                value = grad[pl.ds(pl.multiple_of(b * 8, 8), 8), lanes]
                new = []
                for n in range(per):
                    sr = step_re[j0 + n, :, lanes]
                    si = step_im[j0 + n, :, lanes]
                    pr, pi, qr, qi = state[4 * n : 4 * n + 4]
                    ur, ui = pr + qr, pi + qi
                    new += [
                        pr * sr - pi * si + value,
                        pr * si + pi * sr,
                        ur * sr - ui * si,
                        ur * si + ui * sr,
                    ]
                return tuple(new)

            state = lax.fori_loop(0, SPAN // 8, step, (zero,) * (4 * per))
            for n in range(per):
                sum_re[j0 + n, :, lanes] = state[4 * n]
                sum_im[j0 + n, :, lanes] = state[4 * n + 1]
                mom_re[j0 + n, :, lanes] = state[4 * n + 2]
                mom_im[j0 + n, :, lanes] = state[4 * n + 3]


def filter_moments(grad, step_re, step_im):
    poles, _, width = step_re.shape
    shape = jax.ShapeDtypeStruct((poles, 8, width), f32)
    return pl.pallas_call(
        moment_kernel,
        out_shape=(shape,) * 4,
        cost_estimate=pl.CostEstimate(
            flops=16 * 15 * SPAN * width, bytes_accessed=4 * SPAN * width, transcendentals=0
        ),
        name="moments",
    )(grad, step_re, step_im)


LIVE, KEEP_ONE, KEEP_TWO = 0, 1, 2


def load_masked(order, proj, table, m_scr):
    pieces, rows, _ = proj.shape
    m_scr[0:8, :] = jnp.zeros_like(m_scr[0:8, :])

    def piece(b, _):
        p = order[b]
        at = pl.multiple_of(b * rows, rows)
        live = table[pl.ds(at, rows), LIVE : LIVE + 1]
        m_scr[pl.ds(pl.multiple_of(at + 8, 8), rows), :] = proj[p] * live
        return 0

    lax.fori_loop(0, pieces, piece, 0)


def short_block(m_scr, taps, table, at):
    window = m_scr[pl.ds(at, BLOCK + 8), :]
    one = table[pl.ds(at, BLOCK), KEEP_ONE : KEEP_ONE + 1]
    two = table[pl.ds(at, BLOCK), KEEP_TWO : KEEP_TWO + 1]
    here = window[8:]
    once = window[7 : BLOCK + 7] * one
    twice = window[6 : BLOCK + 6] * two
    short = taps[0:1, :] * here + taps[1:2, :] * once + taps[2:3, :] * twice
    return short, here, once, twice


def pack_document(source, packed, first, count):
    blocks = source.shape[0] // BLOCK
    for kb in range(LONGEST):
        at = pl.multiple_of(jnp.minimum(first + kb, blocks - 1) * BLOCK, BLOCK)
        inside = (kb < count).astype(f32)
        packed[kb * BLOCK : (kb + 1) * BLOCK, :] = (source[pl.ds(at, BLOCK), :] * inside).astype(bf16)


def place_document(result, target, first, count):
    for kb in range(LONGEST):

        @pl.when(kb < count)
        def _():
            at = pl.multiple_of((first + kb) * BLOCK, BLOCK)
            target[pl.ds(at, BLOCK), :] = result[kb * BLOCK : (kb + 1) * BLOCK, :]


def forward_kernel(
    order, first, count, proj, taps, table, spectrum, fwd, inv, gated, long_out, seen, m_scr, u_scr, q_scr, packed
):
    width = long_out.shape[1]
    pieces, rows, _ = proj.shape
    blocks = long_out.shape[0] // BLOCK
    load_masked(order, proj, table, m_scr)

    def block(n, _):
        at = pl.multiple_of(n * BLOCK, BLOCK)
        short, _, _, _ = short_block(m_scr, taps, table, at)
        q_scr[pl.ds(at, BLOCK), :] = short[:, :width]
        u_scr[pl.ds(at, BLOCK), :] = short[:, width : 2 * width] * short[:, 2 * width :]
        return 0

    lax.fori_loop(0, blocks, block, 0)

    def document(d, _):
        pack_document(u_scr, packed, first[d], count[d])
        both = jnp.dot(fwd[...], packed[...], preferred_element_type=f32)
        seen[d] = both.astype(bf16)
        re, im = both[:FREQ], both[FREQ:]
        hr, hi = spectrum[:FREQ], spectrum[FREQ:]
        answer = jnp.concatenate([re * hr - im * hi, re * hi + im * hr], axis=0).astype(bf16)
        result = jnp.dot(inv[...], answer, preferred_element_type=f32)
        place_document(result, long_out, first[d], count[d])
        return 0

    lax.fori_loop(0, seen.shape[0], document, 0)

    def piece(b, _):
        at = pl.multiple_of(b * rows, rows)
        gated[order[b]] = (q_scr[pl.ds(at, rows), :] * long_out[pl.ds(at, rows), :]).astype(bf16)
        return 0

    lax.fori_loop(0, pieces, piece, 0)


def backward_kernel(
    order, first, count, proj, d_gated, long_out, seen, taps, table, spectrum, fwd, inv,
    dz, d_filter, d_taps, m_scr, dy_scr, k_scr, v_scr, ds_scr, packed, d_spec,
):
    width = long_out.shape[1]
    pieces, rows, _ = proj.shape
    slots = long_out.shape[0]
    blocks = slots // BLOCK
    per_piece = rows // BLOCK
    load_masked(order, proj, table, m_scr)
    ds_scr[slots : slots + 8, :] = jnp.zeros_like(ds_scr[slots : slots + 8, :])

    def block(n, _):
        at = pl.multiple_of(n * BLOCK, BLOCK)
        short, _, _, _ = short_block(m_scr, taps, table, at)
        within = pl.multiple_of((n % per_piece) * BLOCK, BLOCK)
        dg = d_gated[order[n // per_piece], pl.ds(within, BLOCK), :]
        dy_scr[pl.ds(at, BLOCK), :] = dg * short[:, :width]
        ds_scr[pl.ds(at, BLOCK), :width] = dg * long_out[pl.ds(at, BLOCK), :]
        k_scr[pl.ds(at, BLOCK), :] = short[:, width : 2 * width]
        v_scr[pl.ds(at, BLOCK), :] = short[:, 2 * width :]
        return 0

    lax.fori_loop(0, blocks, block, 0)
    d_spec[...] = jnp.zeros_like(d_spec)

    def document(d, _):
        pack_document(dy_scr, packed, first[d], count[d])
        both = jnp.dot(fwd[...], packed[...], preferred_element_type=f32)
        re, im = both[:FREQ], both[FREQ:]
        hr, hi = spectrum[:FREQ], spectrum[FREQ:]
        answer = jnp.concatenate([re * hr + im * hi, im * hr - re * hi], axis=0).astype(bf16)
        result = jnp.dot(inv[...], answer, preferred_element_type=f32)
        ur, ui = seen[d, :FREQ].astype(f32), seen[d, FREQ:].astype(f32)
        d_spec[:FREQ] += re * ur + im * ui
        d_spec[FREQ:] += im * ur - re * ui
        for kb in range(LONGEST):

            @pl.when(kb < count[d])
            def _():
                at = pl.multiple_of((first[d] + kb) * BLOCK, BLOCK)
                du = result[kb * BLOCK : (kb + 1) * BLOCK, :]
                ds_scr[pl.ds(at, BLOCK), width : 2 * width] = du * v_scr[pl.ds(at, BLOCK), :]
                ds_scr[pl.ds(at, BLOCK), 2 * width :] = du * k_scr[pl.ds(at, BLOCK), :]

        return 0

    lax.fori_loop(0, seen.shape[0], document, 0)
    d_filter[...] = jnp.dot(inv[...], d_spec[...].astype(bf16), preferred_element_type=f32)
    d_taps[...] = jnp.zeros_like(d_taps)

    def back(n, _):
        at = pl.multiple_of(n * BLOCK, BLOCK)
        window = m_scr[pl.ds(at, BLOCK + 8), :]
        ahead = ds_scr[pl.ds(at, BLOCK + 8), :]
        one = table[pl.ds(at, BLOCK + 8), KEEP_ONE : KEEP_ONE + 1]
        two = table[pl.ds(at, BLOCK + 8), KEEP_TWO : KEEP_TWO + 1]
        live = table[pl.ds(at, BLOCK), LIVE : LIVE + 1]
        ds = ahead[:BLOCK]
        ahead_one = ahead * one
        ahead_two = ahead * two
        dm = (
            taps[0:1, :] * ds
            + taps[1:2, :] * ahead_one[1 : BLOCK + 1]
            + taps[2:3, :] * ahead_two[2 : BLOCK + 2]
        )
        d_taps[0:1, :] += jnp.sum(window[8:] * ds, axis=0, keepdims=True)
        d_taps[1:2, :] += jnp.sum(window[7 : BLOCK + 7] * ahead_one[:BLOCK], axis=0, keepdims=True)
        d_taps[2:3, :] += jnp.sum(window[6 : BLOCK + 6] * ahead_two[:BLOCK], axis=0, keepdims=True)
        within = pl.multiple_of((n % per_piece) * BLOCK, BLOCK)
        dz[order[n // per_piece], pl.ds(within, BLOCK), :] = (dm * live).astype(bf16)
        return 0

    lax.fori_loop(0, blocks, back, 0)


smem = pl.BlockSpec(memory_space=pltpu.SMEM)
vmem = pl.BlockSpec(memory_space=pltpu.VMEM)


def mixer_forward(order, first, count, proj, taps, table, spectrum, fwd, inv):
    pieces, rows, three = proj.shape
    width = three // 3
    slots = pieces * rows
    docs = first.shape[0]
    return pl.pallas_call(
        forward_kernel,
        out_shape=(
            jax.ShapeDtypeStruct((pieces, rows, width), bf16),
            jax.ShapeDtypeStruct((slots, width), f32),
            jax.ShapeDtypeStruct((docs, 2 * FREQ, width), bf16),
        ),
        in_specs=[smem] * 3 + [vmem] * 6,
        out_specs=(vmem,) * 3,
        scratch_shapes=[
            pltpu.VMEM((slots + 8, three), f32),
            pltpu.VMEM((slots, width), f32),
            pltpu.VMEM((slots, width), f32),
            pltpu.VMEM((SPAN, width), bf16),
        ],
        compiler_params=pltpu.CompilerParams(vmem_limit_bytes=40 * 2**20),
        cost_estimate=pl.CostEstimate(
            flops=docs * 8 * FREQ * SPAN * width,
            bytes_accessed=slots * three * 4 + 8 * slots * width,
            transcendentals=0,
        ),
        name="mixer_forward",
    )(order, first, count, proj, taps, table, spectrum, fwd, inv)


def mixer_backward(order, first, count, proj, d_gated, long_out, seen, taps, table, spectrum, fwd, inv):
    pieces, rows, three = proj.shape
    width = three // 3
    slots = pieces * rows
    docs = first.shape[0]
    return pl.pallas_call(
        backward_kernel,
        out_shape=(
            jax.ShapeDtypeStruct((pieces, rows, three), bf16),
            jax.ShapeDtypeStruct((SPAN, width), f32),
            jax.ShapeDtypeStruct((8, three), f32),
        ),
        in_specs=[smem] * 3 + [vmem] * 9,
        out_specs=(vmem,) * 3,
        scratch_shapes=[
            pltpu.VMEM((slots + 8, three), f32),
            pltpu.VMEM((slots, width), f32),
            pltpu.VMEM((slots, width), f32),
            pltpu.VMEM((slots, width), f32),
            pltpu.VMEM((slots + 8, three), f32),
            pltpu.VMEM((SPAN, width), bf16),
            pltpu.VMEM((2 * FREQ, width), f32),
        ],
        compiler_params=pltpu.CompilerParams(vmem_limit_bytes=48 * 2**20),
        cost_estimate=pl.CostEstimate(
            flops=docs * 10 * FREQ * SPAN * width,
            bytes_accessed=slots * three * 8 + 8 * slots * width,
            transcendentals=0,
        ),
        name="mixer_backward",
    )(order, first, count, proj, d_gated, long_out, seen, taps, table, spectrum, fwd, inv)


def layout(doc_blocks, doc_pad, slots):
    block_ends = jnp.cumsum(doc_blocks) * BLOCK
    starts = block_ends - doc_blocks * BLOCK
    places = jnp.arange(slots, dtype=jnp.int32)
    living = (places[None, :] >= starts[:, None]) & (
        places[None, :] < (block_ends - doc_pad)[:, None]
    )
    live = jnp.sum(living.astype(f32), axis=0)
    opening = jnp.sum((places[None, :] == starts[:, None]).astype(f32), axis=0)
    one = 1.0 - opening
    one = one * (places > 0)
    two = one * jnp.concatenate([jnp.zeros((1,), f32), one[:-1]])
    table = jnp.stack([live, one, two], axis=1)
    table = jnp.concatenate([table, jnp.zeros((8, 3), f32)], axis=0)
    return table, starts // BLOCK


def picked(index, count, values):
    hot = index[:, None] == jnp.arange(count)[None, :]
    shape = hot.shape + (1,) * (values.ndim - 1)
    return jnp.sum(jnp.where(hot.reshape(shape), values[None], 0), axis=1)


def body(
    tokens, w_in, w_out, gain_one, short_kernel, decay_rate, pole_angle, residue,
    gain_two, w_gate, w_up, w_down, doc_blocks, doc_pad, cotangent,
):
    wide, narrow = lax.axis_size("wide"), lax.axis_size("narrow")
    wide_at, narrow_at = lax.axis_index("wide"), lax.axis_index("narrow")
    _, local_rows, width = tokens.shape
    slots = local_rows * narrow
    source = tokens[0].astype(f32)
    upstream_low = cotangent[0]
    poles = decay_rate.shape[1]
    own = w_in.shape[2]
    half = own * wide // 2

    small = jnp.concatenate(
        [
            short_kernel.reshape(9, own),
            decay_rate.T,
            pole_angle.T,
            residue.T,
            gain_one[None],
            gain_two[None],
        ],
        axis=0,
    )
    small_halves = gather_wide(small, axis=1)
    count_small = small.shape[0]
    gains = jnp.stack([s[count_small - 2 :].reshape(2, wide // 2, own) for s in small_halves], axis=2)
    gains = gains.reshape(2, wide, own).transpose(1, 0, 2)
    gains = picked(jnp.arange(wide) ^ wide_at, wide, gains.astype(f32)).astype(bf16)
    gain_parts = gather_rows(gains[None])
    offsets = list(range(0, narrow, 2)) + list(range(1, narrow, 2))
    place_of = np.argsort(np.array(offsets))
    order = jnp.asarray(place_of, jnp.int32)
    order = picked(jnp.arange(narrow) ^ narrow_at, narrow, order)
    gain_all = picked(order, narrow, gain_parts.astype(f32))
    gain_all = gain_all.transpose(2, 1, 0, 3).reshape(2, width)
    gain_first, gain_last = gain_all[0], gain_all[1]

    table, first = layout(doc_blocks[0], doc_pad[0], slots)
    count = doc_blocks[0]

    in_piece = w_in.transpose(0, 2, 1)
    out_piece = w_out
    gate_piece, up_piece, down_piece = w_gate.T, w_up.T, w_down.T
    in_halves = gather_wide(in_piece, axis=1)
    out_halves = gather_wide(out_piece)
    gate_halves = gather_wide(gate_piece)
    up_halves = gather_wide(up_piece)
    down_halves = gather_wide(down_piece)

    rate_first = inverse_rms(source)
    low_first = (source * rate_first * gain_first).astype(bf16)
    rows_first = gather_rows(low_first)
    rows_upstream = gather_rows(upstream_low)

    matrix = transform()
    fwd = jnp.asarray(matrix, bf16)
    inv = jnp.asarray(matrix.T / SPAN, bf16)

    tables, kept = [], []
    for s in range(2):
        block = small_halves[s].astype(f32)
        taps = block[:9].reshape(3, 3 * half)
        taps = jnp.concatenate([taps, jnp.zeros((5, 3 * half), f32)], axis=0)
        decay = block[9 : 9 + poles][:, None, :]
        angle = block[9 + poles : 9 + 2 * poles][:, None, :]
        res_re = block[9 + 2 * poles : 9 + 3 * poles][:, None, :]
        res_im = -block[9 + 3 * poles : 9 + 4 * poles][:, None, :]
        lag = jnp.arange(8, dtype=f32)[None, :, None]
        fade = jnp.exp(-decay * lag)
        power_re, power_im = fade * jnp.cos(angle * lag), fade * jnp.sin(angle * lag)
        fade_step = jnp.exp(-decay * 8.0)
        step_re = jnp.broadcast_to(fade_step * jnp.cos(angle * 8.0), power_re.shape)
        step_im = jnp.broadcast_to(fade_step * jnp.sin(angle * 8.0), power_re.shape)
        filt = filter_taps(
            res_re * power_re - res_im * power_im,
            res_re * power_im + res_im * power_re,
            step_re,
            step_im,
        )
        spectrum = lax.dot_general(
            jnp.asarray(matrix),
            filt,
            (((1,), (0,)), ((), ())),
            precision=lax.Precision.HIGHEST,
            preferred_element_type=f32,
        )
        tables.append((taps, spectrum))
        kept.append((power_re, power_im, step_re, step_im, res_re[:, 0], -res_im[:, 0]))

    even = slots // 2
    mixed = []
    for s in range(2):
        taps, spectrum = tables[s]
        weight = in_halves[s].reshape(3 * half, width)
        proj = nt(rows_first, weight).reshape(narrow, local_rows, 3 * half)
        gated, long_out, seen = mixer_forward(
            order, first, count, proj, taps, table, spectrum, fwd, inv
        )
        mixed.append((proj, gated.reshape(slots, half), long_out, seen))
    share_odd = sum(nn(mixed[s][1][even:], out_halves[s]) for s in range(2)).astype(bf16)
    share_even = sum(nn(mixed[s][1][:even], out_halves[s]) for s in range(2)).astype(bf16)
    middle = source + scatter_rows(share_even, share_odd)
    rate_last = inverse_rms(middle)
    rows_second = gather_rows((middle * rate_last * gain_last).astype(bf16))

    down_even, down_odd = 0.0, 0.0
    second_even, second_odd = 0.0, 0.0
    shares = []
    for s in range(2):
        gate_pre = nt(rows_second, gate_halves[s])
        up_pre = nt(rows_second, up_halves[s])
        sig = jax.nn.sigmoid(gate_pre)
        silu = gate_pre * sig
        hidden = (silu * up_pre).astype(bf16)
        d_hidden = nt(rows_upstream, down_halves[s])
        d_gate = (d_hidden * up_pre * sig * (1.0 + gate_pre * (1.0 - sig))).astype(bf16)
        d_up = (d_hidden * silu).astype(bf16)
        second_odd = second_odd + nn(d_gate[even:], gate_halves[s]) + nn(d_up[even:], up_halves[s])
        second_even = second_even + nn(d_gate[:even], gate_halves[s]) + nn(d_up[:even], up_halves[s])
        down_odd = down_odd + nn(hidden[even:], down_halves[s])
        down_even = down_even + nn(hidden[:even], down_halves[s])
        shares.append(
            (
                tn(d_gate, rows_second).astype(bf16),
                tn(d_up, rows_second).astype(bf16),
                tn(hidden, rows_upstream).astype(bf16),
            )
        )
    d_second = scatter_rows(second_even.astype(bf16), second_odd.astype(bf16))
    down_out = scatter_rows(down_even.astype(bf16), down_odd.astype(bf16))
    block_output = (middle + down_out).astype(bf16)
    upstream = upstream_low.astype(f32)
    d_middle = upstream + norm_back(middle, rate_last, gain_last, d_second)
    grad_gain_two = jnp.sum(d_second * middle * rate_last, axis=0)
    gate_share, up_share, down_share = (
        scatter_wide(shares[0][i], shares[1][i]) for i in range(3)
    )

    rows_dmiddle = gather_rows(d_middle.astype(bf16))
    out_parts, in_parts, small_parts = [], [], []
    normed_even, normed_odd = 0.0, 0.0
    for s in range(2):
        proj, gated, long_out, seen = mixed[s]
        taps, spectrum = tables[s]
        d_gated = nt(rows_dmiddle, out_halves[s]).reshape(narrow, local_rows, half)
        out_parts.append(tn(gated, rows_dmiddle).astype(bf16))
        dz, d_filter, d_taps = mixer_backward(
            order, first, count, proj, d_gated, long_out, seen, taps, table, spectrum, fwd, inv
        )
        dz = dz.reshape(slots, 3 * half)
        weight = in_halves[s].reshape(3 * half, width)
        normed_odd = normed_odd + nn(dz[even:], weight)
        normed_even = normed_even + nn(dz[:even], weight)
        in_parts.append(tn(dz, rows_first).astype(bf16).reshape(3, half, width))
        power_re, power_im, step_re, step_im, res_re, res_im = kept[s]
        sum_re, sum_im, mom_re, mom_im = filter_moments(d_filter, step_re, step_im)
        lag = jnp.arange(8, dtype=f32)[None, :, None]
        full_re = lag * sum_re + 8.0 * mom_re
        full_im = lag * sum_im + 8.0 * mom_im
        grad_re = jnp.sum(power_re * sum_re - power_im * sum_im, axis=1)
        grad_im = jnp.sum(power_re * sum_im + power_im * sum_re, axis=1)
        lag_re = jnp.sum(power_re * full_re - power_im * full_im, axis=1)
        lag_im = jnp.sum(power_re * full_im + power_im * full_re, axis=1)
        small_parts.append(
            jnp.concatenate(
                [
                    d_taps[:3].reshape(9, half),
                    -(res_re * lag_re + res_im * lag_im),
                    res_im * lag_re - res_re * lag_im,
                    grad_re,
                    grad_im,
                ],
                axis=0,
            ).astype(bf16)
        )
    d_normed = scatter_rows(normed_even.astype(bf16), normed_odd.astype(bf16))
    out_share = scatter_wide(out_parts[0], out_parts[1])
    in_share = scatter_wide(in_parts[0], in_parts[1], axis=1)
    small_share = scatter_wide(small_parts[0], small_parts[1], axis=1)
    input_grad = (d_middle + norm_back(source, rate_first, gain_first, d_normed)).astype(bf16)
    grad_gain_one = jnp.sum(d_normed * source * rate_first, axis=0)

    grads = jnp.stack([grad_gain_one, grad_gain_two]).reshape(2, wide, narrow, own)
    grads = picked(jnp.arange(narrow) ^ narrow_at, narrow, grads.transpose(2, 1, 0, 3))
    grads = jnp.stack([grads[k] for k in offsets])
    even_places = narrow // 2
    total = grads[:even_places] + swap(grads[even_places:], "narrow", 1)
    summed = total[0]
    for k in range(1, even_places):
        summed = summed + swap(total[k], "narrow", 2 * k)
    summed = picked(jnp.arange(wide) ^ wide_at, wide, summed)
    pairs = summed.reshape(wide // 2, 2, 2, own)
    total = pairs[:, 0] + swap(pairs[:, 1], "wide", 1)
    gain_share = total[0]
    for k in range(1, wide // 2):
        gain_share = gain_share + swap(total[k], "wide", 2 * k)

    at = 9 + poles
    return (
        block_output[None],
        input_grad[None],
        in_share.transpose(0, 2, 1),
        out_share,
        gain_share[0],
        small_share[:9].reshape(3, 3, own),
        small_share[9:at].T,
        small_share[at : at + poles].T,
        small_share[at + poles :].T,
        gain_share[1],
        gate_share.T,
        up_share.T,
        down_share.T,
    )


def solution(mesh):
    both = ("wide", "narrow")
    return jax.shard_map(
        body,
        mesh=mesh,
        in_specs=(
            P("wide", "narrow", None),
            P(None, None, both),
            P(both, None),
            P(both),
            P(None, None, both),
            P(both, None),
            P(both, None),
            P(both, None),
            P(both),
            P(None, both),
            P(None, both),
            P(None, both),
            P("wide", None),
            P("wide", None),
            P("wide", "narrow", None),
        ),
        out_specs=(
            P("wide", "narrow", None),
            P("wide", "narrow", None),
            P(None, None, both),
            P(both, None),
            P(both),
            P(None, None, both),
            P(both, None),
            P(both, None),
            P(both, None),
            P(both),
            P(None, both),
            P(None, both),
            P(None, both),
        ),
        check_vma=False,
    )
```

```python
from functools import partial

import jax
import jax.numpy as jnp
import numpy as np
from jax import lax
from jax.experimental import pallas as pl
from jax.experimental.pallas import tpu as pltpu
from jax.sharding import PartitionSpec as P

BLOCK = 128
LONGEST = 4
SPAN = LONGEST * BLOCK
FREQ = SPAN

epsilon = 1e-06
bf16 = jnp.bfloat16
f32 = jnp.float32


def transform():
    k = np.arange(FREQ)[:, None] * 2 + 1
    t = np.arange(SPAN)[None, :]
    turn = (k * t % (4 * SPAN)) * (2 * np.pi / (4 * SPAN))
    return np.concatenate([np.cos(turn), -np.sin(turn)], axis=0).astype(np.float32)


def nn(a, b):
    return lax.dot_general(a, b, (((1,), (0,)), ((), ())), preferred_element_type=f32)


def nt(a, b):
    return lax.dot_general(a, b, (((1,), (1,)), ((), ())), preferred_element_type=f32)


def tn(a, b):
    return lax.dot_general(a, b, (((0,), (0,)), ((), ())), preferred_element_type=f32)


def swap(values, axis, shift):
    size = lax.axis_size(axis)
    return lax.ppermute(values, axis, [(i, i ^ shift) for i in range(size)])


def ring_of(size):
    return list(range(0, size, 2)) + list(range(size - 1, 0, -2))


def along(values, step):
    outer = lax.axis_size("wide") // 2
    ring = ring_of(outer)
    pairs = [
        (ring[p] * 2 + side, ring[(p + step) % outer] * 2 + side)
        for p in range(outer)
        for side in range(2)
    ]
    return lax.ppermute(values, "wide", pairs)


def ring_offsets(outer):
    near = [sign * h for h in range(1, outer // 2) for sign in (-1, 1)]
    return [0] + near + [outer // 2]


def cut_of(rows):
    cut = (rows // 2 + 15) // 16 * 16
    return cut if cut < rows else rows // 2


def two_parts(values, axis):
    cut = cut_of(values.shape[axis])
    return (
        lax.slice_in_dim(values, 0, cut, axis=axis),
        lax.slice_in_dim(values, cut, values.shape[axis], axis=axis),
    )


def gather_ring(own, axis=0, halves=True):
    outer = lax.axis_size("wide") // 2
    before, after = [own], [own]
    for _ in range(1, outer // 2):
        before.append(along(before[-1], 1))
        after.append(along(after[-1], -1))
    if halves:
        top, _ = two_parts(before[-1], axis)
        _, bottom = two_parts(after[-1], axis)
        opposite = [along(top, 1), along(bottom, -1)]
    else:
        opposite = [along(before[-1], 1)]
    near = [piece for h in range(1, outer // 2) for piece in (before[h], after[h])]
    return [own] + near + opposite, near


def scatter_ring(full, axis=0, halves=True):
    outer = lax.axis_size("wide") // 2
    wire = full.dtype
    chunks = jnp.split(full, outer, axis=axis)
    total = chunks[0].astype(f32)
    most = outer // 2 - 1
    behind = {h: chunks[2 * h - 1].astype(f32) for h in range(1, most + 1)}
    ahead = {h: chunks[2 * h].astype(f32) for h in range(1, most + 1)}
    if halves:
        top, bottom = two_parts(chunks[-1], axis)
        far_top, far_bottom = two_parts(ahead[most], axis)
        got = along(top, 1).astype(f32)
        ahead[most] = jnp.concatenate([far_top + got, far_bottom], axis=axis)
        far_top, far_bottom = two_parts(behind[most], axis)
        got = along(bottom, -1).astype(f32)
        behind[most] = jnp.concatenate([far_top, far_bottom + got], axis=axis)
    else:
        ahead[most] = ahead[most] + along(chunks[-1], 1).astype(f32)
    for h in range(most, 0, -1):
        got = along(ahead[h].astype(wire), 1).astype(f32)
        back = along(behind[h].astype(wire), -1).astype(f32)
        if h > 1:
            ahead[h - 1] = ahead[h - 1] + got
            behind[h - 1] = behind[h - 1] + back
        else:
            total = total + got + back
    return total


def gather_rows(own):
    size = lax.axis_size("narrow")
    half = own.shape[0] // 2
    across = [swap(own, "narrow", k) for k in range(2, size, 2)]
    beside = swap(own, "wide", 1)
    even = jnp.concatenate([own] + across, axis=0)
    odd = swap(even, "narrow", 1)
    parts = [beside]
    for n, k in enumerate(range(2, size, 2)):
        parts.append(swap(across[n][:half], "wide", 1))
        parts.append(swap(beside[half:], "narrow", k))
    other_even = jnp.concatenate(parts, axis=0)
    other_odd = swap(other_even, "narrow", 1)
    return even, odd, other_even, other_odd


def scatter_rows(even, odd, other_even, other_odd):
    size = lax.axis_size("narrow")
    rows = even.shape[0] // (size // 2)
    half = rows // 2
    other = other_even.astype(f32) + swap(other_odd, "narrow", 1).astype(f32)
    mine = even.astype(f32) + swap(odd, "narrow", 1).astype(f32)
    beside_top, beside_bottom = other[:half], other[half:rows]
    out = mine[:rows]
    for n, k in enumerate(range(2, size, 2)):
        at = (n + 1) * rows
        top = swap(other[at : at + half].astype(bf16), "wide", 1).astype(f32)
        bottom = swap(other[at + half : at + rows].astype(bf16), "narrow", k).astype(f32)
        beside_bottom = beside_bottom + bottom
        across = jnp.concatenate([mine[at : at + half] + top, mine[at + half : at + rows]], axis=0)
        out = out + swap(across.astype(bf16), "narrow", k).astype(f32)
    beside = jnp.concatenate([beside_top, beside_bottom], axis=0)
    return out + swap(beside.astype(bf16), "wide", 1).astype(f32)


def inverse_rms(values):
    return lax.rsqrt(jnp.mean(values * values, axis=-1, keepdims=True) + epsilon)


def norm_back(values, rate, gain, grad):
    a = grad * gain
    inner = jnp.mean(a * values, axis=-1, keepdims=True)
    return rate * a - values * (rate * rate * rate) * inner


def filter_kernel(base_re, base_im, step_re, step_im, out):
    poles = base_re.shape[0]
    width = out.shape[1]
    for g in range(width // 128 if width % 128 == 0 else 1):
        lanes = pl.ds(g * 128, min(128, width))
        start = tuple(base_re[j, :, lanes] for j in range(poles)) + tuple(
            base_im[j, :, lanes] for j in range(poles)
        )

        def step(b, state):
            total = state[0]
            for j in range(1, poles):
                total = total + state[j]
            out[pl.ds(pl.multiple_of(b * 8, 8), 8), lanes] = total
            new_re, new_im = [], []
            for j in range(poles):
                sr = step_re[j, :, lanes]
                si = step_im[j, :, lanes]
                new_re.append(state[j] * sr - state[poles + j] * si)
                new_im.append(state[j] * si + state[poles + j] * sr)
            return tuple(new_re) + tuple(new_im)

        lax.fori_loop(0, SPAN // 8, step, start)


def filter_taps(base_re, base_im, step_re, step_im):
    width = base_re.shape[2]
    return pl.pallas_call(
        filter_kernel,
        out_shape=jax.ShapeDtypeStruct((SPAN, width), f32),
        cost_estimate=pl.CostEstimate(
            flops=16 * 7 * SPAN * width, bytes_accessed=4 * SPAN * width, transcendentals=0
        ),
        name="taps",
    )(base_re, base_im, step_re, step_im)


def moment_kernel(grad, step_re, step_im, sum_re, sum_im, mom_re, mom_im):
    poles = step_re.shape[0]
    width = grad.shape[1]
    per = 8
    for g in range(width // 128 if width % 128 == 0 else 1):
        lanes = pl.ds(g * 128, min(128, width))
        for j0 in range(0, poles, per):
            zero = jnp.zeros((8, min(128, width)), f32)

            def step(i, state):
                b = SPAN // 8 - 1 - i
                value = grad[pl.ds(pl.multiple_of(b * 8, 8), 8), lanes]
                new = []
                for n in range(per):
                    sr = step_re[j0 + n, :, lanes]
                    si = step_im[j0 + n, :, lanes]
                    pr, pi, qr, qi = state[4 * n : 4 * n + 4]
                    ur, ui = pr + qr, pi + qi
                    new += [
                        pr * sr - pi * si + value,
                        pr * si + pi * sr,
                        ur * sr - ui * si,
                        ur * si + ui * sr,
                    ]
                return tuple(new)

            state = lax.fori_loop(0, SPAN // 8, step, (zero,) * (4 * per))
            for n in range(per):
                sum_re[j0 + n, :, lanes] = state[4 * n]
                sum_im[j0 + n, :, lanes] = state[4 * n + 1]
                mom_re[j0 + n, :, lanes] = state[4 * n + 2]
                mom_im[j0 + n, :, lanes] = state[4 * n + 3]


def filter_moments(grad, step_re, step_im):
    poles, _, width = step_re.shape
    shape = jax.ShapeDtypeStruct((poles, 8, width), f32)
    return pl.pallas_call(
        moment_kernel,
        out_shape=(shape,) * 4,
        cost_estimate=pl.CostEstimate(
            flops=16 * 15 * SPAN * width, bytes_accessed=4 * SPAN * width, transcendentals=0
        ),
        name="moments",
    )(grad, step_re, step_im)


LIVE, KEEP_ONE, KEEP_TWO = 0, 1, 2


def load_masked(order, proj, table, m_scr):
    pieces, rows, _ = proj.shape
    m_scr[0:8, :] = jnp.zeros_like(m_scr[0:8, :])

    def piece(b, _):
        p = order[b]
        at = pl.multiple_of(b * rows, rows)
        live = table[pl.ds(at, rows), LIVE : LIVE + 1]
        m_scr[pl.ds(pl.multiple_of(at + 8, 8), rows), :] = proj[p] * live
        return 0

    lax.fori_loop(0, pieces, piece, 0)


def short_block(m_scr, taps, table, at):
    window = m_scr[pl.ds(at, BLOCK + 8), :]
    one = table[pl.ds(at, BLOCK), KEEP_ONE : KEEP_ONE + 1]
    two = table[pl.ds(at, BLOCK), KEEP_TWO : KEEP_TWO + 1]
    here = window[8:]
    once = window[7 : BLOCK + 7] * one
    twice = window[6 : BLOCK + 6] * two
    short = taps[0:1, :] * here + taps[1:2, :] * once + taps[2:3, :] * twice
    return short, here, once, twice


def pack_document(source, packed, first, count):
    blocks = source.shape[0] // BLOCK
    for kb in range(LONGEST):
        at = pl.multiple_of(jnp.minimum(first + kb, blocks - 1) * BLOCK, BLOCK)
        inside = (kb < count).astype(f32)
        packed[kb * BLOCK : (kb + 1) * BLOCK, :] = (source[pl.ds(at, BLOCK), :] * inside).astype(bf16)


def place_document(result, target, first, count):
    for kb in range(LONGEST):

        @pl.when(kb < count)
        def _():
            at = pl.multiple_of((first + kb) * BLOCK, BLOCK)
            target[pl.ds(at, BLOCK), :] = result[kb * BLOCK : (kb + 1) * BLOCK, :]


def forward_kernel(
    order, first, count, proj, taps, table, spectrum, fwd, inv, gated, long_out, seen, m_scr, u_scr, q_scr, packed
):
    width = long_out.shape[1]
    pieces, rows, _ = proj.shape
    blocks = long_out.shape[0] // BLOCK
    load_masked(order, proj, table, m_scr)

    def block(n, _):
        at = pl.multiple_of(n * BLOCK, BLOCK)
        short, _, _, _ = short_block(m_scr, taps, table, at)
        q_scr[pl.ds(at, BLOCK), :] = short[:, :width]
        u_scr[pl.ds(at, BLOCK), :] = short[:, width : 2 * width] * short[:, 2 * width :]
        return 0

    lax.fori_loop(0, blocks, block, 0)

    def document(d, _):
        pack_document(u_scr, packed, first[d], count[d])
        both = jnp.dot(fwd[...], packed[...], preferred_element_type=f32)
        seen[d] = both.astype(bf16)
        re, im = both[:FREQ], both[FREQ:]
        hr, hi = spectrum[:FREQ], spectrum[FREQ:]
        answer = jnp.concatenate([re * hr - im * hi, re * hi + im * hr], axis=0).astype(bf16)
        result = jnp.dot(inv[...], answer, preferred_element_type=f32)
        place_document(result, long_out, first[d], count[d])
        return 0

    lax.fori_loop(0, seen.shape[0], document, 0)

    def piece(b, _):
        at = pl.multiple_of(b * rows, rows)
        gated[order[b]] = (q_scr[pl.ds(at, rows), :] * long_out[pl.ds(at, rows), :]).astype(bf16)
        return 0

    lax.fori_loop(0, pieces, piece, 0)


def backward_kernel(
    order, first, count, proj, d_gated, long_out, seen, taps, table, spectrum, fwd, inv,
    dz, d_filter, d_taps, m_scr, dy_scr, k_scr, v_scr, ds_scr, packed, d_spec,
):
    width = long_out.shape[1]
    pieces, rows, _ = proj.shape
    slots = long_out.shape[0]
    blocks = slots // BLOCK
    per_piece = rows // BLOCK
    load_masked(order, proj, table, m_scr)
    ds_scr[slots : slots + 8, :] = jnp.zeros_like(ds_scr[slots : slots + 8, :])

    def block(n, _):
        at = pl.multiple_of(n * BLOCK, BLOCK)
        short, _, _, _ = short_block(m_scr, taps, table, at)
        within = pl.multiple_of((n % per_piece) * BLOCK, BLOCK)
        dg = d_gated[order[n // per_piece], pl.ds(within, BLOCK), :]
        dy_scr[pl.ds(at, BLOCK), :] = dg * short[:, :width]
        ds_scr[pl.ds(at, BLOCK), :width] = dg * long_out[pl.ds(at, BLOCK), :]
        k_scr[pl.ds(at, BLOCK), :] = short[:, width : 2 * width]
        v_scr[pl.ds(at, BLOCK), :] = short[:, 2 * width :]
        return 0

    lax.fori_loop(0, blocks, block, 0)
    d_spec[...] = jnp.zeros_like(d_spec)

    def document(d, _):
        pack_document(dy_scr, packed, first[d], count[d])
        both = jnp.dot(fwd[...], packed[...], preferred_element_type=f32)
        re, im = both[:FREQ], both[FREQ:]
        hr, hi = spectrum[:FREQ], spectrum[FREQ:]
        answer = jnp.concatenate([re * hr + im * hi, im * hr - re * hi], axis=0).astype(bf16)
        result = jnp.dot(inv[...], answer, preferred_element_type=f32)
        ur, ui = seen[d, :FREQ].astype(f32), seen[d, FREQ:].astype(f32)
        d_spec[:FREQ] += re * ur + im * ui
        d_spec[FREQ:] += im * ur - re * ui
        for kb in range(LONGEST):

            @pl.when(kb < count[d])
            def _():
                at = pl.multiple_of((first[d] + kb) * BLOCK, BLOCK)
                du = result[kb * BLOCK : (kb + 1) * BLOCK, :]
                ds_scr[pl.ds(at, BLOCK), width : 2 * width] = du * v_scr[pl.ds(at, BLOCK), :]
                ds_scr[pl.ds(at, BLOCK), 2 * width :] = du * k_scr[pl.ds(at, BLOCK), :]

        return 0

    lax.fori_loop(0, seen.shape[0], document, 0)
    d_filter[...] = jnp.dot(inv[...], d_spec[...].astype(bf16), preferred_element_type=f32)
    d_taps[...] = jnp.zeros_like(d_taps)

    def back(n, _):
        at = pl.multiple_of(n * BLOCK, BLOCK)
        window = m_scr[pl.ds(at, BLOCK + 8), :]
        ahead = ds_scr[pl.ds(at, BLOCK + 8), :]
        one = table[pl.ds(at, BLOCK + 8), KEEP_ONE : KEEP_ONE + 1]
        two = table[pl.ds(at, BLOCK + 8), KEEP_TWO : KEEP_TWO + 1]
        live = table[pl.ds(at, BLOCK), LIVE : LIVE + 1]
        ds = ahead[:BLOCK]
        ahead_one = ahead * one
        ahead_two = ahead * two
        dm = (
            taps[0:1, :] * ds
            + taps[1:2, :] * ahead_one[1 : BLOCK + 1]
            + taps[2:3, :] * ahead_two[2 : BLOCK + 2]
        )
        d_taps[0:1, :] += jnp.sum(window[8:] * ds, axis=0, keepdims=True)
        d_taps[1:2, :] += jnp.sum(window[7 : BLOCK + 7] * ahead_one[:BLOCK], axis=0, keepdims=True)
        d_taps[2:3, :] += jnp.sum(window[6 : BLOCK + 6] * ahead_two[:BLOCK], axis=0, keepdims=True)
        within = pl.multiple_of((n % per_piece) * BLOCK, BLOCK)
        dz[order[n // per_piece], pl.ds(within, BLOCK), :] = (dm * live).astype(bf16)
        return 0

    lax.fori_loop(0, blocks, back, 0)


smem = pl.BlockSpec(memory_space=pltpu.SMEM)
vmem = pl.BlockSpec(memory_space=pltpu.VMEM)


def mixer_forward(order, first, count, proj, taps, table, spectrum, fwd, inv):
    pieces, rows, three = proj.shape
    width = three // 3
    slots = pieces * rows
    docs = first.shape[0]
    return pl.pallas_call(
        forward_kernel,
        out_shape=(
            jax.ShapeDtypeStruct((pieces, rows, width), bf16),
            jax.ShapeDtypeStruct((slots, width), f32),
            jax.ShapeDtypeStruct((docs, 2 * FREQ, width), bf16),
        ),
        in_specs=[smem] * 3 + [vmem] * 6,
        out_specs=(vmem,) * 3,
        scratch_shapes=[
            pltpu.VMEM((slots + 8, three), f32),
            pltpu.VMEM((slots, width), f32),
            pltpu.VMEM((slots, width), f32),
            pltpu.VMEM((SPAN, width), bf16),
        ],
        compiler_params=pltpu.CompilerParams(vmem_limit_bytes=40 * 2**20),
        cost_estimate=pl.CostEstimate(
            flops=docs * 8 * FREQ * SPAN * width,
            bytes_accessed=slots * three * 4 + 8 * slots * width,
            transcendentals=0,
        ),
        name="mixer_forward",
    )(order, first, count, proj, taps, table, spectrum, fwd, inv)


def mixer_backward(order, first, count, proj, d_gated, long_out, seen, taps, table, spectrum, fwd, inv):
    pieces, rows, three = proj.shape
    width = three // 3
    slots = pieces * rows
    docs = first.shape[0]
    return pl.pallas_call(
        backward_kernel,
        out_shape=(
            jax.ShapeDtypeStruct((pieces, rows, three), bf16),
            jax.ShapeDtypeStruct((SPAN, width), f32),
            jax.ShapeDtypeStruct((8, three), f32),
        ),
        in_specs=[smem] * 3 + [vmem] * 9,
        out_specs=(vmem,) * 3,
        scratch_shapes=[
            pltpu.VMEM((slots + 8, three), f32),
            pltpu.VMEM((slots, width), f32),
            pltpu.VMEM((slots, width), f32),
            pltpu.VMEM((slots, width), f32),
            pltpu.VMEM((slots + 8, three), f32),
            pltpu.VMEM((SPAN, width), bf16),
            pltpu.VMEM((2 * FREQ, width), f32),
        ],
        compiler_params=pltpu.CompilerParams(vmem_limit_bytes=48 * 2**20),
        cost_estimate=pl.CostEstimate(
            flops=docs * 10 * FREQ * SPAN * width,
            bytes_accessed=slots * three * 8 + 8 * slots * width,
            transcendentals=0,
        ),
        name="mixer_backward",
    )(order, first, count, proj, d_gated, long_out, seen, taps, table, spectrum, fwd, inv)


def layout(doc_blocks, doc_pad, slots):
    block_ends = jnp.cumsum(doc_blocks) * BLOCK
    starts = block_ends - doc_blocks * BLOCK
    places = jnp.arange(slots, dtype=jnp.int32)
    living = (places[None, :] >= starts[:, None]) & (
        places[None, :] < (block_ends - doc_pad)[:, None]
    )
    live = jnp.sum(living.astype(f32), axis=0)
    opening = jnp.sum((places[None, :] == starts[:, None]).astype(f32), axis=0)
    one = 1.0 - opening
    one = one * (places > 0)
    two = one * jnp.concatenate([jnp.zeros((1,), f32), one[:-1]])
    table = jnp.stack([live, one, two], axis=1)
    table = jnp.concatenate([table, jnp.zeros((8, 3), f32)], axis=0)
    return table, starts // BLOCK


def picked(index, count, values):
    hot = index[:, None] == jnp.arange(count)[None, :]
    shape = hot.shape + (1,) * (values.ndim - 1)
    return jnp.sum(jnp.where(hot.reshape(shape), values[None], 0), axis=1)


def body(
    tokens, w_in, w_out, gain_one, short_kernel, decay_rate, pole_angle, residue,
    gain_two, w_gate, w_up, w_down, doc_blocks, doc_pad, cotangent,
):
    wide, narrow = lax.axis_size("wide"), lax.axis_size("narrow")
    wide_at, narrow_at = lax.axis_index("wide"), lax.axis_index("narrow")
    outer = wide // 2
    _, local_rows, width = tokens.shape
    slots = local_rows * narrow
    even = slots // 2
    source = tokens[0].astype(f32)
    upstream_low = cotangent[0]
    poles = decay_rate.shape[1]
    own = w_in.shape[2]
    channels = own * outer
    hidden_units = w_gate.shape[1] * outer

    ring = np.array(ring_of(outer))
    ring_place = np.argsort(ring)
    tour = picked((wide_at // 2)[None], outer, jnp.asarray(ring_place, jnp.int32))[0]
    piece_places = (tour + jnp.asarray(ring_offsets(outer), jnp.int32)) % outer
    piece_outer = picked(piece_places, outer, jnp.asarray(ring, jnp.int32))
    sides = jnp.arange(2) ^ (wide_at % 2)
    offsets = list(range(0, narrow, 2)) + list(range(1, narrow, 2))
    place_of = np.argsort(np.array(offsets))
    order = picked(jnp.arange(narrow) ^ narrow_at, narrow, jnp.asarray(place_of, jnp.int32))
    narrow_of = jnp.asarray(offsets, jnp.int32) ^ narrow_at

    small = jnp.concatenate(
        [
            short_kernel.reshape(9, own),
            decay_rate.T,
            pole_angle.T,
            residue.T,
            gain_one[None],
            gain_two[None],
        ],
        axis=0,
    )
    small_all = jnp.concatenate(gather_ring(small, axis=1, halves=False)[0], axis=1)
    gains = small_all[small.shape[0] - 2 :].reshape(2, outer, own)
    gains = jnp.stack([gains, swap(gains, "wide", 1)])
    gains = jnp.stack([gains] + [swap(gains, "narrow", k) for k in range(2, narrow, 2)])
    gains = jnp.concatenate([gains, swap(gains, "narrow", 1)], axis=0).astype(f32)
    gains = picked(order, narrow, gains).transpose(1, 3, 0, 2, 4)
    gains = picked(sides, 2, gains).transpose(1, 0, 2, 3, 4)
    hot = piece_outer[None, :] == jnp.arange(outer)[:, None]
    gains = jnp.sum(jnp.where(hot[:, :, None, None, None, None], gains[None], 0), axis=1)
    gain_all = gains.transpose(3, 0, 1, 2, 4).reshape(2, width)
    gain_first, gain_last = gain_all[0], gain_all[1]

    def reduce_gain(values):
        values = values.reshape(outer, 2, narrow, own)
        values = picked(piece_outer, outer, values).transpose(1, 0, 2, 3)
        values = picked(sides, 2, values).transpose(2, 0, 1, 3)
        values = picked(narrow_of, narrow, values)
        total = values[: narrow // 2] + swap(values[narrow // 2 :], "narrow", 1)
        summed = total[0]
        for k in range(1, narrow // 2):
            summed = summed + swap(total[k], "narrow", 2 * k)
        summed = summed[0] + swap(summed[1], "wide", 1)
        return scatter_ring(summed, halves=False)[0]

    documents = jnp.concatenate([doc_blocks, doc_pad], axis=0)
    documents = (documents, swap(documents, "wide", 1))
    tables = [layout(rules[0], rules[1], slots) for rules in documents]

    in_pieces, sent = gather_ring(w_in.transpose(0, 2, 1), axis=1)
    out_own, gate_own, up_own, down_own = w_out, w_gate.T, w_up.T, w_down.T
    out_own, gate_own, *_ = lax.optimization_barrier((out_own, gate_own, *sent))
    out_pieces, _ = gather_ring(out_own)
    gate_pieces, sent = gather_ring(gate_own)
    up_own, *_ = lax.optimization_barrier((up_own, *sent))
    up_pieces, sent = gather_ring(up_own)
    down_own, *_ = lax.optimization_barrier((down_own, *sent))
    down_pieces, _ = gather_ring(down_own)

    rate_first = inverse_rms(source)
    low_first = (source * rate_first * gain_first).astype(bf16)
    first_parts = gather_rows(low_first)
    rows_first = [jnp.concatenate(first_parts[:2], axis=0), jnp.concatenate(first_parts[2:], axis=0)]

    matrix = transform()
    fwd = jnp.asarray(matrix, bf16)
    inv = jnp.asarray(matrix.T / SPAN, bf16)

    block = small_all.astype(f32)
    taps = block[:9].reshape(3, 3 * channels)
    taps = jnp.concatenate([taps, jnp.zeros((5, 3 * channels), f32)], axis=0)
    decay = block[9 : 9 + poles][:, None, :]
    angle = block[9 + poles : 9 + 2 * poles][:, None, :]
    res_re = block[9 + 2 * poles : 9 + 3 * poles][:, None, :]
    res_im = -block[9 + 3 * poles : 9 + 4 * poles][:, None, :]
    lag = jnp.arange(8, dtype=f32)[None, :, None]
    fade = jnp.exp(-decay * lag)
    power_re, power_im = fade * jnp.cos(angle * lag), fade * jnp.sin(angle * lag)
    fade_step = jnp.exp(-decay * 8.0)
    step_re = jnp.broadcast_to(fade_step * jnp.cos(angle * 8.0), power_re.shape)
    step_im = jnp.broadcast_to(fade_step * jnp.sin(angle * 8.0), power_re.shape)
    filt = filter_taps(
        res_re * power_re - res_im * power_im,
        res_re * power_im + res_im * power_re,
        step_re,
        step_im,
    )
    spectrum = lax.dot_general(
        jnp.asarray(matrix),
        filt,
        (((1,), (0,)), ((), ())),
        precision=lax.Precision.HIGHEST,
        preferred_element_type=f32,
    )
    res_re, res_im = res_re[:, 0], -res_im[:, 0]

    in_all = jnp.concatenate(in_pieces, axis=1).reshape(3 * channels, width)
    mixed = []
    for r in range(2):
        table, first = tables[r]
        proj = nt(rows_first[r], in_all).reshape(narrow, local_rows, 3 * channels)
        gated, long_out, seen = mixer_forward(
            order, first, documents[r][0], proj, taps, table, spectrum, fwd, inv
        )
        mixed.append((proj, gated.reshape(slots, channels), long_out, seen))
    out_all = jnp.concatenate(out_pieces, axis=0)
    shares = []
    for r in (1, 0):
        share = nn(mixed[r][1], out_all).astype(bf16)
        shares = [share[:even], share[even:]] + shares
    middle = source + scatter_rows(*shares)
    rate_last = inverse_rms(middle)
    rows_upstream = jnp.concatenate(gather_rows(upstream_low), axis=0)
    rows_second = jnp.concatenate(
        gather_rows((middle * rate_last * gain_last).astype(bf16)), axis=0
    )

    gate_up = jnp.concatenate(gate_pieces + up_pieces, axis=0)
    down_all = jnp.concatenate(down_pieces, axis=0)
    pre = nt(gate_up, rows_second)
    gate_pre, up_pre = pre[:hidden_units], pre[hidden_units:]
    sig = jax.nn.sigmoid(gate_pre)
    silu = gate_pre * sig
    hidden = (silu * up_pre).astype(bf16)
    d_hidden = nt(down_all, rows_upstream)
    d_gate = (d_hidden * up_pre * sig * (1.0 + gate_pre * (1.0 - sig))).astype(bf16)
    d_up = (d_hidden * silu).astype(bf16)
    d_pre = jnp.concatenate([d_gate, d_up], axis=0)
    shares = []
    for r in (1, 0):
        share = tn(d_pre[:, r * slots : (r + 1) * slots], gate_up).astype(bf16)
        shares = [share[:even], share[even:]] + shares
    d_second = scatter_rows(*shares)
    upstream = upstream_low.astype(f32)
    d_middle = upstream + norm_back(middle, rate_last, gain_last, d_second)
    rows_dmiddle = gather_rows(d_middle.astype(bf16))
    rows_dmiddle = [
        jnp.concatenate(rows_dmiddle[:2], axis=0),
        jnp.concatenate(rows_dmiddle[2:], axis=0),
    ]
    down_share = scatter_ring(nn(hidden, rows_upstream).astype(bf16))
    grad_pre = nn(d_pre, rows_second).astype(bf16)
    gate_share = scatter_ring(grad_pre[:hidden_units])
    up_share = scatter_ring(grad_pre[hidden_units:])
    shares = []
    for r in (1, 0):
        share = tn(hidden[:, r * slots : (r + 1) * slots], down_all).astype(bf16)
        shares = [share[:even], share[even:]] + shares
    block_output = (middle + scatter_rows(*shares)).astype(bf16)
    grad_gain_two = jnp.sum(d_second * middle * rate_last, axis=0)

    grad_out, grad_in, d_filter, d_taps = 0.0, 0.0, 0.0, 0.0
    shares, grad_gain_one = [], 0.0
    for r in (1, 0):
        proj, gated, long_out, seen = mixed[r]
        table, first = tables[r]
        d_gated = nt(rows_dmiddle[r], out_all).reshape(narrow, local_rows, channels)
        grad_out = grad_out + tn(gated, rows_dmiddle[r])
        dz, d_filter_row, d_taps_row = mixer_backward(
            order, first, documents[r][0], proj, d_gated, long_out, seen, taps, table,
            spectrum, fwd, inv,
        )
        dz = dz.reshape(slots, 3 * channels)
        d_filter, d_taps = d_filter + d_filter_row, d_taps + d_taps_row
        share = nn(dz, in_all).astype(bf16)
        shares = [share[:even], share[even:]] + shares
        grad_gain_one = grad_gain_one + jnp.sum(
            share.astype(f32) * rows_first[r].astype(f32), axis=0
        )
        grad_in = grad_in + tn(dz, rows_first[r])
    d_normed = scatter_rows(*shares)
    input_grad = (d_middle + norm_back(source, rate_first, gain_first, d_normed)).astype(bf16)
    out_share = scatter_ring(grad_out.astype(bf16))
    in_share = scatter_ring(grad_in.astype(bf16).reshape(3, channels, width), axis=1)

    sum_re, sum_im, mom_re, mom_im = filter_moments(d_filter, step_re, step_im)
    full_re = lag * sum_re + 8.0 * mom_re
    full_im = lag * sum_im + 8.0 * mom_im
    grad_re = jnp.sum(power_re * sum_re - power_im * sum_im, axis=1)
    grad_im = jnp.sum(power_re * sum_im + power_im * sum_re, axis=1)
    lag_re = jnp.sum(power_re * full_re - power_im * full_im, axis=1)
    lag_im = jnp.sum(power_re * full_im + power_im * full_re, axis=1)
    small_grad = jnp.concatenate(
        [
            d_taps[:3].reshape(9, channels),
            -(res_re * lag_re + res_im * lag_im),
            res_im * lag_re - res_re * lag_im,
            grad_re,
            grad_im,
        ],
        axis=0,
    ).astype(bf16)
    small_share = scatter_ring(small_grad, axis=1, halves=False)

    at = 9 + poles
    return (
        block_output[None],
        input_grad[None],
        in_share.transpose(0, 2, 1),
        out_share,
        reduce_gain(grad_gain_one / gain_first),
        small_share[:9].reshape(3, 3, own),
        small_share[9:at].T,
        small_share[at : at + poles].T,
        small_share[at + poles :].T,
        reduce_gain(grad_gain_two),
        gate_share.T,
        up_share.T,
        down_share.T,
    )


def solution(mesh):
    both = ("wide", "narrow")
    return jax.shard_map(
        body,
        mesh=mesh,
        in_specs=(
            P("wide", "narrow", None),
            P(None, None, both),
            P(both, None),
            P(both),
            P(None, None, both),
            P(both, None),
            P(both, None),
            P(both, None),
            P(both),
            P(None, both),
            P(None, both),
            P(None, both),
            P("wide", None),
            P("wide", None),
            P("wide", "narrow", None),
        ),
        out_specs=(
            P("wide", "narrow", None),
            P("wide", "narrow", None),
            P(None, None, both),
            P(both, None),
            P(both),
            P(None, None, both),
            P(both, None),
            P(both, None),
            P(both, None),
            P(both),
            P(None, both),
            P(None, both),
            P(None, both),
        ),
        check_vma=False,
    )
```

```python
from functools import partial

import jax
import jax.numpy as jnp
import numpy as np
from jax import lax
from jax.experimental import pallas as pl
from jax.experimental.pallas import tpu as pltpu
from jax.sharding import PartitionSpec as P

BLOCK = 128
LONGEST = 4
SPAN = LONGEST * BLOCK
FREQ = SPAN

epsilon = 1e-06
bf16 = jnp.bfloat16
f32 = jnp.float32


def transform():
    k = np.arange(FREQ)[:, None] * 2 + 1
    t = np.arange(SPAN)[None, :]
    turn = (k * t % (4 * SPAN)) * (2 * np.pi / (4 * SPAN))
    return np.concatenate([np.cos(turn), -np.sin(turn)], axis=0).astype(np.float32)


def nn(a, b):
    return lax.dot_general(a, b, (((1,), (0,)), ((), ())), preferred_element_type=f32)


def nt(a, b):
    return lax.dot_general(a, b, (((1,), (1,)), ((), ())), preferred_element_type=f32)


def tn(a, b):
    return lax.dot_general(a, b, (((0,), (0,)), ((), ())), preferred_element_type=f32)


def swap(values, axis, shift):
    size = lax.axis_size(axis)
    return lax.ppermute(values, axis, [(i, i ^ shift) for i in range(size)])


def after(values, tokens):
    if not tokens:
        return values
    joined = lax.optimization_barrier(tuple(values) + tuple(tokens))
    return list(joined[: len(values)])


def ring_of(size):
    return list(range(0, size, 2)) + list(range(size - 1, 0, -2))


def along(values, step):
    outer = lax.axis_size("wide") // 2
    ring = ring_of(outer)
    pairs = [
        (ring[p] * 2 + side, ring[(p + step) % outer] * 2 + side)
        for p in range(outer)
        for side in range(2)
    ]
    return lax.ppermute(values, "wide", pairs)


def ring_offsets(outer):
    near = [sign * h for h in range(1, outer // 2) for sign in (-1, 1)]
    return [0] + near + [outer // 2]


def cut_of(rows):
    cut = (rows // 2 + 15) // 16 * 16
    return cut if cut < rows else rows // 2


def two_parts(values, axis):
    cut = cut_of(values.shape[axis])
    return (
        lax.slice_in_dim(values, 0, cut, axis=axis),
        lax.slice_in_dim(values, cut, values.shape[axis], axis=axis),
    )


def gather_ring(own, axis=0, halves=True, tokens=(), later=()):
    outer = lax.axis_size("wide") // 2
    [own] = after([own], list(tokens))
    before, behind = [own], [own]
    for h in range(1, outer // 2):
        one, two = along(before[-1], 1), along(behind[-1], -1)
        if halves:
            one, two = lax.optimization_barrier((one, two))
        before.append(one)
        behind.append(two)
    if halves:
        top, _ = two_parts(before[-1], axis)
        _, bottom = two_parts(behind[-1], axis)
        top, bottom = after([top, bottom], later)
        opposite = [along(top, 1), along(bottom, -1)]
    else:
        opposite = [along(before[-1], 1)]
    near = [piece for h in range(1, outer // 2) for piece in (before[h], behind[h])]
    return [own] + near + opposite, opposite


def scatter_ring(full, axis=0, halves=True, tokens=(), later=()):
    outer = lax.axis_size("wide") // 2
    wire = full.dtype
    chunks = jnp.split(full, outer, axis=axis)
    total = chunks[0].astype(f32)
    most = outer // 2 - 1
    behind = {h: chunks[2 * h - 1].astype(f32) for h in range(1, most + 1)}
    ahead = {h: chunks[2 * h].astype(f32) for h in range(1, most + 1)}
    if halves:
        top, bottom = after(two_parts(chunks[-1], axis), tokens)
        far_top, far_bottom = two_parts(ahead[most], axis)
        got = along(top, 1).astype(f32)
        ahead[most] = jnp.concatenate([far_top + got, far_bottom], axis=axis)
        far_top, far_bottom = two_parts(behind[most], axis)
        got = along(bottom, -1).astype(f32)
        behind[most] = jnp.concatenate([far_top, far_bottom + got], axis=axis)
    else:
        ahead[most] = ahead[most] + along(chunks[-1], 1).astype(f32)
    for h in range(most, 0, -1):
        one, two = ahead[h].astype(wire), behind[h].astype(wire)
        if halves:
            one, two = lax.optimization_barrier((one, two, *later))[:2]
        one, two = along(one, 1), along(two, -1)
        got, back = one.astype(f32), two.astype(f32)
        if h > 1:
            ahead[h - 1] = ahead[h - 1] + got
            behind[h - 1] = behind[h - 1] + back
        else:
            total = total + got + back
    return total, (one, two)


def gather_rows(own, tokens=()):
    size = lax.axis_size("narrow")
    half = own.shape[0] // 2
    [own] = after([own], tokens)
    across = [swap(own, "narrow", k) for k in range(2, size, 2)]
    beside = swap(own, "wide", 1)
    stage_one = across + [beside]
    corner, stage_two = [], []
    for n, k in enumerate(range(2, size, 2)):
        ends = [swap(across[n][:half], "wide", 1), swap(beside[half:], "narrow", k)]
        corner.append(jnp.concatenate(ends, axis=0))
        stage_two += ends
    [own_again] = after([own], stage_one)
    odd = [swap(piece, "narrow", 1) for piece in [own_again] + across]
    other_odd = [swap(piece, "narrow", 1) for piece in [beside] + corner]
    pieces = [own] + across + odd, [beside] + corner + other_odd
    return pieces, (stage_one, stage_two, odd + other_odd)


def scatter_rows(even, odd, other_even, other_odd, tokens=()):
    size = lax.axis_size("narrow")
    rows = even.shape[0] // (size // 2)
    half = rows // 2
    stage_one = [swap(other_odd, "narrow", 1), swap(odd, "narrow", 1)]
    other = other_even.astype(f32) + stage_one[0].astype(f32)
    mine = even.astype(f32) + stage_one[1].astype(f32)
    beside_top, beside_bottom = other[:half], other[half:rows]
    out = mine[:rows]
    corners = other[rows:].astype(bf16)
    [corners] = after([corners], tokens)
    spread, stage_two, stage_three = [], [], []
    for n, k in enumerate(range(2, size, 2)):
        at = n * rows
        ends = [
            swap(corners[at : at + half], "wide", 1),
            swap(corners[at + half : at + rows], "narrow", k),
        ]
        stage_two += ends
        beside_bottom = beside_bottom + ends[1].astype(f32)
        at = at + rows
        spread.append(
            jnp.concatenate(
                [mine[at : at + half] + ends[0].astype(f32), mine[at + half : at + rows]], axis=0
            ).astype(bf16)
        )
    spread.append(jnp.concatenate([beside_top, beside_bottom], axis=0).astype(bf16))
    spread = lax.optimization_barrier(tuple(spread))
    for n, k in enumerate(range(2, size, 2)):
        stage_three.append(swap(spread[n], "narrow", k))
        out = out + stage_three[-1].astype(f32)
    stage_three.append(swap(spread[-1], "wide", 1))
    return out + stage_three[-1].astype(f32), (stage_one, stage_two, stage_three)


def inverse_rms(values):
    return lax.rsqrt(jnp.mean(values * values, axis=-1, keepdims=True) + epsilon)


def norm_back(values, rate, gain, grad):
    a = grad * gain
    inner = jnp.mean(a * values, axis=-1, keepdims=True)
    return rate * a - values * (rate * rate * rate) * inner


def filter_kernel(base_re, base_im, step_re, step_im, out):
    poles = base_re.shape[0]
    width = out.shape[1]
    for g in range(width // 128 if width % 128 == 0 else 1):
        lanes = pl.ds(g * 128, min(128, width))
        start = tuple(base_re[j, :, lanes] for j in range(poles)) + tuple(
            base_im[j, :, lanes] for j in range(poles)
        )

        def step(b, state):
            total = state[0]
            for j in range(1, poles):
                total = total + state[j]
            out[pl.ds(pl.multiple_of(b * 8, 8), 8), lanes] = total
            new_re, new_im = [], []
            for j in range(poles):
                sr = step_re[j, :, lanes]
                si = step_im[j, :, lanes]
                new_re.append(state[j] * sr - state[poles + j] * si)
                new_im.append(state[j] * si + state[poles + j] * sr)
            return tuple(new_re) + tuple(new_im)

        lax.fori_loop(0, SPAN // 8, step, start)


def filter_taps(base_re, base_im, step_re, step_im):
    width = base_re.shape[2]
    return pl.pallas_call(
        filter_kernel,
        out_shape=jax.ShapeDtypeStruct((SPAN, width), f32),
        cost_estimate=pl.CostEstimate(
            flops=16 * 7 * SPAN * width, bytes_accessed=4 * SPAN * width, transcendentals=0
        ),
        name="taps",
    )(base_re, base_im, step_re, step_im)


def moment_kernel(grad, step_re, step_im, sum_re, sum_im, mom_re, mom_im):
    poles = step_re.shape[0]
    width = grad.shape[1]
    per = 8
    for g in range(width // 128 if width % 128 == 0 else 1):
        lanes = pl.ds(g * 128, min(128, width))
        for j0 in range(0, poles, per):
            zero = jnp.zeros((8, min(128, width)), f32)

            def step(i, state):
                b = SPAN // 8 - 1 - i
                value = grad[pl.ds(pl.multiple_of(b * 8, 8), 8), lanes]
                new = []
                for n in range(per):
                    sr = step_re[j0 + n, :, lanes]
                    si = step_im[j0 + n, :, lanes]
                    pr, pi, qr, qi = state[4 * n : 4 * n + 4]
                    ur, ui = pr + qr, pi + qi
                    new += [
                        pr * sr - pi * si + value,
                        pr * si + pi * sr,
                        ur * sr - ui * si,
                        ur * si + ui * sr,
                    ]
                return tuple(new)

            state = lax.fori_loop(0, SPAN // 8, step, (zero,) * (4 * per))
            for n in range(per):
                sum_re[j0 + n, :, lanes] = state[4 * n]
                sum_im[j0 + n, :, lanes] = state[4 * n + 1]
                mom_re[j0 + n, :, lanes] = state[4 * n + 2]
                mom_im[j0 + n, :, lanes] = state[4 * n + 3]


def filter_moments(grad, step_re, step_im):
    poles, _, width = step_re.shape
    shape = jax.ShapeDtypeStruct((poles, 8, width), f32)
    return pl.pallas_call(
        moment_kernel,
        out_shape=(shape,) * 4,
        cost_estimate=pl.CostEstimate(
            flops=16 * 15 * SPAN * width, bytes_accessed=4 * SPAN * width, transcendentals=0
        ),
        name="moments",
    )(grad, step_re, step_im)


LIVE, KEEP_ONE, KEEP_TWO = 0, 1, 2


def load_masked(order, proj, table, m_scr):
    pieces, rows, _ = proj.shape
    m_scr[0:8, :] = jnp.zeros_like(m_scr[0:8, :])

    def piece(b, _):
        p = order[b]
        at = pl.multiple_of(b * rows, rows)
        live = table[pl.ds(at, rows), LIVE : LIVE + 1]
        m_scr[pl.ds(pl.multiple_of(at + 8, 8), rows), :] = proj[p] * live
        return 0

    lax.fori_loop(0, pieces, piece, 0)


def short_block(m_scr, taps, table, at):
    window = m_scr[pl.ds(at, BLOCK + 8), :]
    one = table[pl.ds(at, BLOCK), KEEP_ONE : KEEP_ONE + 1]
    two = table[pl.ds(at, BLOCK), KEEP_TWO : KEEP_TWO + 1]
    here = window[8:]
    once = window[7 : BLOCK + 7] * one
    twice = window[6 : BLOCK + 6] * two
    short = taps[0:1, :] * here + taps[1:2, :] * once + taps[2:3, :] * twice
    return short, here, once, twice


def pack_document(source, packed, first, count):
    blocks = source.shape[0] // BLOCK
    for kb in range(LONGEST):
        at = pl.multiple_of(jnp.minimum(first + kb, blocks - 1) * BLOCK, BLOCK)
        inside = (kb < count).astype(f32)
        packed[kb * BLOCK : (kb + 1) * BLOCK, :] = (source[pl.ds(at, BLOCK), :] * inside).astype(bf16)


def place_document(result, target, first, count):
    for kb in range(LONGEST):

        @pl.when(kb < count)
        def _():
            at = pl.multiple_of((first + kb) * BLOCK, BLOCK)
            target[pl.ds(at, BLOCK), :] = result[kb * BLOCK : (kb + 1) * BLOCK, :]


def forward_kernel(
    order, first, count, proj, taps, table, spectrum, fwd, inv, gated, long_out, seen, m_scr, u_scr, q_scr, packed
):
    width = long_out.shape[1]
    pieces, rows, _ = proj.shape
    blocks = long_out.shape[0] // BLOCK
    load_masked(order, proj, table, m_scr)

    def block(n, _):
        at = pl.multiple_of(n * BLOCK, BLOCK)
        short, _, _, _ = short_block(m_scr, taps, table, at)
        q_scr[pl.ds(at, BLOCK), :] = short[:, :width]
        u_scr[pl.ds(at, BLOCK), :] = short[:, width : 2 * width] * short[:, 2 * width :]
        return 0

    lax.fori_loop(0, blocks, block, 0)

    def document(d, _):
        pack_document(u_scr, packed, first[d], count[d])
        both = jnp.dot(fwd[...], packed[...], preferred_element_type=f32)
        seen[d] = both.astype(bf16)
        re, im = both[:FREQ], both[FREQ:]
        hr, hi = spectrum[:FREQ], spectrum[FREQ:]
        answer = jnp.concatenate([re * hr - im * hi, re * hi + im * hr], axis=0).astype(bf16)
        result = jnp.dot(inv[...], answer, preferred_element_type=f32)
        place_document(result, long_out, first[d], count[d])
        return 0

    lax.fori_loop(0, seen.shape[0], document, 0)

    def piece(b, _):
        at = pl.multiple_of(b * rows, rows)
        gated[order[b]] = (q_scr[pl.ds(at, rows), :] * long_out[pl.ds(at, rows), :]).astype(bf16)
        return 0

    lax.fori_loop(0, pieces, piece, 0)


def backward_kernel(
    order, first, count, proj, d_gated, long_out, seen, taps, table, spectrum, fwd, inv,
    dz, d_filter, d_taps, m_scr, dy_scr, k_scr, v_scr, ds_scr, packed, d_spec,
):
    width = long_out.shape[1]
    pieces, rows, _ = proj.shape
    slots = long_out.shape[0]
    blocks = slots // BLOCK
    per_piece = rows // BLOCK
    load_masked(order, proj, table, m_scr)
    ds_scr[slots : slots + 8, :] = jnp.zeros_like(ds_scr[slots : slots + 8, :])

    def block(n, _):
        at = pl.multiple_of(n * BLOCK, BLOCK)
        short, _, _, _ = short_block(m_scr, taps, table, at)
        within = pl.multiple_of((n % per_piece) * BLOCK, BLOCK)
        dg = d_gated[order[n // per_piece], pl.ds(within, BLOCK), :]
        dy_scr[pl.ds(at, BLOCK), :] = dg * short[:, :width]
        ds_scr[pl.ds(at, BLOCK), :width] = dg * long_out[pl.ds(at, BLOCK), :]
        k_scr[pl.ds(at, BLOCK), :] = short[:, width : 2 * width]
        v_scr[pl.ds(at, BLOCK), :] = short[:, 2 * width :]
        return 0

    lax.fori_loop(0, blocks, block, 0)
    d_spec[...] = jnp.zeros_like(d_spec)

    def document(d, _):
        pack_document(dy_scr, packed, first[d], count[d])
        both = jnp.dot(fwd[...], packed[...], preferred_element_type=f32)
        re, im = both[:FREQ], both[FREQ:]
        hr, hi = spectrum[:FREQ], spectrum[FREQ:]
        answer = jnp.concatenate([re * hr + im * hi, im * hr - re * hi], axis=0).astype(bf16)
        result = jnp.dot(inv[...], answer, preferred_element_type=f32)
        ur, ui = seen[d, :FREQ].astype(f32), seen[d, FREQ:].astype(f32)
        d_spec[:FREQ] += re * ur + im * ui
        d_spec[FREQ:] += im * ur - re * ui
        for kb in range(LONGEST):

            @pl.when(kb < count[d])
            def _():
                at = pl.multiple_of((first[d] + kb) * BLOCK, BLOCK)
                du = result[kb * BLOCK : (kb + 1) * BLOCK, :]
                ds_scr[pl.ds(at, BLOCK), width : 2 * width] = du * v_scr[pl.ds(at, BLOCK), :]
                ds_scr[pl.ds(at, BLOCK), 2 * width :] = du * k_scr[pl.ds(at, BLOCK), :]

        return 0

    lax.fori_loop(0, seen.shape[0], document, 0)
    d_filter[...] = jnp.dot(inv[...], d_spec[...].astype(bf16), preferred_element_type=f32)
    d_taps[...] = jnp.zeros_like(d_taps)

    def back(n, _):
        at = pl.multiple_of(n * BLOCK, BLOCK)
        window = m_scr[pl.ds(at, BLOCK + 8), :]
        ahead = ds_scr[pl.ds(at, BLOCK + 8), :]
        one = table[pl.ds(at, BLOCK + 8), KEEP_ONE : KEEP_ONE + 1]
        two = table[pl.ds(at, BLOCK + 8), KEEP_TWO : KEEP_TWO + 1]
        live = table[pl.ds(at, BLOCK), LIVE : LIVE + 1]
        ds = ahead[:BLOCK]
        ahead_one = ahead * one
        ahead_two = ahead * two
        dm = (
            taps[0:1, :] * ds
            + taps[1:2, :] * ahead_one[1 : BLOCK + 1]
            + taps[2:3, :] * ahead_two[2 : BLOCK + 2]
        )
        d_taps[0:1, :] += jnp.sum(window[8:] * ds, axis=0, keepdims=True)
        d_taps[1:2, :] += jnp.sum(window[7 : BLOCK + 7] * ahead_one[:BLOCK], axis=0, keepdims=True)
        d_taps[2:3, :] += jnp.sum(window[6 : BLOCK + 6] * ahead_two[:BLOCK], axis=0, keepdims=True)
        within = pl.multiple_of((n % per_piece) * BLOCK, BLOCK)
        dz[order[n // per_piece], pl.ds(within, BLOCK), :] = (dm * live).astype(bf16)
        return 0

    lax.fori_loop(0, blocks, back, 0)


smem = pl.BlockSpec(memory_space=pltpu.SMEM)
vmem = pl.BlockSpec(memory_space=pltpu.VMEM)


def mixer_forward(order, first, count, proj, taps, table, spectrum, fwd, inv):
    pieces, rows, three = proj.shape
    width = three // 3
    slots = pieces * rows
    docs = first.shape[0]
    return pl.pallas_call(
        forward_kernel,
        out_shape=(
            jax.ShapeDtypeStruct((pieces, rows, width), bf16),
            jax.ShapeDtypeStruct((slots, width), f32),
            jax.ShapeDtypeStruct((docs, 2 * FREQ, width), bf16),
        ),
        in_specs=[smem] * 3 + [vmem] * 6,
        out_specs=(vmem,) * 3,
        scratch_shapes=[
            pltpu.VMEM((slots + 8, three), f32),
            pltpu.VMEM((slots, width), f32),
            pltpu.VMEM((slots, width), f32),
            pltpu.VMEM((SPAN, width), bf16),
        ],
        compiler_params=pltpu.CompilerParams(vmem_limit_bytes=40 * 2**20),
        cost_estimate=pl.CostEstimate(
            flops=docs * 8 * FREQ * SPAN * width,
            bytes_accessed=slots * three * 4 + 8 * slots * width,
            transcendentals=0,
        ),
        name="mixer_forward",
    )(order, first, count, proj, taps, table, spectrum, fwd, inv)


def mixer_backward(order, first, count, proj, d_gated, long_out, seen, taps, table, spectrum, fwd, inv):
    pieces, rows, three = proj.shape
    width = three // 3
    slots = pieces * rows
    docs = first.shape[0]
    return pl.pallas_call(
        backward_kernel,
        out_shape=(
            jax.ShapeDtypeStruct((pieces, rows, three), bf16),
            jax.ShapeDtypeStruct((SPAN, width), f32),
            jax.ShapeDtypeStruct((8, three), f32),
        ),
        in_specs=[smem] * 3 + [vmem] * 9,
        out_specs=(vmem,) * 3,
        scratch_shapes=[
            pltpu.VMEM((slots + 8, three), f32),
            pltpu.VMEM((slots, width), f32),
            pltpu.VMEM((slots, width), f32),
            pltpu.VMEM((slots, width), f32),
            pltpu.VMEM((slots + 8, three), f32),
            pltpu.VMEM((SPAN, width), bf16),
            pltpu.VMEM((2 * FREQ, width), f32),
        ],
        compiler_params=pltpu.CompilerParams(vmem_limit_bytes=48 * 2**20),
        cost_estimate=pl.CostEstimate(
            flops=docs * 10 * FREQ * SPAN * width,
            bytes_accessed=slots * three * 8 + 8 * slots * width,
            transcendentals=0,
        ),
        name="mixer_backward",
    )(order, first, count, proj, d_gated, long_out, seen, taps, table, spectrum, fwd, inv)


def layout(doc_blocks, doc_pad, slots):
    block_ends = jnp.cumsum(doc_blocks) * BLOCK
    starts = block_ends - doc_blocks * BLOCK
    places = jnp.arange(slots, dtype=jnp.int32)
    living = (places[None, :] >= starts[:, None]) & (
        places[None, :] < (block_ends - doc_pad)[:, None]
    )
    live = jnp.sum(living.astype(f32), axis=0)
    opening = jnp.sum((places[None, :] == starts[:, None]).astype(f32), axis=0)
    one = 1.0 - opening
    one = one * (places > 0)
    two = one * jnp.concatenate([jnp.zeros((1,), f32), one[:-1]])
    table = jnp.stack([live, one, two], axis=1)
    table = jnp.concatenate([table, jnp.zeros((8, 3), f32)], axis=0)
    return table, starts // BLOCK


def picked(index, count, values):
    hot = index[:, None] == jnp.arange(count)[None, :]
    shape = hot.shape + (1,) * (values.ndim - 1)
    return jnp.sum(jnp.where(hot.reshape(shape), values[None], 0), axis=1)


def body(
    tokens, w_in, w_out, gain_one, short_kernel, decay_rate, pole_angle, residue,
    gain_two, w_gate, w_up, w_down, doc_blocks, doc_pad, cotangent,
):
    wide, narrow = lax.axis_size("wide"), lax.axis_size("narrow")
    wide_at, narrow_at = lax.axis_index("wide"), lax.axis_index("narrow")
    outer = wide // 2
    _, local_rows, width = tokens.shape
    slots = local_rows * narrow
    even = slots // 2
    source = tokens[0].astype(f32)
    upstream_low = cotangent[0]
    poles = decay_rate.shape[1]
    own = w_in.shape[2]
    channels = own * outer
    hidden_units = w_gate.shape[1] * outer

    ring = np.array(ring_of(outer))
    ring_place = np.argsort(ring)
    tour = picked((wide_at // 2)[None], outer, jnp.asarray(ring_place, jnp.int32))[0]
    piece_places = (tour + jnp.asarray(ring_offsets(outer), jnp.int32)) % outer
    piece_outer = picked(piece_places, outer, jnp.asarray(ring, jnp.int32))
    sides = jnp.arange(2) ^ (wide_at % 2)
    offsets = list(range(0, narrow, 2)) + list(range(1, narrow, 2))
    place_of = np.argsort(np.array(offsets))
    order = picked(jnp.arange(narrow) ^ narrow_at, narrow, jnp.asarray(place_of, jnp.int32))
    narrow_of = jnp.asarray(offsets, jnp.int32) ^ narrow_at

    (first_own, first_other), first_stages = gather_rows(tokens[0])

    small = jnp.concatenate(
        [
            short_kernel.reshape(9, own),
            decay_rate.T,
            pole_angle.T,
            residue.T,
            gain_one[None],
            gain_two[None],
        ],
        axis=0,
    )
    small_all = jnp.concatenate(gather_ring(small, axis=1, halves=False)[0], axis=1)
    gains = small_all[small.shape[0] - 2 :].reshape(2, outer, own)
    [gains] = after([gains], first_stages[0])
    gains = jnp.stack([gains, swap(gains, "wide", 1)])
    gains = jnp.stack([gains] + [swap(gains, "narrow", k) for k in range(2, narrow, 2)])
    gains = jnp.concatenate([gains, swap(gains, "narrow", 1)], axis=0).astype(f32)
    gains = picked(order, narrow, gains).transpose(1, 3, 0, 2, 4)
    gains = picked(sides, 2, gains).transpose(1, 0, 2, 3, 4)
    hot = piece_outer[None, :] == jnp.arange(outer)[:, None]
    gains = jnp.sum(jnp.where(hot[:, :, None, None, None, None], gains[None], 0), axis=1)
    gain_all = gains.transpose(3, 0, 1, 2, 4).reshape(2, width)
    gain_first, gain_last = gain_all[0], gain_all[1]

    def reduce_gain(values):
        values = values.reshape(2, outer, 2, narrow, own).transpose(1, 2, 3, 0, 4)
        values = picked(piece_outer, outer, values).transpose(1, 0, 2, 3, 4)
        values = picked(sides, 2, values).transpose(2, 0, 1, 3, 4)
        values = picked(narrow_of, narrow, values)
        total = values[: narrow // 2] + swap(values[narrow // 2 :], "narrow", 1)
        summed = total[0]
        for k in range(1, narrow // 2):
            summed = summed + swap(total[k], "narrow", 2 * k)
        summed = summed[0] + swap(summed[1], "wide", 1)
        return scatter_ring(summed, halves=False)[0][0]

    documents = jnp.concatenate([doc_blocks, doc_pad], axis=0)
    [documents] = after([documents], first_stages[0])
    documents = (documents, swap(documents, "wide", 1))
    tables = [layout(rules[0], rules[1], slots) for rules in documents]

    in_pieces, last = gather_ring(w_in.transpose(0, 2, 1), axis=1)
    out_pieces, last = gather_ring(w_out, tokens=list(last) + first_stages[2])

    def normed(pieces):
        values = jnp.concatenate(pieces, axis=0).astype(f32)
        return (values * inverse_rms(values) * gain_first).astype(bf16)

    rate_first = inverse_rms(source)
    rows_first = [normed(first_own), normed(first_other)]
    (upstream_own, upstream_other), _ = gather_rows(upstream_low, first_stages[1])

    matrix = transform()
    fwd = jnp.asarray(matrix, bf16)
    inv = jnp.asarray(matrix.T / SPAN, bf16)

    block = small_all.astype(f32)
    taps = block[:9].reshape(3, 3 * channels)
    taps = jnp.concatenate([taps, jnp.zeros((5, 3 * channels), f32)], axis=0)
    decay = block[9 : 9 + poles][:, None, :]
    angle = block[9 + poles : 9 + 2 * poles][:, None, :]
    res_re = block[9 + 2 * poles : 9 + 3 * poles][:, None, :]
    res_im = -block[9 + 3 * poles : 9 + 4 * poles][:, None, :]
    lag = jnp.arange(8, dtype=f32)[None, :, None]
    fade = jnp.exp(-decay * lag)
    power_re, power_im = fade * jnp.cos(angle * lag), fade * jnp.sin(angle * lag)
    fade_step = jnp.exp(-decay * 8.0)
    step_re = jnp.broadcast_to(fade_step * jnp.cos(angle * 8.0), power_re.shape)
    step_im = jnp.broadcast_to(fade_step * jnp.sin(angle * 8.0), power_re.shape)
    filt = filter_taps(
        res_re * power_re - res_im * power_im,
        res_re * power_im + res_im * power_re,
        step_re,
        step_im,
    )
    spectrum = lax.dot_general(
        jnp.asarray(matrix),
        filt,
        (((1,), (0,)), ((), ())),
        precision=lax.Precision.HIGHEST,
        preferred_element_type=f32,
    )
    res_re, res_im = res_re[:, 0], -res_im[:, 0]

    in_all = jnp.concatenate(in_pieces, axis=1).reshape(3 * channels, width)
    mixed = []
    for r in range(2):
        table, first = tables[r]
        proj = nt(rows_first[r], in_all).reshape(narrow, local_rows, 3 * channels)
        gated, long_out, seen = mixer_forward(
            order, first, documents[r][0], proj, taps, table, spectrum, fwd, inv
        )
        mixed.append((proj, gated.reshape(slots, channels), long_out, seen))
    out_all = jnp.concatenate(out_pieces, axis=0)
    parts = [slice(0, even), slice(even, slots)]
    shares = [nn(mixed[r][1][p], out_all).astype(bf16) for r in range(2) for p in parts]
    mixer_out, stages = scatter_rows(*shares)
    middle = source + mixer_out
    rate_last = inverse_rms(middle)
    rows_upstream = jnp.concatenate(upstream_own + upstream_other, axis=0)
    (second_own, second_other), second_stages = gather_rows(
        (middle * rate_last * gain_last).astype(bf16)
    )
    rows_second = jnp.concatenate(second_own + second_other, axis=0)
    down_pieces, last = gather_ring(w_down.T, tokens=last, later=stages[0])
    gate_pieces, last = gather_ring(w_gate.T, tokens=last + stages[1], later=stages[2])
    up_pieces, last = gather_ring(
        w_up.T, tokens=last + second_stages[0], later=second_stages[1]
    )

    gate_up = jnp.concatenate(gate_pieces + up_pieces, axis=0)
    down_all = jnp.concatenate(down_pieces, axis=0)
    d_hidden = nt(down_all, rows_upstream)
    pre = nt(gate_up, rows_second)
    gate_pre, up_pre = pre[:hidden_units], pre[hidden_units:]
    sig = jax.nn.sigmoid(gate_pre)
    silu = gate_pre * sig
    hidden = (silu * up_pre).astype(bf16)
    d_gate = (d_hidden * up_pre * sig * (1.0 + gate_pre * (1.0 - sig))).astype(bf16)
    d_up = (d_hidden * silu).astype(bf16)
    d_pre = jnp.concatenate([d_gate, d_up], axis=0)
    grad_down = nn(hidden, rows_upstream).astype(bf16)
    d_pre, *_ = after([d_pre], [grad_down])
    parts = [slice(p, p + even) for p in range(0, 2 * slots, even)]
    shares = [tn(d_pre[:, p], gate_up).astype(bf16) for p in parts]
    d_second, stages = scatter_rows(*shares)
    upstream = upstream_low.astype(f32)
    d_middle = upstream + norm_back(middle, rate_last, gain_last, d_second)
    (middle_own, middle_other), middle_stages = gather_rows(d_middle.astype(bf16))
    rows_dmiddle = [jnp.concatenate(middle_own, axis=0), jnp.concatenate(middle_other, axis=0)]
    down_share, last = scatter_ring(grad_down, later=stages[1])
    [d_gate] = after([d_gate], stages[0])
    [d_up] = after([d_up], stages[1])
    grad_pre = jnp.stack([nn(d, rows_second).astype(bf16) for d in (d_gate, d_up)])
    pre_share, last = scatter_ring(
        grad_pre, axis=1, tokens=list(last) + stages[2], later=middle_stages[1]
    )
    [hidden] = after([hidden], [shares[1], shares[3]])
    down_shares = [tn(hidden[:, p], down_all).astype(bf16) for p in parts]
    down_out, _ = scatter_rows(*down_shares, tokens=middle_stages[1])
    block_output = (middle + down_out).astype(bf16)
    grad_gain_two = jnp.sum(d_second * middle * rate_last, axis=0)

    halves = (slice(0, even), slice(even, slots))
    shares, d_rows, grad_gain_one, d_filter, d_taps = [None, None], [None, None], 0.0, 0.0, 0.0
    for r in range(2):
        proj, gated, long_out, seen = mixed[r]
        table, first = tables[r]
        d_gated = nt(rows_dmiddle[r], out_all).reshape(narrow, local_rows, channels)
        dz, d_filter_row, d_taps_row = mixer_backward(
            order, first, documents[r][0], proj, d_gated, long_out, seen, taps, table,
            spectrum, fwd, inv,
        )
        d_rows[r] = dz.reshape(slots, 3 * channels)
        d_filter, d_taps = d_filter + d_filter_row, d_taps + d_taps_row
        shares[r] = [nn(d_rows[r][p], in_all).astype(bf16) for p in halves]
        for n, share in enumerate(shares[r]):
            rows = rows_first[r][n * even : (n + 1) * even]
            grad_gain_one = grad_gain_one + jnp.sum(share.astype(f32) * rows.astype(f32), axis=0)
    d_normed, stages = scatter_rows(*shares[0], *shares[1])
    input_grad = (d_middle + norm_back(source, rate_first, gain_first, d_normed)).astype(bf16)
    done = shares[0] + shares[1]
    d_rows = after(d_rows, done)
    grad_in = sum(tn(d_rows[r], rows_first[r]) for r in range(2)).astype(bf16)
    d_filter, *_ = after([d_filter], [grad_in])
    gated = after([mixed[0][1], mixed[1][1]], stages[1])
    grad_out = sum(tn(gated[r], rows_dmiddle[r]) for r in range(2)).astype(bf16)
    in_share, last = scatter_ring(
        grad_in.reshape(3, channels, width), axis=1, tokens=list(last) + stages[0]
    )
    out_share, _ = scatter_ring(grad_out, tokens=last)
    gain_grads = after([jnp.stack([grad_gain_one / gain_first, grad_gain_two])], stages[1])
    gain_share = reduce_gain(gain_grads[0])

    sum_re, sum_im, mom_re, mom_im = filter_moments(d_filter, step_re, step_im)
    full_re = lag * sum_re + 8.0 * mom_re
    full_im = lag * sum_im + 8.0 * mom_im
    grad_re = jnp.sum(power_re * sum_re - power_im * sum_im, axis=1)
    grad_im = jnp.sum(power_re * sum_im + power_im * sum_re, axis=1)
    lag_re = jnp.sum(power_re * full_re - power_im * full_im, axis=1)
    lag_im = jnp.sum(power_re * full_im + power_im * full_re, axis=1)
    small_grad = jnp.concatenate(
        [
            d_taps[:3].reshape(9, channels),
            -(res_re * lag_re + res_im * lag_im),
            res_im * lag_re - res_re * lag_im,
            grad_re,
            grad_im,
        ],
        axis=0,
    ).astype(bf16)
    [small_grad] = after([small_grad], stages[1])
    small_share, _ = scatter_ring(small_grad, axis=1, halves=False)

    at = 9 + poles
    return (
        block_output[None],
        input_grad[None],
        in_share.transpose(0, 2, 1),
        out_share,
        gain_share[0],
        small_share[:9].reshape(3, 3, own),
        small_share[9:at].T,
        small_share[at : at + poles].T,
        small_share[at + poles :].T,
        gain_share[1],
        pre_share[0].T,
        pre_share[1].T,
        down_share.T,
    )


def solution(mesh):
    both = ("wide", "narrow")
    return jax.shard_map(
        body,
        mesh=mesh,
        in_specs=(
            P("wide", "narrow", None),
            P(None, None, both),
            P(both, None),
            P(both),
            P(None, None, both),
            P(both, None),
            P(both, None),
            P(both, None),
            P(both),
            P(None, both),
            P(None, both),
            P(None, both),
            P("wide", None),
            P("wide", None),
            P("wide", "narrow", None),
        ),
        out_specs=(
            P("wide", "narrow", None),
            P("wide", "narrow", None),
            P(None, None, both),
            P(both, None),
            P(both),
            P(None, None, both),
            P(both, None),
            P(both, None),
            P(both, None),
            P(both),
            P(None, both),
            P(None, both),
            P(None, both),
        ),
        check_vma=False,
    )
```

```python
from functools import partial

import jax
import jax.numpy as jnp
import numpy as np
from jax import lax
from jax.experimental import pallas as pl
from jax.experimental.pallas import tpu as pltpu
from jax.sharding import PartitionSpec as P

BLOCK = 128
LONGEST = 4
SPAN = LONGEST * BLOCK
FREQ = SPAN

epsilon = 1e-06
bf16 = jnp.bfloat16
f32 = jnp.float32


def transform():
    k = np.arange(FREQ)[:, None] * 2 + 1
    t = np.arange(SPAN)[None, :]
    turn = (k * t % (4 * SPAN)) * (2 * np.pi / (4 * SPAN))
    return np.concatenate([np.cos(turn), -np.sin(turn)], axis=0).astype(np.float32)


def nn(a, b):
    return lax.dot_general(a, b, (((1,), (0,)), ((), ())), preferred_element_type=f32)


def nt(a, b):
    return lax.dot_general(a, b, (((1,), (1,)), ((), ())), preferred_element_type=f32)


def tn(a, b):
    return lax.dot_general(a, b, (((0,), (0,)), ((), ())), preferred_element_type=f32)


def swap(values, axis, shift):
    size = lax.axis_size(axis)
    return lax.ppermute(values, axis, [(i, i ^ shift) for i in range(size)])


def after(values, tokens):
    if not tokens:
        return values
    joined = lax.optimization_barrier(tuple(values) + tuple(tokens))
    return list(joined[: len(values)])


def ring_of(size):
    return list(range(0, size, 2)) + list(range(size - 1, 0, -2))


def along(values, step):
    outer = lax.axis_size("wide") // 2
    ring = ring_of(outer)
    pairs = [
        (ring[p] * 2 + side, ring[(p + step) % outer] * 2 + side)
        for p in range(outer)
        for side in range(2)
    ]
    return lax.ppermute(values, "wide", pairs)


def ring_offsets(outer):
    near = [sign * h for h in range(1, outer // 2) for sign in (-1, 1)]
    return [0] + near + [outer // 2]


def cut_of(rows):
    cut = (rows // 2 + 15) // 16 * 16
    return cut if cut < rows else rows // 2


def two_parts(values, axis):
    cut = cut_of(values.shape[axis])
    return (
        lax.slice_in_dim(values, 0, cut, axis=axis),
        lax.slice_in_dim(values, cut, values.shape[axis], axis=axis),
    )


class Gather:
    def __init__(self, own):
        self.most = lax.axis_size("wide") // 4 - 1
        self.before, self.behind, self.opposite = [own], [own], []

    def sends(self):
        if len(self.before) <= self.most:
            return self.before[-1], self.behind[-1]
        return two_parts(self.before[-1], 0)[0], two_parts(self.behind[-1], 0)[1]

    def take(self, got, back):
        if len(self.before) <= self.most:
            self.before.append(got)
            self.behind.append(back)
        else:
            self.opposite = [got, back]

    def pieces(self):
        near = [piece for pair in zip(self.before[1:], self.behind[1:]) for piece in pair]
        return [self.before[0]] + near + [jnp.concatenate(self.opposite, axis=0)]


class Scatter:
    def __init__(self, chunks):
        self.left = len(chunks) // 2 - 1
        self.wire = chunks[0].dtype
        self.total = chunks[0].astype(f32)
        self.behind = [chunk.astype(f32) for chunk in chunks[1:-1:2]]
        self.ahead = [chunk.astype(f32) for chunk in chunks[2:-1:2]]
        self.last = chunks[-1]

    def sends(self):
        if self.last is not None:
            return two_parts(self.last, 0)
        h = self.left - 1
        return self.ahead[h].astype(self.wire), self.behind[h].astype(self.wire)

    def take(self, got, back):
        got, back = got.astype(f32), back.astype(f32)
        h = self.left - 1
        if self.last is not None:
            top, bottom = two_parts(self.ahead[h], 0)
            self.ahead[h] = jnp.concatenate([top + got, bottom], axis=0)
            top, bottom = two_parts(self.behind[h], 0)
            self.behind[h] = jnp.concatenate([top, bottom + back], axis=0)
            self.last = None
            return
        self.left = h
        if h:
            self.ahead[h - 1] = self.ahead[h - 1] + got
            self.behind[h - 1] = self.behind[h - 1] + back
        else:
            self.total = self.total + got + back


def ring_step(items, tokens=()):
    sends = [item.sends() for item in items]
    ways = [one[0] if len(one) == 1 else jnp.concatenate(one, axis=0) for one in zip(*sends)]
    ways = after(ways, list(tokens)) if tokens else lax.optimization_barrier(tuple(ways))
    got, back = along(ways[0], 1), along(ways[1], -1)
    at = [0, 0]
    for item, (ahead, behind) in zip(items, sends):
        ends = [at[0] + ahead.shape[0], at[1] + behind.shape[0]]
        item.take(got[at[0] : ends[0]], back[at[1] : ends[1]])
        at = ends
    return [got, back]


def gather_small(own):
    outer = lax.axis_size("wide") // 2
    pieces = [own]
    for _ in range(1, outer):
        pieces.append(along(pieces[-1], 1))
    order = [-offset % outer for offset in ring_offsets(outer)]
    return jnp.concatenate([pieces[k] for k in order], axis=1)


def scatter_small(chunks):
    offsets = ring_offsets(len(chunks))
    total = chunks[0].astype(f32)
    for chunk, offset in zip(chunks[1:], offsets[1:]):
        total = total + along(chunk, offset).astype(f32)
    return total


def gather_rows(own, tokens=()):
    size = lax.axis_size("narrow")
    half = own.shape[0] // 2
    [own] = after([own], tokens)
    across = [swap(own, "narrow", k) for k in range(2, size, 2)]
    beside = swap(own, "wide", 1)
    stage_one = across + [beside]
    parts, stage_two = [beside], []
    for n, k in enumerate(range(2, size, 2)):
        ends = [swap(across[n][:half], "wide", 1), swap(beside[half:], "narrow", k)]
        parts += ends
        stage_two += ends
    even = jnp.concatenate([own] + across, axis=0)
    other_even = jnp.concatenate(parts, axis=0)
    odd, other_odd = swap(even, "narrow", 1), swap(other_even, "narrow", 1)
    return ([even, odd], [other_even, other_odd]), (stage_one, stage_two, [odd, other_odd])


def scatter_rows(even, odd, other_even, other_odd, tokens=()):
    size = lax.axis_size("narrow")
    rows = even.shape[0] // (size // 2)
    half = rows // 2
    other = other_even.astype(f32) + other_odd.astype(f32)
    mine = even.astype(f32) + odd.astype(f32)
    beside_top, beside_bottom = other[:half], other[half:rows]
    out = mine[:rows]
    corners = other[rows:].astype(bf16)
    [corners] = after([corners], tokens)
    spread, stage_two, stage_three = [], [], []
    for n, k in enumerate(range(2, size, 2)):
        at = n * rows
        ends = [
            swap(corners[at : at + half], "wide", 1),
            swap(corners[at + half : at + rows], "narrow", k),
        ]
        stage_two += ends
        beside_bottom = beside_bottom + ends[1].astype(f32)
        at = at + rows
        spread.append(
            jnp.concatenate(
                [mine[at : at + half] + ends[0].astype(f32), mine[at + half : at + rows]], axis=0
            ).astype(bf16)
        )
    spread.append(jnp.concatenate([beside_top, beside_bottom], axis=0).astype(bf16))
    spread = lax.optimization_barrier(tuple(spread))
    for n, k in enumerate(range(2, size, 2)):
        stage_three.append(swap(spread[n], "narrow", k))
        out = out + stage_three[-1].astype(f32)
    stage_three.append(swap(spread[-1], "wide", 1))
    return out + stage_three[-1].astype(f32), (stage_two, stage_three)


def inverse_rms(values):
    return lax.rsqrt(jnp.mean(values * values, axis=-1, keepdims=True) + epsilon)


def norm_kernel(*refs):
    pieces, gain, out = refs[:-2], refs[-2], refs[-1]
    rows = pieces[0].shape[0]
    step = 32 if rows % 32 == 0 else rows
    for n, piece in enumerate(pieces):

        def part(b, _):
            at = pl.multiple_of(b * step, step)
            values = piece[pl.ds(at, step), :].astype(f32)
            rate = lax.rsqrt(jnp.mean(values * values, axis=-1, keepdims=True) + epsilon)
            to = pl.multiple_of(n * rows + at, step)
            out[pl.ds(to, step), :] = (values * rate * gain[...]).astype(bf16)
            return 0

        lax.fori_loop(0, rows // step, part, 0)


def normed_rows(pieces, gain):
    rows, width = pieces[0].shape
    return pl.pallas_call(
        norm_kernel,
        out_shape=jax.ShapeDtypeStruct((rows * len(pieces), width), bf16),
        cost_estimate=pl.CostEstimate(
            flops=6 * rows * len(pieces) * width,
            bytes_accessed=4 * rows * len(pieces) * width,
            transcendentals=0,
        ),
        name="norm",
    )(*pieces, gain.reshape(1, width))


def norm_back(values, rate, gain, grad):
    a = grad * gain
    inner = jnp.mean(a * values, axis=-1, keepdims=True)
    return rate * a - values * (rate * rate * rate) * inner


def filter_kernel(base_re, base_im, step_re, step_im, out):
    poles = base_re.shape[0]
    width = out.shape[1]
    for g in range(width // 128 if width % 128 == 0 else 1):
        lanes = pl.ds(g * 128, min(128, width))
        start = tuple(base_re[j, :, lanes] for j in range(poles)) + tuple(
            base_im[j, :, lanes] for j in range(poles)
        )

        def step(b, state):
            total = state[0]
            for j in range(1, poles):
                total = total + state[j]
            out[pl.ds(pl.multiple_of(b * 8, 8), 8), lanes] = total
            new_re, new_im = [], []
            for j in range(poles):
                sr = step_re[j, :, lanes]
                si = step_im[j, :, lanes]
                new_re.append(state[j] * sr - state[poles + j] * si)
                new_im.append(state[j] * si + state[poles + j] * sr)
            return tuple(new_re) + tuple(new_im)

        lax.fori_loop(0, SPAN // 8, step, start)


def filter_taps(base_re, base_im, step_re, step_im):
    width = base_re.shape[2]
    return pl.pallas_call(
        filter_kernel,
        out_shape=jax.ShapeDtypeStruct((SPAN, width), f32),
        cost_estimate=pl.CostEstimate(
            flops=16 * 7 * SPAN * width, bytes_accessed=4 * SPAN * width, transcendentals=0
        ),
        name="taps",
    )(base_re, base_im, step_re, step_im)


def moment_kernel(grad, step_re, step_im, sum_re, sum_im, mom_re, mom_im):
    poles = step_re.shape[0]
    width = grad.shape[1]
    per = 8
    for g in range(width // 128 if width % 128 == 0 else 1):
        lanes = pl.ds(g * 128, min(128, width))
        for j0 in range(0, poles, per):
            zero = jnp.zeros((8, min(128, width)), f32)

            def step(i, state):
                b = SPAN // 8 - 1 - i
                value = grad[pl.ds(pl.multiple_of(b * 8, 8), 8), lanes]
                new = []
                for n in range(per):
                    sr = step_re[j0 + n, :, lanes]
                    si = step_im[j0 + n, :, lanes]
                    pr, pi, qr, qi = state[4 * n : 4 * n + 4]
                    ur, ui = pr + qr, pi + qi
                    new += [
                        pr * sr - pi * si + value,
                        pr * si + pi * sr,
                        ur * sr - ui * si,
                        ur * si + ui * sr,
                    ]
                return tuple(new)

            state = lax.fori_loop(0, SPAN // 8, step, (zero,) * (4 * per))
            for n in range(per):
                sum_re[j0 + n, :, lanes] = state[4 * n]
                sum_im[j0 + n, :, lanes] = state[4 * n + 1]
                mom_re[j0 + n, :, lanes] = state[4 * n + 2]
                mom_im[j0 + n, :, lanes] = state[4 * n + 3]


def filter_moments(grad, step_re, step_im):
    poles, _, width = step_re.shape
    shape = jax.ShapeDtypeStruct((poles, 8, width), f32)
    return pl.pallas_call(
        moment_kernel,
        out_shape=(shape,) * 4,
        cost_estimate=pl.CostEstimate(
            flops=16 * 15 * SPAN * width, bytes_accessed=4 * SPAN * width, transcendentals=0
        ),
        name="moments",
    )(grad, step_re, step_im)


LIVE, KEEP_ONE, KEEP_TWO = 0, 1, 2


def load_masked(order, proj, table, m_scr):
    pieces, rows, _ = proj.shape
    m_scr[0:8, :] = jnp.zeros_like(m_scr[0:8, :])

    def piece(b, _):
        p = order[b]
        at = pl.multiple_of(b * rows, rows)
        live = table[pl.ds(at, rows), LIVE : LIVE + 1]
        m_scr[pl.ds(pl.multiple_of(at + 8, 8), rows), :] = proj[p] * live
        return 0

    lax.fori_loop(0, pieces, piece, 0)


def short_block(m_scr, taps, table, at):
    window = m_scr[pl.ds(at, BLOCK + 8), :]
    one = table[pl.ds(at, BLOCK), KEEP_ONE : KEEP_ONE + 1]
    two = table[pl.ds(at, BLOCK), KEEP_TWO : KEEP_TWO + 1]
    here = window[8:]
    once = window[7 : BLOCK + 7] * one
    twice = window[6 : BLOCK + 6] * two
    short = taps[0:1, :] * here + taps[1:2, :] * once + taps[2:3, :] * twice
    return short, here, once, twice


def pack_document(source, packed, first, count):
    blocks = source.shape[0] // BLOCK
    for kb in range(LONGEST):
        at = pl.multiple_of(jnp.minimum(first + kb, blocks - 1) * BLOCK, BLOCK)
        inside = (kb < count).astype(f32)
        packed[kb * BLOCK : (kb + 1) * BLOCK, :] = (source[pl.ds(at, BLOCK), :] * inside).astype(bf16)


def place_document(result, target, first, count):
    for kb in range(LONGEST):

        @pl.when(kb < count)
        def _():
            at = pl.multiple_of((first + kb) * BLOCK, BLOCK)
            target[pl.ds(at, BLOCK), :] = result[kb * BLOCK : (kb + 1) * BLOCK, :]


def forward_kernel(
    order, first, count, proj, taps, table, spectrum, fwd, inv, gated, long_out, seen, m_scr, u_scr, q_scr, packed
):
    width = long_out.shape[1]
    pieces, rows, _ = proj.shape
    blocks = long_out.shape[0] // BLOCK
    load_masked(order, proj, table, m_scr)

    def block(n, _):
        at = pl.multiple_of(n * BLOCK, BLOCK)
        short, _, _, _ = short_block(m_scr, taps, table, at)
        q_scr[pl.ds(at, BLOCK), :] = short[:, :width]
        u_scr[pl.ds(at, BLOCK), :] = short[:, width : 2 * width] * short[:, 2 * width :]
        return 0

    lax.fori_loop(0, blocks, block, 0)

    def document(d, _):
        pack_document(u_scr, packed, first[d], count[d])
        both = jnp.dot(fwd[...], packed[...], preferred_element_type=f32)
        seen[d] = both.astype(bf16)
        re, im = both[:FREQ], both[FREQ:]
        hr, hi = spectrum[:FREQ], spectrum[FREQ:]
        answer = jnp.concatenate([re * hr - im * hi, re * hi + im * hr], axis=0).astype(bf16)
        result = jnp.dot(inv[...], answer, preferred_element_type=f32)
        place_document(result, long_out, first[d], count[d])
        return 0

    lax.fori_loop(0, seen.shape[0], document, 0)

    def piece(b, _):
        at = pl.multiple_of(b * rows, rows)
        gated[order[b]] = (q_scr[pl.ds(at, rows), :] * long_out[pl.ds(at, rows), :]).astype(bf16)
        return 0

    lax.fori_loop(0, pieces, piece, 0)


def backward_kernel(
    order, first, count, proj, d_gated, long_out, seen, taps, table, spectrum, fwd, inv,
    dz, d_filter, d_taps, m_scr, dy_scr, k_scr, v_scr, ds_scr, packed, d_spec,
):
    width = long_out.shape[1]
    pieces, rows, _ = proj.shape
    slots = long_out.shape[0]
    blocks = slots // BLOCK
    per_piece = rows // BLOCK
    load_masked(order, proj, table, m_scr)
    ds_scr[slots : slots + 8, :] = jnp.zeros_like(ds_scr[slots : slots + 8, :])

    def block(n, _):
        at = pl.multiple_of(n * BLOCK, BLOCK)
        short, _, _, _ = short_block(m_scr, taps, table, at)
        within = pl.multiple_of((n % per_piece) * BLOCK, BLOCK)
        dg = d_gated[order[n // per_piece], pl.ds(within, BLOCK), :]
        dy_scr[pl.ds(at, BLOCK), :] = dg * short[:, :width]
        ds_scr[pl.ds(at, BLOCK), :width] = dg * long_out[pl.ds(at, BLOCK), :]
        k_scr[pl.ds(at, BLOCK), :] = short[:, width : 2 * width]
        v_scr[pl.ds(at, BLOCK), :] = short[:, 2 * width :]
        return 0

    lax.fori_loop(0, blocks, block, 0)
    d_spec[...] = jnp.zeros_like(d_spec)

    def document(d, _):
        pack_document(dy_scr, packed, first[d], count[d])
        both = jnp.dot(fwd[...], packed[...], preferred_element_type=f32)
        re, im = both[:FREQ], both[FREQ:]
        hr, hi = spectrum[:FREQ], spectrum[FREQ:]
        answer = jnp.concatenate([re * hr + im * hi, im * hr - re * hi], axis=0).astype(bf16)
        result = jnp.dot(inv[...], answer, preferred_element_type=f32)
        ur, ui = seen[d, :FREQ].astype(f32), seen[d, FREQ:].astype(f32)
        d_spec[:FREQ] += re * ur + im * ui
        d_spec[FREQ:] += im * ur - re * ui
        for kb in range(LONGEST):

            @pl.when(kb < count[d])
            def _():
                at = pl.multiple_of((first[d] + kb) * BLOCK, BLOCK)
                du = result[kb * BLOCK : (kb + 1) * BLOCK, :]
                ds_scr[pl.ds(at, BLOCK), width : 2 * width] = du * v_scr[pl.ds(at, BLOCK), :]
                ds_scr[pl.ds(at, BLOCK), 2 * width :] = du * k_scr[pl.ds(at, BLOCK), :]

        return 0

    lax.fori_loop(0, seen.shape[0], document, 0)
    d_filter[...] = jnp.dot(inv[...], d_spec[...].astype(bf16), preferred_element_type=f32)
    d_taps[...] = jnp.zeros_like(d_taps)

    def back(n, _):
        at = pl.multiple_of(n * BLOCK, BLOCK)
        window = m_scr[pl.ds(at, BLOCK + 8), :]
        ahead = ds_scr[pl.ds(at, BLOCK + 8), :]
        one = table[pl.ds(at, BLOCK + 8), KEEP_ONE : KEEP_ONE + 1]
        two = table[pl.ds(at, BLOCK + 8), KEEP_TWO : KEEP_TWO + 1]
        live = table[pl.ds(at, BLOCK), LIVE : LIVE + 1]
        ds = ahead[:BLOCK]
        ahead_one = ahead * one
        ahead_two = ahead * two
        dm = (
            taps[0:1, :] * ds
            + taps[1:2, :] * ahead_one[1 : BLOCK + 1]
            + taps[2:3, :] * ahead_two[2 : BLOCK + 2]
        )
        d_taps[0:1, :] += jnp.sum(window[8:] * ds, axis=0, keepdims=True)
        d_taps[1:2, :] += jnp.sum(window[7 : BLOCK + 7] * ahead_one[:BLOCK], axis=0, keepdims=True)
        d_taps[2:3, :] += jnp.sum(window[6 : BLOCK + 6] * ahead_two[:BLOCK], axis=0, keepdims=True)
        within = pl.multiple_of((n % per_piece) * BLOCK, BLOCK)
        dz[order[n // per_piece], pl.ds(within, BLOCK), :] = (dm * live).astype(bf16)
        return 0

    lax.fori_loop(0, blocks, back, 0)


smem = pl.BlockSpec(memory_space=pltpu.SMEM)
vmem = pl.BlockSpec(memory_space=pltpu.VMEM)


def mixer_forward(order, first, count, proj, taps, table, spectrum, fwd, inv):
    pieces, rows, three = proj.shape
    width = three // 3
    slots = pieces * rows
    docs = first.shape[0]
    return pl.pallas_call(
        forward_kernel,
        out_shape=(
            jax.ShapeDtypeStruct((pieces, rows, width), bf16),
            jax.ShapeDtypeStruct((slots, width), f32),
            jax.ShapeDtypeStruct((docs, 2 * FREQ, width), bf16),
        ),
        in_specs=[smem] * 3 + [vmem] * 6,
        out_specs=(vmem,) * 3,
        scratch_shapes=[
            pltpu.VMEM((slots + 8, three), f32),
            pltpu.VMEM((slots, width), f32),
            pltpu.VMEM((slots, width), f32),
            pltpu.VMEM((SPAN, width), bf16),
        ],
        compiler_params=pltpu.CompilerParams(vmem_limit_bytes=40 * 2**20),
        cost_estimate=pl.CostEstimate(
            flops=docs * 8 * FREQ * SPAN * width,
            bytes_accessed=slots * three * 4 + 8 * slots * width,
            transcendentals=0,
        ),
        name="mixer_forward",
    )(order, first, count, proj, taps, table, spectrum, fwd, inv)


def mixer_backward(order, first, count, proj, d_gated, long_out, seen, taps, table, spectrum, fwd, inv):
    pieces, rows, three = proj.shape
    width = three // 3
    slots = pieces * rows
    docs = first.shape[0]
    return pl.pallas_call(
        backward_kernel,
        out_shape=(
            jax.ShapeDtypeStruct((pieces, rows, three), bf16),
            jax.ShapeDtypeStruct((SPAN, width), f32),
            jax.ShapeDtypeStruct((8, three), f32),
        ),
        in_specs=[smem] * 3 + [vmem] * 9,
        out_specs=(vmem,) * 3,
        scratch_shapes=[
            pltpu.VMEM((slots + 8, three), f32),
            pltpu.VMEM((slots, width), f32),
            pltpu.VMEM((slots, width), f32),
            pltpu.VMEM((slots, width), f32),
            pltpu.VMEM((slots + 8, three), f32),
            pltpu.VMEM((SPAN, width), bf16),
            pltpu.VMEM((2 * FREQ, width), f32),
        ],
        compiler_params=pltpu.CompilerParams(vmem_limit_bytes=48 * 2**20),
        cost_estimate=pl.CostEstimate(
            flops=docs * 10 * FREQ * SPAN * width,
            bytes_accessed=slots * three * 8 + 8 * slots * width,
            transcendentals=0,
        ),
        name="mixer_backward",
    )(order, first, count, proj, d_gated, long_out, seen, taps, table, spectrum, fwd, inv)


def layout(doc_blocks, doc_pad, slots):
    block_ends = jnp.cumsum(doc_blocks) * BLOCK
    starts = block_ends - doc_blocks * BLOCK
    places = jnp.arange(slots, dtype=jnp.int32)
    living = (places[None, :] >= starts[:, None]) & (
        places[None, :] < (block_ends - doc_pad)[:, None]
    )
    live = jnp.sum(living.astype(f32), axis=0)
    opening = jnp.sum((places[None, :] == starts[:, None]).astype(f32), axis=0)
    one = 1.0 - opening
    one = one * (places > 0)
    two = one * jnp.concatenate([jnp.zeros((1,), f32), one[:-1]])
    table = jnp.stack([live, one, two], axis=1)
    table = jnp.concatenate([table, jnp.zeros((8, 3), f32)], axis=0)
    return table, starts // BLOCK


def picked(index, count, values):
    hot = index[:, None] == jnp.arange(count)[None, :]
    shape = hot.shape + (1,) * (values.ndim - 1)
    return jnp.sum(jnp.where(hot.reshape(shape), values[None], 0), axis=1)


def body(
    tokens, w_in, w_out, gain_one, short_kernel, decay_rate, pole_angle, residue,
    gain_two, w_gate, w_up, w_down, doc_blocks, doc_pad, cotangent,
):
    wide, narrow = lax.axis_size("wide"), lax.axis_size("narrow")
    wide_at, narrow_at = lax.axis_index("wide"), lax.axis_index("narrow")
    outer = wide // 2
    _, local_rows, width = tokens.shape
    slots = local_rows * narrow
    even = slots // 2
    source = tokens[0].astype(f32)
    upstream_low = cotangent[0]
    poles = decay_rate.shape[1]
    own = w_in.shape[2]
    channels = own * outer
    hidden_units = w_gate.shape[1] * outer

    ring = np.array(ring_of(outer))
    ring_place = np.argsort(ring)
    tour = picked((wide_at // 2)[None], outer, jnp.asarray(ring_place, jnp.int32))[0]
    piece_places = (tour + jnp.asarray(ring_offsets(outer), jnp.int32)) % outer
    piece_outer = picked(piece_places, outer, jnp.asarray(ring, jnp.int32))
    sides = jnp.arange(2) ^ (wide_at % 2)
    offsets = list(range(0, narrow, 2)) + list(range(1, narrow, 2))
    place_of = np.argsort(np.array(offsets))
    order = picked(jnp.arange(narrow) ^ narrow_at, narrow, jnp.asarray(place_of, jnp.int32))
    narrow_of = jnp.asarray(offsets, jnp.int32) ^ narrow_at

    (first_own, first_other), first_stages = gather_rows(tokens[0])

    small = jnp.concatenate(
        [
            short_kernel.reshape(9, own),
            decay_rate.T,
            pole_angle.T,
            residue.T,
            gain_one[None],
            gain_two[None],
        ],
        axis=0,
    )
    small_all = gather_small(small)
    gains = small_all[small.shape[0] - 2 :].reshape(2, outer, own)
    [gains] = after([gains], first_stages[0])
    gains = jnp.stack([gains, swap(gains, "wide", 1)])
    gains = jnp.stack([gains] + [swap(gains, "narrow", k) for k in range(2, narrow, 2)])
    gains = jnp.concatenate([gains, swap(gains, "narrow", 1)], axis=0).astype(f32)
    gains = picked(order, narrow, gains).transpose(1, 3, 0, 2, 4)
    gains = picked(sides, 2, gains).transpose(1, 0, 2, 3, 4)
    hot = piece_outer[None, :] == jnp.arange(outer)[:, None]
    gains = jnp.sum(jnp.where(hot[:, :, None, None, None, None], gains[None], 0), axis=1)
    gain_all = gains.transpose(3, 0, 1, 2, 4).reshape(2, width)
    gain_first, gain_last = gain_all[0], gain_all[1]

    def reduce_gain(values, tokens):
        values = values.reshape(2, outer, 2, narrow, own).transpose(1, 2, 3, 0, 4)
        values = picked(piece_outer, outer, values).transpose(1, 0, 2, 3, 4)
        values = picked(sides, 2, values).transpose(2, 0, 1, 3, 4)
        values = picked(narrow_of, narrow, values)
        total = values[: narrow // 2] + swap(values[narrow // 2 :], "narrow", 1)
        summed = total[0]
        for k in range(1, narrow // 2):
            summed = summed + swap(total[k], "narrow", 2 * k)
        summed = summed[0] + swap(summed[1], "wide", 1)
        [summed] = after([summed], tokens)
        return scatter_small([summed[j] for j in range(outer)])

    documents = jnp.concatenate([doc_blocks, doc_pad], axis=0)
    [documents] = after([documents], first_stages[0])
    documents = (documents, swap(documents, "wide", 1))
    tables = [layout(rules[0], rules[1], slots) for rules in documents]

    shards = [w_in.transpose(0, 2, 1).reshape(3 * own, width), w_out, w_down.T, w_gate.T, w_up.T]
    weights = [Gather(shard) for shard in shards]
    steps = outer // 2

    def weight_step(at, tokens):
        active = [weights[i] for i in range(len(weights)) if 0 <= at - i < steps]
        return ring_step(active, tokens)

    last = []
    for at in range(steps - 1):
        last = weight_step(at, last)
    last = weight_step(steps - 1, last + first_stages[0])
    last = weight_step(steps, last + first_stages[1])
    rows_first = [normed_rows(first_own, gain_first), normed_rows(first_other, gain_first)]
    rate_first = inverse_rms(source)
    (upstream_own, upstream_other), _ = gather_rows(upstream_low, first_stages[2])

    matrix = transform()
    fwd = jnp.asarray(matrix, bf16)
    inv = jnp.asarray(matrix.T / SPAN, bf16)

    block = small_all.astype(f32)
    taps = block[:9].reshape(3, 3 * channels)
    taps = jnp.concatenate([taps, jnp.zeros((5, 3 * channels), f32)], axis=0)
    decay = block[9 : 9 + poles][:, None, :]
    angle = block[9 + poles : 9 + 2 * poles][:, None, :]
    res_re = block[9 + 2 * poles : 9 + 3 * poles][:, None, :]
    res_im = -block[9 + 3 * poles : 9 + 4 * poles][:, None, :]
    lag = jnp.arange(8, dtype=f32)[None, :, None]
    fade = jnp.exp(-decay * lag)
    power_re, power_im = fade * jnp.cos(angle * lag), fade * jnp.sin(angle * lag)
    fade_step = jnp.exp(-decay * 8.0)
    step_re = jnp.broadcast_to(fade_step * jnp.cos(angle * 8.0), power_re.shape)
    step_im = jnp.broadcast_to(fade_step * jnp.sin(angle * 8.0), power_re.shape)
    filt = filter_taps(
        res_re * power_re - res_im * power_im,
        res_re * power_im + res_im * power_re,
        step_re,
        step_im,
    )
    spectrum = lax.dot_general(
        jnp.asarray(matrix),
        filt,
        (((1,), (0,)), ((), ())),
        precision=lax.Precision.HIGHEST,
        preferred_element_type=f32,
    )
    res_re, res_im = res_re[:, 0], -res_im[:, 0]

    in_pieces = [piece.reshape(3, own, width) for piece in weights[0].pieces()]
    in_all = jnp.concatenate(in_pieces, axis=1).reshape(3 * channels, width)
    mixed = []
    for r in range(2):
        table, first = tables[r]
        proj = nt(rows_first[r], in_all).reshape(narrow, local_rows, 3 * channels)
        gated, long_out, seen = mixer_forward(
            order, first, documents[r][0], proj, taps, table, spectrum, fwd, inv
        )
        mixed.append((proj, gated.reshape(slots, channels), long_out, seen))
    out_all = jnp.concatenate(weights[1].pieces(), axis=0)
    parts = [slice(0, even), slice(even, slots)]
    shares = [nn(mixed[r][1][p], out_all).astype(bf16) for r in range(2) for p in parts]
    cores = [swap(shares[n], "narrow", 1) for n in (1, 3)]
    mixer_out, stages = scatter_rows(shares[0], cores[0], shares[2], cores[1])
    middle = source + mixer_out
    rate_last = inverse_rms(middle)
    rows_upstream = jnp.concatenate(upstream_own + upstream_other, axis=0)
    (second_own, second_other), second_stages = gather_rows(
        (middle * rate_last * gain_last).astype(bf16)
    )
    rows_second = jnp.concatenate(second_own + second_other, axis=0)
    last = weight_step(steps + 1, last + cores)
    last = weight_step(steps + 2, last + stages[1])
    last = weight_step(steps + 3, last + second_stages[1])
    for at in range(steps + 4, steps + len(weights) - 1):
        last = weight_step(at, last)

    down_all, gate_all = [jnp.concatenate(weights[i].pieces(), axis=0) for i in (2, 3)]
    d_hidden = nt(down_all, rows_upstream)
    gate_pre = nt(gate_all, rows_second)
    up_pieces = after(weights[4].pieces(), [d_hidden, gate_pre])
    up_all = jnp.concatenate(up_pieces, axis=0)
    up_pre = nt(up_all, rows_second)
    sig = jax.nn.sigmoid(gate_pre)
    silu = gate_pre * sig
    hidden = (silu * up_pre).astype(bf16)
    d_gate = (d_hidden * up_pre * sig * (1.0 + gate_pre * (1.0 - sig))).astype(bf16)
    d_up = (d_hidden * silu).astype(bf16)
    grad_down = nn(hidden, rows_upstream).astype(bf16)
    d_gate, d_up = after([d_gate, d_up], [grad_down])
    grads = [Scatter(jnp.split(grad_down, outer, axis=0))]
    last = ring_step(grads)
    parts = [slice(p, p + even) for p in range(0, 2 * slots, even)]

    def second_share(n, tokens=()):
        one, two = after([d_gate, d_up], tokens)
        p = parts[n]
        return (tn(one[:, p], gate_all) + tn(two[:, p], up_all)).astype(bf16)

    odds = [second_share(n) for n in (1, 3)]
    cores = [swap(odd, "narrow", 1) for odd in odds]
    evens = [second_share(n, last) for n in (0, 2)]
    d_second, stages = scatter_rows(evens[0], cores[0], evens[1], cores[1])
    upstream = upstream_low.astype(f32)
    d_middle = upstream + norm_back(middle, rate_last, gain_last, d_second)
    (middle_own, middle_other), middle_stages = gather_rows(d_middle.astype(bf16))
    rows_dmiddle = [jnp.concatenate(middle_own, axis=0), jnp.concatenate(middle_other, axis=0)]
    d_gate, d_up = after([d_gate, d_up], cores)
    for d in (d_gate, d_up):
        grads.append(Scatter(jnp.split(nn(d, rows_second).astype(bf16), outer, axis=0)))
    for at in range(1, steps):
        last = ring_step(grads[:1], last + cores)
    down_last = last
    last = ring_step(grads[1:], last + stages[0])
    for at in range(1, steps):
        last = ring_step(grads[1:], last + stages[1])
    [hidden] = after([hidden], stages[0] + down_last)
    down_shares = [tn(hidden[:, p], down_all).astype(bf16) for p in parts]
    down_shares = after(down_shares, middle_stages[2])
    down_cores = [swap(down_shares[n], "narrow", 1) for n in (1, 3)]
    down_out, down_stages = scatter_rows(
        down_shares[0], down_cores[0], down_shares[2], down_cores[1]
    )
    block_output = (middle + down_out).astype(bf16)
    grad_gain_two = jnp.sum(d_second * middle * rate_last, axis=0)

    grad_out = sum(tn(mixed[r][1], rows_dmiddle[r]) for r in range(2)).astype(bf16)
    out_sum = Scatter(jnp.split(grad_out, outer, axis=0))
    out_last = []
    for at in range(steps):
        last = ring_step([out_sum], last)
        out_last.append(last)
    halves = (slice(0, even), slice(even, slots))
    shares, d_rows, grad_gain_one, d_filter, d_taps = [None, None], [None, None], 0.0, 0.0, 0.0
    for r in range(2):
        proj, gated, long_out, seen = mixed[r]
        table, first = tables[r]
        d_gated = nt(rows_dmiddle[r], out_all).reshape(narrow, local_rows, channels)
        if r == 1:
            [d_gated] = after([d_gated], [grad_out, *shares[0], *down_cores])
        dz, d_filter_row, d_taps_row = mixer_backward(
            order, first, documents[r][0], proj, d_gated, long_out, seen, taps, table,
            spectrum, fwd, inv,
        )
        d_rows[r] = dz.reshape(slots, 3 * channels)
        d_filter, d_taps = d_filter + d_filter_row, d_taps + d_taps_row
        if r == 0:
            shares[r] = [nn(d_rows[r][p], in_all).astype(bf16) for p in halves]
    [ready] = after([d_rows[1]], out_last[0] + down_stages[0])
    odd = nn(ready[halves[1]], in_all).astype(bf16)
    cores = [swap(shares[0][1], "narrow", 1), swap(odd, "narrow", 1)]
    ready = after(d_rows, [odd])
    grad_in = sum(tn(ready[r], rows_first[r]) for r in range(2)).astype(bf16)
    [ready] = after([d_rows[1]], [grad_in] + cores + out_last[-1] + down_stages[1])
    shares[1] = [nn(ready[halves[0]], in_all).astype(bf16), odd]
    d_normed, stages = scatter_rows(shares[0][0], cores[0], shares[1][0], cores[1])
    input_grad = (d_middle + norm_back(source, rate_first, gain_first, d_normed)).astype(bf16)
    for r in range(2):
        for n, share in enumerate(after(shares[r], [shares[1][0]])):
            rows = rows_first[r][n * even : (n + 1) * even]
            grad_gain_one = grad_gain_one + jnp.sum(share.astype(f32) * rows.astype(f32), axis=0)
    chunks = grad_in.reshape(3, outer, own, width)
    in_sum = Scatter([chunks[:, j].reshape(3 * own, width) for j in range(outer)])
    last = ring_step([in_sum], last)
    d_filter, *_ = after([d_filter], last + stages[0])
    for at in range(1, steps):
        last = ring_step([in_sum], last + stages[0])
    gain_grads = after([jnp.stack([grad_gain_one / gain_first, grad_gain_two])], stages[0])
    gain_share = reduce_gain(gain_grads[0], stages[1])

    sum_re, sum_im, mom_re, mom_im = filter_moments(d_filter, step_re, step_im)
    full_re = lag * sum_re + 8.0 * mom_re
    full_im = lag * sum_im + 8.0 * mom_im
    grad_re = jnp.sum(power_re * sum_re - power_im * sum_im, axis=1)
    grad_im = jnp.sum(power_re * sum_im + power_im * sum_re, axis=1)
    lag_re = jnp.sum(power_re * full_re - power_im * full_im, axis=1)
    lag_im = jnp.sum(power_re * full_im + power_im * full_re, axis=1)
    small_grad = jnp.concatenate(
        [
            d_taps[:3].reshape(9, channels),
            -(res_re * lag_re + res_im * lag_im),
            res_im * lag_re - res_re * lag_im,
            grad_re,
            grad_im,
        ],
        axis=0,
    ).astype(bf16)
    [small_grad] = after([small_grad], stages[1])
    small_share = scatter_small(jnp.split(small_grad, outer, axis=1))

    at = 9 + poles
    return (
        block_output[None],
        input_grad[None],
        in_sum.total.reshape(3, own, width).transpose(0, 2, 1),
        out_sum.total,
        gain_share[0],
        small_share[:9].reshape(3, 3, own),
        small_share[9:at].T,
        small_share[at : at + poles].T,
        small_share[at + poles :].T,
        gain_share[1],
        grads[1].total.T,
        grads[2].total.T,
        grads[0].total.T,
    )


def solution(mesh):
    both = ("wide", "narrow")
    return jax.shard_map(
        body,
        mesh=mesh,
        in_specs=(
            P("wide", "narrow", None),
            P(None, None, both),
            P(both, None),
            P(both),
            P(None, None, both),
            P(both, None),
            P(both, None),
            P(both, None),
            P(both),
            P(None, both),
            P(None, both),
            P(None, both),
            P("wide", None),
            P("wide", None),
            P("wide", "narrow", None),
        ),
        out_specs=(
            P("wide", "narrow", None),
            P("wide", "narrow", None),
            P(None, None, both),
            P(both, None),
            P(both),
            P(None, None, both),
            P(both, None),
            P(both, None),
            P(both, None),
            P(both),
            P(None, both),
            P(None, both),
            P(None, both),
        ),
        check_vma=False,
    )
```

```python
from functools import partial

import jax
import jax.numpy as jnp
import numpy as np
from jax import lax
from jax.experimental import pallas as pl
from jax.experimental.pallas import tpu as pltpu
from jax.sharding import PartitionSpec as P

BLOCK = 128
LONGEST = 4
SPAN = LONGEST * BLOCK
FREQ = SPAN

epsilon = 1e-06
bf16 = jnp.bfloat16
f32 = jnp.float32


def transform():
    k = np.arange(FREQ)[:, None] * 2 + 1
    t = np.arange(SPAN)[None, :]
    turn = (k * t % (4 * SPAN)) * (2 * np.pi / (4 * SPAN))
    return np.concatenate([np.cos(turn), -np.sin(turn)], axis=0).astype(np.float32)


def nn(a, b):
    return lax.dot_general(a, b, (((1,), (0,)), ((), ())), preferred_element_type=f32)


def nt(a, b):
    return lax.dot_general(a, b, (((1,), (1,)), ((), ())), preferred_element_type=f32)


def tn(a, b):
    return lax.dot_general(a, b, (((0,), (0,)), ((), ())), preferred_element_type=f32)


def swap(values, axis, shift):
    size = lax.axis_size(axis)
    return lax.ppermute(values, axis, [(i, i ^ shift) for i in range(size)])


def after(values, tokens):
    if not tokens:
        return values
    joined = lax.optimization_barrier(tuple(values) + tuple(tokens))
    return list(joined[: len(values)])


def ring_of(size):
    return list(range(0, size, 2)) + list(range(size - 1, 0, -2))


def along(values, step):
    outer = lax.axis_size("wide") // 2
    ring = ring_of(outer)
    pairs = [
        (ring[p] * 2 + side, ring[(p + step) % outer] * 2 + side)
        for p in range(outer)
        for side in range(2)
    ]
    return lax.ppermute(values, "wide", pairs)


def ring_offsets(outer):
    near = [sign * h for h in range(1, outer // 2) for sign in (-1, 1)]
    return [0] + near + [outer // 2]


def cut_of(rows):
    cut = (rows // 2 + 15) // 16 * 16
    return cut if cut < rows else rows // 2


def two_parts(values, axis):
    cut = cut_of(values.shape[axis])
    return (
        lax.slice_in_dim(values, 0, cut, axis=axis),
        lax.slice_in_dim(values, cut, values.shape[axis], axis=axis),
    )


class Gather:
    def __init__(self, own):
        self.most = lax.axis_size("wide") // 4 - 1
        self.before, self.behind, self.opposite = [own], [own], []

    def sends(self):
        if len(self.before) <= self.most:
            return self.before[-1], self.behind[-1]
        return two_parts(self.before[-1], 0)[0], two_parts(self.behind[-1], 0)[1]

    def take(self, got, back):
        if len(self.before) <= self.most:
            self.before.append(got)
            self.behind.append(back)
        else:
            self.opposite = [got, back]

    def pieces(self):
        near = [piece for pair in zip(self.before[1:], self.behind[1:]) for piece in pair]
        return [self.before[0]] + near + [jnp.concatenate(self.opposite, axis=0)]


class Scatter:
    def __init__(self, chunks):
        self.left = len(chunks) // 2 - 1
        self.wire = chunks[0].dtype
        self.total = chunks[0].astype(f32)
        self.behind = [chunk.astype(f32) for chunk in chunks[1:-1:2]]
        self.ahead = [chunk.astype(f32) for chunk in chunks[2:-1:2]]
        self.last = chunks[-1]

    def sends(self):
        if self.last is not None:
            return two_parts(self.last, 0)
        h = self.left - 1
        return self.ahead[h].astype(self.wire), self.behind[h].astype(self.wire)

    def take(self, got, back):
        got, back = got.astype(f32), back.astype(f32)
        h = self.left - 1
        if self.last is not None:
            top, bottom = two_parts(self.ahead[h], 0)
            self.ahead[h] = jnp.concatenate([top + got, bottom], axis=0)
            top, bottom = two_parts(self.behind[h], 0)
            self.behind[h] = jnp.concatenate([top, bottom + back], axis=0)
            self.last = None
            return
        self.left = h
        if h:
            self.ahead[h - 1] = self.ahead[h - 1] + got
            self.behind[h - 1] = self.behind[h - 1] + back
        else:
            self.total = self.total + got + back


def ring_step(items, tokens=(), arrive=()):
    sends = [item.sends() for item in items]
    ways = [one[0] if len(one) == 1 else jnp.concatenate(one, axis=0) for one in zip(*sends)]
    ways = after(ways, list(tokens)) if tokens else lax.optimization_barrier(tuple(ways))
    got, back = after([along(ways[0], 1), along(ways[1], -1)], list(arrive))
    at = [0, 0]
    for item, (ahead, behind) in zip(items, sends):
        ends = [at[0] + ahead.shape[0], at[1] + behind.shape[0]]
        item.take(got[at[0] : ends[0]], back[at[1] : ends[1]])
        at = ends
    return [got, back]


def gather_small(own):
    outer = lax.axis_size("wide") // 2
    return [own] + [along(own, -offset) for offset in ring_offsets(outer)[1:]]


def scatter_small(chunks):
    offsets = ring_offsets(len(chunks))
    total = chunks[0].astype(f32)
    for chunk, offset in zip(chunks[1:], offsets[1:]):
        total = total + along(chunk, offset).astype(f32)
    return total


def gather_rows(own, tokens=(), later=()):
    size = lax.axis_size("narrow")
    half = own.shape[0] // 2
    [own] = after([own], tokens)
    across = [swap(own, "narrow", k) for k in range(2, size, 2)]
    beside = swap(own, "wide", 1)
    stage_one = across + [beside]
    if later:
        *across, beside = after(across + [beside], later)
    parts, stage_two = [beside], []
    for n, k in enumerate(range(2, size, 2)):
        ends = [swap(across[n][:half], "wide", 1), swap(beside[half:], "narrow", k)]
        parts += ends
        stage_two += ends
    even = jnp.concatenate([own] + across, axis=0)
    other_even = jnp.concatenate(parts, axis=0)
    odd, other_odd = swap(even, "narrow", 1), swap(other_even, "narrow", 1)
    return ([even, odd], [other_even, other_odd]), (stage_one, stage_two, [odd, other_odd])


def scatter_rows(even, odd, other_even, other_odd, tokens=(), later=()):
    size = lax.axis_size("narrow")
    rows = even.shape[0] // (size // 2)
    half = rows // 2
    other = other_even.astype(f32) + other_odd.astype(f32)
    mine = even.astype(f32) + odd.astype(f32)
    beside_top, beside_bottom = other[:half], other[half:rows]
    out = mine[:rows]
    corners = other[rows:].astype(bf16)
    [corners] = after([corners], tokens)
    spread, stage_two, stage_three = [], [], []
    for n, k in enumerate(range(2, size, 2)):
        at = n * rows
        ends = [
            swap(corners[at : at + half], "wide", 1),
            swap(corners[at + half : at + rows], "narrow", k),
        ]
        stage_two += ends
        beside_bottom = beside_bottom + ends[1].astype(f32)
        at = at + rows
        spread.append(
            jnp.concatenate(
                [mine[at : at + half] + ends[0].astype(f32), mine[at + half : at + rows]], axis=0
            ).astype(bf16)
        )
    spread.append(jnp.concatenate([beside_top, beside_bottom], axis=0).astype(bf16))
    spread = after(spread, later) if later else lax.optimization_barrier(tuple(spread))
    for n, k in enumerate(range(2, size, 2)):
        stage_three.append(swap(spread[n], "narrow", k))
        out = out + stage_three[-1].astype(f32)
    stage_three.append(swap(spread[-1], "wide", 1))
    return out + stage_three[-1].astype(f32), (stage_two, stage_three)


def inverse_rms(values):
    return lax.rsqrt(jnp.mean(values * values, axis=-1, keepdims=True) + epsilon)


def norm_kernel(*refs):
    pieces, gain, out = refs[:-2], refs[-2], refs[-1]
    rows = pieces[0].shape[0]
    step = 32 if rows % 32 == 0 else rows
    for n, piece in enumerate(pieces):

        def part(b, _):
            at = pl.multiple_of(b * step, step)
            values = piece[pl.ds(at, step), :].astype(f32)
            rate = lax.rsqrt(jnp.mean(values * values, axis=-1, keepdims=True) + epsilon)
            to = pl.multiple_of(n * rows + at, step)
            out[pl.ds(to, step), :] = (values * rate * gain[...]).astype(bf16)
            return 0

        lax.fori_loop(0, rows // step, part, 0)


def normed_rows(pieces, gain):
    rows, width = pieces[0].shape
    return pl.pallas_call(
        norm_kernel,
        out_shape=jax.ShapeDtypeStruct((rows * len(pieces), width), bf16),
        cost_estimate=light,
        name="norm",
    )(*pieces, gain.reshape(1, width))


def norm_back(values, rate, gain, grad):
    a = grad * gain
    inner = jnp.mean(a * values, axis=-1, keepdims=True)
    return rate * a - values * (rate * rate * rate) * inner


light = pl.CostEstimate(flops=1024, bytes_accessed=1024, transcendentals=0)


def filter_kernel(base_re, base_im, step_re, step_im, out):
    poles = base_re.shape[0]
    width = out.shape[1]
    for g in range(width // 128 if width % 128 == 0 else 1):
        lanes = pl.ds(g * 128, min(128, width))
        start = tuple(base_re[j, :, lanes] for j in range(poles)) + tuple(
            base_im[j, :, lanes] for j in range(poles)
        )

        def step(b, state):
            total = state[0]
            for j in range(1, poles):
                total = total + state[j]
            out[pl.ds(pl.multiple_of(b * 8, 8), 8), lanes] = total
            new_re, new_im = [], []
            for j in range(poles):
                sr = step_re[j, :, lanes]
                si = step_im[j, :, lanes]
                new_re.append(state[j] * sr - state[poles + j] * si)
                new_im.append(state[j] * si + state[poles + j] * sr)
            return tuple(new_re) + tuple(new_im)

        lax.fori_loop(0, SPAN // 8, step, start)


def filter_taps(base_re, base_im, step_re, step_im):
    width = base_re.shape[2]
    return pl.pallas_call(
        filter_kernel,
        out_shape=jax.ShapeDtypeStruct((SPAN, width), f32),
        cost_estimate=light,
        name="taps",
    )(base_re, base_im, step_re, step_im)


def moment_kernel(grad, step_re, step_im, sum_re, sum_im, mom_re, mom_im):
    poles = step_re.shape[0]
    width = grad.shape[1]
    per = 8
    for g in range(width // 128 if width % 128 == 0 else 1):
        lanes = pl.ds(g * 128, min(128, width))
        for j0 in range(0, poles, per):
            zero = jnp.zeros((8, min(128, width)), f32)

            def step(i, state):
                b = SPAN // 8 - 1 - i
                value = grad[pl.ds(pl.multiple_of(b * 8, 8), 8), lanes]
                new = []
                for n in range(per):
                    sr = step_re[j0 + n, :, lanes]
                    si = step_im[j0 + n, :, lanes]
                    pr, pi, qr, qi = state[4 * n : 4 * n + 4]
                    ur, ui = pr + qr, pi + qi
                    new += [
                        pr * sr - pi * si + value,
                        pr * si + pi * sr,
                        ur * sr - ui * si,
                        ur * si + ui * sr,
                    ]
                return tuple(new)

            state = lax.fori_loop(0, SPAN // 8, step, (zero,) * (4 * per))
            for n in range(per):
                sum_re[j0 + n, :, lanes] = state[4 * n]
                sum_im[j0 + n, :, lanes] = state[4 * n + 1]
                mom_re[j0 + n, :, lanes] = state[4 * n + 2]
                mom_im[j0 + n, :, lanes] = state[4 * n + 3]


SIDE = 512


def product_kernel(a, b, out, turned=None, *, kind):
    if kind == "tn":

        @pl.when(pl.program_id(0) == 0)
        def _():
            turned[...] = a[...].T

        value = nn(turned[...], b[...])
    else:
        value = (nn if kind == "nn" else nt)(a[...], b[...])
    out[...] = value.astype(out.dtype)


def product(a, b, kind, dtype, at=0):
    if kind == "tn":
        depth, rows = a.shape[0], SIDE
        a_spec = pl.BlockSpec((depth, SIDE), lambda i: (0, at))
        scratch = [pltpu.VMEM((SIDE, depth), a.dtype)]
    else:
        rows, depth = a.shape
        a_spec = pl.BlockSpec((rows, depth), lambda i: (0, 0))
        scratch = []
    columns = b.shape[0] if kind == "nt" else b.shape[1]
    if kind == "nt":
        b_spec = pl.BlockSpec((SIDE, depth), lambda i: (i, 0))
    else:
        b_spec = pl.BlockSpec((depth, SIDE), lambda i: (0, i))
    return pl.pallas_call(
        partial(product_kernel, kind=kind),
        grid=(columns // SIDE,),
        out_shape=jax.ShapeDtypeStruct((rows, columns), dtype),
        in_specs=[a_spec, b_spec],
        out_specs=pl.BlockSpec((rows, SIDE), lambda i: (0, i)),
        scratch_shapes=scratch,
        cost_estimate=light,
        name="product",
    )(a, b)


def filter_moments(grad, step_re, step_im):
    poles, _, width = step_re.shape
    shape = jax.ShapeDtypeStruct((poles, 8, width), f32)
    return pl.pallas_call(
        moment_kernel,
        out_shape=(shape,) * 4,
        cost_estimate=pl.CostEstimate(
            flops=16 * 15 * SPAN * width, bytes_accessed=4 * SPAN * width, transcendentals=0
        ),
        name="moments",
    )(grad, step_re, step_im)


LIVE, KEEP_ONE, KEEP_TWO = 0, 1, 2


def load_masked(order, proj, table, m_scr):
    pieces, rows, _ = proj.shape
    m_scr[0:8, :] = jnp.zeros_like(m_scr[0:8, :])

    def piece(b, _):
        p = order[b]
        at = pl.multiple_of(b * rows, rows)
        live = table[pl.ds(at, rows), LIVE : LIVE + 1]
        m_scr[pl.ds(pl.multiple_of(at + 8, 8), rows), :] = proj[p] * live
        return 0

    lax.fori_loop(0, pieces, piece, 0)


def short_block(m_scr, taps, table, at):
    window = m_scr[pl.ds(at, BLOCK + 8), :]
    one = table[pl.ds(at, BLOCK), KEEP_ONE : KEEP_ONE + 1]
    two = table[pl.ds(at, BLOCK), KEEP_TWO : KEEP_TWO + 1]
    here = window[8:]
    once = window[7 : BLOCK + 7] * one
    twice = window[6 : BLOCK + 6] * two
    short = taps[0:1, :] * here + taps[1:2, :] * once + taps[2:3, :] * twice
    return short, here, once, twice


def pack_document(source, packed, first, count):
    blocks = source.shape[0] // BLOCK
    for kb in range(LONGEST):
        at = pl.multiple_of(jnp.minimum(first + kb, blocks - 1) * BLOCK, BLOCK)
        inside = (kb < count).astype(f32)
        packed[kb * BLOCK : (kb + 1) * BLOCK, :] = (source[pl.ds(at, BLOCK), :] * inside).astype(bf16)


def place_document(result, target, first, count):
    for kb in range(LONGEST):

        @pl.when(kb < count)
        def _():
            at = pl.multiple_of((first + kb) * BLOCK, BLOCK)
            target[pl.ds(at, BLOCK), :] = result[kb * BLOCK : (kb + 1) * BLOCK, :]


def forward_kernel(
    order, first, count, proj, taps, table, spectrum, fwd, inv, gated, long_out, seen, m_scr, u_scr, q_scr, packed
):
    width = long_out.shape[1]
    pieces, rows, _ = proj.shape
    blocks = long_out.shape[0] // BLOCK
    load_masked(order, proj, table, m_scr)

    def block(n, _):
        at = pl.multiple_of(n * BLOCK, BLOCK)
        short, _, _, _ = short_block(m_scr, taps, table, at)
        q_scr[pl.ds(at, BLOCK), :] = short[:, :width]
        u_scr[pl.ds(at, BLOCK), :] = short[:, width : 2 * width] * short[:, 2 * width :]
        return 0

    lax.fori_loop(0, blocks, block, 0)

    def document(d, _):
        pack_document(u_scr, packed, first[d], count[d])
        both = jnp.dot(fwd[...], packed[...], preferred_element_type=f32)
        seen[d] = both.astype(bf16)
        re, im = both[:FREQ], both[FREQ:]
        hr, hi = spectrum[:FREQ], spectrum[FREQ:]
        answer = jnp.concatenate([re * hr - im * hi, re * hi + im * hr], axis=0).astype(bf16)
        result = jnp.dot(inv[...], answer, preferred_element_type=f32)
        place_document(result, long_out, first[d], count[d])
        return 0

    lax.fori_loop(0, seen.shape[0], document, 0)

    def piece(b, _):
        at = pl.multiple_of(b * rows, rows)
        gated[order[b]] = (q_scr[pl.ds(at, rows), :] * long_out[pl.ds(at, rows), :]).astype(bf16)
        return 0

    lax.fori_loop(0, pieces, piece, 0)


def backward_kernel(
    order, first, count, proj, d_gated, long_out, seen, taps, table, spectrum, fwd, inv,
    dz, d_filter, d_taps, m_scr, dy_scr, k_scr, v_scr, ds_scr, packed, d_spec,
):
    width = long_out.shape[1]
    pieces, rows, _ = proj.shape
    slots = long_out.shape[0]
    blocks = slots // BLOCK
    per_piece = rows // BLOCK
    load_masked(order, proj, table, m_scr)
    ds_scr[slots : slots + 8, :] = jnp.zeros_like(ds_scr[slots : slots + 8, :])

    def block(n, _):
        at = pl.multiple_of(n * BLOCK, BLOCK)
        short, _, _, _ = short_block(m_scr, taps, table, at)
        within = pl.multiple_of((n % per_piece) * BLOCK, BLOCK)
        dg = d_gated[order[n // per_piece], pl.ds(within, BLOCK), :]
        dy_scr[pl.ds(at, BLOCK), :] = dg * short[:, :width]
        ds_scr[pl.ds(at, BLOCK), :width] = dg * long_out[pl.ds(at, BLOCK), :]
        k_scr[pl.ds(at, BLOCK), :] = short[:, width : 2 * width]
        v_scr[pl.ds(at, BLOCK), :] = short[:, 2 * width :]
        return 0

    lax.fori_loop(0, blocks, block, 0)
    d_spec[...] = jnp.zeros_like(d_spec)

    def document(d, _):
        pack_document(dy_scr, packed, first[d], count[d])
        both = jnp.dot(fwd[...], packed[...], preferred_element_type=f32)
        re, im = both[:FREQ], both[FREQ:]
        hr, hi = spectrum[:FREQ], spectrum[FREQ:]
        answer = jnp.concatenate([re * hr + im * hi, im * hr - re * hi], axis=0).astype(bf16)
        result = jnp.dot(inv[...], answer, preferred_element_type=f32)
        ur, ui = seen[d, :FREQ].astype(f32), seen[d, FREQ:].astype(f32)
        d_spec[:FREQ] += re * ur + im * ui
        d_spec[FREQ:] += im * ur - re * ui
        for kb in range(LONGEST):

            @pl.when(kb < count[d])
            def _():
                at = pl.multiple_of((first[d] + kb) * BLOCK, BLOCK)
                du = result[kb * BLOCK : (kb + 1) * BLOCK, :]
                ds_scr[pl.ds(at, BLOCK), width : 2 * width] = du * v_scr[pl.ds(at, BLOCK), :]
                ds_scr[pl.ds(at, BLOCK), 2 * width :] = du * k_scr[pl.ds(at, BLOCK), :]

        return 0

    lax.fori_loop(0, seen.shape[0], document, 0)
    d_filter[...] = jnp.dot(inv[...], d_spec[...].astype(bf16), preferred_element_type=f32)
    d_taps[...] = jnp.zeros_like(d_taps)

    def back(n, _):
        at = pl.multiple_of(n * BLOCK, BLOCK)
        window = m_scr[pl.ds(at, BLOCK + 8), :]
        ahead = ds_scr[pl.ds(at, BLOCK + 8), :]
        one = table[pl.ds(at, BLOCK + 8), KEEP_ONE : KEEP_ONE + 1]
        two = table[pl.ds(at, BLOCK + 8), KEEP_TWO : KEEP_TWO + 1]
        live = table[pl.ds(at, BLOCK), LIVE : LIVE + 1]
        ds = ahead[:BLOCK]
        ahead_one = ahead * one
        ahead_two = ahead * two
        dm = (
            taps[0:1, :] * ds
            + taps[1:2, :] * ahead_one[1 : BLOCK + 1]
            + taps[2:3, :] * ahead_two[2 : BLOCK + 2]
        )
        d_taps[0:1, :] += jnp.sum(window[8:] * ds, axis=0, keepdims=True)
        d_taps[1:2, :] += jnp.sum(window[7 : BLOCK + 7] * ahead_one[:BLOCK], axis=0, keepdims=True)
        d_taps[2:3, :] += jnp.sum(window[6 : BLOCK + 6] * ahead_two[:BLOCK], axis=0, keepdims=True)
        within = pl.multiple_of((n % per_piece) * BLOCK, BLOCK)
        dz[order[n // per_piece], pl.ds(within, BLOCK), :] = (dm * live).astype(bf16)
        return 0

    lax.fori_loop(0, blocks, back, 0)


smem = pl.BlockSpec(memory_space=pltpu.SMEM)
vmem = pl.BlockSpec(memory_space=pltpu.VMEM)


def mixer_forward(order, first, count, proj, taps, table, spectrum, fwd, inv):
    pieces, rows, three = proj.shape
    width = three // 3
    slots = pieces * rows
    docs = first.shape[0]
    return pl.pallas_call(
        forward_kernel,
        out_shape=(
            jax.ShapeDtypeStruct((pieces, rows, width), bf16),
            jax.ShapeDtypeStruct((slots, width), f32),
            jax.ShapeDtypeStruct((docs, 2 * FREQ, width), bf16),
        ),
        in_specs=[smem] * 3 + [vmem] * 6,
        out_specs=(vmem,) * 3,
        scratch_shapes=[
            pltpu.VMEM((slots + 8, three), f32),
            pltpu.VMEM((slots, width), f32),
            pltpu.VMEM((slots, width), f32),
            pltpu.VMEM((SPAN, width), bf16),
        ],
        compiler_params=pltpu.CompilerParams(vmem_limit_bytes=40 * 2**20),
        cost_estimate=light,
        name="mixer_forward",
    )(order, first, count, proj, taps, table, spectrum, fwd, inv)


def mixer_backward(order, first, count, proj, d_gated, long_out, seen, taps, table, spectrum, fwd, inv):
    pieces, rows, three = proj.shape
    width = three // 3
    slots = pieces * rows
    docs = first.shape[0]
    return pl.pallas_call(
        backward_kernel,
        out_shape=(
            jax.ShapeDtypeStruct((pieces, rows, three), bf16),
            jax.ShapeDtypeStruct((SPAN, width), f32),
            jax.ShapeDtypeStruct((8, three), f32),
        ),
        in_specs=[smem] * 3 + [vmem] * 9,
        out_specs=(vmem,) * 3,
        scratch_shapes=[
            pltpu.VMEM((slots + 8, three), f32),
            pltpu.VMEM((slots, width), f32),
            pltpu.VMEM((slots, width), f32),
            pltpu.VMEM((slots, width), f32),
            pltpu.VMEM((slots + 8, three), f32),
            pltpu.VMEM((SPAN, width), bf16),
            pltpu.VMEM((2 * FREQ, width), f32),
        ],
        compiler_params=pltpu.CompilerParams(vmem_limit_bytes=48 * 2**20),
        cost_estimate=light,
        name="mixer_backward",
    )(order, first, count, proj, d_gated, long_out, seen, taps, table, spectrum, fwd, inv)


def layout(doc_blocks, doc_pad, slots):
    block_ends = jnp.cumsum(doc_blocks) * BLOCK
    starts = block_ends - doc_blocks * BLOCK
    places = jnp.arange(slots, dtype=jnp.int32)
    living = (places[None, :] >= starts[:, None]) & (
        places[None, :] < (block_ends - doc_pad)[:, None]
    )
    live = jnp.sum(living.astype(f32), axis=0)
    opening = jnp.sum((places[None, :] == starts[:, None]).astype(f32), axis=0)
    one = 1.0 - opening
    one = one * (places > 0)
    two = one * jnp.concatenate([jnp.zeros((1,), f32), one[:-1]])
    table = jnp.stack([live, one, two], axis=1)
    table = jnp.concatenate([table, jnp.zeros((8, 3), f32)], axis=0)
    return table, starts // BLOCK


def picked(index, count, values):
    hot = index[:, None] == jnp.arange(count)[None, :]
    shape = hot.shape + (1,) * (values.ndim - 1)
    return jnp.sum(jnp.where(hot.reshape(shape), values[None], 0), axis=1)


def body(
    tokens, w_in, w_out, gain_one, short_kernel, decay_rate, pole_angle, residue,
    gain_two, w_gate, w_up, w_down, doc_blocks, doc_pad, cotangent,
):
    wide, narrow = lax.axis_size("wide"), lax.axis_size("narrow")
    wide_at, narrow_at = lax.axis_index("wide"), lax.axis_index("narrow")
    outer = wide // 2
    _, local_rows, width = tokens.shape
    slots = local_rows * narrow
    even = slots // 2
    source = tokens[0].astype(f32)
    upstream_low = cotangent[0]
    poles = decay_rate.shape[1]
    own = w_in.shape[2]
    channels = own * outer
    hidden_units = w_gate.shape[1] * outer

    ring = np.array(ring_of(outer))
    ring_place = np.argsort(ring)
    tour = picked((wide_at // 2)[None], outer, jnp.asarray(ring_place, jnp.int32))[0]
    piece_places = (tour + jnp.asarray(ring_offsets(outer), jnp.int32)) % outer
    piece_outer = picked(piece_places, outer, jnp.asarray(ring, jnp.int32))
    sides = jnp.arange(2) ^ (wide_at % 2)
    offsets = list(range(0, narrow, 2)) + list(range(1, narrow, 2))
    place_of = np.argsort(np.array(offsets))
    order = picked(jnp.arange(narrow) ^ narrow_at, narrow, jnp.asarray(place_of, jnp.int32))
    narrow_of = jnp.asarray(offsets, jnp.int32) ^ narrow_at

    small = jnp.concatenate(
        [
            short_kernel.reshape(9, own),
            decay_rate.T,
            pole_angle.T,
            residue.T,
            gain_one[None],
            gain_two[None],
        ],
        axis=0,
    )
    small_pieces = gather_small(small)
    small_all = jnp.concatenate(small_pieces, axis=1)
    (first_own, first_other), first_stages = gather_rows(tokens[0], small_pieces[1:])
    gains = small_all[small.shape[0] - 2 :].reshape(2, outer, own)
    gains = jnp.stack([gains, swap(gains, "wide", 1)])
    gains = jnp.stack([gains] + [swap(gains, "narrow", k) for k in range(2, narrow, 2)])
    gains = jnp.concatenate([gains, swap(gains, "narrow", 1)], axis=0).astype(f32)
    gains = picked(order, narrow, gains).transpose(1, 3, 0, 2, 4)
    gains = picked(sides, 2, gains).transpose(1, 0, 2, 3, 4)
    hot = piece_outer[None, :] == jnp.arange(outer)[:, None]
    gains = jnp.sum(jnp.where(hot[:, :, None, None, None, None], gains[None], 0), axis=1)
    gain_all = gains.transpose(3, 0, 1, 2, 4).reshape(2, width)
    gain_first, gain_last = gain_all[0], gain_all[1]

    def reduce_gain(values, tokens):
        values = values.reshape(2, outer, 2, narrow, own).transpose(1, 2, 3, 0, 4)
        values = picked(piece_outer, outer, values).transpose(1, 0, 2, 3, 4)
        values = picked(sides, 2, values).transpose(2, 0, 1, 3, 4)
        values = picked(narrow_of, narrow, values)
        total = values[: narrow // 2] + swap(values[narrow // 2 :], "narrow", 1)
        summed = total[0]
        for k in range(1, narrow // 2):
            summed = summed + swap(total[k], "narrow", 2 * k)
        summed = summed[0] + swap(summed[1], "wide", 1)
        [summed] = after([summed], tokens)
        return scatter_small([summed[j] for j in range(outer)])

    documents = jnp.concatenate([doc_blocks, doc_pad], axis=0)
    [documents] = after([documents], small_pieces[1:])
    documents = (documents, swap(documents, "wide", 1))
    tables = [layout(rules[0], rules[1], slots) for rules in documents]

    shards = [w_in.transpose(0, 2, 1).reshape(3 * own, width), w_out, w_down.T, w_gate.T, w_up.T]
    weights = [Gather(shard) for shard in shards]
    in_all, out_all, down_all, gate_all, up_all = weights
    steps = outer // 2
    last = []
    for at in range(steps - 1):
        last = ring_step([in_all], last)
    last = ring_step([in_all, out_all], last + first_stages[0])
    for at in range(1, steps):
        last = ring_step([out_all], last)

    def normed(pieces):
        values = jnp.concatenate(pieces, axis=0).astype(f32)
        return (values * inverse_rms(values) * gain_first).astype(bf16)

    rows_first = [normed(first_own), normed(first_other)]
    rate_first = inverse_rms(source)
    (upstream_own, upstream_other), upstream_stages = gather_rows(upstream_low, first_stages[2])

    matrix = transform()
    fwd = jnp.asarray(matrix, bf16)
    inv = jnp.asarray(matrix.T / SPAN, bf16)

    block = small_all.astype(f32)
    taps = block[:9].reshape(3, 3 * channels)
    taps = jnp.concatenate([taps, jnp.zeros((5, 3 * channels), f32)], axis=0)
    decay = block[9 : 9 + poles][:, None, :]
    angle = block[9 + poles : 9 + 2 * poles][:, None, :]
    res_re = block[9 + 2 * poles : 9 + 3 * poles][:, None, :]
    res_im = -block[9 + 3 * poles : 9 + 4 * poles][:, None, :]
    lag = jnp.arange(8, dtype=f32)[None, :, None]
    fade = jnp.exp(-decay * lag)
    power_re, power_im = fade * jnp.cos(angle * lag), fade * jnp.sin(angle * lag)
    fade_step = jnp.exp(-decay * 8.0)
    step_re = jnp.broadcast_to(fade_step * jnp.cos(angle * 8.0), power_re.shape)
    step_im = jnp.broadcast_to(fade_step * jnp.sin(angle * 8.0), power_re.shape)
    filt = filter_taps(
        res_re * power_re - res_im * power_im,
        res_re * power_im + res_im * power_re,
        step_re,
        step_im,
    )
    spectrum = lax.dot_general(
        jnp.asarray(matrix),
        filt,
        (((1,), (0,)), ((), ())),
        precision=lax.Precision.HIGHEST,
        preferred_element_type=f32,
    )
    res_re, res_im = res_re[:, 0], -res_im[:, 0]

    in_pieces = [piece.reshape(3, own, width) for piece in in_all.pieces()]
    in_all = jnp.concatenate(in_pieces, axis=1).reshape(3 * channels, width)
    mixed = []
    for r in range(2):
        table, first = tables[r]
        proj = nt(rows_first[r], in_all).reshape(narrow, local_rows, 3 * channels)
        gated, long_out, seen = mixer_forward(
            order, first, documents[r][0], proj, taps, table, spectrum, fwd, inv
        )
        mixed.append((proj, gated.reshape(slots, channels), long_out, seen))
    out_last = last
    out_all = jnp.concatenate(out_all.pieces(), axis=0)
    parts = [slice(0, even), slice(even, slots)]
    odds = [nn(mixed[r][1][parts[1]], out_all).astype(bf16) for r in range(2)]
    cores = [swap(odd, "narrow", 1) for odd in odds]
    for at in range(steps - 1):
        last = ring_step([down_all], last)
    ready = after([mixed[0][1], mixed[1][1]], last + upstream_stages[0])
    evens = [nn(ready[r][parts[0]], out_all).astype(bf16) for r in range(2)]
    last_two = last
    for at in range(1, steps):
        last_two = ring_step([down_all], last_two, cores)
    last_three = ring_step([gate_all], last_two)
    for at in range(1, steps - 1):
        last_three = ring_step([gate_all], last_three)
    mixer_out, stages = scatter_rows(
        evens[0], cores[0], evens[1], cores[1], upstream_stages[1], last_two
    )
    middle = source + mixer_out
    rate_last = inverse_rms(middle)
    rows_upstream = jnp.concatenate(upstream_own + upstream_other, axis=0)
    low_second = (middle * rate_last * gain_last).astype(bf16)
    last_four = ring_step([gate_all], last_three + stages[1])
    (second_own, second_other), second_stages = gather_rows(low_second, last_three, last_four)
    rows_second = jnp.concatenate(second_own + second_other, axis=0)
    last = ring_step([up_all], last_four + second_stages[0], second_stages[2])
    for at in range(1, steps):
        last = ring_step([up_all], last)

    down_all, gate_all = [jnp.concatenate(w.pieces(), axis=0) for w in (down_all, gate_all)]
    d_hidden = product(down_all, rows_upstream, "nt", f32)
    gate_pre = product(gate_all, rows_second, "nt", f32)
    up_pieces = after(up_all.pieces(), [d_hidden, gate_pre])
    up_all = jnp.concatenate(up_pieces, axis=0)
    up_pre = nt(up_all, rows_second)
    sig = jax.nn.sigmoid(gate_pre)
    silu = gate_pre * sig
    hidden = (silu * up_pre).astype(bf16)
    d_gate = (d_hidden * up_pre * sig * (1.0 + gate_pre * (1.0 - sig))).astype(bf16)
    d_up = (d_hidden * silu).astype(bf16)
    grad_down = product(hidden, rows_upstream, "nn", bf16)
    d_gate, d_up = after([d_gate, d_up], [grad_down])
    parts = [slice(p, p + even) for p in range(0, 2 * slots, even)]
    grads = [Scatter(jnp.split(grad_down, outer, axis=0))]
    last = ring_step(grads)

    def second_share(n, tokens=()):
        one, two = after([d_gate, d_up], tokens)
        p = parts[n]
        return (tn(one[:, p], gate_all) + tn(two[:, p], up_all)).astype(bf16)

    odds = [second_share(n) for n in (1, 3)]
    cores = [swap(odd, "narrow", 1) for odd in odds]
    evens = [second_share(0), second_share(2, last)]
    d_second, stages = scatter_rows(evens[0], cores[0], evens[1], cores[1])
    upstream = upstream_low.astype(f32)
    d_middle = upstream + norm_back(middle, rate_last, gain_last, d_second)
    (middle_own, middle_other), middle_stages = gather_rows(d_middle.astype(bf16))
    rows_dmiddle = [jnp.concatenate(middle_own, axis=0), jnp.concatenate(middle_other, axis=0)]
    [d_gate] = after([d_gate], cores + evens)
    grad_gate = product(d_gate, rows_second, "nn", bf16)
    [d_up] = after([d_up], stages[0] + [grad_gate])
    grad_up = product(d_up, rows_second, "nn", bf16)
    [hidden] = after([hidden], [grad_up])
    down_shares = [product(hidden, down_all, "tn", bf16, n) for n in (0, 1)]
    for at in range(1, steps):
        last = ring_step(grads, last, down_shares)
    [hidden] = after([hidden], last)
    down_shares += [product(hidden, down_all, "tn", bf16, n) for n in (2, 3)]
    pair = [Scatter(jnp.split(grad, outer, axis=0)) for grad in (grad_gate, grad_up)]
    grads += pair
    last = ring_step(pair, list(last) + down_shares[:2], middle_stages[0])
    for at in range(1, steps):
        last = ring_step(pair, last, middle_stages[2])
    pair_last = last
    down_shares = after(down_shares, middle_stages[2])
    down_cores = [swap(down_shares[n], "narrow", 1) for n in (1, 3)]
    down_out, down_stages = scatter_rows(
        down_shares[0], down_cores[0], down_shares[2], down_cores[1]
    )
    block_output = (middle + down_out).astype(bf16)
    grad_gain_two = jnp.sum(d_second * middle * rate_last, axis=0)

    grad_out = sum(tn(mixed[r][1], rows_dmiddle[r]) for r in range(2)).astype(bf16)
    out_sum = Scatter(jnp.split(grad_out, outer, axis=0))
    out_last = []
    for at in range(steps):
        last = ring_step([out_sum], last)
        out_last.append(last)
    halves = (slice(0, even), slice(even, slots))
    shares, d_rows, grad_gain_one, d_filter, d_taps = [None, None], [None, None], 0.0, 0.0, 0.0
    for r in range(2):
        proj, gated, long_out, seen = mixed[r]
        table, first = tables[r]
        d_gated = nt(rows_dmiddle[r], out_all).reshape(narrow, local_rows, channels)
        if r == 1:
            [d_gated] = after([d_gated], [grad_out, *shares[0], *down_cores])
        dz, d_filter_row, d_taps_row = mixer_backward(
            order, first, documents[r][0], proj, d_gated, long_out, seen, taps, table,
            spectrum, fwd, inv,
        )
        d_rows[r] = dz.reshape(slots, 3 * channels)
        d_filter, d_taps = d_filter + d_filter_row, d_taps + d_taps_row
        if r == 0:
            [ready] = after([d_rows[r]], pair_last)
            shares[r] = [nn(ready[p], in_all).astype(bf16) for p in halves]
    [ready] = after([d_rows[1]], out_last[0] + down_stages[0])
    odd = nn(ready[halves[1]], in_all).astype(bf16)
    cores = [swap(shares[0][1], "narrow", 1), swap(odd, "narrow", 1)]
    ready = after(d_rows, [odd])
    grad_in = sum(tn(ready[r], rows_first[r]) for r in range(2)).astype(bf16)
    [ready] = after([d_rows[1]], [grad_in] + cores + out_last[-1] + down_stages[1])
    shares[1] = [nn(ready[halves[0]], in_all).astype(bf16), odd]
    d_normed, stages = scatter_rows(shares[0][0], cores[0], shares[1][0], cores[1])
    input_grad = (d_middle + norm_back(source, rate_first, gain_first, d_normed)).astype(bf16)
    for r in range(2):
        for n, share in enumerate(after(shares[r], [shares[1][0]])):
            rows = rows_first[r][n * even : (n + 1) * even]
            grad_gain_one = grad_gain_one + jnp.sum(share.astype(f32) * rows.astype(f32), axis=0)
    chunks = grad_in.reshape(3, outer, own, width)
    in_sum = Scatter([chunks[:, j].reshape(3 * own, width) for j in range(outer)])
    last = ring_step([in_sum], last)
    d_filter, *_ = after([d_filter], last + stages[0])
    gain_grads = after([jnp.stack([grad_gain_one / gain_first, grad_gain_two])], stages[0])
    gain_share = reduce_gain(gain_grads[0], stages[1])

    sum_re, sum_im, mom_re, mom_im = filter_moments(d_filter, step_re, step_im)
    full_re = lag * sum_re + 8.0 * mom_re
    full_im = lag * sum_im + 8.0 * mom_im
    grad_re = jnp.sum(power_re * sum_re - power_im * sum_im, axis=1)
    grad_im = jnp.sum(power_re * sum_im + power_im * sum_re, axis=1)
    lag_re = jnp.sum(power_re * full_re - power_im * full_im, axis=1)
    lag_im = jnp.sum(power_re * full_im + power_im * full_re, axis=1)
    small_grad = jnp.concatenate(
        [
            d_taps[:3].reshape(9, channels),
            -(res_re * lag_re + res_im * lag_im),
            res_im * lag_re - res_re * lag_im,
            grad_re,
            grad_im,
        ],
        axis=0,
    ).astype(bf16)
    [small_grad] = after([small_grad], stages[1])
    small_share = scatter_small(jnp.split(small_grad, outer, axis=1))

    for at in range(1, steps):
        last = ring_step([in_sum], last + stages[0], [gain_share, small_share])

    at = 9 + poles
    return (
        block_output[None],
        input_grad[None],
        in_sum.total.reshape(3, own, width).transpose(0, 2, 1),
        out_sum.total,
        gain_share[0],
        small_share[:9].reshape(3, 3, own),
        small_share[9:at].T,
        small_share[at : at + poles].T,
        small_share[at + poles :].T,
        gain_share[1],
        grads[1].total.T,
        grads[2].total.T,
        grads[0].total.T,
    )


def solution(mesh):
    both = ("wide", "narrow")
    return jax.shard_map(
        body,
        mesh=mesh,
        in_specs=(
            P("wide", "narrow", None),
            P(None, None, both),
            P(both, None),
            P(both),
            P(None, None, both),
            P(both, None),
            P(both, None),
            P(both, None),
            P(both),
            P(None, both),
            P(None, both),
            P(None, both),
            P("wide", None),
            P("wide", None),
            P("wide", "narrow", None),
        ),
        out_specs=(
            P("wide", "narrow", None),
            P("wide", "narrow", None),
            P(None, None, both),
            P(both, None),
            P(both),
            P(None, None, both),
            P(both, None),
            P(both, None),
            P(both, None),
            P(both),
            P(None, both),
            P(None, both),
            P(None, both),
        ),
        check_vma=False,
    )
```

```python
from functools import partial

import jax
import jax.numpy as jnp
import numpy as np
from jax import lax
from jax.experimental import pallas as pl
from jax.experimental.pallas import tpu as pltpu
from jax.sharding import PartitionSpec as P

BLOCK = 128
LONGEST = 4
SPAN = LONGEST * BLOCK
FREQ = SPAN

epsilon = 1e-06
bf16 = jnp.bfloat16
f32 = jnp.float32


def transform():
    k = np.arange(FREQ)[:, None] * 2 + 1
    t = np.arange(SPAN)[None, :]
    turn = (k * t % (4 * SPAN)) * (2 * np.pi / (4 * SPAN))
    return np.concatenate([np.cos(turn), -np.sin(turn)], axis=0).astype(np.float32)


def nn(a, b):
    return lax.dot_general(a, b, (((1,), (0,)), ((), ())), preferred_element_type=f32)


def nt(a, b):
    return lax.dot_general(a, b, (((1,), (1,)), ((), ())), preferred_element_type=f32)


def tn(a, b):
    return lax.dot_general(a, b, (((0,), (0,)), ((), ())), preferred_element_type=f32)


def swap(values, axis, shift):
    size = lax.axis_size(axis)
    return lax.ppermute(values, axis, [(i, i ^ shift) for i in range(size)])


def after(values, tokens):
    if not tokens:
        return values
    joined = lax.optimization_barrier(tuple(values) + tuple(tokens))
    return list(joined[: len(values)])


def ring_of(size):
    return list(range(0, size, 2)) + list(range(size - 1, 0, -2))


def along(values, step):
    outer = lax.axis_size("wide") // 2
    ring = ring_of(outer)
    pairs = [
        (ring[p] * 2 + side, ring[(p + step) % outer] * 2 + side)
        for p in range(outer)
        for side in range(2)
    ]
    return lax.ppermute(values, "wide", pairs)


def ring_offsets(outer):
    near = [sign * h for h in range(1, outer // 2) for sign in (-1, 1)]
    return [0] + near + [outer // 2]


def cut_of(rows):
    cut = (rows // 2 + 15) // 16 * 16
    return cut if cut < rows else rows // 2


def two_parts(values, axis):
    cut = cut_of(values.shape[axis])
    return (
        lax.slice_in_dim(values, 0, cut, axis=axis),
        lax.slice_in_dim(values, cut, values.shape[axis], axis=axis),
    )


class Gather:
    def __init__(self, own):
        self.most = lax.axis_size("wide") // 4 - 1
        self.before, self.behind, self.opposite = [own], [own], []

    def sends(self):
        if len(self.before) <= self.most:
            return self.before[-1], self.behind[-1]
        return two_parts(self.before[-1], 0)[0], two_parts(self.behind[-1], 0)[1]

    def take(self, got, back):
        if len(self.before) <= self.most:
            self.before.append(got)
            self.behind.append(back)
        else:
            self.opposite = [got, back]

    def pieces(self):
        near = [piece for pair in zip(self.before[1:], self.behind[1:]) for piece in pair]
        return [self.before[0]] + near + [jnp.concatenate(self.opposite, axis=0)]


class Scatter:
    def __init__(self, chunks):
        self.left = len(chunks) // 2 - 1
        self.wire = chunks[0].dtype
        self.total = chunks[0].astype(f32)
        self.behind = [chunk.astype(f32) for chunk in chunks[1:-1:2]]
        self.ahead = [chunk.astype(f32) for chunk in chunks[2:-1:2]]
        self.last = chunks[-1]

    def sends(self):
        if self.last is not None:
            return two_parts(self.last, 0)
        h = self.left - 1
        return self.ahead[h].astype(self.wire), self.behind[h].astype(self.wire)

    def take(self, got, back):
        got, back = got.astype(f32), back.astype(f32)
        h = self.left - 1
        if self.last is not None:
            top, bottom = two_parts(self.ahead[h], 0)
            self.ahead[h] = jnp.concatenate([top + got, bottom], axis=0)
            top, bottom = two_parts(self.behind[h], 0)
            self.behind[h] = jnp.concatenate([top, bottom + back], axis=0)
            self.last = None
            return
        self.left = h
        if h:
            self.ahead[h - 1] = self.ahead[h - 1] + got
            self.behind[h - 1] = self.behind[h - 1] + back
        else:
            self.total = self.total + got + back


def ring_step(items, tokens=(), arrive=()):
    sends = [item.sends() for item in items]
    ways = [one[0] if len(one) == 1 else jnp.concatenate(one, axis=0) for one in zip(*sends)]
    ways = after(ways, list(tokens)) if tokens else lax.optimization_barrier(tuple(ways))
    got, back = after([along(ways[0], 1), along(ways[1], -1)], list(arrive))
    at = [0, 0]
    for item, (ahead, behind) in zip(items, sends):
        ends = [at[0] + ahead.shape[0], at[1] + behind.shape[0]]
        item.take(got[at[0] : ends[0]], back[at[1] : ends[1]])
        at = ends
    return [got, back]


def gather_small(own):
    outer = lax.axis_size("wide") // 2
    return [own] + [along(own, -offset) for offset in ring_offsets(outer)[1:]]


def scatter_small(chunks):
    offsets = ring_offsets(len(chunks))
    total = chunks[0].astype(f32)
    for chunk, offset in zip(chunks[1:], offsets[1:]):
        total = total + along(chunk, offset).astype(f32)
    return total


def gather_rows(own, tokens=(), later=(), single=False):
    size = lax.axis_size("narrow")
    half = own.shape[0] // 2
    [own] = after([own], tokens)
    across = [swap(own, "narrow", k) for k in range(2, size, 2)]
    beside = swap(own, "wide", 1)
    stage_one = across + [beside]
    if later:
        *across, beside = after(across + [beside], later)
    parts, stage_two = [beside], []
    for n, k in enumerate(range(2, size, 2)):
        ends = [swap(across[n][:half], "wide", 1), swap(beside[half:], "narrow", k)]
        parts += ends
        stage_two += ends
    even = jnp.concatenate([own] + across, axis=0)
    other_even = jnp.concatenate(parts, axis=0)
    odd = swap(even, "narrow", 1)
    if single:
        [other_even] = after([other_even], [odd])
    other_odd = swap(other_even, "narrow", 1)
    return ([even, odd], [other_even, other_odd]), (stage_one, stage_two, [odd, other_odd])


def scatter_rows(even, odd, other_even, other_odd, tokens=(), later=()):
    size = lax.axis_size("narrow")
    rows = even.shape[0] // (size // 2)
    half = rows // 2
    other = other_even.astype(f32) + other_odd.astype(f32)
    mine = even.astype(f32) + odd.astype(f32)
    beside_top, beside_bottom = other[:half], other[half:rows]
    out = mine[:rows]
    corners = other[rows:].astype(bf16)
    [corners] = after([corners], tokens)
    spread, stage_two, stage_three = [], [], []
    for n, k in enumerate(range(2, size, 2)):
        at = n * rows
        ends = [
            swap(corners[at : at + half], "wide", 1),
            swap(corners[at + half : at + rows], "narrow", k),
        ]
        stage_two += ends
        beside_bottom = beside_bottom + ends[1].astype(f32)
        at = at + rows
        spread.append(
            jnp.concatenate(
                [mine[at : at + half] + ends[0].astype(f32), mine[at + half : at + rows]], axis=0
            ).astype(bf16)
        )
    spread.append(jnp.concatenate([beside_top, beside_bottom], axis=0).astype(bf16))
    spread = after(spread, later) if later else lax.optimization_barrier(tuple(spread))
    for n, k in enumerate(range(2, size, 2)):
        stage_three.append(swap(spread[n], "narrow", k))
        out = out + stage_three[-1].astype(f32)
    stage_three.append(swap(spread[-1], "wide", 1))
    return out + stage_three[-1].astype(f32), (stage_two, stage_three)


def inverse_rms(values):
    return lax.rsqrt(jnp.mean(values * values, axis=-1, keepdims=True) + epsilon)


def norm_kernel(*refs):
    pieces, gain, out = refs[:-2], refs[-2], refs[-1]
    rows = pieces[0].shape[0]
    step = 32 if rows % 32 == 0 else rows
    for n, piece in enumerate(pieces):

        def part(b, _):
            at = pl.multiple_of(b * step, step)
            values = piece[pl.ds(at, step), :].astype(f32)
            rate = lax.rsqrt(jnp.mean(values * values, axis=-1, keepdims=True) + epsilon)
            to = pl.multiple_of(n * rows + at, step)
            out[pl.ds(to, step), :] = (values * rate * gain[...]).astype(bf16)
            return 0

        lax.fori_loop(0, rows // step, part, 0)


def normed_rows(pieces, gain):
    rows, width = pieces[0].shape
    return pl.pallas_call(
        norm_kernel,
        out_shape=jax.ShapeDtypeStruct((rows * len(pieces), width), bf16),
        cost_estimate=light,
        name="norm",
    )(*pieces, gain.reshape(1, width))


def norm_back(values, rate, gain, grad):
    a = grad * gain
    inner = jnp.mean(a * values, axis=-1, keepdims=True)
    return rate * a - values * (rate * rate * rate) * inner


light = pl.CostEstimate(flops=1024, bytes_accessed=1024, transcendentals=0)


def filter_kernel(base_re, base_im, step_re, step_im, out):
    poles = base_re.shape[0]
    width = out.shape[1]
    for g in range(width // 128 if width % 128 == 0 else 1):
        lanes = pl.ds(g * 128, min(128, width))
        start = tuple(base_re[j, :, lanes] for j in range(poles)) + tuple(
            base_im[j, :, lanes] for j in range(poles)
        )

        def step(b, state):
            total = state[0]
            for j in range(1, poles):
                total = total + state[j]
            out[pl.ds(pl.multiple_of(b * 8, 8), 8), lanes] = total
            new_re, new_im = [], []
            for j in range(poles):
                sr = step_re[j, :, lanes]
                si = step_im[j, :, lanes]
                new_re.append(state[j] * sr - state[poles + j] * si)
                new_im.append(state[j] * si + state[poles + j] * sr)
            return tuple(new_re) + tuple(new_im)

        lax.fori_loop(0, SPAN // 8, step, start)


def filter_taps(base_re, base_im, step_re, step_im):
    width = base_re.shape[2]
    return pl.pallas_call(
        filter_kernel,
        out_shape=jax.ShapeDtypeStruct((SPAN, width), f32),
        cost_estimate=light,
        name="taps",
    )(base_re, base_im, step_re, step_im)


def moment_kernel(grad, step_re, step_im, sum_re, sum_im, mom_re, mom_im):
    poles = step_re.shape[0]
    width = grad.shape[1]
    per = 8
    for g in range(width // 128 if width % 128 == 0 else 1):
        lanes = pl.ds(g * 128, min(128, width))
        for j0 in range(0, poles, per):
            zero = jnp.zeros((8, min(128, width)), f32)

            def step(i, state):
                b = SPAN // 8 - 1 - i
                value = grad[pl.ds(pl.multiple_of(b * 8, 8), 8), lanes]
                new = []
                for n in range(per):
                    sr = step_re[j0 + n, :, lanes]
                    si = step_im[j0 + n, :, lanes]
                    pr, pi, qr, qi = state[4 * n : 4 * n + 4]
                    ur, ui = pr + qr, pi + qi
                    new += [
                        pr * sr - pi * si + value,
                        pr * si + pi * sr,
                        ur * sr - ui * si,
                        ur * si + ui * sr,
                    ]
                return tuple(new)

            state = lax.fori_loop(0, SPAN // 8, step, (zero,) * (4 * per))
            for n in range(per):
                sum_re[j0 + n, :, lanes] = state[4 * n]
                sum_im[j0 + n, :, lanes] = state[4 * n + 1]
                mom_re[j0 + n, :, lanes] = state[4 * n + 2]
                mom_im[j0 + n, :, lanes] = state[4 * n + 3]


SIDE = 512


def product_kernel(a, b, out, turned=None, *, kind):
    if kind == "tn":

        @pl.when(pl.program_id(0) == 0)
        def _():
            turned[...] = a[...].T

        value = nn(turned[...], b[...])
    else:
        value = (nn if kind == "nn" else nt)(a[...], b[...])
    out[...] = value.astype(out.dtype)


def product(a, b, kind, dtype, at=None):
    if kind == "tn":
        depth, rows = a.shape[0], SIDE
        a_spec = pl.BlockSpec((depth, SIDE), lambda i: (0, at))
        scratch = [pltpu.VMEM((SIDE, depth), a.dtype)]
    else:
        rows, depth = a.shape if at is None else (SIDE, a.shape[1])
        a_spec = pl.BlockSpec((rows, depth), lambda i: (at or 0, 0))
        scratch = []
    columns = b.shape[0] if kind == "nt" else b.shape[1]
    side = max(s for s in (512, 384, 256, 128, columns) if columns % s == 0 and s <= 512)
    if kind == "nt":
        b_spec = pl.BlockSpec((side, depth), lambda i: (i, 0))
    else:
        b_spec = pl.BlockSpec((depth, side), lambda i: (0, i))
    return pl.pallas_call(
        partial(product_kernel, kind=kind),
        grid=(columns // side,),
        out_shape=jax.ShapeDtypeStruct((rows, columns), dtype),
        in_specs=[a_spec, b_spec],
        out_specs=pl.BlockSpec((rows, side), lambda i: (0, i)),
        scratch_shapes=scratch,
        cost_estimate=light,
        name="product",
    )(a, b)


def filter_moments(grad, step_re, step_im):
    poles, _, width = step_re.shape
    shape = jax.ShapeDtypeStruct((poles, 8, width), f32)
    return pl.pallas_call(
        moment_kernel,
        out_shape=(shape,) * 4,
        cost_estimate=pl.CostEstimate(
            flops=16 * 15 * SPAN * width, bytes_accessed=4 * SPAN * width, transcendentals=0
        ),
        name="moments",
    )(grad, step_re, step_im)


LIVE, KEEP_ONE, KEEP_TWO = 0, 1, 2


def load_masked(order, proj, table, m_scr):
    pieces, rows, _ = proj.shape
    m_scr[0:8, :] = jnp.zeros_like(m_scr[0:8, :])

    def piece(b, _):
        p = order[b]
        at = pl.multiple_of(b * rows, rows)
        live = table[pl.ds(at, rows), LIVE : LIVE + 1]
        m_scr[pl.ds(pl.multiple_of(at + 8, 8), rows), :] = proj[p] * live
        return 0

    lax.fori_loop(0, pieces, piece, 0)


def short_block(m_scr, taps, table, at):
    window = m_scr[pl.ds(at, BLOCK + 8), :]
    one = table[pl.ds(at, BLOCK), KEEP_ONE : KEEP_ONE + 1]
    two = table[pl.ds(at, BLOCK), KEEP_TWO : KEEP_TWO + 1]
    here = window[8:]
    once = window[7 : BLOCK + 7] * one
    twice = window[6 : BLOCK + 6] * two
    short = taps[0:1, :] * here + taps[1:2, :] * once + taps[2:3, :] * twice
    return short, here, once, twice


def pack_document(source, packed, first, count):
    blocks = source.shape[0] // BLOCK
    for kb in range(LONGEST):
        at = pl.multiple_of(jnp.minimum(first + kb, blocks - 1) * BLOCK, BLOCK)
        inside = (kb < count).astype(f32)
        packed[kb * BLOCK : (kb + 1) * BLOCK, :] = (source[pl.ds(at, BLOCK), :] * inside).astype(bf16)


def place_document(result, target, first, count):
    for kb in range(LONGEST):

        @pl.when(kb < count)
        def _():
            at = pl.multiple_of((first + kb) * BLOCK, BLOCK)
            target[pl.ds(at, BLOCK), :] = result[kb * BLOCK : (kb + 1) * BLOCK, :]


def forward_kernel(
    order, first, count, proj, taps, table, spectrum, fwd, inv, gated, long_out, seen, m_scr, u_scr, q_scr, packed
):
    width = long_out.shape[1]
    pieces, rows, _ = proj.shape
    blocks = long_out.shape[0] // BLOCK
    load_masked(order, proj, table, m_scr)

    def block(n, _):
        at = pl.multiple_of(n * BLOCK, BLOCK)
        short, _, _, _ = short_block(m_scr, taps, table, at)
        q_scr[pl.ds(at, BLOCK), :] = short[:, :width]
        u_scr[pl.ds(at, BLOCK), :] = short[:, width : 2 * width] * short[:, 2 * width :]
        return 0

    lax.fori_loop(0, blocks, block, 0)

    def document(d, _):
        pack_document(u_scr, packed, first[d], count[d])
        both = jnp.dot(fwd[...], packed[...], preferred_element_type=f32)
        seen[d] = both.astype(bf16)
        re, im = both[:FREQ], both[FREQ:]
        hr, hi = spectrum[:FREQ], spectrum[FREQ:]
        answer = jnp.concatenate([re * hr - im * hi, re * hi + im * hr], axis=0).astype(bf16)
        result = jnp.dot(inv[...], answer, preferred_element_type=f32)
        place_document(result, long_out, first[d], count[d])
        return 0

    lax.fori_loop(0, seen.shape[0], document, 0)

    def piece(b, _):
        at = pl.multiple_of(b * rows, rows)
        gated[order[b]] = (q_scr[pl.ds(at, rows), :] * long_out[pl.ds(at, rows), :]).astype(bf16)
        return 0

    lax.fori_loop(0, pieces, piece, 0)


def backward_kernel(
    order, first, count, proj, d_gated, long_out, seen, taps, table, spectrum, fwd, inv,
    dz, d_filter, d_taps, m_scr, dy_scr, k_scr, v_scr, ds_scr, packed, d_spec,
):
    width = long_out.shape[1]
    pieces, rows, _ = proj.shape
    slots = long_out.shape[0]
    blocks = slots // BLOCK
    per_piece = rows // BLOCK
    load_masked(order, proj, table, m_scr)
    ds_scr[slots : slots + 8, :] = jnp.zeros_like(ds_scr[slots : slots + 8, :])

    def block(n, _):
        at = pl.multiple_of(n * BLOCK, BLOCK)
        short, _, _, _ = short_block(m_scr, taps, table, at)
        within = pl.multiple_of((n % per_piece) * BLOCK, BLOCK)
        dg = d_gated[order[n // per_piece], pl.ds(within, BLOCK), :]
        dy_scr[pl.ds(at, BLOCK), :] = dg * short[:, :width]
        ds_scr[pl.ds(at, BLOCK), :width] = dg * long_out[pl.ds(at, BLOCK), :]
        k_scr[pl.ds(at, BLOCK), :] = short[:, width : 2 * width]
        v_scr[pl.ds(at, BLOCK), :] = short[:, 2 * width :]
        return 0

    lax.fori_loop(0, blocks, block, 0)
    d_spec[...] = jnp.zeros_like(d_spec)

    def document(d, _):
        pack_document(dy_scr, packed, first[d], count[d])
        both = jnp.dot(fwd[...], packed[...], preferred_element_type=f32)
        re, im = both[:FREQ], both[FREQ:]
        hr, hi = spectrum[:FREQ], spectrum[FREQ:]
        answer = jnp.concatenate([re * hr + im * hi, im * hr - re * hi], axis=0).astype(bf16)
        result = jnp.dot(inv[...], answer, preferred_element_type=f32)
        ur, ui = seen[d, :FREQ].astype(f32), seen[d, FREQ:].astype(f32)
        d_spec[:FREQ] += re * ur + im * ui
        d_spec[FREQ:] += im * ur - re * ui
        for kb in range(LONGEST):

            @pl.when(kb < count[d])
            def _():
                at = pl.multiple_of((first[d] + kb) * BLOCK, BLOCK)
                du = result[kb * BLOCK : (kb + 1) * BLOCK, :]
                ds_scr[pl.ds(at, BLOCK), width : 2 * width] = du * v_scr[pl.ds(at, BLOCK), :]
                ds_scr[pl.ds(at, BLOCK), 2 * width :] = du * k_scr[pl.ds(at, BLOCK), :]

        return 0

    lax.fori_loop(0, seen.shape[0], document, 0)
    d_filter[...] = jnp.dot(inv[...], d_spec[...].astype(bf16), preferred_element_type=f32)
    d_taps[...] = jnp.zeros_like(d_taps)

    def back(n, _):
        at = pl.multiple_of(n * BLOCK, BLOCK)
        window = m_scr[pl.ds(at, BLOCK + 8), :]
        ahead = ds_scr[pl.ds(at, BLOCK + 8), :]
        one = table[pl.ds(at, BLOCK + 8), KEEP_ONE : KEEP_ONE + 1]
        two = table[pl.ds(at, BLOCK + 8), KEEP_TWO : KEEP_TWO + 1]
        live = table[pl.ds(at, BLOCK), LIVE : LIVE + 1]
        ds = ahead[:BLOCK]
        ahead_one = ahead * one
        ahead_two = ahead * two
        dm = (
            taps[0:1, :] * ds
            + taps[1:2, :] * ahead_one[1 : BLOCK + 1]
            + taps[2:3, :] * ahead_two[2 : BLOCK + 2]
        )
        d_taps[0:1, :] += jnp.sum(window[8:] * ds, axis=0, keepdims=True)
        d_taps[1:2, :] += jnp.sum(window[7 : BLOCK + 7] * ahead_one[:BLOCK], axis=0, keepdims=True)
        d_taps[2:3, :] += jnp.sum(window[6 : BLOCK + 6] * ahead_two[:BLOCK], axis=0, keepdims=True)
        within = pl.multiple_of((n % per_piece) * BLOCK, BLOCK)
        dz[order[n // per_piece], pl.ds(within, BLOCK), :] = (dm * live).astype(bf16)
        return 0

    lax.fori_loop(0, blocks, back, 0)


smem = pl.BlockSpec(memory_space=pltpu.SMEM)
vmem = pl.BlockSpec(memory_space=pltpu.VMEM)


def mixer_forward(order, first, count, proj, taps, table, spectrum, fwd, inv):
    pieces, rows, three = proj.shape
    width = three // 3
    slots = pieces * rows
    docs = first.shape[0]
    return pl.pallas_call(
        forward_kernel,
        out_shape=(
            jax.ShapeDtypeStruct((pieces, rows, width), bf16),
            jax.ShapeDtypeStruct((slots, width), f32),
            jax.ShapeDtypeStruct((docs, 2 * FREQ, width), bf16),
        ),
        in_specs=[smem] * 3 + [vmem] * 6,
        out_specs=(vmem,) * 3,
        scratch_shapes=[
            pltpu.VMEM((slots + 8, three), f32),
            pltpu.VMEM((slots, width), f32),
            pltpu.VMEM((slots, width), f32),
            pltpu.VMEM((SPAN, width), bf16),
        ],
        compiler_params=pltpu.CompilerParams(vmem_limit_bytes=40 * 2**20),
        cost_estimate=light,
        name="mixer_forward",
    )(order, first, count, proj, taps, table, spectrum, fwd, inv)


def mixer_backward(order, first, count, proj, d_gated, long_out, seen, taps, table, spectrum, fwd, inv):
    pieces, rows, three = proj.shape
    width = three // 3
    slots = pieces * rows
    docs = first.shape[0]
    return pl.pallas_call(
        backward_kernel,
        out_shape=(
            jax.ShapeDtypeStruct((pieces, rows, three), bf16),
            jax.ShapeDtypeStruct((SPAN, width), f32),
            jax.ShapeDtypeStruct((8, three), f32),
        ),
        in_specs=[smem] * 3 + [vmem] * 9,
        out_specs=(vmem,) * 3,
        scratch_shapes=[
            pltpu.VMEM((slots + 8, three), f32),
            pltpu.VMEM((slots, width), f32),
            pltpu.VMEM((slots, width), f32),
            pltpu.VMEM((slots, width), f32),
            pltpu.VMEM((slots + 8, three), f32),
            pltpu.VMEM((SPAN, width), bf16),
            pltpu.VMEM((2 * FREQ, width), f32),
        ],
        compiler_params=pltpu.CompilerParams(vmem_limit_bytes=48 * 2**20),
        cost_estimate=light,
        name="mixer_backward",
    )(order, first, count, proj, d_gated, long_out, seen, taps, table, spectrum, fwd, inv)


def layout(doc_blocks, doc_pad, slots):
    block_ends = jnp.cumsum(doc_blocks) * BLOCK
    starts = block_ends - doc_blocks * BLOCK
    places = jnp.arange(slots, dtype=jnp.int32)
    living = (places[None, :] >= starts[:, None]) & (
        places[None, :] < (block_ends - doc_pad)[:, None]
    )
    live = jnp.sum(living.astype(f32), axis=0)
    opening = jnp.sum((places[None, :] == starts[:, None]).astype(f32), axis=0)
    one = 1.0 - opening
    one = one * (places > 0)
    two = one * jnp.concatenate([jnp.zeros((1,), f32), one[:-1]])
    table = jnp.stack([live, one, two], axis=1)
    table = jnp.concatenate([table, jnp.zeros((8, 3), f32)], axis=0)
    return table, starts // BLOCK


def picked(index, count, values):
    hot = index[:, None] == jnp.arange(count)[None, :]
    shape = hot.shape + (1,) * (values.ndim - 1)
    return jnp.sum(jnp.where(hot.reshape(shape), values[None], 0), axis=1)


def body(
    tokens, w_in, w_out, gain_one, short_kernel, decay_rate, pole_angle, residue,
    gain_two, w_gate, w_up, w_down, doc_blocks, doc_pad, cotangent,
):
    wide, narrow = lax.axis_size("wide"), lax.axis_size("narrow")
    wide_at, narrow_at = lax.axis_index("wide"), lax.axis_index("narrow")
    outer = wide // 2
    _, local_rows, width = tokens.shape
    slots = local_rows * narrow
    even = slots // 2
    source = tokens[0].astype(f32)
    upstream_low = cotangent[0]
    poles = decay_rate.shape[1]
    own = w_in.shape[2]
    channels = own * outer
    hidden_units = w_gate.shape[1] * outer

    ring = np.array(ring_of(outer))
    ring_place = np.argsort(ring)
    tour = picked((wide_at // 2)[None], outer, jnp.asarray(ring_place, jnp.int32))[0]
    piece_places = (tour + jnp.asarray(ring_offsets(outer), jnp.int32)) % outer
    piece_outer = picked(piece_places, outer, jnp.asarray(ring, jnp.int32))
    sides = jnp.arange(2) ^ (wide_at % 2)
    offsets = list(range(0, narrow, 2)) + list(range(1, narrow, 2))
    place_of = np.argsort(np.array(offsets))
    order = picked(jnp.arange(narrow) ^ narrow_at, narrow, jnp.asarray(place_of, jnp.int32))
    narrow_of = jnp.asarray(offsets, jnp.int32) ^ narrow_at

    small = jnp.concatenate(
        [
            short_kernel.reshape(9, own),
            decay_rate.T,
            pole_angle.T,
            residue.T,
            gain_one[None],
            gain_two[None],
        ],
        axis=0,
    )
    small_pieces = gather_small(small)
    small_all = jnp.concatenate(small_pieces, axis=1)
    (first_own, first_other), first_stages = gather_rows(tokens[0])
    gains = small_all[small.shape[0] - 2 :].reshape(2, outer, own)
    gains = jnp.stack([gains, swap(gains, "wide", 1)])
    gains = jnp.stack([gains] + [swap(gains, "narrow", k) for k in range(2, narrow, 2)])
    gains = jnp.concatenate([gains, swap(gains, "narrow", 1)], axis=0).astype(f32)
    gains = picked(order, narrow, gains).transpose(1, 3, 0, 2, 4)
    gains = picked(sides, 2, gains).transpose(1, 0, 2, 3, 4)
    hot = piece_outer[None, :] == jnp.arange(outer)[:, None]
    gains = jnp.sum(jnp.where(hot[:, :, None, None, None, None], gains[None], 0), axis=1)
    gain_all = gains.transpose(3, 0, 1, 2, 4).reshape(2, width)
    gain_first, gain_last = gain_all[0], gain_all[1]

    def reduce_gain(values, tokens):
        values = values.reshape(2, outer, 2, narrow, own).transpose(1, 2, 3, 0, 4)
        values = picked(piece_outer, outer, values).transpose(1, 0, 2, 3, 4)
        values = picked(sides, 2, values).transpose(2, 0, 1, 3, 4)
        values = picked(narrow_of, narrow, values)
        total = values[: narrow // 2] + swap(values[narrow // 2 :], "narrow", 1)
        summed = total[0]
        for k in range(1, narrow // 2):
            summed = summed + swap(total[k], "narrow", 2 * k)
        summed = summed[0] + swap(summed[1], "wide", 1)
        [summed] = after([summed], tokens)
        return scatter_small([summed[j] for j in range(outer)])

    documents = jnp.concatenate([doc_blocks, doc_pad], axis=0)
    [documents] = after([documents], small_pieces[1:])
    documents = (documents, swap(documents, "wide", 1))
    tables = [layout(rules[0], rules[1], slots) for rules in documents]

    shards = [w_in.transpose(0, 2, 1).reshape(3 * own, width), w_out, w_down.T, w_gate.T, w_up.T]
    weights = [Gather(shard) for shard in shards]
    in_all, out_all, down_all, gate_all, up_all = weights
    steps = outer // 2
    last = small_pieces[1:]
    for at in range(steps - 1):
        last = ring_step([in_all], last)
    last = ring_step([in_all, out_all], last)
    for at in range(1, steps):
        last = ring_step([out_all], last)

    def normed(pieces):
        values = jnp.concatenate(pieces, axis=0).astype(f32)
        return (values * inverse_rms(values) * gain_first).astype(bf16)

    rows_first = [normed(first_own), normed(first_other)]
    rate_first = inverse_rms(source)
    (upstream_own, upstream_other), upstream_stages = gather_rows(
        upstream_low, first_stages[2], (), True
    )

    matrix = transform()
    fwd = jnp.asarray(matrix, bf16)
    inv = jnp.asarray(matrix.T / SPAN, bf16)

    block = small_all.astype(f32)
    taps = block[:9].reshape(3, 3 * channels)
    taps = jnp.concatenate([taps, jnp.zeros((5, 3 * channels), f32)], axis=0)
    decay = block[9 : 9 + poles][:, None, :]
    angle = block[9 + poles : 9 + 2 * poles][:, None, :]
    res_re = block[9 + 2 * poles : 9 + 3 * poles][:, None, :]
    res_im = -block[9 + 3 * poles : 9 + 4 * poles][:, None, :]
    lag = jnp.arange(8, dtype=f32)[None, :, None]
    fade = jnp.exp(-decay * lag)
    power_re, power_im = fade * jnp.cos(angle * lag), fade * jnp.sin(angle * lag)
    fade_step = jnp.exp(-decay * 8.0)
    step_re = jnp.broadcast_to(fade_step * jnp.cos(angle * 8.0), power_re.shape)
    step_im = jnp.broadcast_to(fade_step * jnp.sin(angle * 8.0), power_re.shape)
    filt = filter_taps(
        res_re * power_re - res_im * power_im,
        res_re * power_im + res_im * power_re,
        step_re,
        step_im,
    )
    spectrum = lax.dot_general(
        jnp.asarray(matrix),
        filt,
        (((1,), (0,)), ((), ())),
        precision=lax.Precision.HIGHEST,
        preferred_element_type=f32,
    )
    res_re, res_im = res_re[:, 0], -res_im[:, 0]

    in_pieces = [piece.reshape(3, own, width) for piece in in_all.pieces()]
    in_all = jnp.concatenate(in_pieces, axis=1).reshape(3 * channels, width)
    mixed = []
    for r in range(2):
        table, first = tables[r]
        proj = product(rows_first[r], in_all, "nt", f32)
        proj = proj.reshape(narrow, local_rows, 3 * channels)
        gated, long_out, seen = mixer_forward(
            order, first, documents[r][0], proj, taps, table, spectrum, fwd, inv
        )
        mixed.append((proj, gated.reshape(slots, channels), long_out, seen))
    out_last = last
    out_all = jnp.concatenate(out_all.pieces(), axis=0)
    parts = [slice(0, even), slice(even, slots)]
    odds = [product(mixed[r][1], out_all, "nn", bf16, 1) for r in range(2)]
    cores = [swap(odd, "narrow", 1) for odd in odds]
    for at in range(steps - 1):
        last = ring_step([down_all], last)
    ready = after([mixed[0][1], mixed[1][1]], last + upstream_stages[0])
    evens = [nn(ready[r][parts[0]], out_all).astype(bf16) for r in range(2)]
    last_two = last
    for at in range(1, steps):
        last_two = ring_step([down_all], last_two, cores)
    last_three = ring_step([gate_all], last_two)
    for at in range(1, steps - 1):
        last_three = ring_step([gate_all], last_three)
    mixer_out, stages = scatter_rows(
        evens[0], cores[0], evens[1], cores[1], upstream_stages[1], last_two
    )
    middle = source + mixer_out
    rate_last = inverse_rms(middle)
    rows_upstream = jnp.concatenate(upstream_own + upstream_other, axis=0)
    low_second = (middle * rate_last * gain_last).astype(bf16)
    last_four = ring_step([gate_all], last_three + stages[1])
    (second_own, second_other), second_stages = gather_rows(low_second, last_three, last_four)
    rows_second = jnp.concatenate(second_own + second_other, axis=0)
    last = ring_step([up_all], last_four + second_stages[0], second_stages[2])
    for at in range(1, steps):
        last = ring_step([up_all], last)

    down_all, gate_all = [jnp.concatenate(w.pieces(), axis=0) for w in (down_all, gate_all)]
    d_hidden = product(down_all, rows_upstream, "nt", f32)
    gate_pre = product(gate_all, rows_second, "nt", f32)
    up_pieces = after(up_all.pieces(), [d_hidden, gate_pre])
    up_all = jnp.concatenate(up_pieces, axis=0)
    up_pre = nt(up_all, rows_second)
    sig = jax.nn.sigmoid(gate_pre)
    silu = gate_pre * sig
    hidden = (silu * up_pre).astype(bf16)
    d_gate = (d_hidden * up_pre * sig * (1.0 + gate_pre * (1.0 - sig))).astype(bf16)
    d_up = (d_hidden * silu).astype(bf16)
    grad_down = product(hidden, rows_upstream, "nn", bf16)
    d_gate, d_up = after([d_gate, d_up], [grad_down])
    parts = [slice(p, p + even) for p in range(0, 2 * slots, even)]
    grads = [Scatter(jnp.split(grad_down, outer, axis=0))]

    def second_share(n):
        p = parts[n]
        return (tn(d_gate[:, p], gate_all) + tn(d_up[:, p], up_all)).astype(bf16)

    odds = [second_share(n) for n in (1, 3)]
    cores = [swap(odd, "narrow", 1) for odd in odds]
    evens = [second_share(0), second_share(2)]
    last = ring_step(grads, (), evens)
    d_second, stages = scatter_rows(evens[0], cores[0], evens[1], cores[1])
    upstream = upstream_low.astype(f32)
    d_middle = upstream + norm_back(middle, rate_last, gain_last, d_second)
    (middle_own, middle_other), middle_stages = gather_rows(d_middle.astype(bf16))
    rows_dmiddle = [jnp.concatenate(middle_own, axis=0), jnp.concatenate(middle_other, axis=0)]
    [d_gate] = after([d_gate], cores + evens)
    grad_gate = product(d_gate, rows_second, "nn", bf16)
    [d_up] = after([d_up], stages[0] + [grad_gate])
    grad_up = product(d_up, rows_second, "nn", bf16)
    [hidden] = after([hidden], [grad_up])
    down_shares = [product(hidden, down_all, "tn", bf16, n) for n in (0, 1)]
    for at in range(1, steps):
        last = ring_step(grads, last, [grad_up])
    down_shares += [product(hidden, down_all, "tn", bf16, n) for n in (2, 3)]
    pair = [Scatter(jnp.split(grad, outer, axis=0)) for grad in (grad_gate, grad_up)]
    grads += pair
    last = ring_step(pair, last, middle_stages[0])
    down_cores = [swap(down_shares[n], "narrow", 1) for n in (1, 3)]
    down_out, down_stages = scatter_rows(
        down_shares[0], down_cores[0], down_shares[2], down_cores[1], middle_stages[1]
    )
    block_output = (middle + down_out).astype(bf16)
    grad_gain_two = jnp.sum(d_second * middle * rate_last, axis=0)

    grad_out = sum(tn(mixed[r][1], rows_dmiddle[r]) for r in range(2)).astype(bf16)
    halves = (slice(0, even), slice(even, slots))
    shares, d_rows, grad_gain_one, d_filter, d_taps = [None, None], [None, None], 0.0, 0.0, 0.0
    for r in range(2):
        proj, gated, long_out, seen = mixed[r]
        table, first = tables[r]
        d_gated = nt(rows_dmiddle[r], out_all).reshape(narrow, local_rows, channels)
        if r == 0:
            for at in range(1, steps):
                last = ring_step(pair[:1], last, [d_gated])
        if r == 1:
            [d_gated] = after([d_gated], [grad_out, *shares[0], *down_stages[1]])
        dz, d_filter_row, d_taps_row = mixer_backward(
            order, first, documents[r][0], proj, d_gated, long_out, seen, taps, table,
            spectrum, fwd, inv,
        )
        d_rows[r] = dz.reshape(slots, 3 * channels)
        d_filter, d_taps = d_filter + d_filter_row, d_taps + d_taps_row
        if r == 0:
            [ready] = after([d_rows[r]], down_stages[0])
            shares[r] = [nn(ready[p], in_all).astype(bf16) for p in halves]
    for at in range(1, steps):
        last = ring_step(pair[1:], last, [d_rows[1]])
    out_sum = Scatter(jnp.split(grad_out, outer, axis=0))
    for at in range(steps):
        last = ring_step([out_sum], last)
    odd = nn(d_rows[1][halves[1]], in_all).astype(bf16)
    cores = [swap(shares[0][1], "narrow", 1), swap(odd, "narrow", 1)]
    ready = after(d_rows, [odd])
    grad_in = sum(tn(ready[r], rows_first[r]) for r in range(2)).astype(bf16)
    [ready] = after([d_rows[1]], [grad_in] + cores)
    shares[1] = [nn(ready[halves[0]], in_all).astype(bf16), odd]
    d_normed, stages = scatter_rows(shares[0][0], cores[0], shares[1][0], cores[1])
    input_grad = (d_middle + norm_back(source, rate_first, gain_first, d_normed)).astype(bf16)
    for r in range(2):
        for n, share in enumerate(after(shares[r], [shares[1][0]])):
            rows = rows_first[r][n * even : (n + 1) * even]
            grad_gain_one = grad_gain_one + jnp.sum(share.astype(f32) * rows.astype(f32), axis=0)
    chunks = grad_in.reshape(3, outer, own, width)
    in_sum = Scatter([chunks[:, j].reshape(3 * own, width) for j in range(outer)])
    last = ring_step([in_sum], last, stages[0])
    d_filter, *_ = after([d_filter], last + stages[0])
    gain_grads = after([jnp.stack([grad_gain_one / gain_first, grad_gain_two])], stages[0])
    gain_share = reduce_gain(gain_grads[0], stages[1])

    sum_re, sum_im, mom_re, mom_im = filter_moments(d_filter, step_re, step_im)
    full_re = lag * sum_re + 8.0 * mom_re
    full_im = lag * sum_im + 8.0 * mom_im
    grad_re = jnp.sum(power_re * sum_re - power_im * sum_im, axis=1)
    grad_im = jnp.sum(power_re * sum_im + power_im * sum_re, axis=1)
    lag_re = jnp.sum(power_re * full_re - power_im * full_im, axis=1)
    lag_im = jnp.sum(power_re * full_im + power_im * full_re, axis=1)
    small_grad = jnp.concatenate(
        [
            d_taps[:3].reshape(9, channels),
            -(res_re * lag_re + res_im * lag_im),
            res_im * lag_re - res_re * lag_im,
            grad_re,
            grad_im,
        ],
        axis=0,
    ).astype(bf16)
    [small_grad] = after([small_grad], stages[1])
    small_share = scatter_small(jnp.split(small_grad, outer, axis=1))

    for at in range(1, steps):
        last = ring_step([in_sum], last, [gain_share, small_share])

    at = 9 + poles
    return (
        block_output[None],
        input_grad[None],
        in_sum.total.reshape(3, own, width).transpose(0, 2, 1),
        out_sum.total,
        gain_share[0],
        small_share[:9].reshape(3, 3, own),
        small_share[9:at].T,
        small_share[at : at + poles].T,
        small_share[at + poles :].T,
        gain_share[1],
        grads[1].total.T,
        grads[2].total.T,
        grads[0].total.T,
    )


def solution(mesh):
    both = ("wide", "narrow")
    return jax.shard_map(
        body,
        mesh=mesh,
        in_specs=(
            P("wide", "narrow", None),
            P(None, None, both),
            P(both, None),
            P(both),
            P(None, None, both),
            P(both, None),
            P(both, None),
            P(both, None),
            P(both),
            P(None, both),
            P(None, both),
            P(None, both),
            P("wide", None),
            P("wide", None),
            P("wide", "narrow", None),
        ),
        out_specs=(
            P("wide", "narrow", None),
            P("wide", "narrow", None),
            P(None, None, both),
            P(both, None),
            P(both),
            P(None, None, both),
            P(both, None),
            P(both, None),
            P(both, None),
            P(both),
            P(None, both),
            P(None, both),
            P(None, both),
        ),
        check_vma=False,
    )
```

```python
from functools import partial

import jax
import jax.numpy as jnp
import numpy as np
from jax import lax
from jax.experimental import pallas as pl
from jax.experimental.pallas import tpu as pltpu
from jax.sharding import PartitionSpec as P

BLOCK = 128
LONGEST = 4
SPAN = LONGEST * BLOCK
FREQ = SPAN

epsilon = 1e-06
bf16 = jnp.bfloat16
f32 = jnp.float32


def transform():
    k = np.arange(FREQ)[:, None] * 2 + 1
    t = np.arange(SPAN)[None, :]
    turn = (k * t % (4 * SPAN)) * (2 * np.pi / (4 * SPAN))
    return np.concatenate([np.cos(turn), -np.sin(turn)], axis=0).astype(np.float32)


def nn(a, b):
    return lax.dot_general(a, b, (((1,), (0,)), ((), ())), preferred_element_type=f32)


def nt(a, b):
    return lax.dot_general(a, b, (((1,), (1,)), ((), ())), preferred_element_type=f32)


def tn(a, b):
    return lax.dot_general(a, b, (((0,), (0,)), ((), ())), preferred_element_type=f32)


def swap(values, axis, shift):
    size = lax.axis_size(axis)
    return lax.ppermute(values, axis, [(i, i ^ shift) for i in range(size)])


def after(values, tokens):
    if not tokens:
        return values
    joined = lax.optimization_barrier(tuple(values) + tuple(tokens))
    return list(joined[: len(values)])


def ring_of(size):
    return list(range(0, size, 2)) + list(range(size - 1, 0, -2))


def along(values, step):
    outer = lax.axis_size("wide") // 2
    ring = ring_of(outer)
    pairs = [
        (ring[p] * 2 + side, ring[(p + step) % outer] * 2 + side)
        for p in range(outer)
        for side in range(2)
    ]
    return lax.ppermute(values, "wide", pairs)


def ring_offsets(outer):
    near = [sign * h for h in range(1, outer // 2) for sign in (-1, 1)]
    return [0] + near + [outer // 2]


def cut_of(rows):
    cut = (rows // 2 + 15) // 16 * 16
    return cut if cut < rows else rows // 2


def two_parts(values, axis):
    cut = cut_of(values.shape[axis])
    return (
        lax.slice_in_dim(values, 0, cut, axis=axis),
        lax.slice_in_dim(values, cut, values.shape[axis], axis=axis),
    )


class Gather:
    def __init__(self, own):
        self.most = lax.axis_size("wide") // 4 - 1
        self.before, self.behind, self.opposite = [own], [own], []

    def sends(self):
        if len(self.before) <= self.most:
            return self.before[-1], self.behind[-1]
        return two_parts(self.before[-1], 0)[0], two_parts(self.behind[-1], 0)[1]

    def take(self, got, back):
        if len(self.before) <= self.most:
            self.before.append(got)
            self.behind.append(back)
        else:
            self.opposite = [got, back]

    def pieces(self):
        near = [piece for pair in zip(self.before[1:], self.behind[1:]) for piece in pair]
        return [self.before[0]] + near + [jnp.concatenate(self.opposite, axis=0)]


class Scatter:
    def __init__(self, chunks):
        self.left = len(chunks) // 2 - 1
        self.wire = chunks[0].dtype
        self.total = chunks[0].astype(f32)
        self.behind = [chunk.astype(f32) for chunk in chunks[1:-1:2]]
        self.ahead = [chunk.astype(f32) for chunk in chunks[2:-1:2]]
        self.last = chunks[-1]

    def sends(self):
        if self.last is not None:
            return two_parts(self.last, 0)
        h = self.left - 1
        return self.ahead[h].astype(self.wire), self.behind[h].astype(self.wire)

    def take(self, got, back):
        got, back = got.astype(f32), back.astype(f32)
        h = self.left - 1
        if self.last is not None:
            top, bottom = two_parts(self.ahead[h], 0)
            self.ahead[h] = jnp.concatenate([top + got, bottom], axis=0)
            top, bottom = two_parts(self.behind[h], 0)
            self.behind[h] = jnp.concatenate([top, bottom + back], axis=0)
            self.last = None
            return
        self.left = h
        if h:
            self.ahead[h - 1] = self.ahead[h - 1] + got
            self.behind[h - 1] = self.behind[h - 1] + back
        else:
            self.total = self.total + got + back


def ring_step(items, tokens=(), arrive=()):
    sends = [item.sends() for item in items]
    ways = [one[0] if len(one) == 1 else jnp.concatenate(one, axis=0) for one in zip(*sends)]
    ways = after(ways, list(tokens)) if tokens else lax.optimization_barrier(tuple(ways))
    got, back = after([along(ways[0], 1), along(ways[1], -1)], list(arrive))
    at = [0, 0]
    for item, (ahead, behind) in zip(items, sends):
        ends = [at[0] + ahead.shape[0], at[1] + behind.shape[0]]
        item.take(got[at[0] : ends[0]], back[at[1] : ends[1]])
        at = ends
    return [got, back]


def gather_small(own):
    outer = lax.axis_size("wide") // 2
    return [own] + [along(own, -offset) for offset in ring_offsets(outer)[1:]]


def scatter_small(chunks):
    offsets = ring_offsets(len(chunks))
    total = chunks[0].astype(f32)
    for chunk, offset in zip(chunks[1:], offsets[1:]):
        total = total + along(chunk, offset).astype(f32)
    return total


def gather_rows(own, tokens=(), later=(), single=False):
    size = lax.axis_size("narrow")
    half = own.shape[0] // 2
    [own] = after([own], tokens)
    across = [swap(own, "narrow", k) for k in range(2, size, 2)]
    beside = swap(own, "wide", 1)
    stage_one = across + [beside]
    if later:
        *across, beside = after(across + [beside], later)
    parts, stage_two = [beside], []
    for n, k in enumerate(range(2, size, 2)):
        ends = [swap(across[n][:half], "wide", 1), swap(beside[half:], "narrow", k)]
        parts += ends
        stage_two += ends
    even = jnp.concatenate([own] + across, axis=0)
    other_even = jnp.concatenate(parts, axis=0)
    odd = swap(even, "narrow", 1)
    if single:
        [other_even] = after([other_even], [odd])
    other_odd = swap(other_even, "narrow", 1)
    return ([even, odd], [other_even, other_odd]), (stage_one, stage_two, [odd, other_odd])


def scatter_rows(even, odd, other_even, other_odd, tokens=(), later=()):
    size = lax.axis_size("narrow")
    rows = even.shape[0] // (size // 2)
    half = rows // 2
    other = other_even.astype(f32) + other_odd.astype(f32)
    mine = even.astype(f32) + odd.astype(f32)
    beside_top, beside_bottom = other[:half], other[half:rows]
    out = mine[:rows]
    corners = other[rows:].astype(bf16)
    [corners] = after([corners], tokens)
    spread, stage_two, stage_three = [], [], []
    for n, k in enumerate(range(2, size, 2)):
        at = n * rows
        ends = [
            swap(corners[at : at + half], "wide", 1),
            swap(corners[at + half : at + rows], "narrow", k),
        ]
        stage_two += ends
        beside_bottom = beside_bottom + ends[1].astype(f32)
        at = at + rows
        spread.append(
            jnp.concatenate(
                [mine[at : at + half] + ends[0].astype(f32), mine[at + half : at + rows]], axis=0
            ).astype(bf16)
        )
    spread.append(jnp.concatenate([beside_top, beside_bottom], axis=0).astype(bf16))
    spread = after(spread, later) if later else lax.optimization_barrier(tuple(spread))
    for n, k in enumerate(range(2, size, 2)):
        stage_three.append(swap(spread[n], "narrow", k))
        out = out + stage_three[-1].astype(f32)
    stage_three.append(swap(spread[-1], "wide", 1))
    return out + stage_three[-1].astype(f32), (stage_two, stage_three)


def inverse_rms(values):
    return lax.rsqrt(jnp.mean(values * values, axis=-1, keepdims=True) + epsilon)


def norm_kernel(*refs):
    pieces, gain, out = refs[:-2], refs[-2], refs[-1]
    rows = pieces[0].shape[0]
    step = 32 if rows % 32 == 0 else rows
    for n, piece in enumerate(pieces):

        def part(b, _):
            at = pl.multiple_of(b * step, step)
            values = piece[pl.ds(at, step), :].astype(f32)
            rate = lax.rsqrt(jnp.mean(values * values, axis=-1, keepdims=True) + epsilon)
            to = pl.multiple_of(n * rows + at, step)
            out[pl.ds(to, step), :] = (values * rate * gain[...]).astype(bf16)
            return 0

        lax.fori_loop(0, rows // step, part, 0)


def normed_rows(pieces, gain):
    rows, width = pieces[0].shape
    return pl.pallas_call(
        norm_kernel,
        out_shape=jax.ShapeDtypeStruct((rows * len(pieces), width), bf16),
        cost_estimate=light,
        name="norm",
    )(*pieces, gain.reshape(1, width))


def norm_back(values, rate, gain, grad):
    a = grad * gain
    inner = jnp.mean(a * values, axis=-1, keepdims=True)
    return rate * a - values * (rate * rate * rate) * inner


light = pl.CostEstimate(flops=1024, bytes_accessed=1024, transcendentals=0)


def filter_kernel(base_re, base_im, step_re, step_im, out):
    poles = base_re.shape[0]
    width = out.shape[1]
    for g in range(width // 128 if width % 128 == 0 else 1):
        lanes = pl.ds(g * 128, min(128, width))
        start = tuple(base_re[j, :, lanes] for j in range(poles)) + tuple(
            base_im[j, :, lanes] for j in range(poles)
        )

        def step(b, state):
            total = state[0]
            for j in range(1, poles):
                total = total + state[j]
            out[pl.ds(pl.multiple_of(b * 8, 8), 8), lanes] = total
            new_re, new_im = [], []
            for j in range(poles):
                sr = step_re[j, :, lanes]
                si = step_im[j, :, lanes]
                new_re.append(state[j] * sr - state[poles + j] * si)
                new_im.append(state[j] * si + state[poles + j] * sr)
            return tuple(new_re) + tuple(new_im)

        lax.fori_loop(0, SPAN // 8, step, start)


def filter_taps(base_re, base_im, step_re, step_im):
    width = base_re.shape[2]
    return pl.pallas_call(
        filter_kernel,
        out_shape=jax.ShapeDtypeStruct((SPAN, width), f32),
        cost_estimate=light,
        name="taps",
    )(base_re, base_im, step_re, step_im)


def moment_kernel(grad, step_re, step_im, sum_re, sum_im, mom_re, mom_im):
    poles = step_re.shape[0]
    width = grad.shape[1]
    per = 8
    for g in range(width // 128 if width % 128 == 0 else 1):
        lanes = pl.ds(g * 128, min(128, width))
        for j0 in range(0, poles, per):
            zero = jnp.zeros((8, min(128, width)), f32)

            def step(i, state):
                b = SPAN // 8 - 1 - i
                value = grad[pl.ds(pl.multiple_of(b * 8, 8), 8), lanes]
                new = []
                for n in range(per):
                    sr = step_re[j0 + n, :, lanes]
                    si = step_im[j0 + n, :, lanes]
                    pr, pi, qr, qi = state[4 * n : 4 * n + 4]
                    ur, ui = pr + qr, pi + qi
                    new += [
                        pr * sr - pi * si + value,
                        pr * si + pi * sr,
                        ur * sr - ui * si,
                        ur * si + ui * sr,
                    ]
                return tuple(new)

            state = lax.fori_loop(0, SPAN // 8, step, (zero,) * (4 * per))
            for n in range(per):
                sum_re[j0 + n, :, lanes] = state[4 * n]
                sum_im[j0 + n, :, lanes] = state[4 * n + 1]
                mom_re[j0 + n, :, lanes] = state[4 * n + 2]
                mom_im[j0 + n, :, lanes] = state[4 * n + 3]


SIDE = 512


def product_kernel(a, b, out, turned=None, *, kind):
    if kind == "tn":

        @pl.when(pl.program_id(0) == 0)
        def _():
            turned[...] = a[...].T

        value = nn(turned[...], b[...])
    else:
        value = (nn if kind == "nn" else nt)(a[...], b[...])
    out[...] = value.astype(out.dtype)


def product(a, b, kind, dtype, at=None):
    if kind == "tn":
        depth, rows = a.shape[0], SIDE
        a_spec = pl.BlockSpec((depth, SIDE), lambda i: (0, at))
        scratch = [pltpu.VMEM((SIDE, depth), a.dtype)]
    else:
        rows, depth = a.shape if at is None else (SIDE, a.shape[1])
        a_spec = pl.BlockSpec((rows, depth), lambda i: (at or 0, 0))
        scratch = []
    columns = b.shape[0] if kind == "nt" else b.shape[1]
    side = max(s for s in (512, 384, 256, 128, columns) if columns % s == 0 and s <= 512)
    if kind == "nt":
        b_spec = pl.BlockSpec((side, depth), lambda i: (i, 0))
    else:
        b_spec = pl.BlockSpec((depth, side), lambda i: (0, i))
    return pl.pallas_call(
        partial(product_kernel, kind=kind),
        grid=(columns // side,),
        out_shape=jax.ShapeDtypeStruct((rows, columns), dtype),
        in_specs=[a_spec, b_spec],
        out_specs=pl.BlockSpec((rows, side), lambda i: (0, i)),
        scratch_shapes=scratch,
        cost_estimate=light,
        name="product",
    )(a, b)


def filter_moments(grad, step_re, step_im):
    poles, _, width = step_re.shape
    shape = jax.ShapeDtypeStruct((poles, 8, width), f32)
    return pl.pallas_call(
        moment_kernel,
        out_shape=(shape,) * 4,
        cost_estimate=pl.CostEstimate(
            flops=16 * 15 * SPAN * width, bytes_accessed=4 * SPAN * width, transcendentals=0
        ),
        name="moments",
    )(grad, step_re, step_im)


LIVE, KEEP_ONE, KEEP_TWO = 0, 1, 2


def load_masked(order, proj, table, m_scr):
    pieces, rows, _ = proj.shape
    m_scr[0:8, :] = jnp.zeros_like(m_scr[0:8, :])

    def piece(b, _):
        p = order[b]
        at = pl.multiple_of(b * rows, rows)
        live = table[pl.ds(at, rows), LIVE : LIVE + 1]
        m_scr[pl.ds(pl.multiple_of(at + 8, 8), rows), :] = proj[p] * live
        return 0

    lax.fori_loop(0, pieces, piece, 0)


def short_block(m_scr, taps, table, at):
    window = m_scr[pl.ds(at, BLOCK + 8), :]
    one = table[pl.ds(at, BLOCK), KEEP_ONE : KEEP_ONE + 1]
    two = table[pl.ds(at, BLOCK), KEEP_TWO : KEEP_TWO + 1]
    here = window[8:]
    once = window[7 : BLOCK + 7] * one
    twice = window[6 : BLOCK + 6] * two
    short = taps[0:1, :] * here + taps[1:2, :] * once + taps[2:3, :] * twice
    return short, here, once, twice


def pack_document(source, packed, first, count):
    blocks = source.shape[0] // BLOCK
    for kb in range(LONGEST):
        at = pl.multiple_of(jnp.minimum(first + kb, blocks - 1) * BLOCK, BLOCK)
        inside = (kb < count).astype(f32)
        packed[kb * BLOCK : (kb + 1) * BLOCK, :] = (source[pl.ds(at, BLOCK), :] * inside).astype(bf16)


def place_document(result, target, first, count):
    for kb in range(LONGEST):

        @pl.when(kb < count)
        def _():
            at = pl.multiple_of((first + kb) * BLOCK, BLOCK)
            target[pl.ds(at, BLOCK), :] = result[kb * BLOCK : (kb + 1) * BLOCK, :]


def forward_kernel(
    order, first, count, proj, taps, table, spectrum, fwd, inv, gated, long_out, seen, m_scr, u_scr, q_scr, packed
):
    width = long_out.shape[1]
    pieces, rows, _ = proj.shape
    blocks = long_out.shape[0] // BLOCK
    load_masked(order, proj, table, m_scr)

    def block(n, _):
        at = pl.multiple_of(n * BLOCK, BLOCK)
        short, _, _, _ = short_block(m_scr, taps, table, at)
        q_scr[pl.ds(at, BLOCK), :] = short[:, :width]
        u_scr[pl.ds(at, BLOCK), :] = short[:, width : 2 * width] * short[:, 2 * width :]
        return 0

    lax.fori_loop(0, blocks, block, 0)

    def document(d, _):
        pack_document(u_scr, packed, first[d], count[d])
        both = jnp.dot(fwd[...], packed[...], preferred_element_type=f32)
        seen[d] = both.astype(bf16)
        re, im = both[:FREQ], both[FREQ:]
        hr, hi = spectrum[:FREQ], spectrum[FREQ:]
        answer = jnp.concatenate([re * hr - im * hi, re * hi + im * hr], axis=0).astype(bf16)
        result = jnp.dot(inv[...], answer, preferred_element_type=f32)
        place_document(result, long_out, first[d], count[d])
        return 0

    lax.fori_loop(0, seen.shape[0], document, 0)

    def piece(b, _):
        at = pl.multiple_of(b * rows, rows)
        gated[order[b]] = (q_scr[pl.ds(at, rows), :] * long_out[pl.ds(at, rows), :]).astype(bf16)
        return 0

    lax.fori_loop(0, pieces, piece, 0)


def backward_kernel(
    order, first, count, proj, d_gated, long_out, seen, taps, table, spectrum, fwd, inv,
    dz, d_filter, d_taps, m_scr, dy_scr, k_scr, v_scr, ds_scr, packed, d_spec,
):
    width = long_out.shape[1]
    pieces, rows, _ = proj.shape
    slots = long_out.shape[0]
    blocks = slots // BLOCK
    per_piece = rows // BLOCK
    load_masked(order, proj, table, m_scr)
    ds_scr[slots : slots + 8, :] = jnp.zeros_like(ds_scr[slots : slots + 8, :])

    def block(n, _):
        at = pl.multiple_of(n * BLOCK, BLOCK)
        short, _, _, _ = short_block(m_scr, taps, table, at)
        within = pl.multiple_of((n % per_piece) * BLOCK, BLOCK)
        dg = d_gated[order[n // per_piece], pl.ds(within, BLOCK), :]
        dy_scr[pl.ds(at, BLOCK), :] = dg * short[:, :width]
        ds_scr[pl.ds(at, BLOCK), :width] = dg * long_out[pl.ds(at, BLOCK), :]
        k_scr[pl.ds(at, BLOCK), :] = short[:, width : 2 * width]
        v_scr[pl.ds(at, BLOCK), :] = short[:, 2 * width :]
        return 0

    lax.fori_loop(0, blocks, block, 0)
    d_spec[...] = jnp.zeros_like(d_spec)

    def document(d, _):
        pack_document(dy_scr, packed, first[d], count[d])
        both = jnp.dot(fwd[...], packed[...], preferred_element_type=f32)
        re, im = both[:FREQ], both[FREQ:]
        hr, hi = spectrum[:FREQ], spectrum[FREQ:]
        answer = jnp.concatenate([re * hr + im * hi, im * hr - re * hi], axis=0).astype(bf16)
        result = jnp.dot(inv[...], answer, preferred_element_type=f32)
        ur, ui = seen[d, :FREQ].astype(f32), seen[d, FREQ:].astype(f32)
        d_spec[:FREQ] += re * ur + im * ui
        d_spec[FREQ:] += im * ur - re * ui
        for kb in range(LONGEST):

            @pl.when(kb < count[d])
            def _():
                at = pl.multiple_of((first[d] + kb) * BLOCK, BLOCK)
                du = result[kb * BLOCK : (kb + 1) * BLOCK, :]
                ds_scr[pl.ds(at, BLOCK), width : 2 * width] = du * v_scr[pl.ds(at, BLOCK), :]
                ds_scr[pl.ds(at, BLOCK), 2 * width :] = du * k_scr[pl.ds(at, BLOCK), :]

        return 0

    lax.fori_loop(0, seen.shape[0], document, 0)
    d_filter[...] = jnp.dot(inv[...], d_spec[...].astype(bf16), preferred_element_type=f32)
    d_taps[...] = jnp.zeros_like(d_taps)

    def back(n, _):
        at = pl.multiple_of(n * BLOCK, BLOCK)
        window = m_scr[pl.ds(at, BLOCK + 8), :]
        ahead = ds_scr[pl.ds(at, BLOCK + 8), :]
        one = table[pl.ds(at, BLOCK + 8), KEEP_ONE : KEEP_ONE + 1]
        two = table[pl.ds(at, BLOCK + 8), KEEP_TWO : KEEP_TWO + 1]
        live = table[pl.ds(at, BLOCK), LIVE : LIVE + 1]
        ds = ahead[:BLOCK]
        ahead_one = ahead * one
        ahead_two = ahead * two
        dm = (
            taps[0:1, :] * ds
            + taps[1:2, :] * ahead_one[1 : BLOCK + 1]
            + taps[2:3, :] * ahead_two[2 : BLOCK + 2]
        )
        d_taps[0:1, :] += jnp.sum(window[8:] * ds, axis=0, keepdims=True)
        d_taps[1:2, :] += jnp.sum(window[7 : BLOCK + 7] * ahead_one[:BLOCK], axis=0, keepdims=True)
        d_taps[2:3, :] += jnp.sum(window[6 : BLOCK + 6] * ahead_two[:BLOCK], axis=0, keepdims=True)
        within = pl.multiple_of((n % per_piece) * BLOCK, BLOCK)
        dz[order[n // per_piece], pl.ds(within, BLOCK), :] = (dm * live).astype(bf16)
        return 0

    lax.fori_loop(0, blocks, back, 0)


smem = pl.BlockSpec(memory_space=pltpu.SMEM)
vmem = pl.BlockSpec(memory_space=pltpu.VMEM)


def mixer_forward(order, first, count, proj, taps, table, spectrum, fwd, inv):
    pieces, rows, three = proj.shape
    width = three // 3
    slots = pieces * rows
    docs = first.shape[0]
    return pl.pallas_call(
        forward_kernel,
        out_shape=(
            jax.ShapeDtypeStruct((pieces, rows, width), bf16),
            jax.ShapeDtypeStruct((slots, width), f32),
            jax.ShapeDtypeStruct((docs, 2 * FREQ, width), bf16),
        ),
        in_specs=[smem] * 3 + [vmem] * 6,
        out_specs=(vmem,) * 3,
        scratch_shapes=[
            pltpu.VMEM((slots + 8, three), f32),
            pltpu.VMEM((slots, width), f32),
            pltpu.VMEM((slots, width), f32),
            pltpu.VMEM((SPAN, width), bf16),
        ],
        compiler_params=pltpu.CompilerParams(vmem_limit_bytes=40 * 2**20),
        cost_estimate=light,
        name="mixer_forward",
    )(order, first, count, proj, taps, table, spectrum, fwd, inv)


def mixer_backward(order, first, count, proj, d_gated, long_out, seen, taps, table, spectrum, fwd, inv):
    pieces, rows, three = proj.shape
    width = three // 3
    slots = pieces * rows
    docs = first.shape[0]
    return pl.pallas_call(
        backward_kernel,
        out_shape=(
            jax.ShapeDtypeStruct((pieces, rows, three), bf16),
            jax.ShapeDtypeStruct((SPAN, width), f32),
            jax.ShapeDtypeStruct((8, three), f32),
        ),
        in_specs=[smem] * 3 + [vmem] * 9,
        out_specs=(vmem,) * 3,
        scratch_shapes=[
            pltpu.VMEM((slots + 8, three), f32),
            pltpu.VMEM((slots, width), f32),
            pltpu.VMEM((slots, width), f32),
            pltpu.VMEM((slots, width), f32),
            pltpu.VMEM((slots + 8, three), f32),
            pltpu.VMEM((SPAN, width), bf16),
            pltpu.VMEM((2 * FREQ, width), f32),
        ],
        compiler_params=pltpu.CompilerParams(vmem_limit_bytes=48 * 2**20),
        cost_estimate=light,
        name="mixer_backward",
    )(order, first, count, proj, d_gated, long_out, seen, taps, table, spectrum, fwd, inv)


def layout(doc_blocks, doc_pad, slots):
    block_ends = jnp.cumsum(doc_blocks) * BLOCK
    starts = block_ends - doc_blocks * BLOCK
    places = jnp.arange(slots, dtype=jnp.int32)
    living = (places[None, :] >= starts[:, None]) & (
        places[None, :] < (block_ends - doc_pad)[:, None]
    )
    live = jnp.sum(living.astype(f32), axis=0)
    opening = jnp.sum((places[None, :] == starts[:, None]).astype(f32), axis=0)
    one = 1.0 - opening
    one = one * (places > 0)
    two = one * jnp.concatenate([jnp.zeros((1,), f32), one[:-1]])
    table = jnp.stack([live, one, two], axis=1)
    table = jnp.concatenate([table, jnp.zeros((8, 3), f32)], axis=0)
    return table, starts // BLOCK


def picked(index, count, values):
    hot = index[:, None] == jnp.arange(count)[None, :]
    shape = hot.shape + (1,) * (values.ndim - 1)
    return jnp.sum(jnp.where(hot.reshape(shape), values[None], 0), axis=1)


def body(
    tokens, w_in, w_out, gain_one, short_kernel, decay_rate, pole_angle, residue,
    gain_two, w_gate, w_up, w_down, doc_blocks, doc_pad, cotangent,
):
    wide, narrow = lax.axis_size("wide"), lax.axis_size("narrow")
    wide_at, narrow_at = lax.axis_index("wide"), lax.axis_index("narrow")
    outer = wide // 2
    _, local_rows, width = tokens.shape
    slots = local_rows * narrow
    even = slots // 2
    source = tokens[0].astype(f32)
    upstream_low = cotangent[0]
    poles = decay_rate.shape[1]
    own = w_in.shape[2]
    channels = own * outer
    hidden_units = w_gate.shape[1] * outer

    ring = np.array(ring_of(outer))
    ring_place = np.argsort(ring)
    tour = picked((wide_at // 2)[None], outer, jnp.asarray(ring_place, jnp.int32))[0]
    piece_places = (tour + jnp.asarray(ring_offsets(outer), jnp.int32)) % outer
    piece_outer = picked(piece_places, outer, jnp.asarray(ring, jnp.int32))
    sides = jnp.arange(2) ^ (wide_at % 2)
    offsets = list(range(0, narrow, 2)) + list(range(1, narrow, 2))
    place_of = np.argsort(np.array(offsets))
    order = picked(jnp.arange(narrow) ^ narrow_at, narrow, jnp.asarray(place_of, jnp.int32))
    narrow_of = jnp.asarray(offsets, jnp.int32) ^ narrow_at

    small = jnp.concatenate(
        [
            short_kernel.reshape(9, own),
            decay_rate.T,
            pole_angle.T,
            residue.T,
            gain_one[None],
            gain_two[None],
        ],
        axis=0,
    )
    small_pieces = gather_small(small)
    small_all = jnp.concatenate(small_pieces, axis=1)
    (first_own, first_other), first_stages = gather_rows(tokens[0])
    gains = small_all[small.shape[0] - 2 :].reshape(2, outer, own)
    gains = jnp.stack([gains, swap(gains, "wide", 1)])
    gains = jnp.stack([gains] + [swap(gains, "narrow", k) for k in range(2, narrow, 2)])
    gains = jnp.concatenate([gains, swap(gains, "narrow", 1)], axis=0).astype(f32)
    gains = picked(order, narrow, gains).transpose(1, 3, 0, 2, 4)
    gains = picked(sides, 2, gains).transpose(1, 0, 2, 3, 4)
    hot = piece_outer[None, :] == jnp.arange(outer)[:, None]
    gains = jnp.sum(jnp.where(hot[:, :, None, None, None, None], gains[None], 0), axis=1)
    gain_all = gains.transpose(3, 0, 1, 2, 4).reshape(2, width)
    gain_first, gain_last = gain_all[0], gain_all[1]

    def reduce_gain(values, tokens):
        values = values.reshape(2, outer, 2, narrow, own).transpose(1, 2, 3, 0, 4)
        values = picked(piece_outer, outer, values).transpose(1, 0, 2, 3, 4)
        values = picked(sides, 2, values).transpose(2, 0, 1, 3, 4)
        values = picked(narrow_of, narrow, values)
        total = values[: narrow // 2] + swap(values[narrow // 2 :], "narrow", 1)
        summed = total[0]
        for k in range(1, narrow // 2):
            summed = summed + swap(total[k], "narrow", 2 * k)
        summed = summed[0] + swap(summed[1], "wide", 1)
        [summed] = after([summed], tokens)
        return scatter_small([summed[j] for j in range(outer)])

    documents = jnp.concatenate([doc_blocks, doc_pad], axis=0)
    [documents] = after([documents], small_pieces[1:])
    documents = (documents, swap(documents, "wide", 1))
    tables = [layout(rules[0], rules[1], slots) for rules in documents]

    shards = [w_in.transpose(0, 2, 1).reshape(3 * own, width), w_out, w_down.T, w_gate.T, w_up.T]
    weights = [Gather(shard) for shard in shards]
    in_all, out_all, down_all, gate_all, up_all = weights
    steps = outer // 2
    last = small_pieces[1:]
    for at in range(steps):
        last = ring_step([in_all, out_all], last)

    def normed(pieces):
        values = jnp.concatenate(pieces, axis=0).astype(f32)
        return (values * inverse_rms(values) * gain_first).astype(bf16)

    rows_first = lax.optimization_barrier([normed(first_own), normed(first_other)])
    rate_first = inverse_rms(source)
    (upstream_own, upstream_other), upstream_stages = gather_rows(
        upstream_low, first_stages[2], (), True
    )

    matrix = transform()
    fwd = jnp.asarray(matrix, bf16)
    inv = jnp.asarray(matrix.T / SPAN, bf16)

    block = small_all.astype(f32)
    taps = block[:9].reshape(3, 3 * channels)
    taps = jnp.concatenate([taps, jnp.zeros((5, 3 * channels), f32)], axis=0)
    decay = block[9 : 9 + poles][:, None, :]
    angle = block[9 + poles : 9 + 2 * poles][:, None, :]
    res_re = block[9 + 2 * poles : 9 + 3 * poles][:, None, :]
    res_im = -block[9 + 3 * poles : 9 + 4 * poles][:, None, :]
    lag = jnp.arange(8, dtype=f32)[None, :, None]
    fade = jnp.exp(-decay * lag)
    power_re, power_im = fade * jnp.cos(angle * lag), fade * jnp.sin(angle * lag)
    fade_step = jnp.exp(-decay * 8.0)
    step_re = jnp.broadcast_to(fade_step * jnp.cos(angle * 8.0), power_re.shape)
    step_im = jnp.broadcast_to(fade_step * jnp.sin(angle * 8.0), power_re.shape)
    filt = filter_taps(
        res_re * power_re - res_im * power_im,
        res_re * power_im + res_im * power_re,
        step_re,
        step_im,
    )
    spectrum = lax.dot_general(
        jnp.asarray(matrix),
        filt,
        (((1,), (0,)), ((), ())),
        precision=lax.Precision.HIGHEST,
        preferred_element_type=f32,
    )
    res_re, res_im = res_re[:, 0], -res_im[:, 0]

    in_pieces = [piece.reshape(3, own, width) for piece in in_all.pieces()]
    in_all = jnp.concatenate(in_pieces, axis=1).reshape(3 * channels, width)
    mixed = []
    for r in range(2):
        table, first = tables[r]
        proj = nt(rows_first[r], in_all).reshape(narrow, local_rows, 3 * channels)
        gated, long_out, seen = mixer_forward(
            order, first, documents[r][0], proj, taps, table, spectrum, fwd, inv
        )
        mixed.append((proj, gated.reshape(slots, channels), long_out, seen))
    out_last = last
    out_all = jnp.concatenate(out_all.pieces(), axis=0)
    parts = [slice(0, even), slice(even, slots)]
    ready = [mixed[0][1], after([mixed[1][1]], upstream_stages[0])[0]]
    odds = [nn(ready[r][parts[1]], out_all).astype(bf16) for r in range(2)]
    cores = [swap(odd, "narrow", 1) for odd in odds]
    for at in range(steps - 1):
        last = ring_step([down_all, gate_all], last, odds)
    last_two = last
    for at in range(steps - 1):
        last_two = ring_step([up_all], last_two)
    ready = after([mixed[0][1], mixed[1][1]], upstream_stages[0])
    evens = [nn(ready[r][parts[0]], out_all).astype(bf16) for r in range(2)]
    mixer_out, stages = scatter_rows(
        evens[0], cores[0], evens[1], cores[1], upstream_stages[1] + last
    )
    middle = source + mixer_out
    rate_last = inverse_rms(middle)
    rows_upstream = jnp.concatenate(upstream_own + upstream_other, axis=0)
    low_second = (middle * rate_last * gain_last).astype(bf16)
    (second_own, second_other), second_stages = gather_rows(low_second, last_two + upstream_stages[2])
    rows_second = jnp.concatenate(second_own + second_other, axis=0)
    last = ring_step([down_all, gate_all, up_all], last_two + stages[1], second_stages[1])

    down_all, gate_all = [jnp.concatenate(w.pieces(), axis=0) for w in (down_all, gate_all)]
    up_all = jnp.concatenate(up_all.pieces(), axis=0)
    d_hidden = nt(down_all, rows_upstream)
    gate_pre = nt(gate_all, rows_second)
    up_pre = nt(up_all, rows_second)
    sig = jax.nn.sigmoid(gate_pre)
    silu = gate_pre * sig
    hidden = (silu * up_pre).astype(bf16)
    d_gate = (d_hidden * up_pre * sig * (1.0 + gate_pre * (1.0 - sig))).astype(bf16)
    d_up = (d_hidden * silu).astype(bf16)
    grad_down = product(hidden, rows_upstream, "nn", bf16)
    d_gate, d_up = after([d_gate, d_up], [grad_down])
    parts = [slice(p, p + even) for p in range(0, 2 * slots, even)]
    grads = [Scatter(jnp.split(grad_down, outer, axis=0))]

    def second_share(n):
        p = parts[n]
        return (tn(d_gate[:, p], gate_all) + tn(d_up[:, p], up_all)).astype(bf16)

    odds = [second_share(n) for n in (1, 3)]
    cores = [swap(odd, "narrow", 1) for odd in odds]
    evens = [second_share(0), second_share(2)]
    d_second, stages = scatter_rows(evens[0], cores[0], evens[1], cores[1])
    upstream = upstream_low.astype(f32)
    d_middle = upstream + norm_back(middle, rate_last, gain_last, d_second)
    (middle_own, middle_other), middle_stages = gather_rows(d_middle.astype(bf16))
    rows_dmiddle = [jnp.concatenate(middle_own, axis=0), jnp.concatenate(middle_other, axis=0)]
    [d_gate] = after([d_gate], cores + evens)
    grad_gate = product(d_gate, rows_second, "nn", bf16)
    [d_up] = after([d_up], stages[0] + [grad_gate])
    grad_up = product(d_up, rows_second, "nn", bf16)
    [hidden] = after([hidden], [grad_up])
    down_shares = [product(hidden, down_all, "tn", bf16, n) for n in (0, 1)]
    down_shares += [product(hidden, down_all, "tn", bf16, n) for n in (2, 3)]
    pair = [Scatter(jnp.split(grad, outer, axis=0)) for grad in (grad_gate, grad_up)]
    grads += pair
    last = ring_step(grads, (), middle_stages[0])
    down_shares = after(down_shares, middle_stages[1])
    down_cores = [swap(down_shares[n], "narrow", 1) for n in (1, 3)]
    down_out, down_stages = scatter_rows(
        down_shares[0], down_cores[0], down_shares[2], down_cores[1]
    )
    block_output = (middle + down_out).astype(bf16)
    grad_gain_two = jnp.sum(d_second * middle * rate_last, axis=0)

    grad_out = sum(tn(mixed[r][1], rows_dmiddle[r]) for r in range(2)).astype(bf16)
    halves = (slice(0, even), slice(even, slots))
    shares, d_rows, grad_gain_one, d_filter, d_taps = [None, None], [None, None], 0.0, 0.0, 0.0
    for r in range(2):
        proj, gated, long_out, seen = mixed[r]
        table, first = tables[r]
        d_gated = nt(rows_dmiddle[r], out_all).reshape(narrow, local_rows, channels)
        if r == 1:
            [d_gated] = after([d_gated], [grad_out, *shares[0], *down_stages[0]])
        dz, d_filter_row, d_taps_row = mixer_backward(
            order, first, documents[r][0], proj, d_gated, long_out, seen, taps, table,
            spectrum, fwd, inv,
        )
        d_rows[r] = dz.reshape(slots, 3 * channels)
        d_filter, d_taps = d_filter + d_filter_row, d_taps + d_taps_row
        if r == 0:
            shares[r] = [nn(d_rows[r][p], in_all).astype(bf16) for p in halves]
    [ready] = after([d_rows[1]], down_stages[1])
    odd = nn(ready[halves[1]], in_all).astype(bf16)
    cores = [swap(shares[0][1], "narrow", 1), swap(odd, "narrow", 1)]
    ready = after(d_rows, [odd])
    grad_in = sum(tn(ready[r], rows_first[r]) for r in range(2)).astype(bf16)
    for at in range(1, steps):
        last = ring_step(grads, last, [grad_in])
    [ready] = after([d_rows[1]], [grad_in] + cores)
    shares[1] = [nn(ready[halves[0]], in_all).astype(bf16), odd]
    d_normed, stages = scatter_rows(shares[0][0], cores[0], shares[1][0], cores[1])
    input_grad = (d_middle + norm_back(source, rate_first, gain_first, d_normed)).astype(bf16)
    for r in range(2):
        for n, share in enumerate(after(shares[r], [shares[1][0]])):
            rows = rows_first[r][n * even : (n + 1) * even]
            grad_gain_one = grad_gain_one + jnp.sum(share.astype(f32) * rows.astype(f32), axis=0)
    chunks = grad_in.reshape(3, outer, own, width)
    in_sum = Scatter([chunks[:, j].reshape(3 * own, width) for j in range(outer)])
    out_sum = Scatter(jnp.split(grad_out, outer, axis=0))
    last = ring_step([in_sum, out_sum], last, stages[0])
    d_filter, *_ = after([d_filter], last + stages[0])
    gain_grads = after([jnp.stack([grad_gain_one / gain_first, grad_gain_two])], stages[0])
    gain_share = reduce_gain(gain_grads[0], stages[1])

    sum_re, sum_im, mom_re, mom_im = filter_moments(d_filter, step_re, step_im)
    full_re = lag * sum_re + 8.0 * mom_re
    full_im = lag * sum_im + 8.0 * mom_im
    grad_re = jnp.sum(power_re * sum_re - power_im * sum_im, axis=1)
    grad_im = jnp.sum(power_re * sum_im + power_im * sum_re, axis=1)
    lag_re = jnp.sum(power_re * full_re - power_im * full_im, axis=1)
    lag_im = jnp.sum(power_re * full_im + power_im * full_re, axis=1)
    small_grad = jnp.concatenate(
        [
            d_taps[:3].reshape(9, channels),
            -(res_re * lag_re + res_im * lag_im),
            res_im * lag_re - res_re * lag_im,
            grad_re,
            grad_im,
        ],
        axis=0,
    ).astype(bf16)
    [small_grad] = after([small_grad], stages[1])
    small_share = scatter_small(jnp.split(small_grad, outer, axis=1))

    for at in range(1, steps):
        last = ring_step([in_sum, out_sum], last, [gain_share, small_share])

    at = 9 + poles
    return (
        block_output[None],
        input_grad[None],
        in_sum.total.reshape(3, own, width).transpose(0, 2, 1),
        out_sum.total,
        gain_share[0],
        small_share[:9].reshape(3, 3, own),
        small_share[9:at].T,
        small_share[at : at + poles].T,
        small_share[at + poles :].T,
        gain_share[1],
        grads[1].total.T,
        grads[2].total.T,
        grads[0].total.T,
    )


def solution(mesh):
    both = ("wide", "narrow")
    return jax.shard_map(
        body,
        mesh=mesh,
        in_specs=(
            P("wide", "narrow", None),
            P(None, None, both),
            P(both, None),
            P(both),
            P(None, None, both),
            P(both, None),
            P(both, None),
            P(both, None),
            P(both),
            P(None, both),
            P(None, both),
            P(None, both),
            P("wide", None),
            P("wide", None),
            P("wide", "narrow", None),
        ),
        out_specs=(
            P("wide", "narrow", None),
            P("wide", "narrow", None),
            P(None, None, both),
            P(both, None),
            P(both),
            P(None, None, both),
            P(both, None),
            P(both, None),
            P(both, None),
            P(both),
            P(None, both),
            P(None, both),
            P(None, both),
        ),
        check_vma=False,
    )
```

```python
from functools import partial

import jax
import jax.numpy as jnp
import numpy as np
from jax import lax
from jax.experimental import pallas as pl
from jax.experimental.pallas import tpu as pltpu
from jax.sharding import PartitionSpec as P

BLOCK = 128
LONGEST = 4
SPAN = LONGEST * BLOCK
FREQ = SPAN

epsilon = 1e-06
bf16 = jnp.bfloat16
f32 = jnp.float32


def transform():
    k = np.arange(FREQ)[:, None] * 2 + 1
    t = np.arange(SPAN)[None, :]
    turn = (k * t % (4 * SPAN)) * (2 * np.pi / (4 * SPAN))
    return np.concatenate([np.cos(turn), -np.sin(turn)], axis=0).astype(np.float32)


def nn(a, b):
    return lax.dot_general(a, b, (((1,), (0,)), ((), ())), preferred_element_type=f32)


def nt(a, b):
    return lax.dot_general(a, b, (((1,), (1,)), ((), ())), preferred_element_type=f32)


def tn(a, b):
    return lax.dot_general(a, b, (((0,), (0,)), ((), ())), preferred_element_type=f32)


def swap(values, axis, shift):
    size = lax.axis_size(axis)
    return lax.ppermute(values, axis, [(i, i ^ shift) for i in range(size)])


def after(values, tokens):
    if not tokens:
        return values
    joined = lax.optimization_barrier(tuple(values) + tuple(tokens))
    return list(joined[: len(values)])


def ring_of(size):
    return list(range(0, size, 2)) + list(range(size - 1, 0, -2))


def along(values, step):
    outer = lax.axis_size("wide") // 2
    ring = ring_of(outer)
    pairs = [
        (ring[p] * 2 + side, ring[(p + step) % outer] * 2 + side)
        for p in range(outer)
        for side in range(2)
    ]
    return lax.ppermute(values, "wide", pairs)


def ring_offsets(outer):
    near = [sign * h for h in range(1, outer // 2) for sign in (-1, 1)]
    return [0] + near + [outer // 2]


def cut_of(rows):
    cut = (rows // 2 + 15) // 16 * 16
    return cut if cut < rows else rows // 2


def two_parts(values, axis):
    cut = cut_of(values.shape[axis])
    return (
        lax.slice_in_dim(values, 0, cut, axis=axis),
        lax.slice_in_dim(values, cut, values.shape[axis], axis=axis),
    )


class Gather:
    def __init__(self, own):
        self.most = lax.axis_size("wide") // 4 - 1
        self.before, self.behind, self.opposite = [own], [own], []

    def sends(self):
        if len(self.before) <= self.most:
            return self.before[-1], self.behind[-1]
        return two_parts(self.before[-1], 0)[0], two_parts(self.behind[-1], 0)[1]

    def take(self, got, back):
        if len(self.before) <= self.most:
            self.before.append(got)
            self.behind.append(back)
        else:
            self.opposite = [got, back]

    def pieces(self):
        near = [piece for pair in zip(self.before[1:], self.behind[1:]) for piece in pair]
        return [self.before[0]] + near + [jnp.concatenate(self.opposite, axis=0)]


class Scatter:
    def __init__(self, chunks):
        self.left = len(chunks) // 2 - 1
        self.wire = chunks[0].dtype
        self.total = chunks[0].astype(f32)
        self.behind = [chunk.astype(f32) for chunk in chunks[1:-1:2]]
        self.ahead = [chunk.astype(f32) for chunk in chunks[2:-1:2]]
        self.last = chunks[-1]

    def sends(self):
        if self.last is not None:
            return two_parts(self.last, 0)
        h = self.left - 1
        return self.ahead[h].astype(self.wire), self.behind[h].astype(self.wire)

    def take(self, got, back):
        got, back = got.astype(f32), back.astype(f32)
        h = self.left - 1
        if self.last is not None:
            top, bottom = two_parts(self.ahead[h], 0)
            self.ahead[h] = jnp.concatenate([top + got, bottom], axis=0)
            top, bottom = two_parts(self.behind[h], 0)
            self.behind[h] = jnp.concatenate([top, bottom + back], axis=0)
            self.last = None
            return
        self.left = h
        if h:
            self.ahead[h - 1] = self.ahead[h - 1] + got
            self.behind[h - 1] = self.behind[h - 1] + back
        else:
            self.total = self.total + got + back


def ring_step(items, tokens=(), arrive=()):
    sends = [item.sends() for item in items]
    ways = [one[0] if len(one) == 1 else jnp.concatenate(one, axis=0) for one in zip(*sends)]
    ways = after(ways, list(tokens)) if tokens else lax.optimization_barrier(tuple(ways))
    got, back = after([along(ways[0], 1), along(ways[1], -1)], list(arrive))
    at = [0, 0]
    for item, (ahead, behind) in zip(items, sends):
        ends = [at[0] + ahead.shape[0], at[1] + behind.shape[0]]
        item.take(got[at[0] : ends[0]], back[at[1] : ends[1]])
        at = ends
    return [got, back]


def gather_small(own):
    outer = lax.axis_size("wide") // 2
    return [own] + [along(own, -offset) for offset in ring_offsets(outer)[1:]]


def scatter_small(chunks):
    offsets = ring_offsets(len(chunks))
    total = chunks[0].astype(f32)
    for chunk, offset in zip(chunks[1:], offsets[1:]):
        total = total + along(chunk, offset).astype(f32)
    return total


def gather_rows(own, tokens=(), later=(), single=False):
    size = lax.axis_size("narrow")
    half = own.shape[0] // 2
    [own] = after([own], tokens)
    across = [swap(own, "narrow", k) for k in range(2, size, 2)]
    beside = swap(own, "wide", 1)
    stage_one = across + [beside]
    if later:
        *across, beside = after(across + [beside], later)
    parts, stage_two = [beside], []
    for n, k in enumerate(range(2, size, 2)):
        ends = [swap(across[n][:half], "wide", 1), swap(beside[half:], "narrow", k)]
        parts += ends
        stage_two += ends
    even = jnp.concatenate([own] + across, axis=0)
    other_even = jnp.concatenate(parts, axis=0)
    odd = swap(even, "narrow", 1)
    if single:
        [other_even] = after([other_even], [odd])
    other_odd = swap(other_even, "narrow", 1)
    return ([even, odd], [other_even, other_odd]), (stage_one, stage_two, [odd, other_odd])


def scatter_rows(even, odd, other_even, other_odd, tokens=(), later=()):
    size = lax.axis_size("narrow")
    rows = even.shape[0] // (size // 2)
    half = rows // 2
    other = other_even.astype(f32) + other_odd.astype(f32)
    mine = even.astype(f32) + odd.astype(f32)
    beside_top, beside_bottom = other[:half], other[half:rows]
    out = mine[:rows]
    corners = other[rows:].astype(bf16)
    [corners] = after([corners], tokens)
    spread, stage_two, stage_three = [], [], []
    for n, k in enumerate(range(2, size, 2)):
        at = n * rows
        ends = [
            swap(corners[at : at + half], "wide", 1),
            swap(corners[at + half : at + rows], "narrow", k),
        ]
        stage_two += ends
        beside_bottom = beside_bottom + ends[1].astype(f32)
        at = at + rows
        spread.append(
            jnp.concatenate(
                [mine[at : at + half] + ends[0].astype(f32), mine[at + half : at + rows]], axis=0
            ).astype(bf16)
        )
    spread.append(jnp.concatenate([beside_top, beside_bottom], axis=0).astype(bf16))
    spread = after(spread, later) if later else lax.optimization_barrier(tuple(spread))
    for n, k in enumerate(range(2, size, 2)):
        stage_three.append(swap(spread[n], "narrow", k))
        out = out + stage_three[-1].astype(f32)
    stage_three.append(swap(spread[-1], "wide", 1))
    return out + stage_three[-1].astype(f32), (stage_two, stage_three)


def inverse_rms(values):
    return lax.rsqrt(jnp.mean(values * values, axis=-1, keepdims=True) + epsilon)


def norm_kernel(*refs):
    pieces, gain, out = refs[:-2], refs[-2], refs[-1]
    rows = pieces[0].shape[0]
    step = 32 if rows % 32 == 0 else rows
    for n, piece in enumerate(pieces):

        def part(b, _):
            at = pl.multiple_of(b * step, step)
            values = piece[pl.ds(at, step), :].astype(f32)
            rate = lax.rsqrt(jnp.mean(values * values, axis=-1, keepdims=True) + epsilon)
            to = pl.multiple_of(n * rows + at, step)
            out[pl.ds(to, step), :] = (values * rate * gain[...]).astype(bf16)
            return 0

        lax.fori_loop(0, rows // step, part, 0)


def normed_rows(pieces, gain):
    rows, width = pieces[0].shape
    return pl.pallas_call(
        norm_kernel,
        out_shape=jax.ShapeDtypeStruct((rows * len(pieces), width), bf16),
        cost_estimate=light,
        name="norm",
    )(*pieces, gain.reshape(1, width))


def norm_back(values, rate, gain, grad):
    a = grad * gain
    inner = jnp.mean(a * values, axis=-1, keepdims=True)
    return rate * a - values * (rate * rate * rate) * inner


light = pl.CostEstimate(flops=1024, bytes_accessed=1024, transcendentals=0)


def filter_kernel(base_re, base_im, step_re, step_im, out):
    poles = base_re.shape[0]
    width = out.shape[1]
    for g in range(width // 128 if width % 128 == 0 else 1):
        lanes = pl.ds(g * 128, min(128, width))
        start = tuple(base_re[j, :, lanes] for j in range(poles)) + tuple(
            base_im[j, :, lanes] for j in range(poles)
        )

        def step(b, state):
            total = state[0]
            for j in range(1, poles):
                total = total + state[j]
            out[pl.ds(pl.multiple_of(b * 8, 8), 8), lanes] = total
            new_re, new_im = [], []
            for j in range(poles):
                sr = step_re[j, :, lanes]
                si = step_im[j, :, lanes]
                new_re.append(state[j] * sr - state[poles + j] * si)
                new_im.append(state[j] * si + state[poles + j] * sr)
            return tuple(new_re) + tuple(new_im)

        lax.fori_loop(0, SPAN // 8, step, start)


def filter_taps(base_re, base_im, step_re, step_im):
    width = base_re.shape[2]
    return pl.pallas_call(
        filter_kernel,
        out_shape=jax.ShapeDtypeStruct((SPAN, width), f32),
        cost_estimate=light,
        name="taps",
    )(base_re, base_im, step_re, step_im)


def moment_kernel(grad, step_re, step_im, sum_re, sum_im, mom_re, mom_im):
    poles = step_re.shape[0]
    width = grad.shape[1]
    per = 8
    for g in range(width // 128 if width % 128 == 0 else 1):
        lanes = pl.ds(g * 128, min(128, width))
        for j0 in range(0, poles, per):
            zero = jnp.zeros((8, min(128, width)), f32)

            def step(i, state):
                b = SPAN // 8 - 1 - i
                value = grad[pl.ds(pl.multiple_of(b * 8, 8), 8), lanes]
                new = []
                for n in range(per):
                    sr = step_re[j0 + n, :, lanes]
                    si = step_im[j0 + n, :, lanes]
                    pr, pi, qr, qi = state[4 * n : 4 * n + 4]
                    ur, ui = pr + qr, pi + qi
                    new += [
                        pr * sr - pi * si + value,
                        pr * si + pi * sr,
                        ur * sr - ui * si,
                        ur * si + ui * sr,
                    ]
                return tuple(new)

            state = lax.fori_loop(0, SPAN // 8, step, (zero,) * (4 * per))
            for n in range(per):
                sum_re[j0 + n, :, lanes] = state[4 * n]
                sum_im[j0 + n, :, lanes] = state[4 * n + 1]
                mom_re[j0 + n, :, lanes] = state[4 * n + 2]
                mom_im[j0 + n, :, lanes] = state[4 * n + 3]


SIDE = 512


def product_kernel(a, b, out, turned=None, *, kind):
    if kind == "tn":

        @pl.when(pl.program_id(0) == 0)
        def _():
            turned[...] = a[...].T

        value = nn(turned[...], b[...])
    else:
        value = (nn if kind == "nn" else nt)(a[...], b[...])
    out[...] = value.astype(out.dtype)


def product(a, b, kind, dtype, at=None):
    if kind == "tn":
        depth, rows = a.shape[0], SIDE
        a_spec = pl.BlockSpec((depth, SIDE), lambda i: (0, at))
        scratch = [pltpu.VMEM((SIDE, depth), a.dtype)]
    else:
        rows, depth = a.shape if at is None else (SIDE, a.shape[1])
        a_spec = pl.BlockSpec((rows, depth), lambda i: (at or 0, 0))
        scratch = []
    columns = b.shape[0] if kind == "nt" else b.shape[1]
    side = max(s for s in (512, 384, 256, 128, columns) if columns % s == 0 and s <= 512)
    if kind == "nt":
        b_spec = pl.BlockSpec((side, depth), lambda i: (i, 0))
    else:
        b_spec = pl.BlockSpec((depth, side), lambda i: (0, i))
    return pl.pallas_call(
        partial(product_kernel, kind=kind),
        grid=(columns // side,),
        out_shape=jax.ShapeDtypeStruct((rows, columns), dtype),
        in_specs=[a_spec, b_spec],
        out_specs=pl.BlockSpec((rows, side), lambda i: (0, i)),
        scratch_shapes=scratch,
        cost_estimate=light,
        name="product",
    )(a, b)


def filter_moments(grad, step_re, step_im):
    poles, _, width = step_re.shape
    shape = jax.ShapeDtypeStruct((poles, 8, width), f32)
    return pl.pallas_call(
        moment_kernel,
        out_shape=(shape,) * 4,
        cost_estimate=light,
        name="moments",
    )(grad, step_re, step_im)


LIVE, KEEP_ONE, KEEP_TWO = 0, 1, 2


def load_masked(order, proj, table, m_scr):
    pieces, rows, _ = proj.shape
    m_scr[0:8, :] = jnp.zeros_like(m_scr[0:8, :])

    def piece(b, _):
        p = order[b]
        at = pl.multiple_of(b * rows, rows)
        live = table[pl.ds(at, rows), LIVE : LIVE + 1]
        m_scr[pl.ds(pl.multiple_of(at + 8, 8), rows), :] = proj[p] * live
        return 0

    lax.fori_loop(0, pieces, piece, 0)


def short_block(m_scr, taps, table, at):
    window = m_scr[pl.ds(at, BLOCK + 8), :]
    one = table[pl.ds(at, BLOCK), KEEP_ONE : KEEP_ONE + 1]
    two = table[pl.ds(at, BLOCK), KEEP_TWO : KEEP_TWO + 1]
    here = window[8:]
    once = window[7 : BLOCK + 7] * one
    twice = window[6 : BLOCK + 6] * two
    short = taps[0:1, :] * here + taps[1:2, :] * once + taps[2:3, :] * twice
    return short, here, once, twice


def pack_document(source, packed, first, count):
    blocks = source.shape[0] // BLOCK
    for kb in range(LONGEST):
        at = pl.multiple_of(jnp.minimum(first + kb, blocks - 1) * BLOCK, BLOCK)
        inside = (kb < count).astype(f32)
        packed[kb * BLOCK : (kb + 1) * BLOCK, :] = (source[pl.ds(at, BLOCK), :] * inside).astype(bf16)


def place_document(result, target, first, count):
    for kb in range(LONGEST):

        @pl.when(kb < count)
        def _():
            at = pl.multiple_of((first + kb) * BLOCK, BLOCK)
            target[pl.ds(at, BLOCK), :] = result[kb * BLOCK : (kb + 1) * BLOCK, :]


def forward_kernel(
    order, first, count, proj, taps, table, spectrum, fwd, inv, gated, long_out, seen, m_scr, u_scr, q_scr, packed
):
    width = long_out.shape[1]
    pieces, rows, _ = proj.shape
    blocks = long_out.shape[0] // BLOCK
    load_masked(order, proj, table, m_scr)

    def block(n, _):
        at = pl.multiple_of(n * BLOCK, BLOCK)
        short, _, _, _ = short_block(m_scr, taps, table, at)
        q_scr[pl.ds(at, BLOCK), :] = short[:, :width]
        u_scr[pl.ds(at, BLOCK), :] = short[:, width : 2 * width] * short[:, 2 * width :]
        return 0

    lax.fori_loop(0, blocks, block, 0)

    def document(d, _):
        pack_document(u_scr, packed, first[d], count[d])
        both = jnp.dot(fwd[...], packed[...], preferred_element_type=f32)
        seen[d] = both.astype(bf16)
        re, im = both[:FREQ], both[FREQ:]
        hr, hi = spectrum[:FREQ], spectrum[FREQ:]
        answer = jnp.concatenate([re * hr - im * hi, re * hi + im * hr], axis=0).astype(bf16)
        result = jnp.dot(inv[...], answer, preferred_element_type=f32)
        place_document(result, long_out, first[d], count[d])
        return 0

    lax.fori_loop(0, seen.shape[0], document, 0)

    def piece(b, _):
        at = pl.multiple_of(b * rows, rows)
        gated[order[b]] = (q_scr[pl.ds(at, rows), :] * long_out[pl.ds(at, rows), :]).astype(bf16)
        return 0

    lax.fori_loop(0, pieces, piece, 0)


def backward_kernel(
    order, first, count, proj, d_gated, long_out, seen, taps, table, spectrum, fwd, inv,
    dz, d_filter, d_taps, m_scr, dy_scr, k_scr, v_scr, ds_scr, packed, d_spec,
):
    width = long_out.shape[1]
    pieces, rows, _ = proj.shape
    slots = long_out.shape[0]
    blocks = slots // BLOCK
    per_piece = rows // BLOCK
    load_masked(order, proj, table, m_scr)
    ds_scr[slots : slots + 8, :] = jnp.zeros_like(ds_scr[slots : slots + 8, :])

    def block(n, _):
        at = pl.multiple_of(n * BLOCK, BLOCK)
        short, _, _, _ = short_block(m_scr, taps, table, at)
        within = pl.multiple_of((n % per_piece) * BLOCK, BLOCK)
        dg = d_gated[order[n // per_piece], pl.ds(within, BLOCK), :]
        dy_scr[pl.ds(at, BLOCK), :] = dg * short[:, :width]
        ds_scr[pl.ds(at, BLOCK), :width] = dg * long_out[pl.ds(at, BLOCK), :]
        k_scr[pl.ds(at, BLOCK), :] = short[:, width : 2 * width]
        v_scr[pl.ds(at, BLOCK), :] = short[:, 2 * width :]
        return 0

    lax.fori_loop(0, blocks, block, 0)
    d_spec[...] = jnp.zeros_like(d_spec)

    def document(d, _):
        pack_document(dy_scr, packed, first[d], count[d])
        both = jnp.dot(fwd[...], packed[...], preferred_element_type=f32)
        re, im = both[:FREQ], both[FREQ:]
        hr, hi = spectrum[:FREQ], spectrum[FREQ:]
        answer = jnp.concatenate([re * hr + im * hi, im * hr - re * hi], axis=0).astype(bf16)
        result = jnp.dot(inv[...], answer, preferred_element_type=f32)
        ur, ui = seen[d, :FREQ].astype(f32), seen[d, FREQ:].astype(f32)
        d_spec[:FREQ] += re * ur + im * ui
        d_spec[FREQ:] += im * ur - re * ui
        for kb in range(LONGEST):

            @pl.when(kb < count[d])
            def _():
                at = pl.multiple_of((first[d] + kb) * BLOCK, BLOCK)
                du = result[kb * BLOCK : (kb + 1) * BLOCK, :]
                ds_scr[pl.ds(at, BLOCK), width : 2 * width] = du * v_scr[pl.ds(at, BLOCK), :]
                ds_scr[pl.ds(at, BLOCK), 2 * width :] = du * k_scr[pl.ds(at, BLOCK), :]

        return 0

    lax.fori_loop(0, seen.shape[0], document, 0)
    d_filter[...] = jnp.dot(inv[...], d_spec[...].astype(bf16), preferred_element_type=f32)
    d_taps[...] = jnp.zeros_like(d_taps)

    def back(n, _):
        at = pl.multiple_of(n * BLOCK, BLOCK)
        window = m_scr[pl.ds(at, BLOCK + 8), :]
        ahead = ds_scr[pl.ds(at, BLOCK + 8), :]
        one = table[pl.ds(at, BLOCK + 8), KEEP_ONE : KEEP_ONE + 1]
        two = table[pl.ds(at, BLOCK + 8), KEEP_TWO : KEEP_TWO + 1]
        live = table[pl.ds(at, BLOCK), LIVE : LIVE + 1]
        ds = ahead[:BLOCK]
        ahead_one = ahead * one
        ahead_two = ahead * two
        dm = (
            taps[0:1, :] * ds
            + taps[1:2, :] * ahead_one[1 : BLOCK + 1]
            + taps[2:3, :] * ahead_two[2 : BLOCK + 2]
        )
        d_taps[0:1, :] += jnp.sum(window[8:] * ds, axis=0, keepdims=True)
        d_taps[1:2, :] += jnp.sum(window[7 : BLOCK + 7] * ahead_one[:BLOCK], axis=0, keepdims=True)
        d_taps[2:3, :] += jnp.sum(window[6 : BLOCK + 6] * ahead_two[:BLOCK], axis=0, keepdims=True)
        within = pl.multiple_of((n % per_piece) * BLOCK, BLOCK)
        dz[order[n // per_piece], pl.ds(within, BLOCK), :] = (dm * live).astype(bf16)
        return 0

    lax.fori_loop(0, blocks, back, 0)


smem = pl.BlockSpec(memory_space=pltpu.SMEM)
vmem = pl.BlockSpec(memory_space=pltpu.VMEM)


def mixer_forward(order, first, count, proj, taps, table, spectrum, fwd, inv):
    pieces, rows, three = proj.shape
    width = three // 3
    slots = pieces * rows
    docs = first.shape[0]
    return pl.pallas_call(
        forward_kernel,
        out_shape=(
            jax.ShapeDtypeStruct((pieces, rows, width), bf16),
            jax.ShapeDtypeStruct((slots, width), f32),
            jax.ShapeDtypeStruct((docs, 2 * FREQ, width), bf16),
        ),
        in_specs=[smem] * 3 + [vmem] * 6,
        out_specs=(vmem,) * 3,
        scratch_shapes=[
            pltpu.VMEM((slots + 8, three), f32),
            pltpu.VMEM((slots, width), f32),
            pltpu.VMEM((slots, width), f32),
            pltpu.VMEM((SPAN, width), bf16),
        ],
        compiler_params=pltpu.CompilerParams(vmem_limit_bytes=40 * 2**20),
        cost_estimate=light,
        name="mixer_forward",
    )(order, first, count, proj, taps, table, spectrum, fwd, inv)


def mixer_backward(order, first, count, proj, d_gated, long_out, seen, taps, table, spectrum, fwd, inv):
    pieces, rows, three = proj.shape
    width = three // 3
    slots = pieces * rows
    docs = first.shape[0]
    return pl.pallas_call(
        backward_kernel,
        out_shape=(
            jax.ShapeDtypeStruct((pieces, rows, three), bf16),
            jax.ShapeDtypeStruct((SPAN, width), f32),
            jax.ShapeDtypeStruct((8, three), f32),
        ),
        in_specs=[smem] * 3 + [vmem] * 9,
        out_specs=(vmem,) * 3,
        scratch_shapes=[
            pltpu.VMEM((slots + 8, three), f32),
            pltpu.VMEM((slots, width), f32),
            pltpu.VMEM((slots, width), f32),
            pltpu.VMEM((slots, width), f32),
            pltpu.VMEM((slots + 8, three), f32),
            pltpu.VMEM((SPAN, width), bf16),
            pltpu.VMEM((2 * FREQ, width), f32),
        ],
        compiler_params=pltpu.CompilerParams(vmem_limit_bytes=48 * 2**20),
        cost_estimate=light,
        name="mixer_backward",
    )(order, first, count, proj, d_gated, long_out, seen, taps, table, spectrum, fwd, inv)


def layout(doc_blocks, doc_pad, slots):
    block_ends = jnp.cumsum(doc_blocks) * BLOCK
    starts = block_ends - doc_blocks * BLOCK
    places = jnp.arange(slots, dtype=jnp.int32)
    living = (places[None, :] >= starts[:, None]) & (
        places[None, :] < (block_ends - doc_pad)[:, None]
    )
    live = jnp.sum(living.astype(f32), axis=0)
    opening = jnp.sum((places[None, :] == starts[:, None]).astype(f32), axis=0)
    one = 1.0 - opening
    one = one * (places > 0)
    two = one * jnp.concatenate([jnp.zeros((1,), f32), one[:-1]])
    table = jnp.stack([live, one, two], axis=1)
    table = jnp.concatenate([table, jnp.zeros((8, 3), f32)], axis=0)
    return table, starts // BLOCK


def picked(index, count, values):
    hot = index[:, None] == jnp.arange(count)[None, :]
    shape = hot.shape + (1,) * (values.ndim - 1)
    return jnp.sum(jnp.where(hot.reshape(shape), values[None], 0), axis=1)


def body(
    tokens, w_in, w_out, gain_one, short_kernel, decay_rate, pole_angle, residue,
    gain_two, w_gate, w_up, w_down, doc_blocks, doc_pad, cotangent,
):
    wide, narrow = lax.axis_size("wide"), lax.axis_size("narrow")
    wide_at, narrow_at = lax.axis_index("wide"), lax.axis_index("narrow")
    outer = wide // 2
    _, local_rows, width = tokens.shape
    slots = local_rows * narrow
    even = slots // 2
    source = tokens[0].astype(f32)
    upstream_low = cotangent[0]
    poles = decay_rate.shape[1]
    own = w_in.shape[2]
    channels = own * outer
    hidden_units = w_gate.shape[1] * outer

    ring = np.array(ring_of(outer))
    ring_place = np.argsort(ring)
    tour = picked((wide_at // 2)[None], outer, jnp.asarray(ring_place, jnp.int32))[0]
    piece_places = (tour + jnp.asarray(ring_offsets(outer), jnp.int32)) % outer
    piece_outer = picked(piece_places, outer, jnp.asarray(ring, jnp.int32))
    sides = jnp.arange(2) ^ (wide_at % 2)
    offsets = list(range(0, narrow, 2)) + list(range(1, narrow, 2))
    place_of = np.argsort(np.array(offsets))
    order = picked(jnp.arange(narrow) ^ narrow_at, narrow, jnp.asarray(place_of, jnp.int32))
    narrow_of = jnp.asarray(offsets, jnp.int32) ^ narrow_at

    small = jnp.concatenate(
        [
            short_kernel.reshape(9, own),
            decay_rate.T,
            pole_angle.T,
            residue.T,
            gain_one[None],
            gain_two[None],
        ],
        axis=0,
    )
    small_pieces = gather_small(small)
    small_all = jnp.concatenate(small_pieces, axis=1)
    (first_own, first_other), first_stages = gather_rows(tokens[0], small_pieces[1:])
    gains = small_all[small.shape[0] - 2 :].reshape(2, outer, own)
    gains = jnp.stack([gains, swap(gains, "wide", 1)])
    gains = jnp.stack([gains] + [swap(gains, "narrow", k) for k in range(2, narrow, 2)])
    gains = jnp.concatenate([gains, swap(gains, "narrow", 1)], axis=0).astype(f32)
    gains = picked(order, narrow, gains).transpose(1, 3, 0, 2, 4)
    gains = picked(sides, 2, gains).transpose(1, 0, 2, 3, 4)
    hot = piece_outer[None, :] == jnp.arange(outer)[:, None]
    gains = jnp.sum(jnp.where(hot[:, :, None, None, None, None], gains[None], 0), axis=1)
    gain_all = gains.transpose(3, 0, 1, 2, 4).reshape(2, width)
    gain_first, gain_last = gain_all[0], gain_all[1]

    def place_gain(values):
        values = values.reshape(2, outer, 2, narrow, own).transpose(1, 2, 3, 0, 4)
        values = picked(piece_outer, outer, values).transpose(1, 0, 2, 3, 4)
        values = picked(sides, 2, values).transpose(2, 0, 1, 3, 4)
        values = picked(narrow_of, narrow, values)
        total = values[: narrow // 2] + swap(values[narrow // 2 :], "narrow", 1)
        summed = total[0]
        for k in range(1, narrow // 2):
            summed = summed + swap(total[k], "narrow", 2 * k)
        summed = summed[0] + swap(summed[1], "wide", 1)
        return summed

    documents = jnp.concatenate([doc_blocks, doc_pad], axis=0)
    [documents] = after([documents], small_pieces[1:])
    documents = (documents, swap(documents, "wide", 1))
    tables = [layout(rules[0], rules[1], slots) for rules in documents]

    shards = [w_in.transpose(0, 2, 1).reshape(3 * own, width), w_out, w_down.T, w_gate.T, w_up.T]
    weights = [Gather(shard) for shard in shards]
    in_all, out_all, down_all, gate_all, up_all = weights
    steps = outer // 2
    last = []
    for at in range(steps):
        last = ring_step([in_all, out_all], last)

    def normed(pieces):
        values = jnp.concatenate(pieces, axis=0).astype(f32)
        return (values * inverse_rms(values) * gain_first).astype(bf16)

    rows_first = lax.optimization_barrier([normed(first_own), normed(first_other)])
    rate_first = inverse_rms(source)
    (upstream_own, upstream_other), upstream_stages = gather_rows(
        upstream_low, first_stages[2], (), True
    )

    matrix = transform()
    fwd = jnp.asarray(matrix, bf16)
    inv = jnp.asarray(matrix.T / SPAN, bf16)

    block = small_all.astype(f32)
    taps = block[:9].reshape(3, 3 * channels)
    taps = jnp.concatenate([taps, jnp.zeros((5, 3 * channels), f32)], axis=0)
    decay = block[9 : 9 + poles][:, None, :]
    angle = block[9 + poles : 9 + 2 * poles][:, None, :]
    res_re = block[9 + 2 * poles : 9 + 3 * poles][:, None, :]
    res_im = -block[9 + 3 * poles : 9 + 4 * poles][:, None, :]
    lag = jnp.arange(8, dtype=f32)[None, :, None]
    fade = jnp.exp(-decay * lag)
    power_re, power_im = fade * jnp.cos(angle * lag), fade * jnp.sin(angle * lag)
    fade_step = jnp.exp(-decay * 8.0)
    step_re = jnp.broadcast_to(fade_step * jnp.cos(angle * 8.0), power_re.shape)
    step_im = jnp.broadcast_to(fade_step * jnp.sin(angle * 8.0), power_re.shape)
    filt = filter_taps(
        res_re * power_re - res_im * power_im,
        res_re * power_im + res_im * power_re,
        step_re,
        step_im,
    )
    spectrum = lax.dot_general(
        jnp.asarray(matrix),
        filt,
        (((1,), (0,)), ((), ())),
        precision=lax.Precision.HIGHEST,
        preferred_element_type=f32,
    )
    res_re, res_im = res_re[:, 0], -res_im[:, 0]

    in_pieces = [piece.reshape(3, own, width) for piece in in_all.pieces()]
    in_all = jnp.concatenate(in_pieces, axis=1).reshape(3 * channels, width)
    mixed = []
    for r in range(2):
        table, first = tables[r]
        proj = nt(rows_first[r], in_all).reshape(narrow, local_rows, 3 * channels)
        gated, long_out, seen = mixer_forward(
            order, first, documents[r][0], proj, taps, table, spectrum, fwd, inv
        )
        mixed.append((proj, gated.reshape(slots, channels), long_out, seen))
    out_last = last
    out_all = jnp.concatenate(out_all.pieces(), axis=0)
    parts = [slice(0, even), slice(even, slots)]
    ready = [mixed[0][1], after([mixed[1][1]], upstream_stages[0])[0]]
    odds = [nn(ready[r][parts[1]], out_all).astype(bf16) for r in range(2)]
    cores = [swap(odd, "narrow", 1) for odd in odds]
    for at in range(steps - 1):
        last = ring_step([down_all, gate_all], last, odds)
    last_two = last
    for at in range(steps - 1):
        last_two = ring_step([up_all] if at else [down_all, up_all], last_two)
    ready = after([mixed[0][1], mixed[1][1]], upstream_stages[0])
    evens = [nn(ready[r][parts[0]], out_all).astype(bf16) for r in range(2)]
    mixer_out, stages = scatter_rows(
        evens[0], cores[0], evens[1], cores[1], upstream_stages[1] + last
    )
    middle = source + mixer_out
    rate_last = inverse_rms(middle)
    rows_upstream = jnp.concatenate(upstream_own + upstream_other, axis=0)
    low_second = (middle * rate_last * gain_last).astype(bf16)
    (second_own, second_other), second_stages = gather_rows(low_second, last_two + upstream_stages[2])
    rows_second = jnp.concatenate(second_own + second_other, axis=0)
    last = ring_step([gate_all, up_all], last_two, second_stages[1])

    down_all, gate_all = [jnp.concatenate(w.pieces(), axis=0) for w in (down_all, gate_all)]
    up_all = jnp.concatenate(up_all.pieces(), axis=0)
    d_hidden = nt(down_all, rows_upstream)
    gate_pre = nt(gate_all, rows_second)
    up_pre = nt(up_all, rows_second)
    sig = jax.nn.sigmoid(gate_pre)
    silu = gate_pre * sig
    hidden = (silu * up_pre).astype(bf16)
    d_gate = (d_hidden * up_pre * sig * (1.0 + gate_pre * (1.0 - sig))).astype(bf16)
    d_up = (d_hidden * silu).astype(bf16)
    parts = [slice(p, p + even) for p in range(0, 2 * slots, even)]
    def second_share(n):
        p = parts[n]
        return (tn(d_gate[:, p], gate_all) + tn(d_up[:, p], up_all)).astype(bf16)

    odds = [second_share(n) for n in (1, 3)]
    cores = [swap(odd, "narrow", 1) for odd in odds]
    evens = [second_share(0), second_share(2)]
    d_second, stages = scatter_rows(evens[0], cores[0], evens[1], cores[1])
    upstream = upstream_low.astype(f32)
    d_middle = upstream + norm_back(middle, rate_last, gain_last, d_second)
    (middle_own, middle_other), middle_stages = gather_rows(d_middle.astype(bf16))
    rows_dmiddle = [jnp.concatenate(middle_own, axis=0), jnp.concatenate(middle_other, axis=0)]
    [hidden] = after([hidden], cores + evens)
    grad_down = product(hidden, rows_upstream, "nn", bf16)
    grads = [Scatter(jnp.split(grad_down, outer, axis=0))]
    [d_gate] = after([d_gate], stages[0])
    grad_gate = product(d_gate, rows_second, "nn", bf16)
    [d_up] = after([d_up], [grad_gate])
    grad_up = product(d_up, rows_second, "nn", bf16)
    [hidden] = after([hidden], [grad_up])
    down_shares = [product(hidden, down_all, "tn", bf16, n) for n in (0, 1)]
    down_shares += [product(hidden, down_all, "tn", bf16, n) for n in (2, 3)]
    pair = [Scatter(jnp.split(grad, outer, axis=0)) for grad in (grad_gate, grad_up)]
    grads += pair
    last = ring_step(grads, (), middle_stages[0])
    down_shares = after(down_shares, middle_stages[1])
    down_cores = [swap(down_shares[n], "narrow", 1) for n in (1, 3)]
    down_out, down_stages = scatter_rows(
        down_shares[0], down_cores[0], down_shares[2], down_cores[1]
    )
    block_output = (middle + down_out).astype(bf16)
    grad_gain_two = jnp.sum(d_second * middle * rate_last, axis=0)

    grad_out = sum(tn(mixed[r][1], rows_dmiddle[r]) for r in range(2)).astype(bf16)
    halves = (slice(0, even), slice(even, slots))
    shares, d_rows, grad_gain_one, d_filter, d_taps = [None, None], [None, None], 0.0, 0.0, 0.0
    for r in range(2):
        proj, gated, long_out, seen = mixed[r]
        table, first = tables[r]
        d_gated = nt(rows_dmiddle[r], out_all).reshape(narrow, local_rows, channels)
        if r == 1:
            [d_gated] = after([d_gated], [grad_out, *shares[0], *down_stages[0]])
        dz, d_filter_row, d_taps_row = mixer_backward(
            order, first, documents[r][0], proj, d_gated, long_out, seen, taps, table,
            spectrum, fwd, inv,
        )
        d_rows[r] = dz.reshape(slots, 3 * channels)
        d_filter, d_taps = d_filter + d_filter_row, d_taps + d_taps_row
        if r == 0:
            shares[r] = [nn(d_rows[r][p], in_all).astype(bf16) for p in halves]
    [ready] = after([d_rows[1]], down_stages[1])
    odd = nn(ready[halves[1]], in_all).astype(bf16)
    cores = [swap(shares[0][1], "narrow", 1), swap(odd, "narrow", 1)]
    ready = after(d_rows, [odd])
    grad_in = sum(tn(ready[r], rows_first[r]) for r in range(2)).astype(bf16)
    for at in range(1, steps):
        last = ring_step(grads, last, [grad_in])
    [ready] = after([d_rows[1]], [grad_in] + cores)
    shares[1] = [nn(ready[halves[0]], in_all).astype(bf16), odd]
    d_normed, stages = scatter_rows(shares[0][0], cores[0], shares[1][0], cores[1])
    input_grad = (d_middle + norm_back(source, rate_first, gain_first, d_normed)).astype(bf16)
    for r in range(2):
        for n, share in enumerate(after(shares[r], [shares[1][0]])):
            rows = rows_first[r][n * even : (n + 1) * even]
            grad_gain_one = grad_gain_one + jnp.sum(share.astype(f32) * rows.astype(f32), axis=0)
    chunks = grad_in.reshape(3, outer, own, width)
    in_sum = Scatter([chunks[:, j].reshape(3 * own, width) for j in range(outer)])
    out_sum = Scatter(jnp.split(grad_out, outer, axis=0))
    d_filter, *_ = after([d_filter], last + [grad_in])
    gain_grads = jnp.stack([grad_gain_one / gain_first, grad_gain_two])
    sum_re, sum_im, mom_re, mom_im = filter_moments(d_filter, step_re, step_im)
    full_re = lag * sum_re + 8.0 * mom_re
    full_im = lag * sum_im + 8.0 * mom_im
    grad_re = jnp.sum(power_re * sum_re - power_im * sum_im, axis=1)
    grad_im = jnp.sum(power_re * sum_im + power_im * sum_re, axis=1)
    lag_re = jnp.sum(power_re * full_re - power_im * full_im, axis=1)
    lag_im = jnp.sum(power_re * full_im + power_im * full_re, axis=1)
    small_grad = jnp.concatenate(
        [
            d_taps[:3].reshape(9, channels),
            -(res_re * lag_re + res_im * lag_im),
            res_im * lag_re - res_re * lag_im,
            grad_re,
            grad_im,
        ],
        axis=0,
    ).astype(bf16)
    last = ring_step([in_sum, out_sum], last, stages[0] + [gain_grads, small_grad])
    gain_sums = place_gain(gain_grads).transpose(1, 0, 2).reshape(2, channels)
    gain_high = gain_sums.astype(bf16)
    gain_low = (gain_sums - gain_high.astype(f32)).astype(bf16)
    small_grad = jnp.concatenate([small_grad, gain_high, gain_low], axis=0)
    for at in range(1, steps):
        last = ring_step([in_sum], last)
    [small_grad] = after([small_grad], last)
    small_share = scatter_small(jnp.split(small_grad, outer, axis=1))
    gain_share = small_share[-4:-2] + small_share[-2:]
    for at in range(1, steps):
        last = ring_step([out_sum], last)

    at = 9 + poles
    return (
        block_output[None],
        input_grad[None],
        in_sum.total.reshape(3, own, width).transpose(0, 2, 1),
        out_sum.total,
        gain_share[0],
        small_share[:9].reshape(3, 3, own),
        small_share[9:at].T,
        small_share[at : at + poles].T,
        small_share[at + poles : at + 3 * poles].T,
        gain_share[1],
        grads[1].total.T,
        grads[2].total.T,
        grads[0].total.T,
    )


def solution(mesh):
    both = ("wide", "narrow")
    return jax.shard_map(
        body,
        mesh=mesh,
        in_specs=(
            P("wide", "narrow", None),
            P(None, None, both),
            P(both, None),
            P(both),
            P(None, None, both),
            P(both, None),
            P(both, None),
            P(both, None),
            P(both),
            P(None, both),
            P(None, both),
            P(None, both),
            P("wide", None),
            P("wide", None),
            P("wide", "narrow", None),
        ),
        out_specs=(
            P("wide", "narrow", None),
            P("wide", "narrow", None),
            P(None, None, both),
            P(both, None),
            P(both),
            P(None, None, both),
            P(both, None),
            P(both, None),
            P(both, None),
            P(both),
            P(None, both),
            P(None, both),
            P(None, both),
        ),
        check_vma=False,
    )
```

```python
from functools import partial

import jax
import jax.numpy as jnp
import numpy as np
from jax import lax
from jax.experimental import pallas as pl
from jax.experimental.pallas import tpu as pltpu
from jax.sharding import PartitionSpec as P

BLOCK = 128
LONGEST = 4
SPAN = LONGEST * BLOCK
FREQ = SPAN

epsilon = 1e-06
bf16 = jnp.bfloat16
f32 = jnp.float32


def transform():
    k = np.arange(FREQ)[:, None] * 2 + 1
    t = np.arange(SPAN)[None, :]
    turn = (k * t % (4 * SPAN)) * (2 * np.pi / (4 * SPAN))
    return np.concatenate([np.cos(turn), -np.sin(turn)], axis=0).astype(np.float32)


def nn(a, b):
    return lax.dot_general(a, b, (((1,), (0,)), ((), ())), preferred_element_type=f32)


def nt(a, b):
    return lax.dot_general(a, b, (((1,), (1,)), ((), ())), preferred_element_type=f32)


def tn(a, b):
    return lax.dot_general(a, b, (((0,), (0,)), ((), ())), preferred_element_type=f32)


def swap(values, axis, shift):
    size = lax.axis_size(axis)
    return lax.ppermute(values, axis, [(i, i ^ shift) for i in range(size)])


def after(values, tokens):
    if not tokens:
        return values
    joined = lax.optimization_barrier(tuple(values) + tuple(tokens))
    return list(joined[: len(values)])


def ring_of(size):
    return list(range(0, size, 2)) + list(range(size - 1, 0, -2))


def along(values, step):
    outer = lax.axis_size("wide") // 2
    ring = ring_of(outer)
    pairs = [
        (ring[p] * 2 + side, ring[(p + step) % outer] * 2 + side)
        for p in range(outer)
        for side in range(2)
    ]
    return lax.ppermute(values, "wide", pairs)


def ring_offsets(outer):
    near = [sign * h for h in range(1, outer // 2) for sign in (-1, 1)]
    return [0] + near + [outer // 2]


def cut_of(rows):
    cut = (rows // 2 + 15) // 16 * 16
    return cut if cut < rows else rows // 2


def two_parts(values, axis):
    cut = cut_of(values.shape[axis])
    return (
        lax.slice_in_dim(values, 0, cut, axis=axis),
        lax.slice_in_dim(values, cut, values.shape[axis], axis=axis),
    )


class Gather:
    def __init__(self, own):
        self.most = lax.axis_size("wide") // 4 - 1
        self.before, self.behind, self.opposite = [own], [own], []

    def sends(self):
        if len(self.before) <= self.most:
            return self.before[-1], self.behind[-1]
        return two_parts(self.before[-1], 0)[0], two_parts(self.behind[-1], 0)[1]

    def take(self, got, back):
        if len(self.before) <= self.most:
            self.before.append(got)
            self.behind.append(back)
        else:
            self.opposite = [got, back]

    def pieces(self):
        near = [piece for pair in zip(self.before[1:], self.behind[1:]) for piece in pair]
        return [self.before[0]] + near + [jnp.concatenate(self.opposite, axis=0)]


class Scatter:
    def __init__(self, chunks):
        self.left = len(chunks) // 2 - 1
        self.wire = chunks[0].dtype
        self.total = chunks[0].astype(f32)
        self.behind = [chunk.astype(f32) for chunk in chunks[1:-1:2]]
        self.ahead = [chunk.astype(f32) for chunk in chunks[2:-1:2]]
        self.last = chunks[-1]

    def sends(self):
        if self.last is not None:
            return two_parts(self.last, 0)
        h = self.left - 1
        return self.ahead[h].astype(self.wire), self.behind[h].astype(self.wire)

    def take(self, got, back):
        got, back = got.astype(f32), back.astype(f32)
        h = self.left - 1
        if self.last is not None:
            top, bottom = two_parts(self.ahead[h], 0)
            self.ahead[h] = jnp.concatenate([top + got, bottom], axis=0)
            top, bottom = two_parts(self.behind[h], 0)
            self.behind[h] = jnp.concatenate([top, bottom + back], axis=0)
            self.last = None
            return
        self.left = h
        if h:
            self.ahead[h - 1] = self.ahead[h - 1] + got
            self.behind[h - 1] = self.behind[h - 1] + back
        else:
            self.total = self.total + got + back


def ring_step(items, tokens=(), arrive=()):
    sends = [item.sends() for item in items]
    ways = [one[0] if len(one) == 1 else jnp.concatenate(one, axis=0) for one in zip(*sends)]
    ways = after(ways, list(tokens)) if tokens else lax.optimization_barrier(tuple(ways))
    got, back = after([along(ways[0], 1), along(ways[1], -1)], list(arrive))
    at = [0, 0]
    for item, (ahead, behind) in zip(items, sends):
        ends = [at[0] + ahead.shape[0], at[1] + behind.shape[0]]
        item.take(got[at[0] : ends[0]], back[at[1] : ends[1]])
        at = ends
    return [got, back]


def gather_small(own):
    outer = lax.axis_size("wide") // 2
    return [own] + [along(own, -offset) for offset in ring_offsets(outer)[1:]]


def scatter_small(chunks):
    offsets = ring_offsets(len(chunks))
    total = chunks[0].astype(f32)
    for chunk, offset in zip(chunks[1:], offsets[1:]):
        total = total + along(chunk, offset).astype(f32)
    return total


def gather_rows(own, tokens=(), later=(), single=False):
    size = lax.axis_size("narrow")
    half = own.shape[0] // 2
    [own] = after([own], tokens)
    across = [swap(own, "narrow", k) for k in range(2, size, 2)]
    beside = swap(own, "wide", 1)
    stage_one = across + [beside]
    if later:
        *across, beside = after(across + [beside], later)
    parts, stage_two = [beside], []
    for n, k in enumerate(range(2, size, 2)):
        ends = [swap(across[n][:half], "wide", 1), swap(beside[half:], "narrow", k)]
        parts += ends
        stage_two += ends
    even = jnp.concatenate([own] + across, axis=0)
    other_even = jnp.concatenate(parts, axis=0)
    odd = swap(even, "narrow", 1)
    if single:
        [other_even] = after([other_even], [odd])
    other_odd = swap(other_even, "narrow", 1)
    return ([even, odd], [other_even, other_odd]), (stage_one, stage_two, [odd, other_odd])


def scatter_rows(even, odd, other_even, other_odd, tokens=(), later=()):
    size = lax.axis_size("narrow")
    rows = even.shape[0] // (size // 2)
    half = rows // 2
    other = other_even.astype(f32) + other_odd.astype(f32)
    mine = even.astype(f32) + odd.astype(f32)
    beside_top, beside_bottom = other[:half], other[half:rows]
    out = mine[:rows]
    corners = other[rows:].astype(bf16)
    [corners] = after([corners], tokens)
    spread, stage_two, stage_three = [], [], []
    for n, k in enumerate(range(2, size, 2)):
        at = n * rows
        ends = [
            swap(corners[at : at + half], "wide", 1),
            swap(corners[at + half : at + rows], "narrow", k),
        ]
        stage_two += ends
        beside_bottom = beside_bottom + ends[1].astype(f32)
        at = at + rows
        spread.append(
            jnp.concatenate(
                [mine[at : at + half] + ends[0].astype(f32), mine[at + half : at + rows]], axis=0
            ).astype(bf16)
        )
    spread.append(jnp.concatenate([beside_top, beside_bottom], axis=0).astype(bf16))
    spread = after(spread, later) if later else lax.optimization_barrier(tuple(spread))
    for n, k in enumerate(range(2, size, 2)):
        stage_three.append(swap(spread[n], "narrow", k))
        out = out + stage_three[-1].astype(f32)
    stage_three.append(swap(spread[-1], "wide", 1))
    return out + stage_three[-1].astype(f32), (stage_two, stage_three)


def inverse_rms(values):
    return lax.rsqrt(jnp.mean(values * values, axis=-1, keepdims=True) + epsilon)


def norm_kernel(*refs):
    pieces, gain, out = refs[:-2], refs[-2], refs[-1]
    rows = pieces[0].shape[0]
    step = 32 if rows % 32 == 0 else rows
    for n, piece in enumerate(pieces):

        def part(b, _):
            at = pl.multiple_of(b * step, step)
            values = piece[pl.ds(at, step), :].astype(f32)
            rate = lax.rsqrt(jnp.mean(values * values, axis=-1, keepdims=True) + epsilon)
            to = pl.multiple_of(n * rows + at, step)
            out[pl.ds(to, step), :] = (values * rate * gain[...]).astype(bf16)
            return 0

        lax.fori_loop(0, rows // step, part, 0)


def normed_rows(pieces, gain):
    rows, width = pieces[0].shape
    return pl.pallas_call(
        norm_kernel,
        out_shape=jax.ShapeDtypeStruct((rows * len(pieces), width), bf16),
        cost_estimate=light,
        name="norm",
    )(*pieces, gain.reshape(1, width))


def norm_back(values, rate, gain, grad):
    a = grad * gain
    inner = jnp.mean(a * values, axis=-1, keepdims=True)
    return rate * a - values * (rate * rate * rate) * inner


light = pl.CostEstimate(flops=1024, bytes_accessed=1024, transcendentals=0)


def filter_kernel(base_re, base_im, step_re, step_im, out):
    poles = base_re.shape[0]
    width = out.shape[1]
    for g in range(width // 128 if width % 128 == 0 else 1):
        lanes = pl.ds(g * 128, min(128, width))
        start = tuple(base_re[j, :, lanes] for j in range(poles)) + tuple(
            base_im[j, :, lanes] for j in range(poles)
        )

        def step(b, state):
            total = state[0]
            for j in range(1, poles):
                total = total + state[j]
            out[pl.ds(pl.multiple_of(b * 8, 8), 8), lanes] = total
            new_re, new_im = [], []
            for j in range(poles):
                sr = step_re[j, :, lanes]
                si = step_im[j, :, lanes]
                new_re.append(state[j] * sr - state[poles + j] * si)
                new_im.append(state[j] * si + state[poles + j] * sr)
            return tuple(new_re) + tuple(new_im)

        lax.fori_loop(0, SPAN // 8, step, start)


def filter_taps(base_re, base_im, step_re, step_im):
    width = base_re.shape[2]
    return pl.pallas_call(
        filter_kernel,
        out_shape=jax.ShapeDtypeStruct((SPAN, width), f32),
        cost_estimate=light,
        name="taps",
    )(base_re, base_im, step_re, step_im)


def moment_kernel(grad, step_re, step_im, sum_re, sum_im, mom_re, mom_im):
    poles = step_re.shape[0]
    width = grad.shape[1]
    per = 8
    for g in range(width // 128 if width % 128 == 0 else 1):
        lanes = pl.ds(g * 128, min(128, width))
        for j0 in range(0, poles, per):
            zero = jnp.zeros((8, min(128, width)), f32)

            def step(i, state):
                b = SPAN // 8 - 1 - i
                value = grad[pl.ds(pl.multiple_of(b * 8, 8), 8), lanes]
                new = []
                for n in range(per):
                    sr = step_re[j0 + n, :, lanes]
                    si = step_im[j0 + n, :, lanes]
                    pr, pi, qr, qi = state[4 * n : 4 * n + 4]
                    ur, ui = pr + qr, pi + qi
                    new += [
                        pr * sr - pi * si + value,
                        pr * si + pi * sr,
                        ur * sr - ui * si,
                        ur * si + ui * sr,
                    ]
                return tuple(new)

            state = lax.fori_loop(0, SPAN // 8, step, (zero,) * (4 * per))
            for n in range(per):
                sum_re[j0 + n, :, lanes] = state[4 * n]
                sum_im[j0 + n, :, lanes] = state[4 * n + 1]
                mom_re[j0 + n, :, lanes] = state[4 * n + 2]
                mom_im[j0 + n, :, lanes] = state[4 * n + 3]


SIDE = 512


def product_kernel(a, b, out, turned=None, *, kind):
    if kind == "tn":

        @pl.when(pl.program_id(0) == 0)
        def _():
            turned[...] = a[...].T

        value = nn(turned[...], b[...])
    else:
        value = (nn if kind == "nn" else nt)(a[...], b[...])
    out[...] = value.astype(out.dtype)


def product(a, b, kind, dtype, at=None):
    if kind == "tn":
        depth, rows = a.shape[0], SIDE
        a_spec = pl.BlockSpec((depth, SIDE), lambda i: (0, at))
        scratch = [pltpu.VMEM((SIDE, depth), a.dtype)]
    else:
        rows, depth = a.shape if at is None else (SIDE, a.shape[1])
        a_spec = pl.BlockSpec((rows, depth), lambda i: (at or 0, 0))
        scratch = []
    columns = b.shape[0] if kind == "nt" else b.shape[1]
    side = max(s for s in (512, 384, 256, 128, columns) if columns % s == 0 and s <= 512)
    if kind == "nt":
        b_spec = pl.BlockSpec((side, depth), lambda i: (i, 0))
    else:
        b_spec = pl.BlockSpec((depth, side), lambda i: (0, i))
    return pl.pallas_call(
        partial(product_kernel, kind=kind),
        grid=(columns // side,),
        out_shape=jax.ShapeDtypeStruct((rows, columns), dtype),
        in_specs=[a_spec, b_spec],
        out_specs=pl.BlockSpec((rows, side), lambda i: (0, i)),
        scratch_shapes=scratch,
        cost_estimate=light,
        name="product",
    )(a, b)


def filter_moments(grad, step_re, step_im):
    poles, _, width = step_re.shape
    shape = jax.ShapeDtypeStruct((poles, 8, width), f32)
    return pl.pallas_call(
        moment_kernel,
        out_shape=(shape,) * 4,
        cost_estimate=light,
        name="moments",
    )(grad, step_re, step_im)


LIVE, KEEP_ONE, KEEP_TWO = 0, 1, 2


def load_masked(order, proj, table, m_scr):
    pieces, rows, _ = proj.shape
    m_scr[0:8, :] = jnp.zeros_like(m_scr[0:8, :])

    def piece(b, _):
        p = order[b]
        at = pl.multiple_of(b * rows, rows)
        live = table[pl.ds(at, rows), LIVE : LIVE + 1]
        m_scr[pl.ds(pl.multiple_of(at + 8, 8), rows), :] = proj[p] * live
        return 0

    lax.fori_loop(0, pieces, piece, 0)


def short_block(m_scr, taps, table, at):
    window = m_scr[pl.ds(at, BLOCK + 8), :]
    one = table[pl.ds(at, BLOCK), KEEP_ONE : KEEP_ONE + 1]
    two = table[pl.ds(at, BLOCK), KEEP_TWO : KEEP_TWO + 1]
    here = window[8:]
    once = window[7 : BLOCK + 7] * one
    twice = window[6 : BLOCK + 6] * two
    short = taps[0:1, :] * here + taps[1:2, :] * once + taps[2:3, :] * twice
    return short, here, once, twice


def pack_document(source, packed, first, count):
    blocks = source.shape[0] // BLOCK
    for kb in range(LONGEST):
        at = pl.multiple_of(jnp.minimum(first + kb, blocks - 1) * BLOCK, BLOCK)
        inside = (kb < count).astype(f32)
        packed[kb * BLOCK : (kb + 1) * BLOCK, :] = (source[pl.ds(at, BLOCK), :] * inside).astype(bf16)


def place_document(result, target, first, count):
    for kb in range(LONGEST):

        @pl.when(kb < count)
        def _():
            at = pl.multiple_of((first + kb) * BLOCK, BLOCK)
            target[pl.ds(at, BLOCK), :] = result[kb * BLOCK : (kb + 1) * BLOCK, :]


def forward_kernel(
    order, first, count, proj, taps, table, spectrum, fwd, inv, gated, long_out, seen, m_scr, u_scr, q_scr, packed
):
    width = long_out.shape[1]
    pieces, rows, _ = proj.shape
    blocks = long_out.shape[0] // BLOCK
    load_masked(order, proj, table, m_scr)

    def block(n, _):
        at = pl.multiple_of(n * BLOCK, BLOCK)
        short, _, _, _ = short_block(m_scr, taps, table, at)
        q_scr[pl.ds(at, BLOCK), :] = short[:, :width]
        u_scr[pl.ds(at, BLOCK), :] = short[:, width : 2 * width] * short[:, 2 * width :]
        return 0

    lax.fori_loop(0, blocks, block, 0)

    def document(d, _):
        pack_document(u_scr, packed, first[d], count[d])
        both = jnp.dot(fwd[...], packed[...], preferred_element_type=f32)
        seen[d] = both.astype(bf16)
        re, im = both[:FREQ], both[FREQ:]
        hr, hi = spectrum[:FREQ], spectrum[FREQ:]
        answer = jnp.concatenate([re * hr - im * hi, re * hi + im * hr], axis=0).astype(bf16)
        result = jnp.dot(inv[...], answer, preferred_element_type=f32)
        place_document(result, long_out, first[d], count[d])
        return 0

    lax.fori_loop(0, seen.shape[0], document, 0)

    def piece(b, _):
        at = pl.multiple_of(b * rows, rows)
        gated[order[b]] = (q_scr[pl.ds(at, rows), :] * long_out[pl.ds(at, rows), :]).astype(bf16)
        return 0

    lax.fori_loop(0, pieces, piece, 0)


def backward_kernel(
    order, first, count, proj, d_gated, long_out, seen, taps, table, spectrum, fwd, inv,
    dz, d_filter, d_taps, m_scr, dy_scr, k_scr, v_scr, ds_scr, packed, d_spec,
):
    width = long_out.shape[1]
    pieces, rows, _ = proj.shape
    slots = long_out.shape[0]
    blocks = slots // BLOCK
    per_piece = rows // BLOCK
    load_masked(order, proj, table, m_scr)
    ds_scr[slots : slots + 8, :] = jnp.zeros_like(ds_scr[slots : slots + 8, :])

    def block(n, _):
        at = pl.multiple_of(n * BLOCK, BLOCK)
        short, _, _, _ = short_block(m_scr, taps, table, at)
        within = pl.multiple_of((n % per_piece) * BLOCK, BLOCK)
        dg = d_gated[order[n // per_piece], pl.ds(within, BLOCK), :]
        dy_scr[pl.ds(at, BLOCK), :] = dg * short[:, :width]
        ds_scr[pl.ds(at, BLOCK), :width] = dg * long_out[pl.ds(at, BLOCK), :]
        k_scr[pl.ds(at, BLOCK), :] = short[:, width : 2 * width]
        v_scr[pl.ds(at, BLOCK), :] = short[:, 2 * width :]
        return 0

    lax.fori_loop(0, blocks, block, 0)
    d_spec[...] = jnp.zeros_like(d_spec)

    def document(d, _):
        pack_document(dy_scr, packed, first[d], count[d])
        both = jnp.dot(fwd[...], packed[...], preferred_element_type=f32)
        re, im = both[:FREQ], both[FREQ:]
        hr, hi = spectrum[:FREQ], spectrum[FREQ:]
        answer = jnp.concatenate([re * hr + im * hi, im * hr - re * hi], axis=0).astype(bf16)
        result = jnp.dot(inv[...], answer, preferred_element_type=f32)
        ur, ui = seen[d, :FREQ].astype(f32), seen[d, FREQ:].astype(f32)
        d_spec[:FREQ] += re * ur + im * ui
        d_spec[FREQ:] += im * ur - re * ui
        for kb in range(LONGEST):

            @pl.when(kb < count[d])
            def _():
                at = pl.multiple_of((first[d] + kb) * BLOCK, BLOCK)
                du = result[kb * BLOCK : (kb + 1) * BLOCK, :]
                ds_scr[pl.ds(at, BLOCK), width : 2 * width] = du * v_scr[pl.ds(at, BLOCK), :]
                ds_scr[pl.ds(at, BLOCK), 2 * width :] = du * k_scr[pl.ds(at, BLOCK), :]

        return 0

    lax.fori_loop(0, seen.shape[0], document, 0)
    d_filter[...] = jnp.dot(inv[...], d_spec[...].astype(bf16), preferred_element_type=f32)
    d_taps[...] = jnp.zeros_like(d_taps)

    def back(n, _):
        at = pl.multiple_of(n * BLOCK, BLOCK)
        window = m_scr[pl.ds(at, BLOCK + 8), :]
        ahead = ds_scr[pl.ds(at, BLOCK + 8), :]
        one = table[pl.ds(at, BLOCK + 8), KEEP_ONE : KEEP_ONE + 1]
        two = table[pl.ds(at, BLOCK + 8), KEEP_TWO : KEEP_TWO + 1]
        live = table[pl.ds(at, BLOCK), LIVE : LIVE + 1]
        ds = ahead[:BLOCK]
        ahead_one = ahead * one
        ahead_two = ahead * two
        dm = (
            taps[0:1, :] * ds
            + taps[1:2, :] * ahead_one[1 : BLOCK + 1]
            + taps[2:3, :] * ahead_two[2 : BLOCK + 2]
        )
        d_taps[0:1, :] += jnp.sum(window[8:] * ds, axis=0, keepdims=True)
        d_taps[1:2, :] += jnp.sum(window[7 : BLOCK + 7] * ahead_one[:BLOCK], axis=0, keepdims=True)
        d_taps[2:3, :] += jnp.sum(window[6 : BLOCK + 6] * ahead_two[:BLOCK], axis=0, keepdims=True)
        within = pl.multiple_of((n % per_piece) * BLOCK, BLOCK)
        dz[order[n // per_piece], pl.ds(within, BLOCK), :] = (dm * live).astype(bf16)
        return 0

    lax.fori_loop(0, blocks, back, 0)


smem = pl.BlockSpec(memory_space=pltpu.SMEM)
vmem = pl.BlockSpec(memory_space=pltpu.VMEM)


def mixer_forward(order, first, count, proj, taps, table, spectrum, fwd, inv):
    pieces, rows, three = proj.shape
    width = three // 3
    slots = pieces * rows
    docs = first.shape[0]
    return pl.pallas_call(
        forward_kernel,
        out_shape=(
            jax.ShapeDtypeStruct((pieces, rows, width), bf16),
            jax.ShapeDtypeStruct((slots, width), f32),
            jax.ShapeDtypeStruct((docs, 2 * FREQ, width), bf16),
        ),
        in_specs=[smem] * 3 + [vmem] * 6,
        out_specs=(vmem,) * 3,
        scratch_shapes=[
            pltpu.VMEM((slots + 8, three), f32),
            pltpu.VMEM((slots, width), f32),
            pltpu.VMEM((slots, width), f32),
            pltpu.VMEM((SPAN, width), bf16),
        ],
        compiler_params=pltpu.CompilerParams(vmem_limit_bytes=40 * 2**20),
        cost_estimate=light,
        name="mixer_forward",
    )(order, first, count, proj, taps, table, spectrum, fwd, inv)


def mixer_backward(order, first, count, proj, d_gated, long_out, seen, taps, table, spectrum, fwd, inv):
    pieces, rows, three = proj.shape
    width = three // 3
    slots = pieces * rows
    docs = first.shape[0]
    return pl.pallas_call(
        backward_kernel,
        out_shape=(
            jax.ShapeDtypeStruct((pieces, rows, three), bf16),
            jax.ShapeDtypeStruct((SPAN, width), f32),
            jax.ShapeDtypeStruct((8, three), f32),
        ),
        in_specs=[smem] * 3 + [vmem] * 9,
        out_specs=(vmem,) * 3,
        scratch_shapes=[
            pltpu.VMEM((slots + 8, three), f32),
            pltpu.VMEM((slots, width), f32),
            pltpu.VMEM((slots, width), f32),
            pltpu.VMEM((slots, width), f32),
            pltpu.VMEM((slots + 8, three), f32),
            pltpu.VMEM((SPAN, width), bf16),
            pltpu.VMEM((2 * FREQ, width), f32),
        ],
        compiler_params=pltpu.CompilerParams(vmem_limit_bytes=48 * 2**20),
        cost_estimate=light,
        name="mixer_backward",
    )(order, first, count, proj, d_gated, long_out, seen, taps, table, spectrum, fwd, inv)


def layout(doc_blocks, doc_pad, slots):
    block_ends = jnp.cumsum(doc_blocks) * BLOCK
    starts = block_ends - doc_blocks * BLOCK
    places = jnp.arange(slots, dtype=jnp.int32)
    living = (places[None, :] >= starts[:, None]) & (
        places[None, :] < (block_ends - doc_pad)[:, None]
    )
    live = jnp.sum(living.astype(f32), axis=0)
    opening = jnp.sum((places[None, :] == starts[:, None]).astype(f32), axis=0)
    one = 1.0 - opening
    one = one * (places > 0)
    two = one * jnp.concatenate([jnp.zeros((1,), f32), one[:-1]])
    table = jnp.stack([live, one, two], axis=1)
    table = jnp.concatenate([table, jnp.zeros((8, 3), f32)], axis=0)
    return table, starts // BLOCK


def picked(index, count, values):
    hot = index[:, None] == jnp.arange(count)[None, :]
    shape = hot.shape + (1,) * (values.ndim - 1)
    return jnp.sum(jnp.where(hot.reshape(shape), values[None], 0), axis=1)


def body(
    tokens, w_in, w_out, gain_one, short_kernel, decay_rate, pole_angle, residue,
    gain_two, w_gate, w_up, w_down, doc_blocks, doc_pad, cotangent,
):
    wide, narrow = lax.axis_size("wide"), lax.axis_size("narrow")
    wide_at, narrow_at = lax.axis_index("wide"), lax.axis_index("narrow")
    outer = wide // 2
    _, local_rows, width = tokens.shape
    slots = local_rows * narrow
    even = slots // 2
    source = tokens[0].astype(f32)
    upstream_low = cotangent[0]
    poles = decay_rate.shape[1]
    own = w_in.shape[2]
    channels = own * outer
    hidden_units = w_gate.shape[1] * outer

    ring = np.array(ring_of(outer))
    ring_place = np.argsort(ring)
    tour = picked((wide_at // 2)[None], outer, jnp.asarray(ring_place, jnp.int32))[0]
    piece_places = (tour + jnp.asarray(ring_offsets(outer), jnp.int32)) % outer
    piece_outer = picked(piece_places, outer, jnp.asarray(ring, jnp.int32))
    sides = jnp.arange(2) ^ (wide_at % 2)
    offsets = list(range(0, narrow, 2)) + list(range(1, narrow, 2))
    place_of = np.argsort(np.array(offsets))
    order = picked(jnp.arange(narrow) ^ narrow_at, narrow, jnp.asarray(place_of, jnp.int32))
    narrow_of = jnp.asarray(offsets, jnp.int32) ^ narrow_at

    small = jnp.concatenate(
        [
            short_kernel.reshape(9, own),
            decay_rate.T,
            pole_angle.T,
            residue.T,
            gain_one[None],
            gain_two[None],
        ],
        axis=0,
    )
    small_pieces = gather_small(small)
    small_all = jnp.concatenate(small_pieces, axis=1)
    (first_own, first_other), first_stages = gather_rows(tokens[0], small_pieces[1:])
    gains = small_all[small.shape[0] - 2 :].reshape(2, outer, own)
    gains = jnp.stack([gains, swap(gains, "wide", 1)])
    gains = jnp.stack([gains] + [swap(gains, "narrow", k) for k in range(2, narrow, 2)])
    gains = jnp.concatenate([gains, swap(gains, "narrow", 1)], axis=0).astype(f32)
    gains = picked(order, narrow, gains).transpose(1, 3, 0, 2, 4)
    gains = picked(sides, 2, gains).transpose(1, 0, 2, 3, 4)
    hot = piece_outer[None, :] == jnp.arange(outer)[:, None]
    gains = jnp.sum(jnp.where(hot[:, :, None, None, None, None], gains[None], 0), axis=1)
    gain_all = gains.transpose(3, 0, 1, 2, 4).reshape(2, width)
    gain_first, gain_last = gain_all[0], gain_all[1]

    def place_gain(values):
        values = values.reshape(2, outer, 2, narrow, own).transpose(1, 2, 3, 0, 4)
        values = picked(piece_outer, outer, values).transpose(1, 0, 2, 3, 4)
        values = picked(sides, 2, values).transpose(2, 0, 1, 3, 4)
        values = picked(narrow_of, narrow, values)
        total = values[: narrow // 2] + swap(values[narrow // 2 :], "narrow", 1)
        summed = total[0]
        for k in range(1, narrow // 2):
            summed = summed + swap(total[k], "narrow", 2 * k)
        summed = summed[0] + swap(summed[1], "wide", 1)
        return summed

    documents = jnp.concatenate([doc_blocks, doc_pad], axis=0)
    [documents] = after([documents], small_pieces[1:])
    documents = (documents, swap(documents, "wide", 1))
    tables = [layout(rules[0], rules[1], slots) for rules in documents]

    shards = [w_in.transpose(0, 2, 1).reshape(3 * own, width), w_out, w_down.T, w_gate.T, w_up.T]
    weights = [Gather(shard) for shard in shards]
    in_all, out_all, down_all, gate_all, up_all = weights
    steps = outer // 2
    last = []
    for at in range(steps):
        last = ring_step([in_all, out_all], last)

    def normed(pieces):
        values = jnp.concatenate(pieces, axis=0).astype(f32)
        return (values * inverse_rms(values) * gain_first).astype(bf16)

    rows_first = lax.optimization_barrier([normed(first_own), normed(first_other)])
    rate_first = inverse_rms(source)
    (upstream_own, upstream_other), upstream_stages = gather_rows(
        upstream_low, first_stages[2], (), True
    )

    matrix = transform()
    fwd = jnp.asarray(matrix, bf16)
    inv = jnp.asarray(matrix.T / SPAN, bf16)

    block = small_all.astype(f32)
    taps = block[:9].reshape(3, 3 * channels)
    taps = jnp.concatenate([taps, jnp.zeros((5, 3 * channels), f32)], axis=0)
    decay = block[9 : 9 + poles][:, None, :]
    angle = block[9 + poles : 9 + 2 * poles][:, None, :]
    res_re = block[9 + 2 * poles : 9 + 3 * poles][:, None, :]
    res_im = -block[9 + 3 * poles : 9 + 4 * poles][:, None, :]
    lag = jnp.arange(8, dtype=f32)[None, :, None]
    fade = jnp.exp(-decay * lag)
    power_re, power_im = fade * jnp.cos(angle * lag), fade * jnp.sin(angle * lag)
    fade_step = jnp.exp(-decay * 8.0)
    step_re = jnp.broadcast_to(fade_step * jnp.cos(angle * 8.0), power_re.shape)
    step_im = jnp.broadcast_to(fade_step * jnp.sin(angle * 8.0), power_re.shape)
    filt = filter_taps(
        res_re * power_re - res_im * power_im,
        res_re * power_im + res_im * power_re,
        step_re,
        step_im,
    )
    spectrum = lax.dot_general(
        jnp.asarray(matrix),
        filt,
        (((1,), (0,)), ((), ())),
        precision=lax.Precision.HIGHEST,
        preferred_element_type=f32,
    )
    res_re, res_im = res_re[:, 0], -res_im[:, 0]

    in_pieces = [piece.reshape(3, own, width) for piece in in_all.pieces()]
    in_all = jnp.concatenate(in_pieces, axis=1).reshape(3 * channels, width)
    mixed = []
    for r in range(2):
        table, first = tables[r]
        proj = nt(rows_first[r], in_all).reshape(narrow, local_rows, 3 * channels)
        gated, long_out, seen = mixer_forward(
            order, first, documents[r][0], proj, taps, table, spectrum, fwd, inv
        )
        mixed.append((proj, gated.reshape(slots, channels), long_out, seen))
    out_last = last
    out_all = jnp.concatenate(out_all.pieces(), axis=0)
    parts = [slice(0, even), slice(even, slots)]
    ready = [mixed[0][1], after([mixed[1][1]], upstream_stages[0])[0]]
    odds = [nn(ready[r][parts[1]], out_all).astype(bf16) for r in range(2)]
    cores = [swap(odd, "narrow", 1) for odd in odds]
    for at in range(steps - 1):
        last = ring_step([down_all, gate_all], last, odds)
    last_two = last
    for at in range(steps - 1):
        last_two = ring_step([up_all] if at else [down_all, up_all], last_two)
    ready = after([mixed[0][1], mixed[1][1]], upstream_stages[0])
    evens = [nn(ready[r][parts[0]], out_all).astype(bf16) for r in range(2)]
    mixer_out, stages = scatter_rows(
        evens[0], cores[0], evens[1], cores[1], upstream_stages[1] + last
    )
    middle = source + mixer_out
    rate_last = inverse_rms(middle)
    rows_upstream = jnp.concatenate(upstream_own + upstream_other, axis=0)
    low_second = (middle * rate_last * gain_last).astype(bf16)
    (second_own, second_other), second_stages = gather_rows(low_second, last_two + upstream_stages[2])
    rows_second = jnp.concatenate(second_own + second_other, axis=0)
    last = ring_step([gate_all, up_all], last_two, second_stages[1])

    down_all, gate_all = [jnp.concatenate(w.pieces(), axis=0) for w in (down_all, gate_all)]
    up_all = jnp.concatenate(up_all.pieces(), axis=0)
    d_hidden = nt(down_all, rows_upstream)
    gate_pre = nt(gate_all, rows_second)
    up_pre = nt(up_all, rows_second)
    sig = jax.nn.sigmoid(gate_pre)
    silu = gate_pre * sig
    hidden = (silu * up_pre).astype(bf16)
    d_gate = (d_hidden * up_pre * sig * (1.0 + gate_pre * (1.0 - sig))).astype(bf16)
    d_up = (d_hidden * silu).astype(bf16)
    parts = [slice(p, p + even) for p in range(0, 2 * slots, even)]
    def second_share(n):
        p = parts[n]
        return (tn(d_gate[:, p], gate_all) + tn(d_up[:, p], up_all)).astype(bf16)

    odds = [second_share(n) for n in (1, 3)]
    cores = [swap(odd, "narrow", 1) for odd in odds]
    evens = [second_share(0), second_share(2)]
    [ready] = after([hidden], cores + evens)
    grad_down = product(ready, rows_upstream, "nn", bf16)
    d_second, stages = scatter_rows(evens[0], cores[0], evens[1], cores[1], (), [grad_down])
    upstream = upstream_low.astype(f32)
    d_middle = upstream + norm_back(middle, rate_last, gain_last, d_second)
    (middle_own, middle_other), middle_stages = gather_rows(d_middle.astype(bf16))
    rows_dmiddle = [jnp.concatenate(middle_own, axis=0), jnp.concatenate(middle_other, axis=0)]
    grads = [Scatter(jnp.split(grad_down, outer, axis=0))]
    [d_gate] = after([d_gate], stages[0])
    grad_gate = product(d_gate, rows_second, "nn", bf16)
    [d_up] = after([d_up], [grad_gate])
    grad_up = product(d_up, rows_second, "nn", bf16)
    [hidden] = after([hidden], [grad_up])
    down_shares = [product(hidden, down_all, "tn", bf16, n) for n in (0, 1)]
    down_shares += [product(hidden, down_all, "tn", bf16, n) for n in (2, 3)]
    pair = [Scatter(jnp.split(grad, outer, axis=0)) for grad in (grad_gate, grad_up)]
    grads += pair
    last = ring_step(grads, (), middle_stages[0])
    down_shares = after(down_shares, middle_stages[1])
    down_cores = [swap(down_shares[n], "narrow", 1) for n in (1, 3)]
    down_out, down_stages = scatter_rows(
        down_shares[0], down_cores[0], down_shares[2], down_cores[1]
    )
    block_output = (middle + down_out).astype(bf16)
    grad_gain_two = jnp.sum(d_second * middle * rate_last, axis=0)

    grad_out = sum(tn(mixed[r][1], rows_dmiddle[r]) for r in range(2)).astype(bf16)
    halves = (slice(0, even), slice(even, slots))
    shares, d_rows, grad_gain_one, d_filter, d_taps = [None, None], [None, None], 0.0, 0.0, 0.0
    for r in range(2):
        proj, gated, long_out, seen = mixed[r]
        table, first = tables[r]
        d_gated = nt(rows_dmiddle[r], out_all).reshape(narrow, local_rows, channels)
        if r == 1:
            [d_gated] = after([d_gated], [grad_out, *shares[0], *down_stages[0]])
        dz, d_filter_row, d_taps_row = mixer_backward(
            order, first, documents[r][0], proj, d_gated, long_out, seen, taps, table,
            spectrum, fwd, inv,
        )
        d_rows[r] = dz.reshape(slots, 3 * channels)
        d_filter, d_taps = d_filter + d_filter_row, d_taps + d_taps_row
        if r == 0:
            shares[r] = [nn(d_rows[r][p], in_all).astype(bf16) for p in halves]
    [ready] = after([d_rows[1]], down_stages[1])
    odd = nn(ready[halves[1]], in_all).astype(bf16)
    cores = [swap(shares[0][1], "narrow", 1), swap(odd, "narrow", 1)]
    ready = after(d_rows, [odd])
    grad_in = sum(tn(ready[r], rows_first[r]) for r in range(2)).astype(bf16)
    for at in range(1, steps):
        last = ring_step(grads, last, [grad_in])
    [ready] = after([d_rows[1]], [grad_in] + cores)
    shares[1] = [nn(ready[halves[0]], in_all).astype(bf16), odd]
    d_normed, stages = scatter_rows(shares[0][0], cores[0], shares[1][0], cores[1])
    input_grad = (d_middle + norm_back(source, rate_first, gain_first, d_normed)).astype(bf16)
    for r in range(2):
        for n, share in enumerate(after(shares[r], [shares[1][0]])):
            rows = rows_first[r][n * even : (n + 1) * even]
            grad_gain_one = grad_gain_one + jnp.sum(share.astype(f32) * rows.astype(f32), axis=0)
    chunks = grad_in.reshape(3, outer, own, width)
    in_sum = Scatter([chunks[:, j].reshape(3 * own, width) for j in range(outer)])
    out_sum = Scatter(jnp.split(grad_out, outer, axis=0))
    last = ring_step([in_sum, out_sum], last)
    d_filter, *_ = after([d_filter], last + stages[0])
    gain_grads = jnp.stack([grad_gain_one / gain_first, grad_gain_two])
    [gain_grads] = after([gain_grads], stages[0])
    sum_re, sum_im, mom_re, mom_im = filter_moments(d_filter, step_re, step_im)
    full_re = lag * sum_re + 8.0 * mom_re
    full_im = lag * sum_im + 8.0 * mom_im
    grad_re = jnp.sum(power_re * sum_re - power_im * sum_im, axis=1)
    grad_im = jnp.sum(power_re * sum_im + power_im * sum_re, axis=1)
    lag_re = jnp.sum(power_re * full_re - power_im * full_im, axis=1)
    lag_im = jnp.sum(power_re * full_im + power_im * full_re, axis=1)
    small_grad = jnp.concatenate(
        [
            d_taps[:3].reshape(9, channels),
            -(res_re * lag_re + res_im * lag_im),
            res_im * lag_re - res_re * lag_im,
            grad_re,
            grad_im,
        ],
        axis=0,
    ).astype(bf16)
    gain_sums = place_gain(gain_grads).transpose(1, 0, 2).reshape(2, channels)
    gain_high = gain_sums.astype(bf16)
    gain_low = (gain_sums - gain_high.astype(f32)).astype(bf16)
    small_grad = jnp.concatenate([small_grad, gain_high, gain_low], axis=0)
    [small_grad] = after([small_grad], stages[1])
    small_share = scatter_small(jnp.split(small_grad, outer, axis=1))
    gain_share = small_share[-4:-2] + small_share[-2:]
    for at in range(1, steps):
        last = ring_step([in_sum, out_sum], last, [small_share])

    at = 9 + poles
    return (
        block_output[None],
        input_grad[None],
        in_sum.total.reshape(3, own, width).transpose(0, 2, 1),
        out_sum.total,
        gain_share[0],
        small_share[:9].reshape(3, 3, own),
        small_share[9:at].T,
        small_share[at : at + poles].T,
        small_share[at + poles : at + 3 * poles].T,
        gain_share[1],
        grads[1].total.T,
        grads[2].total.T,
        grads[0].total.T,
    )


def solution(mesh):
    both = ("wide", "narrow")
    return jax.shard_map(
        body,
        mesh=mesh,
        in_specs=(
            P("wide", "narrow", None),
            P(None, None, both),
            P(both, None),
            P(both),
            P(None, None, both),
            P(both, None),
            P(both, None),
            P(both, None),
            P(both),
            P(None, both),
            P(None, both),
            P(None, both),
            P("wide", None),
            P("wide", None),
            P("wide", "narrow", None),
        ),
        out_specs=(
            P("wide", "narrow", None),
            P("wide", "narrow", None),
            P(None, None, both),
            P(both, None),
            P(both),
            P(None, None, both),
            P(both, None),
            P(both, None),
            P(both, None),
            P(both),
            P(None, both),
            P(None, both),
            P(None, both),
        ),
        check_vma=False,
    )
```

```python
from functools import partial

import jax
import jax.numpy as jnp
import numpy as np
from jax import lax
from jax.experimental import pallas as pl
from jax.experimental.pallas import tpu as pltpu
from jax.sharding import PartitionSpec as P

BLOCK = 128
LONGEST = 4
SPAN = LONGEST * BLOCK
FREQ = SPAN

epsilon = 1e-06
bf16 = jnp.bfloat16
f32 = jnp.float32


def transform():
    k = np.arange(FREQ)[:, None] * 2 + 1
    t = np.arange(SPAN)[None, :]
    turn = (k * t % (4 * SPAN)) * (2 * np.pi / (4 * SPAN))
    return np.concatenate([np.cos(turn), -np.sin(turn)], axis=0).astype(np.float32)


def nn(a, b):
    return lax.dot_general(a, b, (((1,), (0,)), ((), ())), preferred_element_type=f32)


def nt(a, b):
    return lax.dot_general(a, b, (((1,), (1,)), ((), ())), preferred_element_type=f32)


def tn(a, b):
    return lax.dot_general(a, b, (((0,), (0,)), ((), ())), preferred_element_type=f32)


def swap(values, axis, shift):
    size = lax.axis_size(axis)
    return lax.ppermute(values, axis, [(i, i ^ shift) for i in range(size)])


def after(values, tokens):
    if not tokens:
        return values
    joined = lax.optimization_barrier(tuple(values) + tuple(tokens))
    return list(joined[: len(values)])


def ring_of(size):
    return list(range(0, size, 2)) + list(range(size - 1, 0, -2))


def along(values, step):
    outer = lax.axis_size("wide") // 2
    ring = ring_of(outer)
    pairs = [
        (ring[p] * 2 + side, ring[(p + step) % outer] * 2 + side)
        for p in range(outer)
        for side in range(2)
    ]
    return lax.ppermute(values, "wide", pairs)


def ring_offsets(outer):
    near = [sign * h for h in range(1, outer // 2) for sign in (-1, 1)]
    return [0] + near + [outer // 2]


def cut_of(rows):
    cut = (rows // 2 + 15) // 16 * 16
    return cut if cut < rows else rows // 2


def two_parts(values, axis):
    cut = cut_of(values.shape[axis])
    return (
        lax.slice_in_dim(values, 0, cut, axis=axis),
        lax.slice_in_dim(values, cut, values.shape[axis], axis=axis),
    )


class Gather:
    def __init__(self, own):
        self.most = lax.axis_size("wide") // 4 - 1
        self.before, self.behind, self.opposite = [own], [own], []

    def sends(self):
        if len(self.before) <= self.most:
            return self.before[-1], self.behind[-1]
        return two_parts(self.before[-1], 0)[0], two_parts(self.behind[-1], 0)[1]

    def take(self, got, back):
        if len(self.before) <= self.most:
            self.before.append(got)
            self.behind.append(back)
        else:
            self.opposite = [got, back]

    def pieces(self):
        near = [piece for pair in zip(self.before[1:], self.behind[1:]) for piece in pair]
        return [self.before[0]] + near + [jnp.concatenate(self.opposite, axis=0)]


class Scatter:
    def __init__(self, chunks):
        self.left = len(chunks) // 2 - 1
        self.wire = chunks[0].dtype
        self.total = chunks[0].astype(f32)
        self.behind = [chunk.astype(f32) for chunk in chunks[1:-1:2]]
        self.ahead = [chunk.astype(f32) for chunk in chunks[2:-1:2]]
        self.last = chunks[-1]

    def sends(self):
        if self.last is not None:
            return two_parts(self.last, 0)
        h = self.left - 1
        return self.ahead[h].astype(self.wire), self.behind[h].astype(self.wire)

    def take(self, got, back):
        got, back = got.astype(f32), back.astype(f32)
        h = self.left - 1
        if self.last is not None:
            top, bottom = two_parts(self.ahead[h], 0)
            self.ahead[h] = jnp.concatenate([top + got, bottom], axis=0)
            top, bottom = two_parts(self.behind[h], 0)
            self.behind[h] = jnp.concatenate([top, bottom + back], axis=0)
            self.last = None
            return
        self.left = h
        if h:
            self.ahead[h - 1] = self.ahead[h - 1] + got
            self.behind[h - 1] = self.behind[h - 1] + back
        else:
            self.total = self.total + got + back


def ring_step(items, tokens=(), arrive=()):
    sends = [item.sends() for item in items]
    ways = [one[0] if len(one) == 1 else jnp.concatenate(one, axis=0) for one in zip(*sends)]
    ways = after(ways, list(tokens)) if tokens else lax.optimization_barrier(tuple(ways))
    got, back = after([along(ways[0], 1), along(ways[1], -1)], list(arrive))
    at = [0, 0]
    for item, (ahead, behind) in zip(items, sends):
        ends = [at[0] + ahead.shape[0], at[1] + behind.shape[0]]
        item.take(got[at[0] : ends[0]], back[at[1] : ends[1]])
        at = ends
    return [got, back]


def gather_small(own):
    outer = lax.axis_size("wide") // 2
    return [own] + [along(own, -offset) for offset in ring_offsets(outer)[1:]]


def scatter_small(chunks):
    offsets = ring_offsets(len(chunks))
    total = chunks[0].astype(f32)
    for chunk, offset in zip(chunks[1:], offsets[1:]):
        total = total + along(chunk, offset).astype(f32)
    return total


def gather_rows(own, tokens=(), later=(), single=False):
    size = lax.axis_size("narrow")
    half = own.shape[0] // 2
    [own] = after([own], tokens)
    across = [swap(own, "narrow", k) for k in range(2, size, 2)]
    beside = swap(own, "wide", 1)
    stage_one = across + [beside]
    if later:
        *across, beside = after(across + [beside], later)
    parts, stage_two = [beside], []
    for n, k in enumerate(range(2, size, 2)):
        ends = [swap(across[n][:half], "wide", 1), swap(beside[half:], "narrow", k)]
        parts += ends
        stage_two += ends
    even = jnp.concatenate([own] + across, axis=0)
    other_even = jnp.concatenate(parts, axis=0)
    odd = swap(even, "narrow", 1)
    if single:
        [other_even] = after([other_even], [odd])
    other_odd = swap(other_even, "narrow", 1)
    return ([even, odd], [other_even, other_odd]), (stage_one, stage_two, [odd, other_odd])


def scatter_rows(even, odd, other_even, other_odd, tokens=(), later=()):
    size = lax.axis_size("narrow")
    rows = even.shape[0] // (size // 2)
    half = rows // 2
    other = other_even.astype(f32) + other_odd.astype(f32)
    mine = even.astype(f32) + odd.astype(f32)
    beside_top, beside_bottom = other[:half], other[half:rows]
    out = mine[:rows]
    corners = other[rows:].astype(bf16)
    [corners] = after([corners], tokens)
    spread, stage_two, stage_three = [], [], []
    for n, k in enumerate(range(2, size, 2)):
        at = n * rows
        ends = [
            swap(corners[at : at + half], "wide", 1),
            swap(corners[at + half : at + rows], "narrow", k),
        ]
        stage_two += ends
        beside_bottom = beside_bottom + ends[1].astype(f32)
        at = at + rows
        spread.append(
            jnp.concatenate(
                [mine[at : at + half] + ends[0].astype(f32), mine[at + half : at + rows]], axis=0
            ).astype(bf16)
        )
    spread.append(jnp.concatenate([beside_top, beside_bottom], axis=0).astype(bf16))
    spread = after(spread, later) if later else lax.optimization_barrier(tuple(spread))
    for n, k in enumerate(range(2, size, 2)):
        stage_three.append(swap(spread[n], "narrow", k))
        out = out + stage_three[-1].astype(f32)
    stage_three.append(swap(spread[-1], "wide", 1))
    return out + stage_three[-1].astype(f32), (stage_two, stage_three)


def inverse_rms(values):
    return lax.rsqrt(jnp.mean(values * values, axis=-1, keepdims=True) + epsilon)


def norm_kernel(*refs):
    pieces, gain, out = refs[:-2], refs[-2], refs[-1]
    rows = pieces[0].shape[0]
    step = 32 if rows % 32 == 0 else rows
    for n, piece in enumerate(pieces):

        def part(b, _):
            at = pl.multiple_of(b * step, step)
            values = piece[pl.ds(at, step), :].astype(f32)
            rate = lax.rsqrt(jnp.mean(values * values, axis=-1, keepdims=True) + epsilon)
            to = pl.multiple_of(n * rows + at, step)
            out[pl.ds(to, step), :] = (values * rate * gain[...]).astype(bf16)
            return 0

        lax.fori_loop(0, rows // step, part, 0)


def normed_rows(pieces, gain):
    rows, width = pieces[0].shape
    return pl.pallas_call(
        norm_kernel,
        out_shape=jax.ShapeDtypeStruct((rows * len(pieces), width), bf16),
        cost_estimate=light,
        name="norm",
    )(*pieces, gain.reshape(1, width))


def norm_back(values, rate, gain, grad):
    a = grad * gain
    inner = jnp.mean(a * values, axis=-1, keepdims=True)
    return rate * a - values * (rate * rate * rate) * inner


light = pl.CostEstimate(flops=1024, bytes_accessed=1024, transcendentals=0)


def filter_kernel(base_re, base_im, step_re, step_im, out):
    poles = base_re.shape[0]
    width = out.shape[1]
    for g in range(width // 128 if width % 128 == 0 else 1):
        lanes = pl.ds(g * 128, min(128, width))
        start = tuple(base_re[j, :, lanes] for j in range(poles)) + tuple(
            base_im[j, :, lanes] for j in range(poles)
        )

        def step(b, state):
            total = state[0]
            for j in range(1, poles):
                total = total + state[j]
            out[pl.ds(pl.multiple_of(b * 8, 8), 8), lanes] = total
            new_re, new_im = [], []
            for j in range(poles):
                sr = step_re[j, :, lanes]
                si = step_im[j, :, lanes]
                new_re.append(state[j] * sr - state[poles + j] * si)
                new_im.append(state[j] * si + state[poles + j] * sr)
            return tuple(new_re) + tuple(new_im)

        lax.fori_loop(0, SPAN // 8, step, start)


def filter_taps(base_re, base_im, step_re, step_im):
    width = base_re.shape[2]
    return pl.pallas_call(
        filter_kernel,
        out_shape=jax.ShapeDtypeStruct((SPAN, width), f32),
        cost_estimate=light,
        name="taps",
    )(base_re, base_im, step_re, step_im)


def moment_kernel(grad, step_re, step_im, sum_re, sum_im, mom_re, mom_im):
    poles = step_re.shape[0]
    width = grad.shape[1]
    per = 8
    for g in range(width // 128 if width % 128 == 0 else 1):
        lanes = pl.ds(g * 128, min(128, width))
        for j0 in range(0, poles, per):
            zero = jnp.zeros((8, min(128, width)), f32)

            def step(i, state):
                b = SPAN // 8 - 1 - i
                value = grad[pl.ds(pl.multiple_of(b * 8, 8), 8), lanes]
                new = []
                for n in range(per):
                    sr = step_re[j0 + n, :, lanes]
                    si = step_im[j0 + n, :, lanes]
                    pr, pi, qr, qi = state[4 * n : 4 * n + 4]
                    ur, ui = pr + qr, pi + qi
                    new += [
                        pr * sr - pi * si + value,
                        pr * si + pi * sr,
                        ur * sr - ui * si,
                        ur * si + ui * sr,
                    ]
                return tuple(new)

            state = lax.fori_loop(0, SPAN // 8, step, (zero,) * (4 * per))
            for n in range(per):
                sum_re[j0 + n, :, lanes] = state[4 * n]
                sum_im[j0 + n, :, lanes] = state[4 * n + 1]
                mom_re[j0 + n, :, lanes] = state[4 * n + 2]
                mom_im[j0 + n, :, lanes] = state[4 * n + 3]


SIDE = 512


def product_kernel(a, b, out, turned=None, *, kind):
    if kind == "tn":

        @pl.when(pl.program_id(0) == 0)
        def _():
            turned[...] = a[...].T

        value = nn(turned[...], b[...])
    else:
        value = (nn if kind == "nn" else nt)(a[...], b[...])
    out[...] = value.astype(out.dtype)


def product(a, b, kind, dtype, at=None):
    if kind == "tn":
        depth, rows = a.shape[0], SIDE
        a_spec = pl.BlockSpec((depth, SIDE), lambda i: (0, at))
        scratch = [pltpu.VMEM((SIDE, depth), a.dtype)]
    else:
        rows, depth = a.shape if at is None else (SIDE, a.shape[1])
        a_spec = pl.BlockSpec((rows, depth), lambda i: (at or 0, 0))
        scratch = []
    columns = b.shape[0] if kind == "nt" else b.shape[1]
    side = max(s for s in (512, 384, 256, 128, columns) if columns % s == 0 and s <= 512)
    if kind == "nt":
        b_spec = pl.BlockSpec((side, depth), lambda i: (i, 0))
    else:
        b_spec = pl.BlockSpec((depth, side), lambda i: (0, i))
    return pl.pallas_call(
        partial(product_kernel, kind=kind),
        grid=(columns // side,),
        out_shape=jax.ShapeDtypeStruct((rows, columns), dtype),
        in_specs=[a_spec, b_spec],
        out_specs=pl.BlockSpec((rows, side), lambda i: (0, i)),
        scratch_shapes=scratch,
        cost_estimate=light,
        name="product",
    )(a, b)


def filter_moments(grad, step_re, step_im):
    poles, _, width = step_re.shape
    shape = jax.ShapeDtypeStruct((poles, 8, width), f32)
    return pl.pallas_call(
        moment_kernel,
        out_shape=(shape,) * 4,
        cost_estimate=pl.CostEstimate(
            flops=16 * 15 * SPAN * width, bytes_accessed=4 * SPAN * width, transcendentals=0
        ),
        name="moments",
    )(grad, step_re, step_im)


LIVE, KEEP_ONE, KEEP_TWO = 0, 1, 2


def load_masked(order, proj, table, m_scr):
    pieces, rows, _ = proj.shape
    m_scr[0:8, :] = jnp.zeros_like(m_scr[0:8, :])

    def piece(b, _):
        p = order[b]
        at = pl.multiple_of(b * rows, rows)
        live = table[pl.ds(at, rows), LIVE : LIVE + 1]
        m_scr[pl.ds(pl.multiple_of(at + 8, 8), rows), :] = proj[p] * live
        return 0

    lax.fori_loop(0, pieces, piece, 0)


def short_block(m_scr, taps, table, at):
    window = m_scr[pl.ds(at, BLOCK + 8), :]
    one = table[pl.ds(at, BLOCK), KEEP_ONE : KEEP_ONE + 1]
    two = table[pl.ds(at, BLOCK), KEEP_TWO : KEEP_TWO + 1]
    here = window[8:]
    once = window[7 : BLOCK + 7] * one
    twice = window[6 : BLOCK + 6] * two
    short = taps[0:1, :] * here + taps[1:2, :] * once + taps[2:3, :] * twice
    return short, here, once, twice


def pack_document(source, packed, first, count):
    blocks = source.shape[0] // BLOCK
    for kb in range(LONGEST):
        at = pl.multiple_of(jnp.minimum(first + kb, blocks - 1) * BLOCK, BLOCK)
        inside = (kb < count).astype(f32)
        packed[kb * BLOCK : (kb + 1) * BLOCK, :] = (source[pl.ds(at, BLOCK), :] * inside).astype(bf16)


def place_document(result, target, first, count):
    for kb in range(LONGEST):

        @pl.when(kb < count)
        def _():
            at = pl.multiple_of((first + kb) * BLOCK, BLOCK)
            target[pl.ds(at, BLOCK), :] = result[kb * BLOCK : (kb + 1) * BLOCK, :]


def forward_kernel(
    order, first, count, proj, taps, table, spectrum, fwd, inv, gated, long_out, seen, m_scr, u_scr, q_scr, packed
):
    width = long_out.shape[1]
    pieces, rows, _ = proj.shape
    blocks = long_out.shape[0] // BLOCK
    load_masked(order, proj, table, m_scr)

    def block(n, _):
        at = pl.multiple_of(n * BLOCK, BLOCK)
        short, _, _, _ = short_block(m_scr, taps, table, at)
        q_scr[pl.ds(at, BLOCK), :] = short[:, :width]
        u_scr[pl.ds(at, BLOCK), :] = short[:, width : 2 * width] * short[:, 2 * width :]
        return 0

    lax.fori_loop(0, blocks, block, 0)

    def document(d, _):
        pack_document(u_scr, packed, first[d], count[d])
        both = jnp.dot(fwd[...], packed[...], preferred_element_type=f32)
        seen[d] = both.astype(bf16)
        re, im = both[:FREQ], both[FREQ:]
        hr, hi = spectrum[:FREQ], spectrum[FREQ:]
        answer = jnp.concatenate([re * hr - im * hi, re * hi + im * hr], axis=0).astype(bf16)
        result = jnp.dot(inv[...], answer, preferred_element_type=f32)
        place_document(result, long_out, first[d], count[d])
        return 0

    lax.fori_loop(0, seen.shape[0], document, 0)

    def piece(b, _):
        at = pl.multiple_of(b * rows, rows)
        gated[order[b]] = (q_scr[pl.ds(at, rows), :] * long_out[pl.ds(at, rows), :]).astype(bf16)
        return 0

    lax.fori_loop(0, pieces, piece, 0)


def backward_kernel(
    order, first, count, proj, d_gated, long_out, seen, taps, table, spectrum, fwd, inv,
    dz, d_filter, d_taps, m_scr, dy_scr, k_scr, v_scr, ds_scr, packed, d_spec,
):
    width = long_out.shape[1]
    pieces, rows, _ = proj.shape
    slots = long_out.shape[0]
    blocks = slots // BLOCK
    per_piece = rows // BLOCK
    load_masked(order, proj, table, m_scr)
    ds_scr[slots : slots + 8, :] = jnp.zeros_like(ds_scr[slots : slots + 8, :])

    def block(n, _):
        at = pl.multiple_of(n * BLOCK, BLOCK)
        short, _, _, _ = short_block(m_scr, taps, table, at)
        within = pl.multiple_of((n % per_piece) * BLOCK, BLOCK)
        dg = d_gated[order[n // per_piece], pl.ds(within, BLOCK), :]
        dy_scr[pl.ds(at, BLOCK), :] = dg * short[:, :width]
        ds_scr[pl.ds(at, BLOCK), :width] = dg * long_out[pl.ds(at, BLOCK), :]
        k_scr[pl.ds(at, BLOCK), :] = short[:, width : 2 * width]
        v_scr[pl.ds(at, BLOCK), :] = short[:, 2 * width :]
        return 0

    lax.fori_loop(0, blocks, block, 0)
    d_spec[...] = jnp.zeros_like(d_spec)

    def document(d, _):
        pack_document(dy_scr, packed, first[d], count[d])
        both = jnp.dot(fwd[...], packed[...], preferred_element_type=f32)
        re, im = both[:FREQ], both[FREQ:]
        hr, hi = spectrum[:FREQ], spectrum[FREQ:]
        answer = jnp.concatenate([re * hr + im * hi, im * hr - re * hi], axis=0).astype(bf16)
        result = jnp.dot(inv[...], answer, preferred_element_type=f32)
        ur, ui = seen[d, :FREQ].astype(f32), seen[d, FREQ:].astype(f32)
        d_spec[:FREQ] += re * ur + im * ui
        d_spec[FREQ:] += im * ur - re * ui
        for kb in range(LONGEST):

            @pl.when(kb < count[d])
            def _():
                at = pl.multiple_of((first[d] + kb) * BLOCK, BLOCK)
                du = result[kb * BLOCK : (kb + 1) * BLOCK, :]
                ds_scr[pl.ds(at, BLOCK), width : 2 * width] = du * v_scr[pl.ds(at, BLOCK), :]
                ds_scr[pl.ds(at, BLOCK), 2 * width :] = du * k_scr[pl.ds(at, BLOCK), :]

        return 0

    lax.fori_loop(0, seen.shape[0], document, 0)
    d_filter[...] = jnp.dot(inv[...], d_spec[...].astype(bf16), preferred_element_type=f32)
    d_taps[...] = jnp.zeros_like(d_taps)

    def back(n, _):
        at = pl.multiple_of(n * BLOCK, BLOCK)
        window = m_scr[pl.ds(at, BLOCK + 8), :]
        ahead = ds_scr[pl.ds(at, BLOCK + 8), :]
        one = table[pl.ds(at, BLOCK + 8), KEEP_ONE : KEEP_ONE + 1]
        two = table[pl.ds(at, BLOCK + 8), KEEP_TWO : KEEP_TWO + 1]
        live = table[pl.ds(at, BLOCK), LIVE : LIVE + 1]
        ds = ahead[:BLOCK]
        ahead_one = ahead * one
        ahead_two = ahead * two
        dm = (
            taps[0:1, :] * ds
            + taps[1:2, :] * ahead_one[1 : BLOCK + 1]
            + taps[2:3, :] * ahead_two[2 : BLOCK + 2]
        )
        d_taps[0:1, :] += jnp.sum(window[8:] * ds, axis=0, keepdims=True)
        d_taps[1:2, :] += jnp.sum(window[7 : BLOCK + 7] * ahead_one[:BLOCK], axis=0, keepdims=True)
        d_taps[2:3, :] += jnp.sum(window[6 : BLOCK + 6] * ahead_two[:BLOCK], axis=0, keepdims=True)
        within = pl.multiple_of((n % per_piece) * BLOCK, BLOCK)
        dz[order[n // per_piece], pl.ds(within, BLOCK), :] = (dm * live).astype(bf16)
        return 0

    lax.fori_loop(0, blocks, back, 0)


smem = pl.BlockSpec(memory_space=pltpu.SMEM)
vmem = pl.BlockSpec(memory_space=pltpu.VMEM)


def mixer_forward(order, first, count, proj, taps, table, spectrum, fwd, inv):
    pieces, rows, three = proj.shape
    width = three // 3
    slots = pieces * rows
    docs = first.shape[0]
    return pl.pallas_call(
        forward_kernel,
        out_shape=(
            jax.ShapeDtypeStruct((pieces, rows, width), bf16),
            jax.ShapeDtypeStruct((slots, width), f32),
            jax.ShapeDtypeStruct((docs, 2 * FREQ, width), bf16),
        ),
        in_specs=[smem] * 3 + [vmem] * 6,
        out_specs=(vmem,) * 3,
        scratch_shapes=[
            pltpu.VMEM((slots + 8, three), f32),
            pltpu.VMEM((slots, width), f32),
            pltpu.VMEM((slots, width), f32),
            pltpu.VMEM((SPAN, width), bf16),
        ],
        compiler_params=pltpu.CompilerParams(vmem_limit_bytes=40 * 2**20),
        cost_estimate=light,
        name="mixer_forward",
    )(order, first, count, proj, taps, table, spectrum, fwd, inv)


def mixer_backward(order, first, count, proj, d_gated, long_out, seen, taps, table, spectrum, fwd, inv):
    pieces, rows, three = proj.shape
    width = three // 3
    slots = pieces * rows
    docs = first.shape[0]
    return pl.pallas_call(
        backward_kernel,
        out_shape=(
            jax.ShapeDtypeStruct((pieces, rows, three), bf16),
            jax.ShapeDtypeStruct((SPAN, width), f32),
            jax.ShapeDtypeStruct((8, three), f32),
        ),
        in_specs=[smem] * 3 + [vmem] * 9,
        out_specs=(vmem,) * 3,
        scratch_shapes=[
            pltpu.VMEM((slots + 8, three), f32),
            pltpu.VMEM((slots, width), f32),
            pltpu.VMEM((slots, width), f32),
            pltpu.VMEM((slots, width), f32),
            pltpu.VMEM((slots + 8, three), f32),
            pltpu.VMEM((SPAN, width), bf16),
            pltpu.VMEM((2 * FREQ, width), f32),
        ],
        compiler_params=pltpu.CompilerParams(vmem_limit_bytes=48 * 2**20),
        cost_estimate=light,
        name="mixer_backward",
    )(order, first, count, proj, d_gated, long_out, seen, taps, table, spectrum, fwd, inv)


def layout(doc_blocks, doc_pad, slots):
    block_ends = jnp.cumsum(doc_blocks) * BLOCK
    starts = block_ends - doc_blocks * BLOCK
    places = jnp.arange(slots, dtype=jnp.int32)
    living = (places[None, :] >= starts[:, None]) & (
        places[None, :] < (block_ends - doc_pad)[:, None]
    )
    live = jnp.sum(living.astype(f32), axis=0)
    opening = jnp.sum((places[None, :] == starts[:, None]).astype(f32), axis=0)
    one = 1.0 - opening
    one = one * (places > 0)
    two = one * jnp.concatenate([jnp.zeros((1,), f32), one[:-1]])
    table = jnp.stack([live, one, two], axis=1)
    table = jnp.concatenate([table, jnp.zeros((8, 3), f32)], axis=0)
    return table, starts // BLOCK


def picked(index, count, values):
    hot = index[:, None] == jnp.arange(count)[None, :]
    shape = hot.shape + (1,) * (values.ndim - 1)
    return jnp.sum(jnp.where(hot.reshape(shape), values[None], 0), axis=1)


def body(
    tokens, w_in, w_out, gain_one, short_kernel, decay_rate, pole_angle, residue,
    gain_two, w_gate, w_up, w_down, doc_blocks, doc_pad, cotangent,
):
    wide, narrow = lax.axis_size("wide"), lax.axis_size("narrow")
    wide_at, narrow_at = lax.axis_index("wide"), lax.axis_index("narrow")
    outer = wide // 2
    _, local_rows, width = tokens.shape
    slots = local_rows * narrow
    even = slots // 2
    source = tokens[0].astype(f32)
    upstream_low = cotangent[0]
    poles = decay_rate.shape[1]
    own = w_in.shape[2]
    channels = own * outer
    hidden_units = w_gate.shape[1] * outer

    ring = np.array(ring_of(outer))
    ring_place = np.argsort(ring)
    tour = picked((wide_at // 2)[None], outer, jnp.asarray(ring_place, jnp.int32))[0]
    piece_places = (tour + jnp.asarray(ring_offsets(outer), jnp.int32)) % outer
    piece_outer = picked(piece_places, outer, jnp.asarray(ring, jnp.int32))
    sides = jnp.arange(2) ^ (wide_at % 2)
    offsets = list(range(0, narrow, 2)) + list(range(1, narrow, 2))
    place_of = np.argsort(np.array(offsets))
    order = picked(jnp.arange(narrow) ^ narrow_at, narrow, jnp.asarray(place_of, jnp.int32))
    narrow_of = jnp.asarray(offsets, jnp.int32) ^ narrow_at

    small = jnp.concatenate(
        [
            short_kernel.reshape(9, own),
            decay_rate.T,
            pole_angle.T,
            residue.T,
            gain_one[None],
            gain_two[None],
        ],
        axis=0,
    )
    small_pieces = gather_small(small)
    small_all = jnp.concatenate(small_pieces, axis=1)
    (first_own, first_other), first_stages = gather_rows(tokens[0], small_pieces[1:])
    gains = small_all[small.shape[0] - 2 :].reshape(2, outer, own)
    gains = jnp.stack([gains, swap(gains, "wide", 1)])
    gains = jnp.stack([gains] + [swap(gains, "narrow", k) for k in range(2, narrow, 2)])
    gains = jnp.concatenate([gains, swap(gains, "narrow", 1)], axis=0).astype(f32)
    gains = picked(order, narrow, gains).transpose(1, 3, 0, 2, 4)
    gains = picked(sides, 2, gains).transpose(1, 0, 2, 3, 4)
    hot = piece_outer[None, :] == jnp.arange(outer)[:, None]
    gains = jnp.sum(jnp.where(hot[:, :, None, None, None, None], gains[None], 0), axis=1)
    gain_all = gains.transpose(3, 0, 1, 2, 4).reshape(2, width)
    gain_first, gain_last = gain_all[0], gain_all[1]

    def place_gain(values):
        values = values.reshape(2, outer, 2, narrow, own).transpose(1, 2, 3, 0, 4)
        values = picked(piece_outer, outer, values).transpose(1, 0, 2, 3, 4)
        values = picked(sides, 2, values).transpose(2, 0, 1, 3, 4)
        values = picked(narrow_of, narrow, values)
        total = values[: narrow // 2] + swap(values[narrow // 2 :], "narrow", 1)
        summed = total[0]
        for k in range(1, narrow // 2):
            summed = summed + swap(total[k], "narrow", 2 * k)
        summed = summed[0] + swap(summed[1], "wide", 1)
        return summed

    documents = jnp.concatenate([doc_blocks, doc_pad], axis=0)
    [documents] = after([documents], small_pieces[1:])
    documents = (documents, swap(documents, "wide", 1))
    tables = [layout(rules[0], rules[1], slots) for rules in documents]

    shards = [w_in.transpose(0, 2, 1).reshape(3 * own, width), w_out, w_down.T, w_gate.T, w_up.T]
    weights = [Gather(shard) for shard in shards]
    in_all, out_all, down_all, gate_all, up_all = weights
    steps = outer // 2
    last = []
    for at in range(steps):
        last = ring_step([in_all, out_all], last)

    def normed(pieces):
        values = jnp.concatenate(pieces, axis=0).astype(f32)
        return (values * inverse_rms(values) * gain_first).astype(bf16)

    rows_first = lax.optimization_barrier([normed(first_own), normed(first_other)])
    rate_first = inverse_rms(source)
    (upstream_own, upstream_other), upstream_stages = gather_rows(
        upstream_low, first_stages[2], (), True
    )

    matrix = transform()
    fwd = jnp.asarray(matrix, bf16)
    inv = jnp.asarray(matrix.T / SPAN, bf16)

    block = small_all.astype(f32)
    taps = block[:9].reshape(3, 3 * channels)
    taps = jnp.concatenate([taps, jnp.zeros((5, 3 * channels), f32)], axis=0)
    decay = block[9 : 9 + poles][:, None, :]
    angle = block[9 + poles : 9 + 2 * poles][:, None, :]
    res_re = block[9 + 2 * poles : 9 + 3 * poles][:, None, :]
    res_im = -block[9 + 3 * poles : 9 + 4 * poles][:, None, :]
    lag = jnp.arange(8, dtype=f32)[None, :, None]
    fade = jnp.exp(-decay * lag)
    power_re, power_im = fade * jnp.cos(angle * lag), fade * jnp.sin(angle * lag)
    fade_step = jnp.exp(-decay * 8.0)
    step_re = jnp.broadcast_to(fade_step * jnp.cos(angle * 8.0), power_re.shape)
    step_im = jnp.broadcast_to(fade_step * jnp.sin(angle * 8.0), power_re.shape)
    filt = filter_taps(
        res_re * power_re - res_im * power_im,
        res_re * power_im + res_im * power_re,
        step_re,
        step_im,
    )
    spectrum = lax.dot_general(
        jnp.asarray(matrix),
        filt,
        (((1,), (0,)), ((), ())),
        precision=lax.Precision.HIGHEST,
        preferred_element_type=f32,
    )
    res_re, res_im = res_re[:, 0], -res_im[:, 0]

    in_pieces = [piece.reshape(3, own, width) for piece in in_all.pieces()]
    in_all = jnp.concatenate(in_pieces, axis=1).reshape(3 * channels, width)
    mixed = []
    for r in range(2):
        table, first = tables[r]
        proj = nt(rows_first[r], in_all).reshape(narrow, local_rows, 3 * channels)
        gated, long_out, seen = mixer_forward(
            order, first, documents[r][0], proj, taps, table, spectrum, fwd, inv
        )
        mixed.append((proj, gated.reshape(slots, channels), long_out, seen))
    out_last = last
    out_all = jnp.concatenate(out_all.pieces(), axis=0)
    parts = [slice(0, even), slice(even, slots)]
    ready = [mixed[0][1], after([mixed[1][1]], upstream_stages[0])[0]]
    odds = [nn(ready[r][parts[1]], out_all).astype(bf16) for r in range(2)]
    cores = [swap(odd, "narrow", 1) for odd in odds]
    for at in range(steps - 1):
        last = ring_step([down_all, gate_all], last, odds)
    last_two = last
    for at in range(steps - 1):
        last_two = ring_step([up_all] if at else [down_all, up_all], last_two)
    ready = after([mixed[0][1], mixed[1][1]], upstream_stages[0])
    evens = [nn(ready[r][parts[0]], out_all).astype(bf16) for r in range(2)]
    mixer_out, stages = scatter_rows(
        evens[0], cores[0], evens[1], cores[1], upstream_stages[1] + last
    )
    middle = source + mixer_out
    rate_last = inverse_rms(middle)
    rows_upstream = jnp.concatenate(upstream_own + upstream_other, axis=0)
    low_second = (middle * rate_last * gain_last).astype(bf16)
    (second_own, second_other), second_stages = gather_rows(low_second, last_two + upstream_stages[2])
    rows_second = jnp.concatenate(second_own + second_other, axis=0)
    last = ring_step([gate_all, up_all], last_two, second_stages[1])

    down_all, gate_all = [jnp.concatenate(w.pieces(), axis=0) for w in (down_all, gate_all)]
    up_all = jnp.concatenate(up_all.pieces(), axis=0)
    d_hidden = nt(down_all, rows_upstream)
    gate_pre = nt(gate_all, rows_second)
    up_pre = nt(up_all, rows_second)
    sig = jax.nn.sigmoid(gate_pre)
    silu = gate_pre * sig
    hidden = (silu * up_pre).astype(bf16)
    d_gate = (d_hidden * up_pre * sig * (1.0 + gate_pre * (1.0 - sig))).astype(bf16)
    d_up = (d_hidden * silu).astype(bf16)
    grad_down = product(hidden, rows_upstream, "nn", bf16)
    d_gate, d_up = after([d_gate, d_up], [grad_down])
    parts = [slice(p, p + even) for p in range(0, 2 * slots, even)]

    def second_share(n):
        p = parts[n]
        return (tn(d_gate[:, p], gate_all) + tn(d_up[:, p], up_all)).astype(bf16)

    odds = [second_share(n) for n in (1, 3)]
    cores = [swap(odd, "narrow", 1) for odd in odds]
    evens = [second_share(0), second_share(2)]
    d_second, stages = scatter_rows(evens[0], cores[0], evens[1], cores[1])
    upstream = upstream_low.astype(f32)
    d_middle = upstream + norm_back(middle, rate_last, gain_last, d_second)
    (middle_own, middle_other), middle_stages = gather_rows(d_middle.astype(bf16))
    rows_dmiddle = [jnp.concatenate(middle_own, axis=0), jnp.concatenate(middle_other, axis=0)]
    grads = [Scatter(jnp.split(grad_down, outer, axis=0))]
    [d_gate] = after([d_gate], cores + evens)
    grad_gate = product(d_gate, rows_second, "nn", bf16)
    [d_up] = after([d_up], stages[0] + [grad_gate])
    grad_up = product(d_up, rows_second, "nn", bf16)
    [hidden] = after([hidden], [grad_up])
    down_shares = [product(hidden, down_all, "tn", bf16, n) for n in (0, 1)]
    down_shares += [product(hidden, down_all, "tn", bf16, n) for n in (2, 3)]
    pair = [Scatter(jnp.split(grad, outer, axis=0)) for grad in (grad_gate, grad_up)]
    grads += pair
    last = ring_step(grads, (), middle_stages[1])
    down_shares = after(down_shares, middle_stages[1])
    down_cores = [swap(down_shares[n], "narrow", 1) for n in (1, 3)]
    down_out, down_stages = scatter_rows(
        down_shares[0], down_cores[0], down_shares[2], down_cores[1]
    )
    block_output = (middle + down_out).astype(bf16)
    grad_gain_two = jnp.sum(d_second * middle * rate_last, axis=0)

    grad_out = sum(tn(mixed[r][1], rows_dmiddle[r]) for r in range(2)).astype(bf16)
    halves = (slice(0, even), slice(even, slots))
    shares, d_rows, grad_gain_one, d_filter, d_taps = [None, None], [None, None], 0.0, 0.0, 0.0
    for r in range(2):
        proj, gated, long_out, seen = mixed[r]
        table, first = tables[r]
        d_gated = nt(rows_dmiddle[r], out_all).reshape(narrow, local_rows, channels)
        if r == 1:
            [d_gated] = after([d_gated], [grad_out, *shares[0], *down_stages[0]])
        dz, d_filter_row, d_taps_row = mixer_backward(
            order, first, documents[r][0], proj, d_gated, long_out, seen, taps, table,
            spectrum, fwd, inv,
        )
        d_rows[r] = dz.reshape(slots, 3 * channels)
        d_filter, d_taps = d_filter + d_filter_row, d_taps + d_taps_row
        if r == 0:
            shares[r] = [nn(d_rows[r][p], in_all).astype(bf16) for p in halves]
    [ready] = after([d_rows[1]], down_stages[1])
    odd = nn(ready[halves[1]], in_all).astype(bf16)
    cores = [swap(shares[0][1], "narrow", 1), swap(odd, "narrow", 1)]
    ready = after(d_rows, [odd])
    grad_in = sum(tn(ready[r], rows_first[r]) for r in range(2)).astype(bf16)
    for at in range(1, steps):
        last = ring_step(grads, last, [grad_in])
    [ready] = after([d_rows[1]], [grad_in] + cores)
    shares[1] = [nn(ready[halves[0]], in_all).astype(bf16), odd]
    d_normed, stages = scatter_rows(shares[0][0], cores[0], shares[1][0], cores[1])
    input_grad = (d_middle + norm_back(source, rate_first, gain_first, d_normed)).astype(bf16)
    for r in range(2):
        for n, share in enumerate(after(shares[r], [shares[1][0]])):
            rows = rows_first[r][n * even : (n + 1) * even]
            grad_gain_one = grad_gain_one + jnp.sum(share.astype(f32) * rows.astype(f32), axis=0)
    chunks = grad_in.reshape(3, outer, own, width)
    in_sum = Scatter([chunks[:, j].reshape(3 * own, width) for j in range(outer)])
    out_sum = Scatter(jnp.split(grad_out, outer, axis=0))
    last = ring_step([in_sum, out_sum], last, stages[0])
    d_filter, *_ = after([d_filter], last + stages[0])
    gain_grads = jnp.stack([grad_gain_one / gain_first, grad_gain_two])
    [gain_grads] = after([gain_grads], stages[0])
    sum_re, sum_im, mom_re, mom_im = filter_moments(d_filter, step_re, step_im)
    full_re = lag * sum_re + 8.0 * mom_re
    full_im = lag * sum_im + 8.0 * mom_im
    grad_re = jnp.sum(power_re * sum_re - power_im * sum_im, axis=1)
    grad_im = jnp.sum(power_re * sum_im + power_im * sum_re, axis=1)
    lag_re = jnp.sum(power_re * full_re - power_im * full_im, axis=1)
    lag_im = jnp.sum(power_re * full_im + power_im * full_re, axis=1)
    small_grad = jnp.concatenate(
        [
            d_taps[:3].reshape(9, channels),
            -(res_re * lag_re + res_im * lag_im),
            res_im * lag_re - res_re * lag_im,
            grad_re,
            grad_im,
        ],
        axis=0,
    ).astype(bf16)
    gain_sums = place_gain(gain_grads).transpose(1, 0, 2).reshape(2, channels)
    gain_high = gain_sums.astype(bf16)
    gain_low = (gain_sums - gain_high.astype(f32)).astype(bf16)
    small_grad = jnp.concatenate([small_grad, gain_high, gain_low], axis=0)
    [small_grad] = after([small_grad], stages[1])
    small_share = scatter_small(jnp.split(small_grad, outer, axis=1))
    gain_share = small_share[-4:-2] + small_share[-2:]
    for at in range(1, steps):
        last = ring_step([in_sum, out_sum], last, [small_share])

    at = 9 + poles
    return (
        block_output[None],
        input_grad[None],
        in_sum.total.reshape(3, own, width).transpose(0, 2, 1),
        out_sum.total,
        gain_share[0],
        small_share[:9].reshape(3, 3, own),
        small_share[9:at].T,
        small_share[at : at + poles].T,
        small_share[at + poles : at + 3 * poles].T,
        gain_share[1],
        grads[1].total.T,
        grads[2].total.T,
        grads[0].total.T,
    )


def solution(mesh):
    both = ("wide", "narrow")
    return jax.shard_map(
        body,
        mesh=mesh,
        in_specs=(
            P("wide", "narrow", None),
            P(None, None, both),
            P(both, None),
            P(both),
            P(None, None, both),
            P(both, None),
            P(both, None),
            P(both, None),
            P(both),
            P(None, both),
            P(None, both),
            P(None, both),
            P("wide", None),
            P("wide", None),
            P("wide", "narrow", None),
        ),
        out_specs=(
            P("wide", "narrow", None),
            P("wide", "narrow", None),
            P(None, None, both),
            P(both, None),
            P(both),
            P(None, None, both),
            P(both, None),
            P(both, None),
            P(both, None),
            P(both),
            P(None, both),
            P(None, both),
            P(None, both),
        ),
        check_vma=False,
    )
```

```python
from functools import partial

import jax
import jax.numpy as jnp
import numpy as np
from jax import lax
from jax.experimental import pallas as pl
from jax.experimental.pallas import tpu as pltpu
from jax.sharding import PartitionSpec as P

BLOCK = 128
LONGEST = 4
SPAN = LONGEST * BLOCK
FREQ = SPAN

epsilon = 1e-06
bf16 = jnp.bfloat16
f32 = jnp.float32


def transform():
    k = np.arange(FREQ)[:, None] * 2 + 1
    t = np.arange(SPAN)[None, :]
    turn = (k * t % (4 * SPAN)) * (2 * np.pi / (4 * SPAN))
    return np.concatenate([np.cos(turn), -np.sin(turn)], axis=0).astype(np.float32)


def nn(a, b):
    return lax.dot_general(a, b, (((1,), (0,)), ((), ())), preferred_element_type=f32)


def nt(a, b):
    return lax.dot_general(a, b, (((1,), (1,)), ((), ())), preferred_element_type=f32)


def tn(a, b):
    return lax.dot_general(a, b, (((0,), (0,)), ((), ())), preferred_element_type=f32)


def swap(values, axis, shift):
    size = lax.axis_size(axis)
    return lax.ppermute(values, axis, [(i, i ^ shift) for i in range(size)])


def after(values, tokens):
    if not tokens:
        return values
    joined = lax.optimization_barrier(tuple(values) + tuple(tokens))
    return list(joined[: len(values)])


def ring_of(size):
    return list(range(0, size, 2)) + list(range(size - 1, 0, -2))


def along(values, step):
    outer = lax.axis_size("wide") // 2
    ring = ring_of(outer)
    pairs = [
        (ring[p] * 2 + side, ring[(p + step) % outer] * 2 + side)
        for p in range(outer)
        for side in range(2)
    ]
    return lax.ppermute(values, "wide", pairs)


def ring_offsets(outer):
    near = [sign * h for h in range(1, outer // 2) for sign in (-1, 1)]
    return [0] + near + [outer // 2]


def cut_of(rows):
    cut = (rows // 2 + 15) // 16 * 16
    return cut if cut < rows else rows // 2


def two_parts(values, axis):
    cut = cut_of(values.shape[axis])
    return (
        lax.slice_in_dim(values, 0, cut, axis=axis),
        lax.slice_in_dim(values, cut, values.shape[axis], axis=axis),
    )


class Gather:
    def __init__(self, own):
        self.most = lax.axis_size("wide") // 4 - 1
        self.before, self.behind, self.opposite = [own], [own], []

    def sends(self):
        if len(self.before) <= self.most:
            return self.before[-1], self.behind[-1]
        return two_parts(self.before[-1], 0)[0], two_parts(self.behind[-1], 0)[1]

    def take(self, got, back):
        if len(self.before) <= self.most:
            self.before.append(got)
            self.behind.append(back)
        else:
            self.opposite = [got, back]

    def pieces(self):
        near = [piece for pair in zip(self.before[1:], self.behind[1:]) for piece in pair]
        return [self.before[0]] + near + [jnp.concatenate(self.opposite, axis=0)]


class Scatter:
    def __init__(self, chunks):
        self.left = len(chunks) // 2 - 1
        self.wire = chunks[0].dtype
        self.total = chunks[0].astype(f32)
        self.behind = [chunk.astype(f32) for chunk in chunks[1:-1:2]]
        self.ahead = [chunk.astype(f32) for chunk in chunks[2:-1:2]]
        self.last = chunks[-1]

    def sends(self):
        if self.last is not None:
            return two_parts(self.last, 0)
        h = self.left - 1
        return self.ahead[h].astype(self.wire), self.behind[h].astype(self.wire)

    def take(self, got, back):
        got, back = got.astype(f32), back.astype(f32)
        h = self.left - 1
        if self.last is not None:
            top, bottom = two_parts(self.ahead[h], 0)
            self.ahead[h] = jnp.concatenate([top + got, bottom], axis=0)
            top, bottom = two_parts(self.behind[h], 0)
            self.behind[h] = jnp.concatenate([top, bottom + back], axis=0)
            self.last = None
            return
        self.left = h
        if h:
            self.ahead[h - 1] = self.ahead[h - 1] + got
            self.behind[h - 1] = self.behind[h - 1] + back
        else:
            self.total = self.total + got + back


def ring_step(items, tokens=(), arrive=()):
    sends = [item.sends() for item in items]
    ways = [one[0] if len(one) == 1 else jnp.concatenate(one, axis=0) for one in zip(*sends)]
    ways = after(ways, list(tokens)) if tokens else lax.optimization_barrier(tuple(ways))
    got, back = after([along(ways[0], 1), along(ways[1], -1)], list(arrive))
    at = [0, 0]
    for item, (ahead, behind) in zip(items, sends):
        ends = [at[0] + ahead.shape[0], at[1] + behind.shape[0]]
        item.take(got[at[0] : ends[0]], back[at[1] : ends[1]])
        at = ends
    return [got, back]


def gather_small(own):
    outer = lax.axis_size("wide") // 2
    return [own] + [along(own, -offset) for offset in ring_offsets(outer)[1:]]


def scatter_small(chunks):
    offsets = ring_offsets(len(chunks))
    total = chunks[0].astype(f32)
    for chunk, offset in zip(chunks[1:], offsets[1:]):
        total = total + along(chunk, offset).astype(f32)
    return total


def gather_rows(own, tokens=(), later=(), single=False):
    size = lax.axis_size("narrow")
    half = own.shape[0] // 2
    [own] = after([own], tokens)
    across = [swap(own, "narrow", k) for k in range(2, size, 2)]
    beside = swap(own, "wide", 1)
    stage_one = across + [beside]
    if later:
        *across, beside = after(across + [beside], later)
    parts, stage_two = [beside], []
    for n, k in enumerate(range(2, size, 2)):
        ends = [swap(across[n][:half], "wide", 1), swap(beside[half:], "narrow", k)]
        parts += ends
        stage_two += ends
    even = jnp.concatenate([own] + across, axis=0)
    other_even = jnp.concatenate(parts, axis=0)
    odd = swap(even, "narrow", 1)
    if single:
        [other_even] = after([other_even], [odd])
    other_odd = swap(other_even, "narrow", 1)
    return ([even, odd], [other_even, other_odd]), (stage_one, stage_two, [odd, other_odd])


def scatter_rows(even, odd, other_even, other_odd, tokens=(), later=()):
    size = lax.axis_size("narrow")
    rows = even.shape[0] // (size // 2)
    half = rows // 2
    other = other_even.astype(f32) + other_odd.astype(f32)
    mine = even.astype(f32) + odd.astype(f32)
    beside_top, beside_bottom = other[:half], other[half:rows]
    out = mine[:rows]
    corners = other[rows:].astype(bf16)
    [corners] = after([corners], tokens)
    spread, stage_two, stage_three = [], [], []
    for n, k in enumerate(range(2, size, 2)):
        at = n * rows
        ends = [
            swap(corners[at : at + half], "wide", 1),
            swap(corners[at + half : at + rows], "narrow", k),
        ]
        stage_two += ends
        beside_bottom = beside_bottom + ends[1].astype(f32)
        at = at + rows
        spread.append(
            jnp.concatenate(
                [mine[at : at + half] + ends[0].astype(f32), mine[at + half : at + rows]], axis=0
            ).astype(bf16)
        )
    spread.append(jnp.concatenate([beside_top, beside_bottom], axis=0).astype(bf16))
    spread = after(spread, later) if later else lax.optimization_barrier(tuple(spread))
    for n, k in enumerate(range(2, size, 2)):
        stage_three.append(swap(spread[n], "narrow", k))
        out = out + stage_three[-1].astype(f32)
    stage_three.append(swap(spread[-1], "wide", 1))
    return out + stage_three[-1].astype(f32), (stage_two, stage_three)


def inverse_rms(values):
    return lax.rsqrt(jnp.mean(values * values, axis=-1, keepdims=True) + epsilon)


def norm_kernel(*refs):
    pieces, gain, out = refs[:-2], refs[-2], refs[-1]
    rows = pieces[0].shape[0]
    step = 32 if rows % 32 == 0 else rows
    for n, piece in enumerate(pieces):

        def part(b, _):
            at = pl.multiple_of(b * step, step)
            values = piece[pl.ds(at, step), :].astype(f32)
            rate = lax.rsqrt(jnp.mean(values * values, axis=-1, keepdims=True) + epsilon)
            to = pl.multiple_of(n * rows + at, step)
            out[pl.ds(to, step), :] = (values * rate * gain[...]).astype(bf16)
            return 0

        lax.fori_loop(0, rows // step, part, 0)


def normed_rows(pieces, gain):
    rows, width = pieces[0].shape
    return pl.pallas_call(
        norm_kernel,
        out_shape=jax.ShapeDtypeStruct((rows * len(pieces), width), bf16),
        cost_estimate=light,
        name="norm",
    )(*pieces, gain.reshape(1, width))


def norm_back(values, rate, gain, grad):
    a = grad * gain
    inner = jnp.mean(a * values, axis=-1, keepdims=True)
    return rate * a - values * (rate * rate * rate) * inner


light = pl.CostEstimate(flops=1024, bytes_accessed=1024, transcendentals=0)


def filter_kernel(base_re, base_im, step_re, step_im, out):
    poles = base_re.shape[0]
    width = out.shape[1]
    for g in range(width // 128 if width % 128 == 0 else 1):
        lanes = pl.ds(g * 128, min(128, width))
        start = tuple(base_re[j, :, lanes] for j in range(poles)) + tuple(
            base_im[j, :, lanes] for j in range(poles)
        )

        def step(b, state):
            total = state[0]
            for j in range(1, poles):
                total = total + state[j]
            out[pl.ds(pl.multiple_of(b * 8, 8), 8), lanes] = total
            new_re, new_im = [], []
            for j in range(poles):
                sr = step_re[j, :, lanes]
                si = step_im[j, :, lanes]
                new_re.append(state[j] * sr - state[poles + j] * si)
                new_im.append(state[j] * si + state[poles + j] * sr)
            return tuple(new_re) + tuple(new_im)

        lax.fori_loop(0, SPAN // 8, step, start)


def filter_taps(base_re, base_im, step_re, step_im):
    width = base_re.shape[2]
    return pl.pallas_call(
        filter_kernel,
        out_shape=jax.ShapeDtypeStruct((SPAN, width), f32),
        cost_estimate=light,
        name="taps",
    )(base_re, base_im, step_re, step_im)


def moment_kernel(grad, step_re, step_im, sum_re, sum_im, mom_re, mom_im):
    poles = step_re.shape[0]
    width = grad.shape[1]
    per = 8
    for g in range(width // 128 if width % 128 == 0 else 1):
        lanes = pl.ds(g * 128, min(128, width))
        for j0 in range(0, poles, per):
            zero = jnp.zeros((8, min(128, width)), f32)

            def step(i, state):
                b = SPAN // 8 - 1 - i
                value = grad[pl.ds(pl.multiple_of(b * 8, 8), 8), lanes]
                new = []
                for n in range(per):
                    sr = step_re[j0 + n, :, lanes]
                    si = step_im[j0 + n, :, lanes]
                    pr, pi, qr, qi = state[4 * n : 4 * n + 4]
                    ur, ui = pr + qr, pi + qi
                    new += [
                        pr * sr - pi * si + value,
                        pr * si + pi * sr,
                        ur * sr - ui * si,
                        ur * si + ui * sr,
                    ]
                return tuple(new)

            state = lax.fori_loop(0, SPAN // 8, step, (zero,) * (4 * per))
            for n in range(per):
                sum_re[j0 + n, :, lanes] = state[4 * n]
                sum_im[j0 + n, :, lanes] = state[4 * n + 1]
                mom_re[j0 + n, :, lanes] = state[4 * n + 2]
                mom_im[j0 + n, :, lanes] = state[4 * n + 3]


SIDE = 512


def product_kernel(a, b, out, turned=None, *, kind):
    if kind == "tn":

        @pl.when(pl.program_id(0) == 0)
        def _():
            turned[...] = a[...].T

        value = nn(turned[...], b[...])
    else:
        value = (nn if kind == "nn" else nt)(a[...], b[...])
    out[...] = value.astype(out.dtype)


def product(a, b, kind, dtype, at=None):
    if kind == "tn":
        depth, rows = a.shape[0], SIDE
        a_spec = pl.BlockSpec((depth, SIDE), lambda i: (0, at))
        scratch = [pltpu.VMEM((SIDE, depth), a.dtype)]
    else:
        rows, depth = a.shape if at is None else (SIDE, a.shape[1])
        a_spec = pl.BlockSpec((rows, depth), lambda i: (at or 0, 0))
        scratch = []
    columns = b.shape[0] if kind == "nt" else b.shape[1]
    side = max(s for s in (512, 384, 256, 128, columns) if columns % s == 0 and s <= 512)
    if kind == "nt":
        b_spec = pl.BlockSpec((side, depth), lambda i: (i, 0))
    else:
        b_spec = pl.BlockSpec((depth, side), lambda i: (0, i))
    return pl.pallas_call(
        partial(product_kernel, kind=kind),
        grid=(columns // side,),
        out_shape=jax.ShapeDtypeStruct((rows, columns), dtype),
        in_specs=[a_spec, b_spec],
        out_specs=pl.BlockSpec((rows, side), lambda i: (0, i)),
        scratch_shapes=scratch,
        cost_estimate=light,
        name="product",
    )(a, b)


def filter_moments(grad, step_re, step_im):
    poles, _, width = step_re.shape
    shape = jax.ShapeDtypeStruct((poles, 8, width), f32)
    return pl.pallas_call(
        moment_kernel,
        out_shape=(shape,) * 4,
        cost_estimate=pl.CostEstimate(
            flops=16 * 15 * SPAN * width, bytes_accessed=4 * SPAN * width, transcendentals=0
        ),
        name="moments",
    )(grad, step_re, step_im)


LIVE, KEEP_ONE, KEEP_TWO = 0, 1, 2


def load_masked(order, proj, table, m_scr):
    pieces, rows, _ = proj.shape
    m_scr[0:8, :] = jnp.zeros_like(m_scr[0:8, :])

    def piece(b, _):
        p = order[b]
        at = pl.multiple_of(b * rows, rows)
        live = table[pl.ds(at, rows), LIVE : LIVE + 1]
        m_scr[pl.ds(pl.multiple_of(at + 8, 8), rows), :] = proj[p] * live
        return 0

    lax.fori_loop(0, pieces, piece, 0)


def short_block(m_scr, taps, table, at):
    window = m_scr[pl.ds(at, BLOCK + 8), :]
    one = table[pl.ds(at, BLOCK), KEEP_ONE : KEEP_ONE + 1]
    two = table[pl.ds(at, BLOCK), KEEP_TWO : KEEP_TWO + 1]
    here = window[8:]
    once = window[7 : BLOCK + 7] * one
    twice = window[6 : BLOCK + 6] * two
    short = taps[0:1, :] * here + taps[1:2, :] * once + taps[2:3, :] * twice
    return short, here, once, twice


def pack_document(source, packed, first, count):
    blocks = source.shape[0] // BLOCK
    for kb in range(LONGEST):
        at = pl.multiple_of(jnp.minimum(first + kb, blocks - 1) * BLOCK, BLOCK)
        inside = (kb < count).astype(f32)
        packed[kb * BLOCK : (kb + 1) * BLOCK, :] = (source[pl.ds(at, BLOCK), :] * inside).astype(bf16)


def place_document(result, target, first, count):
    for kb in range(LONGEST):

        @pl.when(kb < count)
        def _():
            at = pl.multiple_of((first + kb) * BLOCK, BLOCK)
            target[pl.ds(at, BLOCK), :] = result[kb * BLOCK : (kb + 1) * BLOCK, :]


def forward_kernel(
    order, first, count, proj, taps, table, spectrum, fwd, inv, gated, long_out, seen, m_scr, u_scr, q_scr, packed
):
    width = long_out.shape[1]
    pieces, rows, _ = proj.shape
    blocks = long_out.shape[0] // BLOCK
    load_masked(order, proj, table, m_scr)

    def block(n, _):
        at = pl.multiple_of(n * BLOCK, BLOCK)
        short, _, _, _ = short_block(m_scr, taps, table, at)
        q_scr[pl.ds(at, BLOCK), :] = short[:, :width]
        u_scr[pl.ds(at, BLOCK), :] = short[:, width : 2 * width] * short[:, 2 * width :]
        return 0

    lax.fori_loop(0, blocks, block, 0)

    def document(d, _):
        pack_document(u_scr, packed, first[d], count[d])
        both = jnp.dot(fwd[...], packed[...], preferred_element_type=f32)
        seen[d] = both.astype(bf16)
        re, im = both[:FREQ], both[FREQ:]
        hr, hi = spectrum[:FREQ], spectrum[FREQ:]
        answer = jnp.concatenate([re * hr - im * hi, re * hi + im * hr], axis=0).astype(bf16)
        result = jnp.dot(inv[...], answer, preferred_element_type=f32)
        place_document(result, long_out, first[d], count[d])
        return 0

    lax.fori_loop(0, seen.shape[0], document, 0)

    def piece(b, _):
        at = pl.multiple_of(b * rows, rows)
        gated[order[b]] = (q_scr[pl.ds(at, rows), :] * long_out[pl.ds(at, rows), :]).astype(bf16)
        return 0

    lax.fori_loop(0, pieces, piece, 0)


def backward_kernel(
    order, first, count, proj, d_gated, long_out, seen, taps, table, spectrum, fwd, inv,
    dz, d_filter, d_taps, m_scr, dy_scr, k_scr, v_scr, ds_scr, packed, d_spec,
):
    width = long_out.shape[1]
    pieces, rows, _ = proj.shape
    slots = long_out.shape[0]
    blocks = slots // BLOCK
    per_piece = rows // BLOCK
    load_masked(order, proj, table, m_scr)
    ds_scr[slots : slots + 8, :] = jnp.zeros_like(ds_scr[slots : slots + 8, :])

    def block(n, _):
        at = pl.multiple_of(n * BLOCK, BLOCK)
        short, _, _, _ = short_block(m_scr, taps, table, at)
        within = pl.multiple_of((n % per_piece) * BLOCK, BLOCK)
        dg = d_gated[order[n // per_piece], pl.ds(within, BLOCK), :]
        dy_scr[pl.ds(at, BLOCK), :] = dg * short[:, :width]
        ds_scr[pl.ds(at, BLOCK), :width] = dg * long_out[pl.ds(at, BLOCK), :]
        k_scr[pl.ds(at, BLOCK), :] = short[:, width : 2 * width]
        v_scr[pl.ds(at, BLOCK), :] = short[:, 2 * width :]
        return 0

    lax.fori_loop(0, blocks, block, 0)
    d_spec[...] = jnp.zeros_like(d_spec)

    def document(d, _):
        pack_document(dy_scr, packed, first[d], count[d])
        both = jnp.dot(fwd[...], packed[...], preferred_element_type=f32)
        re, im = both[:FREQ], both[FREQ:]
        hr, hi = spectrum[:FREQ], spectrum[FREQ:]
        answer = jnp.concatenate([re * hr + im * hi, im * hr - re * hi], axis=0).astype(bf16)
        result = jnp.dot(inv[...], answer, preferred_element_type=f32)
        ur, ui = seen[d, :FREQ].astype(f32), seen[d, FREQ:].astype(f32)
        d_spec[:FREQ] += re * ur + im * ui
        d_spec[FREQ:] += im * ur - re * ui
        for kb in range(LONGEST):

            @pl.when(kb < count[d])
            def _():
                at = pl.multiple_of((first[d] + kb) * BLOCK, BLOCK)
                du = result[kb * BLOCK : (kb + 1) * BLOCK, :]
                ds_scr[pl.ds(at, BLOCK), width : 2 * width] = du * v_scr[pl.ds(at, BLOCK), :]
                ds_scr[pl.ds(at, BLOCK), 2 * width :] = du * k_scr[pl.ds(at, BLOCK), :]

        return 0

    lax.fori_loop(0, seen.shape[0], document, 0)
    d_filter[...] = jnp.dot(inv[...], d_spec[...].astype(bf16), preferred_element_type=f32)
    d_taps[...] = jnp.zeros_like(d_taps)

    def back(n, _):
        at = pl.multiple_of(n * BLOCK, BLOCK)
        window = m_scr[pl.ds(at, BLOCK + 8), :]
        ahead = ds_scr[pl.ds(at, BLOCK + 8), :]
        one = table[pl.ds(at, BLOCK + 8), KEEP_ONE : KEEP_ONE + 1]
        two = table[pl.ds(at, BLOCK + 8), KEEP_TWO : KEEP_TWO + 1]
        live = table[pl.ds(at, BLOCK), LIVE : LIVE + 1]
        ds = ahead[:BLOCK]
        ahead_one = ahead * one
        ahead_two = ahead * two
        dm = (
            taps[0:1, :] * ds
            + taps[1:2, :] * ahead_one[1 : BLOCK + 1]
            + taps[2:3, :] * ahead_two[2 : BLOCK + 2]
        )
        d_taps[0:1, :] += jnp.sum(window[8:] * ds, axis=0, keepdims=True)
        d_taps[1:2, :] += jnp.sum(window[7 : BLOCK + 7] * ahead_one[:BLOCK], axis=0, keepdims=True)
        d_taps[2:3, :] += jnp.sum(window[6 : BLOCK + 6] * ahead_two[:BLOCK], axis=0, keepdims=True)
        within = pl.multiple_of((n % per_piece) * BLOCK, BLOCK)
        dz[order[n // per_piece], pl.ds(within, BLOCK), :] = (dm * live).astype(bf16)
        return 0

    lax.fori_loop(0, blocks, back, 0)


smem = pl.BlockSpec(memory_space=pltpu.SMEM)
vmem = pl.BlockSpec(memory_space=pltpu.VMEM)


def mixer_forward(order, first, count, proj, taps, table, spectrum, fwd, inv):
    pieces, rows, three = proj.shape
    width = three // 3
    slots = pieces * rows
    docs = first.shape[0]
    return pl.pallas_call(
        forward_kernel,
        out_shape=(
            jax.ShapeDtypeStruct((pieces, rows, width), bf16),
            jax.ShapeDtypeStruct((slots, width), f32),
            jax.ShapeDtypeStruct((docs, 2 * FREQ, width), bf16),
        ),
        in_specs=[smem] * 3 + [vmem] * 6,
        out_specs=(vmem,) * 3,
        scratch_shapes=[
            pltpu.VMEM((slots + 8, three), f32),
            pltpu.VMEM((slots, width), f32),
            pltpu.VMEM((slots, width), f32),
            pltpu.VMEM((SPAN, width), bf16),
        ],
        compiler_params=pltpu.CompilerParams(vmem_limit_bytes=40 * 2**20),
        cost_estimate=light,
        name="mixer_forward",
    )(order, first, count, proj, taps, table, spectrum, fwd, inv)


def mixer_backward(order, first, count, proj, d_gated, long_out, seen, taps, table, spectrum, fwd, inv):
    pieces, rows, three = proj.shape
    width = three // 3
    slots = pieces * rows
    docs = first.shape[0]
    return pl.pallas_call(
        backward_kernel,
        out_shape=(
            jax.ShapeDtypeStruct((pieces, rows, three), bf16),
            jax.ShapeDtypeStruct((SPAN, width), f32),
            jax.ShapeDtypeStruct((8, three), f32),
        ),
        in_specs=[smem] * 3 + [vmem] * 9,
        out_specs=(vmem,) * 3,
        scratch_shapes=[
            pltpu.VMEM((slots + 8, three), f32),
            pltpu.VMEM((slots, width), f32),
            pltpu.VMEM((slots, width), f32),
            pltpu.VMEM((slots, width), f32),
            pltpu.VMEM((slots + 8, three), f32),
            pltpu.VMEM((SPAN, width), bf16),
            pltpu.VMEM((2 * FREQ, width), f32),
        ],
        compiler_params=pltpu.CompilerParams(vmem_limit_bytes=48 * 2**20),
        cost_estimate=light,
        name="mixer_backward",
    )(order, first, count, proj, d_gated, long_out, seen, taps, table, spectrum, fwd, inv)


def layout(doc_blocks, doc_pad, slots):
    block_ends = jnp.cumsum(doc_blocks) * BLOCK
    starts = block_ends - doc_blocks * BLOCK
    places = jnp.arange(slots, dtype=jnp.int32)
    living = (places[None, :] >= starts[:, None]) & (
        places[None, :] < (block_ends - doc_pad)[:, None]
    )
    live = jnp.sum(living.astype(f32), axis=0)
    opening = jnp.sum((places[None, :] == starts[:, None]).astype(f32), axis=0)
    one = 1.0 - opening
    one = one * (places > 0)
    two = one * jnp.concatenate([jnp.zeros((1,), f32), one[:-1]])
    table = jnp.stack([live, one, two], axis=1)
    table = jnp.concatenate([table, jnp.zeros((8, 3), f32)], axis=0)
    return table, starts // BLOCK


def picked(index, count, values):
    hot = index[:, None] == jnp.arange(count)[None, :]
    shape = hot.shape + (1,) * (values.ndim - 1)
    return jnp.sum(jnp.where(hot.reshape(shape), values[None], 0), axis=1)


def body(
    tokens, w_in, w_out, gain_one, short_kernel, decay_rate, pole_angle, residue,
    gain_two, w_gate, w_up, w_down, doc_blocks, doc_pad, cotangent,
):
    wide, narrow = lax.axis_size("wide"), lax.axis_size("narrow")
    wide_at, narrow_at = lax.axis_index("wide"), lax.axis_index("narrow")
    outer = wide // 2
    _, local_rows, width = tokens.shape
    slots = local_rows * narrow
    even = slots // 2
    source = tokens[0].astype(f32)
    upstream_low = cotangent[0]
    poles = decay_rate.shape[1]
    own = w_in.shape[2]
    channels = own * outer
    hidden_units = w_gate.shape[1] * outer

    ring = np.array(ring_of(outer))
    ring_place = np.argsort(ring)
    tour = picked((wide_at // 2)[None], outer, jnp.asarray(ring_place, jnp.int32))[0]
    piece_places = (tour + jnp.asarray(ring_offsets(outer), jnp.int32)) % outer
    piece_outer = picked(piece_places, outer, jnp.asarray(ring, jnp.int32))
    sides = jnp.arange(2) ^ (wide_at % 2)
    offsets = list(range(0, narrow, 2)) + list(range(1, narrow, 2))
    place_of = np.argsort(np.array(offsets))
    order = picked(jnp.arange(narrow) ^ narrow_at, narrow, jnp.asarray(place_of, jnp.int32))
    narrow_of = jnp.asarray(offsets, jnp.int32) ^ narrow_at

    small = jnp.concatenate(
        [
            short_kernel.reshape(9, own),
            decay_rate.T,
            pole_angle.T,
            residue.T,
            gain_one[None],
            gain_two[None],
        ],
        axis=0,
    )
    small_pieces = gather_small(small)
    small_all = jnp.concatenate(small_pieces, axis=1)
    (first_own, first_other), first_stages = gather_rows(tokens[0], small_pieces[1:])
    gains = small_all[small.shape[0] - 2 :].reshape(2, outer, own)
    gains = jnp.stack([gains, swap(gains, "wide", 1)])
    gains = jnp.stack([gains] + [swap(gains, "narrow", k) for k in range(2, narrow, 2)])
    gains = jnp.concatenate([gains, swap(gains, "narrow", 1)], axis=0).astype(f32)
    gains = picked(order, narrow, gains).transpose(1, 3, 0, 2, 4)
    gains = picked(sides, 2, gains).transpose(1, 0, 2, 3, 4)
    hot = piece_outer[None, :] == jnp.arange(outer)[:, None]
    gains = jnp.sum(jnp.where(hot[:, :, None, None, None, None], gains[None], 0), axis=1)
    gain_all = gains.transpose(3, 0, 1, 2, 4).reshape(2, width)
    gain_first, gain_last = gain_all[0], gain_all[1]

    def place_gain(values):
        values = values.reshape(2, outer, 2, narrow, own).transpose(1, 2, 3, 0, 4)
        values = picked(piece_outer, outer, values).transpose(1, 0, 2, 3, 4)
        values = picked(sides, 2, values).transpose(2, 0, 1, 3, 4)
        values = picked(narrow_of, narrow, values)
        total = values[: narrow // 2] + swap(values[narrow // 2 :], "narrow", 1)
        summed = total[0]
        for k in range(1, narrow // 2):
            summed = summed + swap(total[k], "narrow", 2 * k)
        summed = summed[0] + swap(summed[1], "wide", 1)
        return summed

    documents = jnp.concatenate([doc_blocks, doc_pad], axis=0)
    [documents] = after([documents], small_pieces[1:])
    documents = (documents, swap(documents, "wide", 1))
    tables = [layout(rules[0], rules[1], slots) for rules in documents]

    shards = [w_in.transpose(0, 2, 1).reshape(3 * own, width), w_out, w_down.T, w_gate.T, w_up.T]
    weights = [Gather(shard) for shard in shards]
    in_all, out_all, down_all, gate_all, up_all = weights
    steps = outer // 2
    last = []
    for at in range(steps):
        last = ring_step([in_all, out_all], last)

    def normed(pieces):
        values = jnp.concatenate(pieces, axis=0).astype(f32)
        return (values * inverse_rms(values) * gain_first).astype(bf16)

    rows_first = lax.optimization_barrier([normed(first_own), normed(first_other)])
    rate_first = inverse_rms(source)
    (upstream_own, upstream_other), upstream_stages = gather_rows(
        upstream_low, first_stages[2], (), True
    )

    matrix = transform()
    fwd = jnp.asarray(matrix, bf16)
    inv = jnp.asarray(matrix.T / SPAN, bf16)

    block = small_all.astype(f32)
    taps = block[:9].reshape(3, 3 * channels)
    taps = jnp.concatenate([taps, jnp.zeros((5, 3 * channels), f32)], axis=0)
    decay = block[9 : 9 + poles][:, None, :]
    angle = block[9 + poles : 9 + 2 * poles][:, None, :]
    res_re = block[9 + 2 * poles : 9 + 3 * poles][:, None, :]
    res_im = -block[9 + 3 * poles : 9 + 4 * poles][:, None, :]
    lag = jnp.arange(8, dtype=f32)[None, :, None]
    fade = jnp.exp(-decay * lag)
    power_re, power_im = fade * jnp.cos(angle * lag), fade * jnp.sin(angle * lag)
    fade_step = jnp.exp(-decay * 8.0)
    step_re = jnp.broadcast_to(fade_step * jnp.cos(angle * 8.0), power_re.shape)
    step_im = jnp.broadcast_to(fade_step * jnp.sin(angle * 8.0), power_re.shape)
    filt = filter_taps(
        res_re * power_re - res_im * power_im,
        res_re * power_im + res_im * power_re,
        step_re,
        step_im,
    )
    spectrum = lax.dot_general(
        jnp.asarray(matrix),
        filt,
        (((1,), (0,)), ((), ())),
        precision=lax.Precision.HIGHEST,
        preferred_element_type=f32,
    )
    res_re, res_im = res_re[:, 0], -res_im[:, 0]

    in_pieces = [piece.reshape(3, own, width) for piece in in_all.pieces()]
    in_all = jnp.concatenate(in_pieces, axis=1).reshape(3 * channels, width)
    mixed = []
    for r in range(2):
        table, first = tables[r]
        proj = nt(rows_first[r], in_all).reshape(narrow, local_rows, 3 * channels)
        gated, long_out, seen = mixer_forward(
            order, first, documents[r][0], proj, taps, table, spectrum, fwd, inv
        )
        mixed.append((proj, gated.reshape(slots, channels), long_out, seen))
    out_last = last
    out_all = jnp.concatenate(out_all.pieces(), axis=0)
    parts = [slice(0, even), slice(even, slots)]
    ready = [mixed[0][1], after([mixed[1][1]], upstream_stages[0])[0]]
    odds = [nn(ready[r][parts[1]], out_all).astype(bf16) for r in range(2)]
    cores = [swap(odd, "narrow", 1) for odd in odds]
    for at in range(steps - 1):
        last = ring_step([down_all, gate_all], last, odds)
    last_two = last
    for at in range(steps - 1):
        last_two = ring_step([up_all], last_two)
    ready = after([mixed[0][1], mixed[1][1]], upstream_stages[0])
    evens = [nn(ready[r][parts[0]], out_all).astype(bf16) for r in range(2)]
    mixer_out, stages = scatter_rows(
        evens[0], cores[0], evens[1], cores[1], upstream_stages[1] + last
    )
    middle = source + mixer_out
    rate_last = inverse_rms(middle)
    rows_upstream = jnp.concatenate(upstream_own + upstream_other, axis=0)
    low_second = (middle * rate_last * gain_last).astype(bf16)
    (second_own, second_other), second_stages = gather_rows(low_second, last_two + upstream_stages[2])
    rows_second = jnp.concatenate(second_own + second_other, axis=0)
    last = ring_step([down_all, gate_all, up_all], last_two, second_stages[1])

    down_all, gate_all = [jnp.concatenate(w.pieces(), axis=0) for w in (down_all, gate_all)]
    up_all = jnp.concatenate(up_all.pieces(), axis=0)
    d_hidden = nt(down_all, rows_upstream)
    gate_pre = nt(gate_all, rows_second)
    up_pre = nt(up_all, rows_second)
    sig = jax.nn.sigmoid(gate_pre)
    silu = gate_pre * sig
    hidden = (silu * up_pre).astype(bf16)
    d_gate = (d_hidden * up_pre * sig * (1.0 + gate_pre * (1.0 - sig))).astype(bf16)
    d_up = (d_hidden * silu).astype(bf16)
    grad_down = product(hidden, rows_upstream, "nn", bf16)
    d_gate, d_up = after([d_gate, d_up], [grad_down])
    parts = [slice(p, p + even) for p in range(0, 2 * slots, even)]

    def second_share(n):
        p = parts[n]
        return (tn(d_gate[:, p], gate_all) + tn(d_up[:, p], up_all)).astype(bf16)

    odds = [second_share(n) for n in (1, 3)]
    cores = [swap(odd, "narrow", 1) for odd in odds]
    evens = [second_share(0), second_share(2)]
    d_second, stages = scatter_rows(evens[0], cores[0], evens[1], cores[1])
    upstream = upstream_low.astype(f32)
    d_middle = upstream + norm_back(middle, rate_last, gain_last, d_second)
    (middle_own, middle_other), middle_stages = gather_rows(d_middle.astype(bf16))
    rows_dmiddle = [jnp.concatenate(middle_own, axis=0), jnp.concatenate(middle_other, axis=0)]
    grads = [Scatter(jnp.split(grad_down, outer, axis=0))]
    [d_gate] = after([d_gate], cores + evens)
    grad_gate = product(d_gate, rows_second, "nn", bf16)
    [d_up] = after([d_up], stages[0] + [grad_gate])
    grad_up = product(d_up, rows_second, "nn", bf16)
    [hidden] = after([hidden], [grad_up])
    down_shares = [product(hidden, down_all, "tn", bf16, n) for n in (0, 1)]
    down_shares += [product(hidden, down_all, "tn", bf16, n) for n in (2, 3)]
    pair = [Scatter(jnp.split(grad, outer, axis=0)) for grad in (grad_gate, grad_up)]
    grads += pair
    last = ring_step(grads, (), middle_stages[1])
    down_shares = after(down_shares, middle_stages[1])
    down_cores = [swap(down_shares[n], "narrow", 1) for n in (1, 3)]
    down_out, down_stages = scatter_rows(
        down_shares[0], down_cores[0], down_shares[2], down_cores[1]
    )
    block_output = (middle + down_out).astype(bf16)
    grad_gain_two = jnp.sum(d_second * middle * rate_last, axis=0)

    grad_out = sum(tn(mixed[r][1], rows_dmiddle[r]) for r in range(2)).astype(bf16)
    halves = (slice(0, even), slice(even, slots))
    shares, d_rows, grad_gain_one, d_filter, d_taps = [None, None], [None, None], 0.0, 0.0, 0.0
    for r in range(2):
        proj, gated, long_out, seen = mixed[r]
        table, first = tables[r]
        d_gated = nt(rows_dmiddle[r], out_all).reshape(narrow, local_rows, channels)
        if r == 1:
            [d_gated] = after([d_gated], [grad_out, *shares[0], *down_stages[0]])
        dz, d_filter_row, d_taps_row = mixer_backward(
            order, first, documents[r][0], proj, d_gated, long_out, seen, taps, table,
            spectrum, fwd, inv,
        )
        d_rows[r] = dz.reshape(slots, 3 * channels)
        d_filter, d_taps = d_filter + d_filter_row, d_taps + d_taps_row
        if r == 0:
            shares[r] = [nn(d_rows[r][p], in_all).astype(bf16) for p in halves]
    [ready] = after([d_rows[1]], down_stages[1])
    odd = nn(ready[halves[1]], in_all).astype(bf16)
    cores = [swap(shares[0][1], "narrow", 1), swap(odd, "narrow", 1)]
    ready = after(d_rows, [odd])
    grad_in = sum(tn(ready[r], rows_first[r]) for r in range(2)).astype(bf16)
    for at in range(1, steps):
        last = ring_step(grads, last, [grad_in])
    [ready] = after([d_rows[1]], [grad_in] + cores)
    shares[1] = [nn(ready[halves[0]], in_all).astype(bf16), odd]
    d_normed, stages = scatter_rows(shares[0][0], cores[0], shares[1][0], cores[1])
    input_grad = (d_middle + norm_back(source, rate_first, gain_first, d_normed)).astype(bf16)
    for r in range(2):
        for n, share in enumerate(after(shares[r], [shares[1][0]])):
            rows = rows_first[r][n * even : (n + 1) * even]
            grad_gain_one = grad_gain_one + jnp.sum(share.astype(f32) * rows.astype(f32), axis=0)
    chunks = grad_in.reshape(3, outer, own, width)
    in_sum = Scatter([chunks[:, j].reshape(3 * own, width) for j in range(outer)])
    out_sum = Scatter(jnp.split(grad_out, outer, axis=0))
    last = ring_step([in_sum, out_sum], last, stages[0])
    d_filter, *_ = after([d_filter], last + stages[0])
    gain_grads = jnp.stack([grad_gain_one / gain_first, grad_gain_two])
    [gain_grads] = after([gain_grads], stages[0])
    sum_re, sum_im, mom_re, mom_im = filter_moments(d_filter, step_re, step_im)
    full_re = lag * sum_re + 8.0 * mom_re
    full_im = lag * sum_im + 8.0 * mom_im
    grad_re = jnp.sum(power_re * sum_re - power_im * sum_im, axis=1)
    grad_im = jnp.sum(power_re * sum_im + power_im * sum_re, axis=1)
    lag_re = jnp.sum(power_re * full_re - power_im * full_im, axis=1)
    lag_im = jnp.sum(power_re * full_im + power_im * full_re, axis=1)
    small_grad = jnp.concatenate(
        [
            d_taps[:3].reshape(9, channels),
            -(res_re * lag_re + res_im * lag_im),
            res_im * lag_re - res_re * lag_im,
            grad_re,
            grad_im,
        ],
        axis=0,
    ).astype(bf16)
    gain_sums = place_gain(gain_grads).transpose(1, 0, 2).reshape(2, channels)
    gain_high = gain_sums.astype(bf16)
    gain_low = (gain_sums - gain_high.astype(f32)).astype(bf16)
    small_grad = jnp.concatenate([small_grad, gain_high, gain_low], axis=0)
    [small_grad] = after([small_grad], stages[1])
    small_share = scatter_small(jnp.split(small_grad, outer, axis=1))
    gain_share = small_share[-4:-2] + small_share[-2:]
    for at in range(1, steps):
        last = ring_step([in_sum, out_sum], last, [small_share])

    at = 9 + poles
    return (
        block_output[None],
        input_grad[None],
        in_sum.total.reshape(3, own, width).transpose(0, 2, 1),
        out_sum.total,
        gain_share[0],
        small_share[:9].reshape(3, 3, own),
        small_share[9:at].T,
        small_share[at : at + poles].T,
        small_share[at + poles : at + 3 * poles].T,
        gain_share[1],
        grads[1].total.T,
        grads[2].total.T,
        grads[0].total.T,
    )


def solution(mesh):
    both = ("wide", "narrow")
    return jax.shard_map(
        body,
        mesh=mesh,
        in_specs=(
            P("wide", "narrow", None),
            P(None, None, both),
            P(both, None),
            P(both),
            P(None, None, both),
            P(both, None),
            P(both, None),
            P(both, None),
            P(both),
            P(None, both),
            P(None, both),
            P(None, both),
            P("wide", None),
            P("wide", None),
            P("wide", "narrow", None),
        ),
        out_specs=(
            P("wide", "narrow", None),
            P("wide", "narrow", None),
            P(None, None, both),
            P(both, None),
            P(both),
            P(None, None, both),
            P(both, None),
            P(both, None),
            P(both, None),
            P(both),
            P(None, both),
            P(None, both),
            P(None, both),
        ),
        check_vma=False,
    )
```
